32 devices in a mesh: dp: 16 (over z, y, core), fsdp: 2 (over x).
Axes of the slice: x: 2, y: 2, z: 4, core: 2. Of those that a mesh axis runs over, the one named last changes fastest.
Arguments:
- latents: bfloat16 [32768, 768], P(('dp', 'fsdp')), may hold values from -6 to 6
- size_tags: int32 [32], P(('dp', 'fsdp')), may hold values from 0 to 1
- timesteps: int32 [32, 4], P(('dp', 'fsdp')), may hold values from 0 to 999
- classes: int32 [32, 4], P(('dp', 'fsdp')), may hold values from 0 to 999
- step_table: bfloat16 [1000, 768], P('fsdp', 'dp'), may hold values from -5 to 5
- class_table: bfloat16 [1000, 768], P('fsdp', 'dp'), may hold values from -5 to 5
- modulation_weight: bfloat16 [768, 4608], P('fsdp', 'dp'), may hold values from -0.21875 to 0.21875
- attn_kernel: bfloat16 [9, 768], P(None, 'dp'), may hold values from -2 to 2
- qkv_weight: bfloat16 [768, 2304], P('fsdp', 'dp'), may hold values from -0.21875 to 0.21875
- proj_weight: bfloat16 [768, 768], P('fsdp', 'dp'), may hold values from -1.75 to 1.75
- expand_weight: bfloat16 [768, 3072], P('fsdp', 'dp'), may hold values from -0.21875 to 0.21875
- ffn_kernel: bfloat16 [9, 3072], P(None, 'dp'), may hold values from -2 to 2
- shrink_weight: bfloat16 [3072, 768], P('fsdp', 'dp'), may hold values from -0.109375 to 0.109375
- cotangent: bfloat16 [32768, 768], P(('dp', 'fsdp')), may hold values from -6 to 6
Outputs:
- block_output: bfloat16 [32768, 768], P(('dp', 'fsdp'))
- input_grad: float32 [32768, 768], P(('dp', 'fsdp'))
- step_table_grad: float32 [1000, 768], P('fsdp', 'dp')
- class_table_grad: float32 [1000, 768], P('fsdp', 'dp')
- modulation_grad: float32 [768, 4608], P('fsdp', 'dp')
- attn_kernel_grad: float32 [9, 768], P(None, 'dp')
- qkv_grad: float32 [768, 2304], P('fsdp', 'dp')
- proj_grad: float32 [768, 768], P('fsdp', 'dp')
- expand_grad: float32 [768, 3072], P('fsdp', 'dp')
- ffn_kernel_grad: float32 [9, 3072], P(None, 'dp')
- shrink_grad: float32 [3072, 768], P('fsdp', 'dp')
The draws below stay inside these ranges and needn't reach their ends.
Inputs may be any that keep to these rules, and one draw needn't show every extreme that they name: `size_tags`: a slot with tag 0 holds one item of 1024 tokens, with tag 1 four items of 16 x 16 tokens. `timesteps`: in a slot with tag 0 only entry 0 is used. `classes`: in a slot with tag 0 only entry 0 is used.
All inputs are finite; a program needn't handle non-finite values.
Results may differ from the reference program's by a relative error of at most 0.019.
The reference program's roundings to bfloat16 on the way count: a program that leaves them out, or rounds other values in their place, can miss the bound.
Values may be sent and summed in bfloat16 or wider, within the bound.
No kernel may reach another device: no remote copies, remote signals or barrier semaphores. Data moves between devices by JAX's collectives and lax.ppermute only.
A program may use at most 384 MiB of HBM per device.

```python
import jax
import jax.numpy as jnp
from jax import lax

D = 768
H = 12
HD = 64
FF = 3072
STEPS = 1000
CLASSES = 1000
SIDE = 32
GROUP = 256
SLOTS = 32
TOKENS = 32768


def place_ends(values, own_key, least, largest):
    spot = [jax.random.randint(jax.random.fold_in(own_key, axis), (), 0, length) for axis, length in enumerate(values.shape)]
    longest = values.shape.index(max(values.shape))
    beside = spot[:longest] + [(spot[longest] + 1) % values.shape[longest]] + spot[longest + 1:]
    return values.at[tuple(spot)].set(least).at[tuple(beside)].set(largest)


def block_scale(rng, shape, cuts, smallest, high):
    loudness, own = 1.0, jax.random.fold_in(rng, 6)
    for dim, blocks in cuts:
        draws = jnp.exp(jax.random.uniform(jax.random.fold_in(own, dim), (blocks,), jnp.float32, smallest / len(cuts), high / len(cuts)))
        loudness = loudness * jnp.repeat(draws, shape[dim] // blocks).reshape([-1 if axis == dim else 1 for axis in range(len(shape))])
    return loudness


def noise(stream_key, shape, deviation, reach, cuts=(), kind=jnp.bfloat16):
    factor_of = block_scale(stream_key, shape, cuts, -0.22, 0.18) if cuts else 1.0
    drawn = jax.random.normal(stream_key, shape, jnp.float32) * deviation * factor_of
    return jnp.minimum(jnp.maximum(drawn, -reach), reach).astype(kind)


def setup_inputs(seed: int = 0) -> dict:
    keys = jax.random.split(jax.random.key(seed), 15)
    latents = noise(keys[0], (TOKENS, D), 1.0, 6.0, ((0, 32),))
    size_tags = place_ends(jax.random.randint(keys[1], (SLOTS,), 0, 2), jax.random.fold_in(keys[1], 1), 0, 1).astype(jnp.int32)
    timesteps = place_ends(jax.random.randint(keys[2], (SLOTS, 4), 0, STEPS), jax.random.fold_in(keys[2], 1), 0, STEPS - 1).astype(jnp.int32)
    classes = place_ends(jax.random.randint(keys[3], (SLOTS, 4), 0, CLASSES), jax.random.fold_in(keys[3], 1), 0, CLASSES - 1).astype(jnp.int32)
    step_table = noise(keys[4], (STEPS, D), 1.0, 5.0, ((0, 2), (1, 16)))
    class_table = noise(keys[5], (CLASSES, D), 1.0, 5.0, ((0, 2), (1, 16)))
    modulation_weight = noise(keys[6], (D, 6 * D), D ** -0.5, 0.21875, ((0, 2), (1, 16)))
    attn_kernel = noise(keys[7], (9, D), 0.33, 2.0, ((1, 16),))
    qkv_weight = noise(keys[8], (D, 3 * D), D ** -0.5, 0.21875, ((0, 2), (1, 16)))
    proj_weight = noise(keys[9], (D, D), (D * 16 // (SIDE * SIDE)) ** -0.5, 1.75, ((0, 2), (1, 16)))
    expand_weight = noise(keys[10], (D, FF), D ** -0.5, 0.21875, ((0, 2), (1, 16)))
    ffn_kernel = noise(keys[11], (9, FF), 0.33, 2.0, ((1, 16),))
    shrink_weight = noise(keys[12], (FF, D), FF ** -0.5, 0.109375, ((0, 2), (1, 16)))
    cotangent = noise(keys[13], (TOKENS, D), 1.0, 6.0, ((0, 32),))
    return {"latents": latents, "size_tags": size_tags, "timesteps": timesteps, "classes": classes, "step_table": step_table, "class_table": class_table, "modulation_weight": modulation_weight, "attn_kernel": attn_kernel, "qkv_weight": qkv_weight, "proj_weight": proj_weight, "expand_weight": expand_weight, "ffn_kernel": ffn_kernel, "shrink_weight": shrink_weight, "cotangent": cotangent}


@jax.custom_vjp
def low(v):
    return lax.optimization_barrier(v.astype(jnp.bfloat16)).astype(jnp.float32)

@jax.custom_vjp
def low_back(v):
    return v

def low_keep(v):
    return (low(v), None)

def low_pass(kept, grad):
    return (grad,)

def back_keep(v):
    return (v, None)

def back_low(kept, grad):
    return (low(grad),)
low.defvjp(low_keep, low_pass)
low_back.defvjp(back_keep, back_low)

def product(left, right):
    return jnp.dot(left, right, precision=lax.Precision.HIGHEST)

def token_items(size_tag):
    row_index = jnp.arange(SIDE, dtype=jnp.int32)
    quadrant = row_index // (SIDE // 2)
    layout = quadrant[:, None] * 2 + quadrant[None, :]
    return (layout * size_tag).reshape(SIDE * SIDE)

def edge_masks(size_tag):
    row_index = jnp.arange(SIDE, dtype=jnp.int32)
    half_side = SIDE // 2
    collected = []
    for offset in (-1, 0, 1):
        neighbour = row_index + offset
        inside = (neighbour >= 0) & (neighbour < SIDE)
        same_item = jnp.maximum(neighbour, 0) // half_side == row_index // half_side
        collected.append((inside & (same_item | (size_tag == 0))).astype(jnp.float32))
    return collected

def depthwise(field, kernel, validity):
    channels = field.shape[-1]
    layout = field.reshape(SIDE, SIDE, channels)
    padded = jnp.pad(layout, ((1, 1), (1, 1), (0, 0)))
    summed = jnp.zeros_like(layout)
    for row_step in range(3):
        for col_step in range(3):
            window = padded[row_step:row_step + SIDE, col_step:col_step + SIDE]
            allowed = validity[row_step][:, None] * validity[col_step][None, :]
            summed = summed + window * allowed[:, :, None] * kernel[row_step * 3 + col_step]
    return summed.reshape(SIDE * SIDE, channels)

def to_groups(field):
    channels = field.shape[-1]
    layout = field.reshape(SIDE // 2, 2, SIDE // 2, 2, channels)
    return layout.transpose(1, 3, 0, 2, 4).reshape(4, GROUP, channels)

def from_groups(field):
    channels = field.shape[-1]
    layout = field.reshape(2, 2, SIDE // 2, SIDE // 2, channels)
    return layout.transpose(2, 0, 3, 1, 4).reshape(SIDE * SIDE, channels)

def same_item_mask(size_tag):
    position = jnp.arange(SIDE // 2, dtype=jnp.int32) // (SIDE // 4)
    labels = ((position[:, None] * 2 + position[None, :]) * size_tag).reshape(GROUP)
    return labels[:, None] == labels[None, :]

def normalize(values):
    centre = values - lax.optimization_barrier(jnp.mean(values, axis=-1, keepdims=True))
    variance = lax.optimization_barrier(jnp.mean(centre * centre, axis=-1, keepdims=True))
    return centre * lax.rsqrt(variance + 1e-06)

def per_token(mod_rows, labels):
    pieces = []
    for component in range(6):
        column = mod_rows[:, component * D:(component + 1) * D]
        chosen = column[0][None, :] * jnp.ones((labels.shape[0], 1), jnp.float32)
        for other_item in range(1, 4):
            chosen = jnp.where((labels == other_item)[:, None], column[other_item][None, :], chosen)
        pieces.append(chosen)
    return tuple(pieces)

def softmax_rows(scores):
    highest = lax.optimization_barrier(jnp.max(scores, axis=-1, keepdims=True))
    raised = jnp.exp(scores - highest)
    return raised / lax.optimization_barrier(jnp.sum(raised, axis=-1, keepdims=True))

def block(tokens, size_tag, steps_row, class_row, step_table, class_table, modulation_weight, attn_kernel, qkv_weight, proj_weight, expand_weight, ffn_kernel, shrink_weight):
    steps_hot = (steps_row[:, None] == jnp.arange(STEPS, dtype=jnp.int32)[None, :]).astype(jnp.float32)
    class_hot = (class_row[:, None] == jnp.arange(CLASSES, dtype=jnp.int32)[None, :]).astype(jnp.float32)
    cond = product(steps_hot, step_table) + product(class_hot, class_table)
    activated = low(jax.nn.silu(cond))
    mod_rows = low_back(product(activated, modulation_weight))
    labels = token_items(size_tag)
    shift_one, scale_one, gate_one, shift_two, scale_two, gate_two = per_token(mod_rows, labels)
    validity = edge_masks(size_tag)
    first = normalize(tokens) * (1.0 + scale_one) + shift_one
    conv_in = low(depthwise(first, attn_kernel, validity))
    qkv = low(low_back(product(conv_in, qkv_weight)))
    grouped = to_groups(qkv).reshape(4, GROUP, 3, H, HD)
    queries = grouped[:, :, 0]
    key_rows = grouped[:, :, 1]
    value_rows = grouped[:, :, 2]
    raw = jnp.einsum('gqhd,gkhd->ghqk', queries, key_rows, precision=lax.Precision.HIGHEST)
    scores = low_back(raw * HD ** (-0.5))
    scores = jnp.where(same_item_mask(size_tag)[None, None], scores, -1e+30)
    probs = low(softmax_rows(scores))
    mixed = jnp.einsum('ghqk,gkhd->gqhd', probs, value_rows, precision=lax.Precision.HIGHEST)
    merged = low(low_back(from_groups(mixed.reshape(4, GROUP, D))))
    attn = low_back(product(merged, proj_weight))
    resid = tokens + gate_one * attn
    second = low(normalize(resid) * (1.0 + scale_two) + shift_two)
    expanded = low_back(product(second, expand_weight))
    conved = depthwise(expanded, ffn_kernel, validity)
    hidden = low(jax.nn.gelu(conved, approximate=True))
    shrunk = low_back(product(hidden, shrink_weight))
    return resid + gate_two * shrunk

def reference(latents, size_tags, timesteps, classes, step_table, class_table, modulation_weight, attn_kernel, qkv_weight, proj_weight, expand_weight, ffn_kernel, shrink_weight, cotangent):
    slot_count = size_tags.shape[0]
    tokens = latents.astype(jnp.float32).reshape(slot_count, SIDE * SIDE, D)
    weights = (step_table.astype(jnp.float32), class_table.astype(jnp.float32), modulation_weight.astype(jnp.float32), attn_kernel.astype(jnp.float32), qkv_weight.astype(jnp.float32), proj_weight.astype(jnp.float32), expand_weight.astype(jnp.float32), ffn_kernel.astype(jnp.float32), shrink_weight.astype(jnp.float32))

    def forward(tokens, step_w, class_w, mod_w, attn_k, qkv_w, proj_w, expand_w, ffn_k, shrink_w):

        def one_slot(packed):
            rows, size_tag, steps_row, class_row = packed
            return block(rows, size_tag, steps_row, class_row, step_w, class_w, mod_w, attn_k, qkv_w, proj_w, expand_w, ffn_k, shrink_w)
        return lax.map(jax.checkpoint(one_slot), (tokens, size_tags, timesteps, classes))
    outputs, pullback = jax.vjp(forward, tokens, *weights)
    grads = pullback(cotangent.astype(jnp.float32).reshape(slot_count, SIDE * SIDE, D))
    return (outputs.reshape(-1, D).astype(jnp.bfloat16), grads[0].reshape(-1, D), grads[1], grads[2], grads[3], grads[4], grads[5], grads[6], grads[7], grads[8], grads[9])
```

```python
import functools

import jax
import jax.numpy as jnp
from jax import lax
from jax.experimental import pallas as pl
from jax.experimental.pallas import tpu as pltpu
from jax.sharding import PartitionSpec as P

D = 768
H = 12
HD = 64
FF = 3072
SIDE = 32
GROUP = 256
TOK = SIDE * SIDE
EPS = 1e-06
NJ, NK, UR, UC = 16, 2, 48, 384
UNITS = 12
CHUNK = 384
MIB = 1024 * 1024
BF = jnp.bfloat16
F32 = jnp.float32
GELU_A = 0.7978845608028654
GELU_B = GELU_A * 0.044715


def dot(left, right, left_dim, right_dim):
    return lax.dot_general(
        left, right, (((left_dim,), (right_dim,)), ((), ())), preferred_element_type=F32
    )


def params(limit=56):
    return pltpu.CompilerParams(vmem_limit_bytes=limit * MIB)


def whole(shape):
    zeros = (0,) * len(shape)
    return pl.BlockSpec(shape, lambda *ids: zeros, pipeline_mode=pl.Buffered(1))


SMEM_SPEC = pl.BlockSpec(memory_space=pltpu.SMEM)


def group_place(natural):
    pair, odd_row = natural // 64, (natural // 32) % 2
    column, odd_column = (natural % 32) // 2, natural % 2
    return (2 * odd_row + odd_column) * 64 + pair * 16 + column


def ungroup_matrix():
    natural = lax.broadcasted_iota(jnp.int32, (256, 256), 0)
    grouped = lax.broadcasted_iota(jnp.int32, (256, 256), 1)
    return jnp.where(group_place(natural) == grouped, 1.0, 0.0).astype(BF)


def group_matrix():
    natural = lax.broadcasted_iota(jnp.int32, (256, 256), 1)
    grouped = lax.broadcasted_iota(jnp.int32, (256, 256), 0)
    return jnp.where(group_place(natural) == grouped, 1.0, 0.0).astype(BF)


def norm_stats(values):
    centre = values - jnp.mean(values, axis=-1, keepdims=True)
    variance = jnp.mean(centre * centre, axis=-1, keepdims=True)
    scale = lax.rsqrt(variance + EPS)
    return centre * scale, scale


def prepare_kernel(latents, cotangent, tokens, gradient, norm, scale):
    order = group_matrix()
    gathered = dot(order, latents[...], 1, 0)
    gradient[...] = dot(order, cotangent[...], 1, 0).reshape(4, 64, D).astype(BF)
    tokens[...] = gathered.reshape(4, 64, D).astype(BF)
    normal, factor = norm_stats(gathered)
    norm[...] = normal.reshape(4, 64, D)
    scale[...] = factor.reshape(4, 64, 1)


def prepare(latents, cotangent):
    flat = pl.BlockSpec((256, D), lambda i: (i, 0))
    split = pl.BlockSpec((4, 64, D), lambda i: (0, i, 0))
    return pl.pallas_call(
        prepare_kernel,
        grid=(4,),
        in_specs=[flat, flat],
        out_specs=[split, split, split, pl.BlockSpec((4, 64, 1), lambda i: (0, i, 0))],
        out_shape=[
            jax.ShapeDtypeStruct((4, GROUP, D), BF),
            jax.ShapeDtypeStruct((4, GROUP, D), BF),
            jax.ShapeDtypeStruct((4, GROUP, D), F32),
            jax.ShapeDtypeStruct((4, GROUP, 1), F32),
        ],
        compiler_params=params(),
        name="prepare",
    )(latents, cotangent)


def edge_columns(tag):
    place = lax.broadcasted_iota(jnp.int32, (16, 128), 0)
    left = jnp.where((place == 0) | ((place == 8) & (tag == 1)), 0.0, 1.0)
    right = jnp.where((place == 15) | ((place == 7) & (tag == 1)), 0.0, 1.0)
    return left, right


def neighbours(even, odd, left, right):
    return pltpu.roll(odd, 1, 0) * left, pltpu.roll(even, 15, 0) * right


def conv_rows(load, kernel, left, right, keep, emit):
    above = None
    partial = None
    for row in range(SIDE + 1):
        taps = None
        if row < SIDE:
            a, p = row % 2, row // 2
            even, odd = load(2 * a, p), load(2 * a + 1, p)
            odd_left, even_right = neighbours(even, odd, left, right)
            taps = []
            for tap in range(3):
                k = [kernel[3 * tap + b] for b in range(3)]
                taps.append(
                    (
                        k[0] * odd_left + k[1] * even + k[2] * odd,
                        k[0] * even + k[1] * odd + k[2] * even_right,
                    )
                )
        crossing = row == SIDE // 2
        if partial is not None:
            a, p = (row - 1) % 2, (row - 1) // 2
            for b in range(2):
                value = partial[b]
                if taps is not None:
                    below = taps[2][b]
                    value = value + (below * keep if crossing else below)
                emit(2 * a + b, p, value)
        if taps is not None:
            partial = []
            for b in range(2):
                value = taps[1][b]
                if above is not None:
                    value = value + (above[b] * keep if crossing else above[b])
                partial.append(value)
            above = taps[0]


def conv_back_rows(load_grad, load_field, kernel, left, right, keep, emit):
    sums = [jnp.zeros((16, 128), F32) for _ in range(9)]
    from_above = None
    partial = None
    field_above = None
    field = (load_field(0, 0), load_field(1, 0))
    for row in range(SIDE + 1):
        crossing = row == SIDE // 2
        taps = None
        if row < SIDE:
            a, p = row % 2, row // 2
            even, odd = load_grad(2 * a, p), load_grad(2 * a + 1, p)
            odd_left, even_right = neighbours(even, odd, left, right)
            picks = ((odd, even, odd_left), (even_right, odd, even))
            taps = []
            for tap in range(3):
                k = [kernel[3 * tap + b] for b in range(3)]
                taps.append(
                    tuple(k[0] * x[0] + k[1] * x[1] + k[2] * x[2] for x in picks)
                )
            field_below = None
            if row + 1 < SIDE:
                a, p = (row + 1) % 2, (row + 1) // 2
                field_below = (load_field(2 * a, p), load_field(2 * a + 1, p))
            for tap, rows in enumerate((field_above, field, field_below)):
                if rows is None:
                    continue
                if (tap == 0 and crossing) or (tap == 2 and row + 1 == SIDE // 2):
                    rows = (rows[0] * keep, rows[1] * keep)
                for b in range(3):
                    sums[3 * tap + b] = (
                        sums[3 * tap + b] + rows[0] * picks[0][b] + rows[1] * picks[1][b]
                    )
            field_above, field = field, field_below
        if partial is not None:
            a, p = (row - 1) % 2, (row - 1) // 2
            for b in range(2):
                value = partial[b]
                if taps is not None:
                    value = value + (taps[0][b] * keep if crossing else taps[0][b])
                emit(2 * a + b, p, value)
        if taps is not None:
            partial = []
            for b in range(2):
                value = taps[1][b]
                if from_above is not None:
                    value = value + (from_above[b] * keep if crossing else from_above[b])
                partial.append(value)
            from_above = taps[2]
    return sums


def first_conv_kernel(tag_ref, norm, mods, kernel, out):
    tag = tag_ref[0]
    left, right = edge_columns(tag)
    keep = 1.0 - tag.astype(F32)
    taps = [jnp.broadcast_to(kernel[i : i + 1, :], (16, 128)) for i in range(9)]

    def load(g, p):
        q = 2 * (p // 8)
        shift = mods[0, q : q + 2].reshape(16, 128)
        scale = mods[1, q : q + 2].reshape(16, 128)
        return norm[g, p * 16 : p * 16 + 16, :] * (1.0 + scale) + shift

    def emit(g, p, value):
        out[g, p * 16 : p * 16 + 16, :] = value.astype(BF)

    conv_rows(load, taps, left, right, keep, emit)


def first_conv(tag, norm, mods, kernel):
    return pl.pallas_call(
        first_conv_kernel,
        grid=(D // 128,),
        in_specs=[
            SMEM_SPEC,
            pl.BlockSpec((4, GROUP, 128), lambda i: (0, 0, i)),
            pl.BlockSpec((6, 4, 8, 128), lambda i: (0, 0, 0, i)),
            pl.BlockSpec((9, 128), lambda i: (0, i)),
        ],
        out_specs=pl.BlockSpec((4, GROUP, 128), lambda i: (0, 0, i)),
        out_shape=jax.ShapeDtypeStruct((4, GROUP, D), BF),
        compiler_params=params(),
        name="first_conv",
    )(tag, norm, mods, kernel)


def join_rows(block, target):
    rows = block.shape[0] * block.shape[2] * UR
    for k in range(NK):
        target[:, k * UC : (k + 1) * UC] = block[:, k].reshape(rows, UC)


def quadrant_rows(mods, index, half):
    return mods[index, pl.ds(2 * half, 2)].reshape(1, 2, 8, D)


def item_bias(tag):
    def label(dim):
        place = lax.broadcasted_iota(jnp.int32, (GROUP, GROUP), dim)
        return 2 * (place // 128) + (place % 16) // 8

    return jnp.where((label(0) == label(1)) | (tag == 0), 0.0, -1e30)


def attend_kernel(
    tag_ref, conv_in, tokens, mods, w_qkv, w_proj, qkv, merged, attn, resid, second, lse,
    full_qkv, full_proj, bias, mixed_t,
):
    @pl.when(pl.program_id(0) == 0)
    def _():
        join_rows(w_qkv, full_qkv)
        join_rows(w_proj, full_proj)
        bias[...] = item_bias(tag_ref[0])

    qkv[0] = dot(full_qkv[...], conv_in[0], 1, 1).astype(BF)

    def head(h, _):
        rows = pl.ds(pl.multiple_of(h * HD, HD), HD)
        queries = qkv[0, rows, :] * jnp.asarray(HD**-0.5, BF)
        keys = qkv[0, pl.ds(pl.multiple_of(D + h * HD, HD), HD), :]
        values = qkv[0, pl.ds(pl.multiple_of(2 * D + h * HD, HD), HD), :]
        scores = dot(keys, queries, 0, 0) + bias[...]
        highest = jnp.max(scores, axis=0, keepdims=True)
        raised = jnp.exp(scores - highest)
        total = jnp.sum(raised, axis=0, keepdims=True)
        probs = (raised * (1.0 / total)).astype(BF)
        lse[0, pl.ds(h, 1), :] = highest + jnp.log(total)
        mixed_t[rows, :] = dot(values, probs, 1, 0).astype(BF)
        return 0

    lax.fori_loop(0, H, head, 0)
    merged[0] = mixed_t[...].T
    projected = dot(merged[0], full_proj[...], 1, 1)
    attn[0] = projected.astype(BF)
    gate = mods[2].reshape(2, 1, 2, 8, D)
    resid[0] = (
        tokens[0].astype(F32) + (projected.reshape(2, 8, 2, 8, D) * gate).reshape(GROUP, D)
    )

    def rows_norm(i, _):
        rows = pl.ds(pl.multiple_of(i * 64, 64), 64)
        normal, _ = norm_stats(resid[0, rows, :])
        half = i // 2
        scaled = normal.reshape(4, 2, 8, D) * (1.0 + quadrant_rows(mods, 4, half))
        value = scaled + quadrant_rows(mods, 3, half)
        second[0, rows, :] = value.reshape(64, D).astype(BF)
        return 0

    lax.fori_loop(0, 4, rows_norm, 0)


def group_spec(*shape):
    return pl.BlockSpec((1,) + shape, lambda g: (g,) + (0,) * len(shape))


def unit_spec(units, start):
    shape = (NJ, NK, units, UR, UC)
    return pl.BlockSpec(
        shape, lambda g: (0, 0, start // units, 0, 0), pipeline_mode=pl.Buffered(1)
    )


def attend(tag, conv_in, tokens, mods, packed):
    return pl.pallas_call(
        attend_kernel,
        grid=(4,),
        in_specs=[
            SMEM_SPEC,
            group_spec(GROUP, D),
            group_spec(GROUP, D),
            whole((6, 4, 8, D)),
            unit_spec(3, 0),
            unit_spec(1, 3),
        ],
        out_specs=[
            group_spec(3 * D, GROUP),
            group_spec(GROUP, D),
            group_spec(GROUP, D),
            group_spec(GROUP, D),
            group_spec(GROUP, D),
            group_spec(16, GROUP),
        ],
        out_shape=[
            jax.ShapeDtypeStruct((4, 3 * D, GROUP), BF),
            jax.ShapeDtypeStruct((4, GROUP, D), BF),
            jax.ShapeDtypeStruct((4, GROUP, D), BF),
            jax.ShapeDtypeStruct((4, GROUP, D), F32),
            jax.ShapeDtypeStruct((4, GROUP, D), BF),
            jax.ShapeDtypeStruct((4, 16, GROUP), F32),
        ],
        scratch_shapes=[
            pltpu.VMEM((3 * D, D), BF),
            pltpu.VMEM((D, D), BF),
            pltpu.VMEM((GROUP, GROUP), F32),
            pltpu.VMEM((D, GROUP), BF),
        ],
        compiler_params=params(),
        name="attend",
    )(tag, conv_in, tokens, mods, packed, packed)


def feed_kernel(
    tag_ref, second, gradient, mods, w_expand, w_shrink, kernel,
    shrunk, d_second, g_expand, g_shrink, g_kernel,
    d_shrunk, d_shrunk_t, weight, field, slope, hidden, d_field,
):
    step = pl.program_id(0)
    tag = tag_ref[0]

    @pl.when(step == 0)
    def _():
        gate = mods[5].reshape(1, 2, 1, 2, 8, D)
        value = gradient[...].astype(F32).reshape(4, 2, 8, 2, 8, D) * gate
        d_shrunk[...] = value.reshape(TOK, D).astype(BF)
        d_shrunk_t[...] = d_shrunk[...].T
        shrunk[...] = jnp.zeros_like(shrunk)
        d_second[...] = jnp.zeros_like(d_second)

    join_rows(w_expand, weight)
    shrink = w_shrink[...].reshape(D, CHUNK)
    left, right = edge_columns(tag)
    keep = 1.0 - tag.astype(F32)
    field[...] = dot(second[...].reshape(TOK, D), weight[...], 1, 1).reshape(4, GROUP, CHUNK)
    slope[...] = dot(d_shrunk[...], shrink, 1, 0).reshape(4, GROUP, CHUNK)

    def lanes(i, _):
        cols = pl.ds(pl.multiple_of(i * 128, 128), 128)
        taps = [jnp.broadcast_to(kernel[t : t + 1, cols], (16, 128)) for t in range(9)]

        def load(g, p):
            return field[g, p * 16 : p * 16 + 16, cols]

        def load_slope(g, p):
            return slope[g, p * 16 : p * 16 + 16, cols]

        def emit(g, p, value):
            square = value * value
            half = 0.5 + 0.5 * jnp.tanh(value * (GELU_A + GELU_B * square))
            out = value * half
            hidden[g, p * 16 : p * 16 + 16, cols] = out.astype(BF)
            rate = half + out * (1.0 - half) * (2.0 * GELU_A + 6.0 * GELU_B * square)
            slope[g, p * 16 : p * 16 + 16, cols] = load_slope(g, p) * rate

        conv_rows(load, taps, left, right, keep, emit)

        def emit_back(g, p, value):
            d_field[g, p * 16 : p * 16 + 16, cols] = value.astype(BF)

        sums = conv_back_rows(load_slope, load, taps, left, right, keep, emit_back)
        for t in range(9):
            g_kernel[t : t + 1, cols] = jnp.sum(sums[t], axis=0, keepdims=True)
        return 0

    lax.fori_loop(0, CHUNK // 128, lanes, 0)
    hid = hidden[...].reshape(TOK, CHUNK)
    d_fld = d_field[...].reshape(TOK, CHUNK)
    shrunk[...] += dot(hid, shrink, 1, 1).reshape(4, GROUP, D)
    d_second[...] += dot(d_fld, weight[...], 1, 0).reshape(4, GROUP, D)
    g_shrink[...] = dot(d_shrunk_t[...], hid, 1, 0).astype(BF).reshape(NJ, 1, 1, UR, UC)
    grad = dot(d_fld, second[...].reshape(TOK, D), 0, 0).astype(BF)
    for k in range(NK):
        g_expand[:, k] = grad[:, k * UC : (k + 1) * UC].reshape(2, 4, UR, UC)


def feed(tag, second, gradient, mods, packed, kernel):
    steps = FF // CHUNK
    return pl.pallas_call(
        feed_kernel,
        grid=(steps,),
        in_specs=[
            SMEM_SPEC,
            whole((4, GROUP, D)),
            whole((4, GROUP, D)),
            whole((6, 4, 8, D)),
            pl.BlockSpec((2, NK, 4, UR, UC), lambda c: (c, 0, 1, 0, 0)),
            pl.BlockSpec((NJ, 1, 1, UR, UC), lambda c: (0, c // 4, 8 + c % 4, 0, 0)),
            pl.BlockSpec((9, CHUNK), lambda c: (0, c)),
        ],
        out_specs=[
            pl.BlockSpec((4, GROUP, D), lambda c: (0, 0, 0)),
            pl.BlockSpec((4, GROUP, D), lambda c: (0, 0, 0)),
            pl.BlockSpec((2, NK, 4, UR, UC), lambda c: (c, 0, 0, 0, 0)),
            pl.BlockSpec((NJ, 1, 1, UR, UC), lambda c: (0, c // 4, c % 4, 0, 0)),
            pl.BlockSpec((9, CHUNK), lambda c: (0, c)),
        ],
        out_shape=[
            jax.ShapeDtypeStruct((4, GROUP, D), F32),
            jax.ShapeDtypeStruct((4, GROUP, D), F32),
            jax.ShapeDtypeStruct((NJ, NK, 4, UR, UC), BF),
            jax.ShapeDtypeStruct((NJ, NK, 4, UR, UC), BF),
            jax.ShapeDtypeStruct((9, FF), F32),
        ],
        scratch_shapes=[
            pltpu.VMEM((TOK, D), BF),
            pltpu.VMEM((D, TOK), BF),
            pltpu.VMEM((CHUNK, D), BF),
            pltpu.VMEM((4, GROUP, CHUNK), F32),
            pltpu.VMEM((4, GROUP, CHUNK), F32),
            pltpu.VMEM((4, GROUP, CHUNK), BF),
            pltpu.VMEM((4, GROUP, CHUNK), BF),
        ],
        compiler_params=params(60),
        name="feed",
    )(tag, second, gradient, mods, packed, packed, kernel)


def attend_back_kernel(
    tag_ref, resid, shrunk, d_second, gradient, attn, mods, qkv, merged, conv_in, lse, w_qkv, w_proj,
    output, d_resid, g_qkv, g_proj, d_conv, sums,
    full_qkv, full_proj, proj_t, bias, d_mixed, d_qkv, acc_qkv, acc_proj, d_attn,
):
    step = pl.program_id(0)

    @pl.when(step == 0)
    def _():
        join_rows(w_qkv, full_qkv)
        join_rows(w_proj, full_proj)
        proj_t[...] = full_proj[...].T
        bias[...] = item_bias(tag_ref[0])
        acc_qkv[...] = jnp.zeros_like(acc_qkv)
        acc_proj[...] = jnp.zeros_like(acc_proj)
        sums[...] = jnp.zeros_like(sums)

    def rows_norm(i, _):
        rows = pl.ds(pl.multiple_of(i * 64, 64), 64)
        half = i // 2
        base = resid[0, rows, :]
        normal, factor = norm_stats(base)
        shrunk_rows = shrunk[0, rows, :]
        outward = gradient[0, rows, :].astype(F32)
        d_sec = d_second[0, rows, :]

        def by_item(value):
            return value.reshape(4, 2, 8, D)

        def add(index, value):
            sums[index, pl.ds(2 * half, 2)] += jnp.sum(by_item(value), axis=0)

        gated = (by_item(shrunk_rows) * quadrant_rows(mods, 5, half)).reshape(64, D)
        output[0, rows, :] = (base + gated).astype(BF)
        add(3, outward * shrunk_rows)
        add(1, d_sec)
        add(2, d_sec * normal)
        inner = (by_item(d_sec) * (1.0 + quadrant_rows(mods, 4, half))).reshape(64, D)
        mean = jnp.mean(inner, axis=-1, keepdims=True)
        along = jnp.mean(inner * normal, axis=-1, keepdims=True)
        back = outward + (inner - mean - normal * along) * factor
        d_resid[0, rows, :] = back
        add(0, back * attn[0, rows, :].astype(F32))
        gated = (by_item(back) * quadrant_rows(mods, 2, half)).reshape(64, D)
        d_attn[rows, :] = gated.astype(BF)
        return 0

    lax.fori_loop(0, 4, rows_norm, 0)
    acc_proj[...] += dot(d_attn[...], merged[0], 0, 0)
    d_mixed[...] = dot(proj_t[...], d_attn[...], 1, 1).astype(BF)

    def head(h, _):
        rows = pl.ds(pl.multiple_of(h * HD, HD), HD)
        key_rows = pl.ds(pl.multiple_of(D + h * HD, HD), HD)
        value_rows = pl.ds(pl.multiple_of(2 * D + h * HD, HD), HD)
        queries = qkv[0, rows, :] * jnp.asarray(HD**-0.5, BF)
        keys = qkv[0, key_rows, :]
        values = qkv[0, value_rows, :]
        d_mix = d_mixed[rows, :]
        probs = jnp.exp(dot(keys, queries, 0, 0) + (bias[...] - lse[0, pl.ds(h, 1), :]))
        d_probs = dot(values, d_mix, 0, 0)
        d_qkv[value_rows, :] = dot(d_mix, probs.astype(BF), 1, 1).astype(BF)
        weighted = probs * d_probs
        inner = jnp.sum(weighted, axis=0, keepdims=True)
        d_scores = (weighted - probs * inner).astype(BF)
        d_qkv[rows, :] = (dot(keys, d_scores, 1, 0) * HD**-0.5).astype(BF)
        d_qkv[key_rows, :] = dot(queries, d_scores, 1, 1).astype(BF)
        return 0

    lax.fori_loop(0, H, head, 0)
    acc_qkv[...] += dot(d_qkv[...], conv_in[0], 1, 0)
    d_conv[0] = dot(d_qkv[...], full_qkv[...], 0, 0)

    @pl.when(step == pl.num_programs(0) - 1)
    def _():
        for k in range(NK):
            cols = slice(k * UC, (k + 1) * UC)
            g_qkv[:, k] = acc_qkv[:, cols].astype(BF).reshape(NJ, 3, UR, UC)
            g_proj[:, k] = acc_proj[:, cols].astype(BF).reshape(NJ, 1, UR, UC)


def attend_back(tag, resid, shrunk, d_second, gradient, attn, mods, qkv, merged, conv_in, lse, packed):
    return pl.pallas_call(
        attend_back_kernel,
        grid=(4,),
        in_specs=[
            SMEM_SPEC,
            group_spec(GROUP, D),
            group_spec(GROUP, D),
            group_spec(GROUP, D),
            group_spec(GROUP, D),
            group_spec(GROUP, D),
            whole((6, 4, 8, D)),
            group_spec(3 * D, GROUP),
            group_spec(GROUP, D),
            group_spec(GROUP, D),
            group_spec(16, GROUP),
            unit_spec(3, 0),
            unit_spec(1, 3),
        ],
        out_specs=[
            group_spec(GROUP, D),
            group_spec(GROUP, D),
            whole((NJ, NK, 3, UR, UC)),
            whole((NJ, NK, 1, UR, UC)),
            group_spec(GROUP, D),
            whole((4, 4, 8, D)),
        ],
        out_shape=[
            jax.ShapeDtypeStruct((4, GROUP, D), BF),
            jax.ShapeDtypeStruct((4, GROUP, D), F32),
            jax.ShapeDtypeStruct((NJ, NK, 3, UR, UC), BF),
            jax.ShapeDtypeStruct((NJ, NK, 1, UR, UC), BF),
            jax.ShapeDtypeStruct((4, GROUP, D), F32),
            jax.ShapeDtypeStruct((4, 4, 8, D), F32),
        ],
        scratch_shapes=[
            pltpu.VMEM((3 * D, D), BF),
            pltpu.VMEM((D, D), BF),
            pltpu.VMEM((D, D), BF),
            pltpu.VMEM((GROUP, GROUP), F32),
            pltpu.VMEM((D, GROUP), BF),
            pltpu.VMEM((3 * D, GROUP), BF),
            pltpu.VMEM((3 * D, D), F32),
            pltpu.VMEM((D, D), F32),
            pltpu.VMEM((GROUP, D), BF),
        ],
        compiler_params=params(60),
        name="attend_back",
    )(tag, resid, shrunk, d_second, gradient, attn, mods, qkv, merged, conv_in, lse, packed, packed)


def finish_kernel(
    tag_ref, d_conv, norm, factor, d_resid, output, mods, kernel,
    block_output, input_grad, g_kernel, sums, d_first, total,
):
    tag = tag_ref[0]
    left, right = edge_columns(tag)
    keep = 1.0 - tag.astype(F32)

    def lanes(i, _):
        cols = pl.ds(pl.multiple_of(i * 128, 128), 128)
        taps = [jnp.broadcast_to(kernel[t : t + 1, cols], (16, 128)) for t in range(9)]

        def load_grad(g, p):
            return d_conv[g, p * 16 : p * 16 + 16, cols]

        def load_field(g, p):
            q = 2 * (p // 8)
            shift = mods[0, q : q + 2, :, cols].reshape(16, 128)
            scale = mods[1, q : q + 2, :, cols].reshape(16, 128)
            return norm[g, p * 16 : p * 16 + 16, cols] * (1.0 + scale) + shift

        def emit(g, p, value):
            d_first[g, p * 16 : p * 16 + 16, cols] = value

        grads = conv_back_rows(load_grad, load_field, taps, left, right, keep, emit)
        for t in range(9):
            g_kernel[t : t + 1, cols] = jnp.sum(grads[t], axis=0, keepdims=True)
        return 0

    lax.fori_loop(0, D // 128, lanes, 0)
    sums[...] = jnp.zeros_like(sums)

    def rows_back(i, _):
        g, part = i // 4, i % 4
        rows = pl.ds(pl.multiple_of(part * 64, 64), 64)
        half = part // 2
        value = d_first[g, rows, :]
        normal = norm[g, rows, :]
        sums[0, pl.ds(2 * half, 2)] += jnp.sum(value.reshape(4, 2, 8, D), axis=0)
        sums[1, pl.ds(2 * half, 2)] += jnp.sum((value * normal).reshape(4, 2, 8, D), axis=0)
        inner = (value.reshape(4, 2, 8, D) * (1.0 + quadrant_rows(mods, 1, half))).reshape(64, D)
        mean = jnp.mean(inner, axis=-1, keepdims=True)
        along = jnp.mean(inner * normal, axis=-1, keepdims=True)
        total[g, rows, :] = (
            d_resid[g, rows, :] + (inner - mean - normal * along) * factor[g, rows, :]
        )
        return 0

    lax.fori_loop(0, 16, rows_back, 0)
    order = ungroup_matrix()

    def place(i, _):
        rows = pl.ds(pl.multiple_of(i * 64, 64), 64)
        target = pl.ds(pl.multiple_of(i * 256, 256), 256)
        grouped = total[:, rows, :].reshape(256, D)
        high = grouped.astype(BF)
        rest = (grouped - high.astype(F32)).astype(BF)
        input_grad[target, :] = dot(order, high, 1, 0) + dot(order, rest, 1, 0)
        block_output[target, :] = dot(order, output[:, rows, :].reshape(256, D), 1, 0).astype(BF)
        return 0

    lax.fori_loop(0, 4, place, 0)


def finish(tag, d_conv, norm, factor, d_resid, output, mods, kernel):
    return pl.pallas_call(
        finish_kernel,
        in_specs=[SMEM_SPEC] + [pl.BlockSpec(memory_space=pltpu.VMEM)] * 7,
        out_specs=[pl.BlockSpec(memory_space=pltpu.VMEM)] * 4,
        out_shape=[
            jax.ShapeDtypeStruct((TOK, D), BF),
            jax.ShapeDtypeStruct((TOK, D), F32),
            jax.ShapeDtypeStruct((9, D), F32),
            jax.ShapeDtypeStruct((2, 4, 8, D), F32),
        ],
        scratch_shapes=[pltpu.VMEM((4, GROUP, D), F32), pltpu.VMEM((4, GROUP, D), F32)],
        compiler_params=params(60),
        name="finish",
    )(tag, d_conv, norm, factor, d_resid, output, mods, kernel)


BOTH = ("dp", "fsdp")


def exchange(pieces):
    return lax.all_to_all(pieces, BOTH, 0, 0, tiled=True)


def pack_shards(qkv, proj, expand, shrink):
    low = shrink.T.reshape(UR, 4, UC).transpose(1, 0, 2).reshape(4 * UR, UC)
    return jnp.concatenate([qkv.T, proj.T, expand.T, low], axis=0)


def gather_packed(nd, nf, qkv, proj, expand, shrink):
    if (nd, nf) == (NJ, NK):
        rows = lax.all_gather(pack_shards(qkv, proj, expand, shrink), BOTH)
        return rows.reshape(NJ, NK, UNITS, UR, UC)

    def full(shard):
        rows = lax.all_gather(shard.T, "fsdp", axis=1, tiled=True)
        return lax.all_gather(rows, "dp", axis=0, tiled=True)

    def split(weight, units):
        return weight.reshape(NJ, units, UR, NK, UC).transpose(0, 3, 1, 2, 4)

    low = full(shrink).reshape(NJ, UR, NK, 4, UC).transpose(0, 2, 3, 1, 4)
    return jnp.concatenate(
        [split(full(qkv), 3), split(full(proj), 1), split(full(expand), 4), low], axis=2
    )


def scatter_packed(nd, nf, parts):
    kinds = [kind for kind, _ in parts]
    if (nd, nf) == (NJ, NK):
        joined = jnp.concatenate([grad for _, grad in parts], axis=2)
        rows = lax.psum_scatter(
            joined.reshape(NJ * NK, -1, UC), BOTH, scatter_dimension=0, tiled=True
        )[0].astype(F32)
        out, start = [], 0
        for kind, grad in parts:
            size = grad.shape[2] * UR
            piece = rows[start : start + size]
            start += size
            if kind == "shrink":
                piece = piece.reshape(4, UR, UC).transpose(1, 0, 2).reshape(UR, 4 * UC)
            out.append(piece.T)
        return out
    out = []
    for kind, grad in parts:
        if kind == "shrink":
            weight = grad.transpose(0, 3, 1, 2, 4).reshape(NJ * UR, -1)
        else:
            weight = grad.transpose(0, 2, 3, 1, 4).reshape(-1, NK * UC)
        columns = lax.psum_scatter(weight, "dp", scatter_dimension=0, tiled=True)
        piece = lax.psum_scatter(columns, "fsdp", scatter_dimension=1, tiled=True)
        out.append(piece.astype(F32).T)
    return out


def condition(nd, nf, timesteps, classes, step_table, class_table, attn_kernel, ffn_kernel):
    slots = nd * nf
    mine = jnp.concatenate([timesteps[0], classes[0]])[None]
    ids = exchange(jnp.broadcast_to(mine, (slots, 8)))
    first_row = lax.axis_index("fsdp") * step_table.shape[0]
    own = first_row + jnp.arange(step_table.shape[0], dtype=jnp.int32)
    step_hot = (ids[:, :4].reshape(-1, 1) == own[None, :]).astype(BF)
    class_hot = (ids[:, 4:].reshape(-1, 1) == own[None, :]).astype(BF)
    part = jnp.dot(step_hot, step_table, preferred_element_type=F32) + jnp.dot(
        class_hot, class_table, preferred_element_type=F32
    )
    cond = lax.psum(part, "fsdp")
    act = jax.nn.silu(cond).astype(BF)
    items, width = act.shape
    filters = jnp.concatenate([attn_kernel, ffn_kernel], axis=1).reshape(-1, width)
    sent = lax.all_gather(jnp.concatenate([act, filters], axis=0), "dp")
    act_all = sent[:, :items].transpose(1, 0, 2).reshape(items, nd * width)
    filters = sent[:, items:].reshape(nd, 9, -1).astype(F32)
    attn_full = filters[:, :, : attn_kernel.shape[1]].transpose(1, 0, 2).reshape(9, -1)
    ffn_full = filters[:, :, attn_kernel.shape[1] :].transpose(1, 0, 2).reshape(9, -1)
    return step_hot, class_hot, cond, act_all, attn_full, ffn_full


def body(
    latents, size_tags, timesteps, classes, step_table, class_table, modulation_weight,
    attn_kernel, qkv_weight, proj_weight, expand_weight, ffn_kernel, shrink_weight, cotangent,
    *, nd, nf,
):
    slots = nd * nf
    tag = size_tags[0]
    packed = gather_packed(nd, nf, qkv_weight, proj_weight, expand_weight, shrink_weight)
    tokens, gradient, norm, factor = prepare(latents, cotangent)
    step_hot, class_hot, cond, act_all, attn_full, ffn_full = condition(
        nd, nf, timesteps, classes, step_table, class_table, attn_kernel, ffn_kernel
    )
    height, width = modulation_weight.shape
    act_rows = lax.dynamic_slice_in_dim(
        act_all, lax.axis_index("fsdp") * height, height, axis=1
    )
    part = jnp.dot(act_rows, modulation_weight, preferred_element_type=F32)
    part = exchange(part.reshape(slots, 4, width)).reshape(nd, nf, 4, width)
    mod_rows = part.sum(axis=1).transpose(1, 0, 2).reshape(4, nd * width)
    chosen = jnp.where(tag == 1, mod_rows, mod_rows[:1])
    mods = jnp.broadcast_to(chosen.reshape(4, 6, 1, D).transpose(1, 0, 2, 3), (6, 4, 8, D))

    conv_in = first_conv(size_tags, norm, mods, attn_full)
    qkv, merged, attn, resid, second, lse = attend(size_tags, conv_in, tokens, mods, packed)
    shrunk, d_second, g_expand, g_shrink, g_ffn = feed(
        size_tags, second, gradient, mods, packed, ffn_full
    )
    expand_grad, shrink_grad = scatter_packed(
        nd, nf, [("expand", g_expand), ("shrink", g_shrink)]
    )
    output, d_resid, g_qkv, g_proj, d_conv, later = attend_back(
        size_tags, resid, shrunk, d_second, gradient, attn, mods, qkv, merged, conv_in, lse, packed
    )
    qkv_grad, proj_grad = scatter_packed(nd, nf, [("qkv", g_qkv), ("proj", g_proj)])
    block_output, input_grad, g_attn, early = finish(
        size_tags, d_conv, norm, factor, d_resid, output, mods, attn_full
    )
    rows = jnp.concatenate([early, later], axis=0).sum(axis=2)
    rows = rows.transpose(1, 0, 2).reshape(4, 6 * D)
    alone = jnp.concatenate([rows.sum(axis=0, keepdims=True), jnp.zeros((3, 6 * D), F32)])
    d_mod = jnp.where(tag == 1, rows, alone).astype(BF)
    pieces = d_mod.reshape(4, nd, 1, width).transpose(1, 2, 0, 3)
    d_mod_all = exchange(jnp.broadcast_to(pieces, (nd, nf, 4, width)).reshape(slots, 4, width))
    d_mod_all = d_mod_all.reshape(slots * 4, width)
    modulation_grad = dot(act_rows, d_mod_all, 0, 0)
    d_act = dot(d_mod_all, modulation_weight, 1, 1)
    spread = lax.dynamic_update_slice_in_dim(
        jnp.zeros((slots * 4, D), F32), d_act, lax.axis_index("fsdp") * height, axis=1
    )
    spread = spread.reshape(slots * 4, nd, 1, -1).transpose(1, 2, 0, 3)
    spread = jnp.broadcast_to(spread, (nd, nf) + spread.shape[2:])
    d_act = exchange(spread.reshape((slots,) + spread.shape[2:])).sum(axis=0)
    gate = jax.nn.sigmoid(cond)
    d_cond = d_act * (gate * (1.0 + cond * (1.0 - gate)))

    def table_grad(hot):
        return lax.dot_general(
            hot.astype(F32), d_cond, (((0,), (0,)), ((), ())), precision=lax.Precision.HIGHEST
        )

    filters = jnp.concatenate([g_attn.reshape(9, nd, -1), g_ffn.reshape(9, nd, -1)], axis=2)
    filters = lax.psum_scatter(filters.transpose(1, 0, 2), "dp", scatter_dimension=0, tiled=True)
    filters = lax.psum(filters[0], "fsdp")
    cut = attn_kernel.shape[1]
    return (
        block_output,
        input_grad,
        table_grad(step_hot),
        table_grad(class_hot),
        modulation_grad,
        filters[:, :cut],
        qkv_grad,
        proj_grad,
        expand_grad,
        filters[:, cut:],
        shrink_grad,
    )


def solution(mesh):
    matrix = P("fsdp", "dp")
    rows = P(BOTH, None)
    filters = P(None, "dp")
    in_specs = (
        rows, P(BOTH), rows, rows, matrix, matrix, matrix, filters, matrix, matrix, matrix,
        filters, matrix, rows,
    )
    out_specs = (
        rows, rows, matrix, matrix, matrix, filters, matrix, matrix, matrix, filters, matrix,
    )
    run = functools.partial(body, nd=mesh.shape["dp"], nf=mesh.shape["fsdp"])
    return jax.shard_map(run, mesh=mesh, in_specs=in_specs, out_specs=out_specs, check_vma=False)
```

```python
import functools

import jax
import jax.numpy as jnp
from jax import lax
from jax.experimental import pallas as pl
from jax.experimental.pallas import tpu as pltpu
from jax.sharding import PartitionSpec as P

D = 768
H = 12
HD = 64
FF = 3072
SIDE = 32
GROUP = 256
TOK = SIDE * SIDE
EPS = 1e-06
NJ, NK, UR, UC = 16, 2, 48, 384
UNITS = 12
CHUNK = 384
MIB = 1024 * 1024
BF = jnp.bfloat16
F32 = jnp.float32
GELU_A = 0.7978845608028654
GELU_B = GELU_A * 0.044715


def dot(left, right, left_dim, right_dim):
    return lax.dot_general(
        left, right, (((left_dim,), (right_dim,)), ((), ())), preferred_element_type=F32
    )


def params(limit=56):
    return pltpu.CompilerParams(vmem_limit_bytes=limit * MIB)


def cost(micros):
    return pl.CostEstimate(flops=int(micros * 1.1e9), transcendentals=0, bytes_accessed=4 * MIB)


def whole(shape):
    zeros = (0,) * len(shape)
    return pl.BlockSpec(shape, lambda *ids: zeros, pipeline_mode=pl.Buffered(1))


SMEM_SPEC = pl.BlockSpec(memory_space=pltpu.SMEM)


def group_place(natural):
    pair, odd_row = natural // 64, (natural // 32) % 2
    column, odd_column = (natural % 32) // 2, natural % 2
    return (2 * odd_row + odd_column) * 64 + pair * 16 + column


def ungroup_matrix():
    natural = lax.broadcasted_iota(jnp.int32, (256, 256), 0)
    grouped = lax.broadcasted_iota(jnp.int32, (256, 256), 1)
    return jnp.where(group_place(natural) == grouped, 1.0, 0.0).astype(BF)


def group_matrix():
    natural = lax.broadcasted_iota(jnp.int32, (256, 256), 1)
    grouped = lax.broadcasted_iota(jnp.int32, (256, 256), 0)
    return jnp.where(group_place(natural) == grouped, 1.0, 0.0).astype(BF)


def norm_stats(values):
    centre = values - jnp.mean(values, axis=-1, keepdims=True)
    variance = jnp.mean(centre * centre, axis=-1, keepdims=True)
    scale = lax.rsqrt(variance + EPS)
    return centre * scale, scale


def prepare_kernel(latents, cotangent, tokens, gradient, norm, scale):
    order = group_matrix()
    gathered = dot(order, latents[...], 1, 0)
    gradient[...] = dot(order, cotangent[...], 1, 0).reshape(4, 64, D).astype(BF)
    tokens[...] = gathered.reshape(4, 64, D).astype(BF)
    normal, factor = norm_stats(gathered)
    norm[...] = normal.reshape(4, 64, D)
    scale[...] = factor.reshape(4, 64, 1)


def prepare(latents, cotangent):
    flat = pl.BlockSpec((256, D), lambda i: (i, 0))
    split = pl.BlockSpec((4, 64, D), lambda i: (0, i, 0))
    return pl.pallas_call(
        prepare_kernel,
        grid=(4,),
        in_specs=[flat, flat],
        out_specs=[split, split, split, pl.BlockSpec((4, 64, 1), lambda i: (0, i, 0))],
        out_shape=[
            jax.ShapeDtypeStruct((4, GROUP, D), BF),
            jax.ShapeDtypeStruct((4, GROUP, D), BF),
            jax.ShapeDtypeStruct((4, GROUP, D), F32),
            jax.ShapeDtypeStruct((4, GROUP, 1), F32),
        ],
        compiler_params=params(),
        cost_estimate=cost(6),
        name="prepare",
    )(latents, cotangent)


def edge_columns(tag):
    place = lax.broadcasted_iota(jnp.int32, (16, 128), 0)
    left = jnp.where((place == 0) | ((place == 8) & (tag == 1)), 0.0, 1.0)
    right = jnp.where((place == 15) | ((place == 7) & (tag == 1)), 0.0, 1.0)
    return left, right


def neighbours(even, odd, left, right):
    return pltpu.roll(odd, 1, 0) * left, pltpu.roll(even, 15, 0) * right


def conv_rows(load, kernel, left, right, keep, emit):
    above = None
    partial = None
    for row in range(SIDE + 1):
        taps = None
        if row < SIDE:
            a, p = row % 2, row // 2
            even, odd = load(2 * a, p), load(2 * a + 1, p)
            odd_left, even_right = neighbours(even, odd, left, right)
            taps = []
            for tap in range(3):
                k = [kernel[3 * tap + b] for b in range(3)]
                taps.append(
                    (
                        k[0] * odd_left + k[1] * even + k[2] * odd,
                        k[0] * even + k[1] * odd + k[2] * even_right,
                    )
                )
        crossing = row == SIDE // 2
        if partial is not None:
            a, p = (row - 1) % 2, (row - 1) // 2
            for b in range(2):
                value = partial[b]
                if taps is not None:
                    below = taps[2][b]
                    value = value + (below * keep if crossing else below)
                emit(2 * a + b, p, value)
        if taps is not None:
            partial = []
            for b in range(2):
                value = taps[1][b]
                if above is not None:
                    value = value + (above[b] * keep if crossing else above[b])
                partial.append(value)
            above = taps[0]


def conv_back_rows(load_grad, load_field, kernel, left, right, keep, emit):
    sums = [jnp.zeros((16, 128), F32) for _ in range(9)]
    from_above = None
    partial = None
    field_above = None
    field = (load_field(0, 0), load_field(1, 0))
    for row in range(SIDE + 1):
        crossing = row == SIDE // 2
        taps = None
        if row < SIDE:
            a, p = row % 2, row // 2
            even, odd = load_grad(2 * a, p), load_grad(2 * a + 1, p)
            odd_left, even_right = neighbours(even, odd, left, right)
            picks = ((odd, even, odd_left), (even_right, odd, even))
            taps = []
            for tap in range(3):
                k = [kernel[3 * tap + b] for b in range(3)]
                taps.append(
                    tuple(k[0] * x[0] + k[1] * x[1] + k[2] * x[2] for x in picks)
                )
            field_below = None
            if row + 1 < SIDE:
                a, p = (row + 1) % 2, (row + 1) // 2
                field_below = (load_field(2 * a, p), load_field(2 * a + 1, p))
            for tap, rows in enumerate((field_above, field, field_below)):
                if rows is None:
                    continue
                if (tap == 0 and crossing) or (tap == 2 and row + 1 == SIDE // 2):
                    rows = (rows[0] * keep, rows[1] * keep)
                for b in range(3):
                    sums[3 * tap + b] = (
                        sums[3 * tap + b] + rows[0] * picks[0][b] + rows[1] * picks[1][b]
                    )
            field_above, field = field, field_below
        if partial is not None:
            a, p = (row - 1) % 2, (row - 1) // 2
            for b in range(2):
                value = partial[b]
                if taps is not None:
                    value = value + (taps[0][b] * keep if crossing else taps[0][b])
                emit(2 * a + b, p, value)
        if taps is not None:
            partial = []
            for b in range(2):
                value = taps[1][b]
                if from_above is not None:
                    value = value + (from_above[b] * keep if crossing else from_above[b])
                partial.append(value)
            from_above = taps[2]
    return sums


def first_conv_kernel(tag_ref, norm, mods, kernel, out):
    tag = tag_ref[0]
    left, right = edge_columns(tag)
    keep = 1.0 - tag.astype(F32)
    taps = [jnp.broadcast_to(kernel[i : i + 1, :], (16, 128)) for i in range(9)]

    def load(g, p):
        q = 2 * (p // 8)
        shift = mods[0, q : q + 2].reshape(16, 128)
        scale = mods[1, q : q + 2].reshape(16, 128)
        return norm[g, p * 16 : p * 16 + 16, :] * (1.0 + scale) + shift

    def emit(g, p, value):
        out[g, p * 16 : p * 16 + 16, :] = value.astype(BF)

    conv_rows(load, taps, left, right, keep, emit)


def first_conv(tag, norm, mods, kernel):
    return pl.pallas_call(
        first_conv_kernel,
        grid=(D // 128,),
        in_specs=[
            SMEM_SPEC,
            pl.BlockSpec((4, GROUP, 128), lambda i: (0, 0, i)),
            pl.BlockSpec((6, 4, 8, 128), lambda i: (0, 0, 0, i)),
            pl.BlockSpec((9, 128), lambda i: (0, i)),
        ],
        out_specs=pl.BlockSpec((4, GROUP, 128), lambda i: (0, 0, i)),
        out_shape=jax.ShapeDtypeStruct((4, GROUP, D), BF),
        compiler_params=params(),
        cost_estimate=cost(6),
        name="first_conv",
    )(tag, norm, mods, kernel)


def join_rows(block, target):
    rows = block.shape[0] * block.shape[2] * UR
    for k in range(NK):
        target[:, k * UC : (k + 1) * UC] = block[:, k].reshape(rows, UC)


def share_out(rows, core, units, keep, send):
    first, count = units
    for k in range(NK):
        part = rows[:, k * UC : (k + 1) * UC].astype(BF)
        part = part.reshape(-1, 2, part.shape[0] // (keep.shape[0] * 2), UC)
        even, odd = part[:, 0], part[:, 1]
        for target, value in (
            (keep, jnp.where(core == 0, even, odd)),
            (send, jnp.where(core == 0, odd, even)),
        ):
            whole_units = value.reshape(value.shape[0], -1, UR, UC)
            target[:, k] = whole_units[:, first : first + count]


def quadrant_rows(mods, index, half):
    return mods[index, pl.ds(2 * half, 2)].reshape(1, 2, 8, D)


def item_bias(tag):
    def label(dim):
        place = lax.broadcasted_iota(jnp.int32, (GROUP, GROUP), dim)
        return 2 * (place // 128) + (place % 16) // 8

    return jnp.where((label(0) == label(1)) | (tag == 0), 0.0, -1e30)


def attend_kernel(
    tag_ref, conv_in, tokens, mods, w_qkv, w_proj, qkv, merged, attn, resid, second, lse,
    full_qkv, full_proj, bias, mixed_t,
):
    @pl.when(pl.program_id(0) == 0)
    def _():
        join_rows(w_qkv, full_qkv)
        join_rows(w_proj, full_proj)
        bias[...] = item_bias(tag_ref[0])

    qkv[0] = dot(full_qkv[...], conv_in[0], 1, 1).astype(BF)

    def head(h, _):
        rows = pl.ds(pl.multiple_of(h * HD, HD), HD)
        queries = qkv[0, rows, :] * jnp.asarray(HD**-0.5, BF)
        keys = qkv[0, pl.ds(pl.multiple_of(D + h * HD, HD), HD), :]
        values = qkv[0, pl.ds(pl.multiple_of(2 * D + h * HD, HD), HD), :]
        scores = dot(keys, queries, 0, 0) + bias[...]
        highest = jnp.max(scores, axis=0, keepdims=True)
        raised = jnp.exp(scores - highest)
        total = jnp.sum(raised, axis=0, keepdims=True)
        probs = (raised * (1.0 / total)).astype(BF)
        lse[0, pl.ds(h, 1), :] = highest + jnp.log(total)
        mixed_t[rows, :] = dot(values, probs, 1, 0).astype(BF)
        return 0

    lax.fori_loop(0, H, head, 0)
    merged[0] = mixed_t[...].T
    projected = dot(merged[0], full_proj[...], 1, 1)
    attn[0] = projected.astype(BF)
    gate = mods[2].reshape(2, 1, 2, 8, D)
    resid[0] = (
        tokens[0].astype(F32) + (projected.reshape(2, 8, 2, 8, D) * gate).reshape(GROUP, D)
    )

    def rows_norm(i, _):
        rows = pl.ds(pl.multiple_of(i * 64, 64), 64)
        normal, _ = norm_stats(resid[0, rows, :])
        half = i // 2
        scaled = normal.reshape(4, 2, 8, D) * (1.0 + quadrant_rows(mods, 4, half))
        value = scaled + quadrant_rows(mods, 3, half)
        second[0, rows, :] = value.reshape(64, D).astype(BF)
        return 0

    lax.fori_loop(0, 4, rows_norm, 0)


def group_spec(*shape):
    return pl.BlockSpec((1,) + shape, lambda g: (g,) + (0,) * len(shape))


def unit_spec(units, start):
    shape = (NJ, NK, units, UR, UC)
    return pl.BlockSpec(
        shape, lambda g: (0, 0, start // units, 0, 0), pipeline_mode=pl.Buffered(1)
    )


def attend(tag, conv_in, tokens, mods, packed):
    return pl.pallas_call(
        attend_kernel,
        grid=(4,),
        in_specs=[
            SMEM_SPEC,
            group_spec(GROUP, D),
            group_spec(GROUP, D),
            whole((6, 4, 8, D)),
            unit_spec(3, 0),
            unit_spec(1, 3),
        ],
        out_specs=[
            group_spec(3 * D, GROUP),
            group_spec(GROUP, D),
            group_spec(GROUP, D),
            group_spec(GROUP, D),
            group_spec(GROUP, D),
            group_spec(16, GROUP),
        ],
        out_shape=[
            jax.ShapeDtypeStruct((4, 3 * D, GROUP), BF),
            jax.ShapeDtypeStruct((4, GROUP, D), BF),
            jax.ShapeDtypeStruct((4, GROUP, D), BF),
            jax.ShapeDtypeStruct((4, GROUP, D), F32),
            jax.ShapeDtypeStruct((4, GROUP, D), BF),
            jax.ShapeDtypeStruct((4, 16, GROUP), F32),
        ],
        scratch_shapes=[
            pltpu.VMEM((3 * D, D), BF),
            pltpu.VMEM((D, D), BF),
            pltpu.VMEM((GROUP, GROUP), F32),
            pltpu.VMEM((D, GROUP), BF),
        ],
        compiler_params=params(),
        cost_estimate=cost(38),
        name="attend",
    )(tag, conv_in, tokens, mods, packed, packed)


def feed_kernel(
    tag_ref, second, gradient, mods, w_expand, w_shrink, kernel,
    shrunk, d_second, keep_expand, send_expand, keep_shrink, send_shrink, g_kernel,
    d_shrunk, d_shrunk_t, weight, field, slope, hidden, d_field,
):
    step = pl.program_id(0)
    tag = tag_ref[0]

    @pl.when(step == 0)
    def _():
        gate = mods[5].reshape(1, 2, 1, 2, 8, D)
        value = gradient[...].astype(F32).reshape(4, 2, 8, 2, 8, D) * gate
        d_shrunk[...] = value.reshape(TOK, D).astype(BF)
        d_shrunk_t[...] = d_shrunk[...].T
        shrunk[...] = jnp.zeros_like(shrunk)
        d_second[...] = jnp.zeros_like(d_second)

    join_rows(w_expand, weight)
    shrink = w_shrink[...].reshape(D, CHUNK)
    left, right = edge_columns(tag)
    keep = 1.0 - tag.astype(F32)
    field[...] = dot(second[...].reshape(TOK, D), weight[...], 1, 1).reshape(4, GROUP, CHUNK)
    slope[...] = dot(d_shrunk[...], shrink, 1, 0).reshape(4, GROUP, CHUNK)

    def lanes(i, _):
        cols = pl.ds(pl.multiple_of(i * 128, 128), 128)
        taps = [jnp.broadcast_to(kernel[t : t + 1, cols], (16, 128)) for t in range(9)]

        def load(g, p):
            return field[g, p * 16 : p * 16 + 16, cols]

        def load_slope(g, p):
            return slope[g, p * 16 : p * 16 + 16, cols]

        def emit(g, p, value):
            square = value * value
            half = 0.5 + 0.5 * jnp.tanh(value * (GELU_A + GELU_B * square))
            out = value * half
            hidden[g, p * 16 : p * 16 + 16, cols] = out.astype(BF)
            rate = half + out * (1.0 - half) * (2.0 * GELU_A + 6.0 * GELU_B * square)
            slope[g, p * 16 : p * 16 + 16, cols] = load_slope(g, p) * rate

        conv_rows(load, taps, left, right, keep, emit)

        def emit_back(g, p, value):
            d_field[g, p * 16 : p * 16 + 16, cols] = value.astype(BF)

        sums = conv_back_rows(load_slope, load, taps, left, right, keep, emit_back)
        for t in range(9):
            g_kernel[t : t + 1, cols] = jnp.sum(sums[t], axis=0, keepdims=True)
        return 0

    lax.fori_loop(0, CHUNK // 128, lanes, 0)
    hid = hidden[...].reshape(TOK, CHUNK)
    d_fld = d_field[...].reshape(TOK, CHUNK)
    shrunk[...] += dot(hid, shrink, 1, 1).reshape(4, GROUP, D)
    d_second[...] += dot(d_fld, weight[...], 1, 0).reshape(4, GROUP, D)
    core = tag_ref[1]
    grad = dot(d_shrunk_t[...], hid, 1, 0).astype(BF).reshape(NJ // 2, 2, UR, UC)
    own, other = jnp.where(core == 0, grad[:, 0], grad[:, 1]), jnp.where(core == 0, grad[:, 1], grad[:, 0])
    keep_shrink[...] = own.reshape(NJ // 2, 1, 1, UR, UC)
    send_shrink[...] = other.reshape(NJ // 2, 1, 1, UR, UC)
    share_out(dot(d_fld, second[...].reshape(TOK, D), 0, 0), core, (0, 4), keep_expand, send_expand)


def packed_half(units):
    return jax.ShapeDtypeStruct((NJ // 2, NK, units, UR, UC), BF)


def feed(tag, second, gradient, mods, packed, kernel):
    steps = FF // CHUNK
    return pl.pallas_call(
        feed_kernel,
        grid=(steps,),
        in_specs=[
            SMEM_SPEC,
            whole((4, GROUP, D)),
            whole((4, GROUP, D)),
            whole((6, 4, 8, D)),
            pl.BlockSpec((2, NK, 4, UR, UC), lambda c: (c, 0, 1, 0, 0)),
            pl.BlockSpec((NJ, 1, 1, UR, UC), lambda c: (0, c // 4, 8 + c % 4, 0, 0)),
            pl.BlockSpec((9, CHUNK), lambda c: (0, c)),
        ],
        out_specs=[
            pl.BlockSpec((4, GROUP, D), lambda c: (0, 0, 0)),
            pl.BlockSpec((4, GROUP, D), lambda c: (0, 0, 0)),
            pl.BlockSpec((1, NK, 4, UR, UC), lambda c: (c, 0, 0, 0, 0)),
            pl.BlockSpec((1, NK, 4, UR, UC), lambda c: (c, 0, 0, 0, 0)),
            pl.BlockSpec((NJ // 2, 1, 1, UR, UC), lambda c: (0, c // 4, c % 4, 0, 0)),
            pl.BlockSpec((NJ // 2, 1, 1, UR, UC), lambda c: (0, c // 4, c % 4, 0, 0)),
            pl.BlockSpec((9, CHUNK), lambda c: (0, c)),
        ],
        out_shape=[
            jax.ShapeDtypeStruct((4, GROUP, D), F32),
            jax.ShapeDtypeStruct((4, GROUP, D), F32),
            packed_half(4),
            packed_half(4),
            packed_half(4),
            packed_half(4),
            jax.ShapeDtypeStruct((9, FF), F32),
        ],
        scratch_shapes=[
            pltpu.VMEM((TOK, D), BF),
            pltpu.VMEM((D, TOK), BF),
            pltpu.VMEM((CHUNK, D), BF),
            pltpu.VMEM((4, GROUP, CHUNK), F32),
            pltpu.VMEM((4, GROUP, CHUNK), F32),
            pltpu.VMEM((4, GROUP, CHUNK), BF),
            pltpu.VMEM((4, GROUP, CHUNK), BF),
        ],
        compiler_params=params(60),
        cost_estimate=cost(80),
        name="feed",
    )(tag, second, gradient, mods, packed, packed, kernel)


def attend_back_kernel(
    tag_ref, resid, shrunk, d_second, gradient, attn, mods, qkv, merged, conv_in, lse, w_qkv, w_proj,
    output, d_resid, keep_a, send_a, keep_b, send_b, d_conv, sums,
    full_qkv, full_proj, proj_t, bias, d_mixed, d_qkv, acc_qkv, acc_proj, d_attn,
):
    step = pl.program_id(0)

    @pl.when(step == 0)
    def _():
        join_rows(w_qkv, full_qkv)
        join_rows(w_proj, full_proj)
        proj_t[...] = full_proj[...].T
        bias[...] = item_bias(tag_ref[0])
        acc_qkv[...] = jnp.zeros_like(acc_qkv)
        acc_proj[...] = jnp.zeros_like(acc_proj)
        sums[...] = jnp.zeros_like(sums)

    def rows_norm(i, _):
        rows = pl.ds(pl.multiple_of(i * 64, 64), 64)
        half = i // 2
        base = resid[0, rows, :]
        normal, factor = norm_stats(base)
        shrunk_rows = shrunk[0, rows, :]
        outward = gradient[0, rows, :].astype(F32)
        d_sec = d_second[0, rows, :]

        def by_item(value):
            return value.reshape(4, 2, 8, D)

        def add(index, value):
            sums[index, pl.ds(2 * half, 2)] += jnp.sum(by_item(value), axis=0)

        gated = (by_item(shrunk_rows) * quadrant_rows(mods, 5, half)).reshape(64, D)
        output[0, rows, :] = (base + gated).astype(BF)
        add(3, outward * shrunk_rows)
        add(1, d_sec)
        add(2, d_sec * normal)
        inner = (by_item(d_sec) * (1.0 + quadrant_rows(mods, 4, half))).reshape(64, D)
        mean = jnp.mean(inner, axis=-1, keepdims=True)
        along = jnp.mean(inner * normal, axis=-1, keepdims=True)
        back = outward + (inner - mean - normal * along) * factor
        d_resid[0, rows, :] = back
        add(0, back * attn[0, rows, :].astype(F32))
        gated = (by_item(back) * quadrant_rows(mods, 2, half)).reshape(64, D)
        d_attn[rows, :] = gated.astype(BF)
        return 0

    lax.fori_loop(0, 4, rows_norm, 0)
    acc_proj[...] += dot(d_attn[...], merged[0], 0, 0)
    d_mixed[...] = dot(proj_t[...], d_attn[...], 1, 1).astype(BF)

    def head(h, _):
        rows = pl.ds(pl.multiple_of(h * HD, HD), HD)
        key_rows = pl.ds(pl.multiple_of(D + h * HD, HD), HD)
        value_rows = pl.ds(pl.multiple_of(2 * D + h * HD, HD), HD)
        queries = qkv[0, rows, :] * jnp.asarray(HD**-0.5, BF)
        keys = qkv[0, key_rows, :]
        values = qkv[0, value_rows, :]
        d_mix = d_mixed[rows, :]
        probs = jnp.exp(dot(keys, queries, 0, 0) + (bias[...] - lse[0, pl.ds(h, 1), :]))
        d_probs = dot(values, d_mix, 0, 0)
        d_qkv[value_rows, :] = dot(d_mix, probs.astype(BF), 1, 1).astype(BF)
        weighted = probs * d_probs
        inner = jnp.sum(weighted, axis=0, keepdims=True)
        d_scores = (weighted - probs * inner).astype(BF)
        d_qkv[rows, :] = (dot(keys, d_scores, 1, 0) * HD**-0.5).astype(BF)
        d_qkv[key_rows, :] = dot(queries, d_scores, 1, 1).astype(BF)
        return 0

    lax.fori_loop(0, H, head, 0)
    acc_qkv[...] += dot(d_qkv[...], conv_in[0], 1, 0)
    d_conv[0] = dot(d_qkv[...], full_qkv[...], 0, 0)

    @pl.when(step == pl.num_programs(0) - 1)
    def _():
        core = tag_ref[1]
        share_out(acc_qkv, core, (0, 2), keep_a, send_a)
        share_out(acc_qkv, core, (2, 1), keep_b.at[:, :, 0:1], send_b.at[:, :, 0:1])
        share_out(acc_proj, core, (0, 1), keep_b.at[:, :, 1:2], send_b.at[:, :, 1:2])


def attend_back(tag, resid, shrunk, d_second, gradient, attn, mods, qkv, merged, conv_in, lse, packed):
    return pl.pallas_call(
        attend_back_kernel,
        grid=(4,),
        in_specs=[
            SMEM_SPEC,
            group_spec(GROUP, D),
            group_spec(GROUP, D),
            group_spec(GROUP, D),
            group_spec(GROUP, D),
            group_spec(GROUP, D),
            whole((6, 4, 8, D)),
            group_spec(3 * D, GROUP),
            group_spec(GROUP, D),
            group_spec(GROUP, D),
            group_spec(16, GROUP),
            unit_spec(3, 0),
            unit_spec(1, 3),
        ],
        out_specs=[
            group_spec(GROUP, D),
            group_spec(GROUP, D),
            whole((NJ // 2, NK, 2, UR, UC)),
            whole((NJ // 2, NK, 2, UR, UC)),
            whole((NJ // 2, NK, 2, UR, UC)),
            whole((NJ // 2, NK, 2, UR, UC)),
            group_spec(GROUP, D),
            whole((4, 4, 8, D)),
        ],
        out_shape=[
            jax.ShapeDtypeStruct((4, GROUP, D), BF),
            jax.ShapeDtypeStruct((4, GROUP, D), F32),
            packed_half(2),
            packed_half(2),
            packed_half(2),
            packed_half(2),
            jax.ShapeDtypeStruct((4, GROUP, D), F32),
            jax.ShapeDtypeStruct((4, 4, 8, D), F32),
        ],
        scratch_shapes=[
            pltpu.VMEM((3 * D, D), BF),
            pltpu.VMEM((D, D), BF),
            pltpu.VMEM((D, D), BF),
            pltpu.VMEM((GROUP, GROUP), F32),
            pltpu.VMEM((D, GROUP), BF),
            pltpu.VMEM((3 * D, GROUP), BF),
            pltpu.VMEM((3 * D, D), F32),
            pltpu.VMEM((D, D), F32),
            pltpu.VMEM((GROUP, D), BF),
        ],
        compiler_params=params(60),
        cost_estimate=cost(49),
        name="attend_back",
    )(tag, resid, shrunk, d_second, gradient, attn, mods, qkv, merged, conv_in, lse, packed, packed)


def finish_kernel(
    tag_ref, d_conv, norm, factor, d_resid, output, mods, kernel,
    block_output, input_grad, g_kernel, sums, d_first, total,
):
    tag = tag_ref[0]
    left, right = edge_columns(tag)
    keep = 1.0 - tag.astype(F32)

    def lanes(i, _):
        cols = pl.ds(pl.multiple_of(i * 128, 128), 128)
        taps = [jnp.broadcast_to(kernel[t : t + 1, cols], (16, 128)) for t in range(9)]

        def load_grad(g, p):
            return d_conv[g, p * 16 : p * 16 + 16, cols]

        def load_field(g, p):
            q = 2 * (p // 8)
            shift = mods[0, q : q + 2, :, cols].reshape(16, 128)
            scale = mods[1, q : q + 2, :, cols].reshape(16, 128)
            return norm[g, p * 16 : p * 16 + 16, cols] * (1.0 + scale) + shift

        def emit(g, p, value):
            d_first[g, p * 16 : p * 16 + 16, cols] = value

        grads = conv_back_rows(load_grad, load_field, taps, left, right, keep, emit)
        for t in range(9):
            g_kernel[t : t + 1, cols] = jnp.sum(grads[t], axis=0, keepdims=True)
        return 0

    lax.fori_loop(0, D // 128, lanes, 0)
    sums[...] = jnp.zeros_like(sums)

    def rows_back(i, _):
        g, part = i // 4, i % 4
        rows = pl.ds(pl.multiple_of(part * 64, 64), 64)
        half = part // 2
        value = d_first[g, rows, :]
        normal = norm[g, rows, :]
        sums[0, pl.ds(2 * half, 2)] += jnp.sum(value.reshape(4, 2, 8, D), axis=0)
        sums[1, pl.ds(2 * half, 2)] += jnp.sum((value * normal).reshape(4, 2, 8, D), axis=0)
        inner = (value.reshape(4, 2, 8, D) * (1.0 + quadrant_rows(mods, 1, half))).reshape(64, D)
        mean = jnp.mean(inner, axis=-1, keepdims=True)
        along = jnp.mean(inner * normal, axis=-1, keepdims=True)
        total[g, rows, :] = (
            d_resid[g, rows, :] + (inner - mean - normal * along) * factor[g, rows, :]
        )
        return 0

    lax.fori_loop(0, 16, rows_back, 0)
    order = ungroup_matrix()

    def place(i, _):
        rows = pl.ds(pl.multiple_of(i * 64, 64), 64)
        target = pl.ds(pl.multiple_of(i * 256, 256), 256)
        grouped = total[:, rows, :].reshape(256, D)
        high = grouped.astype(BF)
        rest = (grouped - high.astype(F32)).astype(BF)
        input_grad[target, :] = dot(order, high, 1, 0) + dot(order, rest, 1, 0)
        block_output[target, :] = dot(order, output[:, rows, :].reshape(256, D), 1, 0).astype(BF)
        return 0

    lax.fori_loop(0, 4, place, 0)


def finish(tag, d_conv, norm, factor, d_resid, output, mods, kernel):
    return pl.pallas_call(
        finish_kernel,
        in_specs=[SMEM_SPEC] + [pl.BlockSpec(memory_space=pltpu.VMEM)] * 7,
        out_specs=[pl.BlockSpec(memory_space=pltpu.VMEM)] * 4,
        out_shape=[
            jax.ShapeDtypeStruct((TOK, D), BF),
            jax.ShapeDtypeStruct((TOK, D), F32),
            jax.ShapeDtypeStruct((9, D), F32),
            jax.ShapeDtypeStruct((2, 4, 8, D), F32),
        ],
        scratch_shapes=[pltpu.VMEM((4, GROUP, D), F32), pltpu.VMEM((4, GROUP, D), F32)],
        compiler_params=params(60),
        cost_estimate=cost(16),
        name="finish",
    )(tag, d_conv, norm, factor, d_resid, output, mods, kernel)


BOTH = ("dp", "fsdp")


def exchange(pieces):
    return lax.all_to_all(pieces, BOTH, 0, 0, tiled=True)


def pack_shards(qkv, proj, expand, shrink):
    low = shrink.T.reshape(UR, 4, UC).transpose(1, 0, 2).reshape(4 * UR, UC)
    return jnp.concatenate([qkv.T, proj.T, expand.T, low], axis=0)


def gather_packed(nd, nf, qkv, proj, expand, shrink):
    if (nd, nf) == (NJ, NK):
        rows = lax.all_gather(pack_shards(qkv, proj, expand, shrink), BOTH)
        return rows.reshape(NJ, NK, UNITS, UR, UC)

    def full(shard):
        rows = lax.all_gather(shard.T, "fsdp", axis=1, tiled=True)
        return lax.all_gather(rows, "dp", axis=0, tiled=True)

    def split(weight, units):
        return weight.reshape(NJ, units, UR, NK, UC).transpose(0, 3, 1, 2, 4)

    low = full(shrink).reshape(NJ, UR, NK, 4, UC).transpose(0, 2, 3, 1, 4)
    return jnp.concatenate(
        [split(full(qkv), 3), split(full(proj), 1), split(full(expand), 4), low], axis=2
    )


def pick(grads, index, axis):
    return lax.dynamic_index_in_dim(grads, index, axis, keepdims=False)


def swap(value, bit):
    if bit is None:
        return lax.ppermute(value, "fsdp", [(0, 1), (1, 0)])
    return lax.ppermute(value, "dp", [(i, i ^ bit) for i in range(NJ)])


def halve(keep, got, axis, bit):
    mine = lax.axis_index("fsdp") if bit is None else (lax.axis_index("dp") // bit) % 2
    sent = pick(keep, 1 - mine, axis) + pick(got, 1 - mine, axis)
    kept = pick(keep, mine, axis) + pick(got, mine, axis)
    return kept, swap(sent, bit)


def last_sum(keep, got):
    place = lax.axis_index("dp") // 4
    total = (pick(keep, place, 0) + pick(got, place, 0)).astype(F32)
    for step in range(1, 4):
        target = (place + step) % 4
        sent = pick(keep, target, 0) + pick(got, target, 0)
        moved = [(i, (i + 4 * step) % NJ) for i in range(NJ)]
        total = total + lax.ppermute(sent, "dp", moved).astype(F32)
    return total


def scatter_packed(nd, nf, keep_a, send_a, keep_b, send_b):
    if (nd, nf) == (NJ, NK):
        a, b = (x.reshape((4, 2) + x.shape[1:]) for x in (keep_a, keep_b))
        got_a, got_b = swap(send_a, 1).reshape(a.shape), swap(send_b, 1).reshape(b.shape)
        a, got_a = halve(a, got_a, 2, None)
        b, got_b = halve(b, got_b, 1, 2)
        a, got_a = halve(a, got_a, 1, 2)
        b, got_b = halve(b, got_b, 1, None)
        return last_sum(a, got_a), last_sum(b, got_b)
    return jnp.stack([keep_a, send_a], axis=1), jnp.stack([keep_b, send_b], axis=1)


def own_shard(nd, nf, kind, units):
    if (nd, nf) == (NJ, NK):
        if kind == "shrink":
            return units.transpose(1, 0, 2).reshape(UR, 4 * UC).T
        return units.reshape(-1, UC).T
    units = units.reshape((NJ,) + units.shape[2:])
    if kind == "shrink":
        weight = units.transpose(0, 3, 1, 2, 4).reshape(NJ * UR, -1)
    else:
        weight = units.transpose(0, 2, 3, 1, 4).reshape(-1, NK * UC)
    columns = lax.psum_scatter(weight, "dp", scatter_dimension=0, tiled=True)
    piece = lax.psum_scatter(columns, "fsdp", scatter_dimension=1, tiled=True)
    return piece.astype(F32).T


def condition(nd, nf, timesteps, classes, step_table, class_table, attn_kernel, ffn_kernel):
    slots = nd * nf
    mine = jnp.concatenate([timesteps[0], classes[0]])[None]
    ids = exchange(jnp.broadcast_to(mine, (slots, 8)))
    first_row = lax.axis_index("fsdp") * step_table.shape[0]
    own = first_row + jnp.arange(step_table.shape[0], dtype=jnp.int32)
    step_hot = (ids[:, :4].reshape(-1, 1) == own[None, :]).astype(BF)
    class_hot = (ids[:, 4:].reshape(-1, 1) == own[None, :]).astype(BF)
    part = jnp.dot(step_hot, step_table, preferred_element_type=F32) + jnp.dot(
        class_hot, class_table, preferred_element_type=F32
    )
    cond = lax.psum(part, "fsdp")
    act = jax.nn.silu(cond).astype(BF)
    items, width = act.shape
    filters = jnp.concatenate([attn_kernel, ffn_kernel], axis=1).reshape(-1, width)
    sent = lax.all_gather(jnp.concatenate([act, filters], axis=0), "dp")
    act_all = sent[:, :items].transpose(1, 0, 2).reshape(items, nd * width)
    filters = sent[:, items:].reshape(nd, 9, -1).astype(F32)
    attn_full = filters[:, :, : attn_kernel.shape[1]].transpose(1, 0, 2).reshape(9, -1)
    ffn_full = filters[:, :, attn_kernel.shape[1] :].transpose(1, 0, 2).reshape(9, -1)
    return step_hot, class_hot, cond, act_all, attn_full, ffn_full


def body(
    latents, size_tags, timesteps, classes, step_table, class_table, modulation_weight,
    attn_kernel, qkv_weight, proj_weight, expand_weight, ffn_kernel, shrink_weight, cotangent,
    *, nd, nf,
):
    slots = nd * nf
    tag = size_tags[0]
    core = lax.axis_index("dp") % 2 if (nd, nf) == (NJ, NK) else jnp.int32(0)
    where = jnp.stack([tag, core])
    packed = gather_packed(nd, nf, qkv_weight, proj_weight, expand_weight, shrink_weight)
    tokens, gradient, norm, factor = prepare(latents, cotangent)
    step_hot, class_hot, cond, act_all, attn_full, ffn_full = condition(
        nd, nf, timesteps, classes, step_table, class_table, attn_kernel, ffn_kernel
    )
    height, width = modulation_weight.shape
    act_rows = lax.dynamic_slice_in_dim(
        act_all, lax.axis_index("fsdp") * height, height, axis=1
    )
    part = jnp.dot(act_rows, modulation_weight, preferred_element_type=F32)
    part = exchange(part.reshape(slots, 4, width)).reshape(nd, nf, 4, width)
    mod_rows = part.sum(axis=1).transpose(1, 0, 2).reshape(4, nd * width)
    chosen = jnp.where(tag == 1, mod_rows, mod_rows[:1])
    mods = jnp.broadcast_to(chosen.reshape(4, 6, 1, D).transpose(1, 0, 2, 3), (6, 4, 8, D))

    conv_in = first_conv(size_tags, norm, mods, attn_full)
    qkv, merged, attn, resid, second, lse = attend(size_tags, conv_in, tokens, mods, packed)
    shrunk, d_second, *grads, g_ffn = feed(where, second, gradient, mods, packed, ffn_full)
    expand, shrink = scatter_packed(nd, nf, *grads)
    output, d_resid, *grads, d_conv, later = attend_back(
        where, resid, shrunk, d_second, gradient, attn, mods, qkv, merged, conv_in, lse, packed
    )
    first, rest = scatter_packed(nd, nf, *grads)
    units = rest.ndim - 3
    proj = lax.slice_in_dim(rest, 1, 2, axis=units)
    joined = jnp.concatenate([first, lax.slice_in_dim(rest, 0, 1, axis=units)], axis=units)
    block_output, input_grad, g_attn, early = finish(
        size_tags, d_conv, norm, factor, d_resid, output, mods, attn_full
    )
    rows = jnp.concatenate([early, later], axis=0).sum(axis=2)
    rows = rows.transpose(1, 0, 2).reshape(4, 6 * D)
    alone = jnp.concatenate([rows.sum(axis=0, keepdims=True), jnp.zeros((3, 6 * D), F32)])
    d_mod = jnp.where(tag == 1, rows, alone).astype(BF)
    filters = jnp.concatenate([g_attn.reshape(9, nd, -1), g_ffn.reshape(9, nd, -1)], axis=2)
    pieces = jnp.concatenate(
        [
            d_mod.astype(F32).reshape(4, nd, width).transpose(1, 0, 2).reshape(nd, -1),
            filters.transpose(1, 0, 2).reshape(nd, -1),
        ],
        axis=1,
    )
    pieces = jnp.broadcast_to(pieces[:, None], (nd, nf, pieces.shape[1])).reshape(slots, 1, -1)
    got = exchange(pieces)[:, 0]
    d_mod_all = got[:, : 4 * width].reshape(slots * 4, width).astype(BF)
    filters = got[:, 4 * width :].sum(axis=0).reshape(9, -1)
    modulation_grad = dot(act_rows, d_mod_all, 0, 0)
    d_act = dot(d_mod_all, modulation_weight, 1, 1)
    spread = lax.dynamic_update_slice_in_dim(
        jnp.zeros((slots * 4, D), F32), d_act, lax.axis_index("fsdp") * height, axis=1
    )
    spread = spread.reshape(slots * 4, nd, 1, -1).transpose(1, 2, 0, 3)
    spread = jnp.broadcast_to(spread, (nd, nf) + spread.shape[2:])
    d_act = exchange(spread.reshape((slots,) + spread.shape[2:])).sum(axis=0)
    gate = jax.nn.sigmoid(cond)
    d_cond = d_act * (gate * (1.0 + cond * (1.0 - gate)))

    def table_grad(hot):
        return lax.dot_general(
            hot.astype(F32), d_cond, (((0,), (0,)), ((), ())), precision=lax.Precision.HIGHEST
        )

    cut = attn_kernel.shape[1]
    return (
        block_output,
        input_grad,
        table_grad(step_hot),
        table_grad(class_hot),
        modulation_grad,
        filters[:, :cut],
        own_shard(nd, nf, "qkv", joined),
        own_shard(nd, nf, "proj", proj),
        own_shard(nd, nf, "expand", expand),
        filters[:, cut:],
        own_shard(nd, nf, "shrink", shrink),
    )


def solution(mesh):
    matrix = P("fsdp", "dp")
    rows = P(BOTH, None)
    filters = P(None, "dp")
    in_specs = (
        rows, P(BOTH), rows, rows, matrix, matrix, matrix, filters, matrix, matrix, matrix,
        filters, matrix, rows,
    )
    out_specs = (
        rows, rows, matrix, matrix, matrix, filters, matrix, matrix, matrix, filters, matrix,
    )
    run = functools.partial(body, nd=mesh.shape["dp"], nf=mesh.shape["fsdp"])
    return jax.shard_map(run, mesh=mesh, in_specs=in_specs, out_specs=out_specs, check_vma=False)
```

```python
import functools

import jax
import jax.numpy as jnp
from jax import lax
from jax.experimental import pallas as pl
from jax.experimental.pallas import tpu as pltpu
from jax.sharding import PartitionSpec as P

D = 768
H = 12
HD = 64
FF = 3072
SIDE = 32
GROUP = 256
TOK = SIDE * SIDE
EPS = 1e-06
NJ, NK, UR, UC = 16, 2, 48, 384
UNITS = 12
CHUNK = 768
MIB = 1024 * 1024
BF = jnp.bfloat16
F32 = jnp.float32
GELU_A = 0.7978845608028654
GELU_B = GELU_A * 0.044715


def dot(left, right, left_dim, right_dim):
    return lax.dot_general(
        left, right, (((left_dim,), (right_dim,)), ((), ())), preferred_element_type=F32
    )


def params(limit=56):
    return pltpu.CompilerParams(vmem_limit_bytes=limit * MIB)


def cost(micros):
    return pl.CostEstimate(flops=int(micros * 1e8), transcendentals=0, bytes_accessed=4 * MIB)


def whole(shape):
    zeros = (0,) * len(shape)
    return pl.BlockSpec(shape, lambda *ids: zeros, pipeline_mode=pl.Buffered(1))


SMEM_SPEC = pl.BlockSpec(memory_space=pltpu.SMEM)


def group_place(natural):
    pair, odd_row = natural // 64, (natural // 32) % 2
    column, odd_column = (natural % 32) // 2, natural % 2
    return (2 * odd_row + odd_column) * 64 + pair * 16 + column


def ungroup_matrix():
    natural = lax.broadcasted_iota(jnp.int32, (256, 256), 0)
    grouped = lax.broadcasted_iota(jnp.int32, (256, 256), 1)
    return jnp.where(group_place(natural) == grouped, 1.0, 0.0).astype(BF)


def group_matrix():
    natural = lax.broadcasted_iota(jnp.int32, (256, 256), 1)
    grouped = lax.broadcasted_iota(jnp.int32, (256, 256), 0)
    return jnp.where(group_place(natural) == grouped, 1.0, 0.0).astype(BF)


def norm_stats(values):
    centre = values - jnp.mean(values, axis=-1, keepdims=True)
    variance = jnp.mean(centre * centre, axis=-1, keepdims=True)
    scale = lax.rsqrt(variance + EPS)
    return centre * scale, scale


def prepare_kernel(latents, cotangent, tokens, gradient, norm, scale):
    order = group_matrix()
    gathered = dot(order, latents[...], 1, 0)
    gradient[...] = dot(order, cotangent[...], 1, 0).reshape(4, 64, D).astype(BF)
    tokens[...] = gathered.reshape(4, 64, D).astype(BF)
    normal, factor = norm_stats(gathered)
    norm[...] = normal.reshape(4, 64, D)
    scale[...] = factor.reshape(4, 64, 1)


def prepare(latents, cotangent):
    flat = pl.BlockSpec((256, D), lambda i: (i, 0))
    split = pl.BlockSpec((4, 64, D), lambda i: (0, i, 0))
    return pl.pallas_call(
        prepare_kernel,
        grid=(4,),
        in_specs=[flat, flat],
        out_specs=[split, split, split, pl.BlockSpec((4, 64, 1), lambda i: (0, i, 0))],
        out_shape=[
            jax.ShapeDtypeStruct((4, GROUP, D), BF),
            jax.ShapeDtypeStruct((4, GROUP, D), BF),
            jax.ShapeDtypeStruct((4, GROUP, D), F32),
            jax.ShapeDtypeStruct((4, GROUP, 1), F32),
        ],
        compiler_params=params(),
        cost_estimate=cost(6),
        name="prepare",
    )(latents, cotangent)


def edge_columns(tag):
    place = lax.broadcasted_iota(jnp.int32, (16, 128), 0)
    left = jnp.where((place == 0) | ((place == 8) & (tag == 1)), 0.0, 1.0)
    right = jnp.where((place == 15) | ((place == 7) & (tag == 1)), 0.0, 1.0)
    return left, right


def neighbours(even, odd, left, right):
    return pltpu.roll(odd, 1, 0) * left, pltpu.roll(even, 15, 0) * right


def conv_rows(load, kernel, left, right, keep, emit):
    above = None
    partial = None
    for row in range(SIDE + 1):
        taps = None
        if row < SIDE:
            a, p = row % 2, row // 2
            even, odd = load(2 * a, p), load(2 * a + 1, p)
            odd_left, even_right = neighbours(even, odd, left, right)
            taps = []
            for tap in range(3):
                k = [kernel[3 * tap + b] for b in range(3)]
                taps.append(
                    (
                        k[0] * odd_left + k[1] * even + k[2] * odd,
                        k[0] * even + k[1] * odd + k[2] * even_right,
                    )
                )
        crossing = row == SIDE // 2
        if partial is not None:
            a, p = (row - 1) % 2, (row - 1) // 2
            for b in range(2):
                value = partial[b]
                if taps is not None:
                    below = taps[2][b]
                    value = value + (below * keep if crossing else below)
                emit(2 * a + b, p, value)
        if taps is not None:
            partial = []
            for b in range(2):
                value = taps[1][b]
                if above is not None:
                    value = value + (above[b] * keep if crossing else above[b])
                partial.append(value)
            above = taps[0]


def conv_back_rows(load_grad, load_field, kernel, left, right, keep, emit):
    sums = [jnp.zeros((16, 128), F32) for _ in range(9)]
    from_above = None
    partial = None
    field_above = None
    field = (load_field(0, 0), load_field(1, 0))
    for row in range(SIDE + 1):
        crossing = row == SIDE // 2
        taps = None
        if row < SIDE:
            a, p = row % 2, row // 2
            even, odd = load_grad(2 * a, p), load_grad(2 * a + 1, p)
            odd_left, even_right = neighbours(even, odd, left, right)
            picks = ((odd, even, odd_left), (even_right, odd, even))
            taps = []
            for tap in range(3):
                k = [kernel[3 * tap + b] for b in range(3)]
                taps.append(
                    tuple(k[0] * x[0] + k[1] * x[1] + k[2] * x[2] for x in picks)
                )
            field_below = None
            if row + 1 < SIDE:
                a, p = (row + 1) % 2, (row + 1) // 2
                field_below = (load_field(2 * a, p), load_field(2 * a + 1, p))
            for tap, rows in enumerate((field_above, field, field_below)):
                if rows is None:
                    continue
                if (tap == 0 and crossing) or (tap == 2 and row + 1 == SIDE // 2):
                    rows = (rows[0] * keep, rows[1] * keep)
                for b in range(3):
                    sums[3 * tap + b] = (
                        sums[3 * tap + b] + rows[0] * picks[0][b] + rows[1] * picks[1][b]
                    )
            field_above, field = field, field_below
        if partial is not None:
            a, p = (row - 1) % 2, (row - 1) // 2
            for b in range(2):
                value = partial[b]
                if taps is not None:
                    value = value + (taps[0][b] * keep if crossing else taps[0][b])
                emit(2 * a + b, p, value)
        if taps is not None:
            partial = []
            for b in range(2):
                value = taps[1][b]
                if from_above is not None:
                    value = value + (from_above[b] * keep if crossing else from_above[b])
                partial.append(value)
            from_above = taps[2]
    return sums


def first_conv_kernel(tag_ref, norm, mods, kernel, out):
    tag = tag_ref[0]
    left, right = edge_columns(tag)
    keep = 1.0 - tag.astype(F32)
    taps = [jnp.broadcast_to(kernel[i : i + 1, :], (16, 128)) for i in range(9)]

    def load(g, p):
        q = 2 * (p // 8)
        shift = mods[0, q : q + 2].reshape(16, 128)
        scale = mods[1, q : q + 2].reshape(16, 128)
        return norm[g, p * 16 : p * 16 + 16, :] * (1.0 + scale) + shift

    def emit(g, p, value):
        out[g, p * 16 : p * 16 + 16, :] = value.astype(BF)

    conv_rows(load, taps, left, right, keep, emit)


def first_conv(tag, norm, mods, kernel):
    return pl.pallas_call(
        first_conv_kernel,
        grid=(D // 128,),
        in_specs=[
            SMEM_SPEC,
            pl.BlockSpec((4, GROUP, 128), lambda i: (0, 0, i)),
            pl.BlockSpec((6, 4, 8, 128), lambda i: (0, 0, 0, i)),
            pl.BlockSpec((9, 128), lambda i: (0, i)),
        ],
        out_specs=pl.BlockSpec((4, GROUP, 128), lambda i: (0, 0, i)),
        out_shape=jax.ShapeDtypeStruct((4, GROUP, D), BF),
        compiler_params=params(),
        cost_estimate=cost(6),
        name="first_conv",
    )(tag, norm, mods, kernel)


def join_rows(block, target):
    rows = block.shape[0] * block.shape[2] * UR
    for k in range(NK):
        target[:, k * UC : (k + 1) * UC] = block[:, k].reshape(rows, UC)


def share_out(rows, core, units, keep, send):
    first, count = units
    for k in range(NK):
        part = rows[:, k * UC : (k + 1) * UC].astype(BF)
        part = part.reshape(-1, 2, part.shape[0] // (keep.shape[0] * 2), UC)
        even, odd = part[:, 0], part[:, 1]
        for target, value in (
            (keep, jnp.where(core == 0, even, odd)),
            (send, jnp.where(core == 0, odd, even)),
        ):
            whole_units = value.reshape(value.shape[0], -1, UR, UC)
            target[:, k] = whole_units[:, first : first + count]


def quadrant_rows(mods, index, half):
    return mods[index, pl.ds(2 * half, 2)].reshape(1, 2, 8, D)


def item_bias(tag):
    def label(dim):
        place = lax.broadcasted_iota(jnp.int32, (GROUP, GROUP), dim)
        return 2 * (place // 128) + (place % 16) // 8

    return jnp.where((label(0) == label(1)) | (tag == 0), 0.0, -1e30)


def attend_kernel(
    tag_ref, conv_in, tokens, mods, w_qkv, w_proj, qkv, merged, attn, resid, second, lse, proj_t,
    full_qkv, full_proj, bias, mixed_t,
):
    @pl.when(pl.program_id(0) == 0)
    def _():
        join_rows(w_qkv, full_qkv)
        join_rows(w_proj, full_proj)
        proj_t[...] = full_proj[...].T
        bias[...] = item_bias(tag_ref[0])

    qkv[0] = dot(full_qkv[...], conv_in[0], 1, 1).astype(BF)

    def head(h, _):
        rows = pl.ds(pl.multiple_of(h * HD, HD), HD)
        queries = qkv[0, rows, :] * jnp.asarray(HD**-0.5, BF)
        keys = qkv[0, pl.ds(pl.multiple_of(D + h * HD, HD), HD), :]
        values = qkv[0, pl.ds(pl.multiple_of(2 * D + h * HD, HD), HD), :]
        scores = dot(keys, queries, 0, 0) + bias[...]
        highest = jnp.max(scores, axis=0, keepdims=True)
        raised = jnp.exp(scores - highest)
        total = jnp.sum(raised, axis=0, keepdims=True)
        probs = (raised * (1.0 / total)).astype(BF)
        lse[0, pl.ds(h, 1), :] = highest + jnp.log(total)
        mixed_t[rows, :] = dot(values, probs, 1, 0).astype(BF)
        return 0

    lax.fori_loop(0, H, head, 0, unroll=6)
    merged[0] = mixed_t[...].T
    projected = dot(merged[0], full_proj[...], 1, 1)
    attn[0] = projected.astype(BF)
    gate = mods[2].reshape(2, 1, 2, 8, D)
    resid[0] = (
        tokens[0].astype(F32) + (projected.reshape(2, 8, 2, 8, D) * gate).reshape(GROUP, D)
    )

    def rows_norm(i, _):
        rows = pl.ds(pl.multiple_of(i * 64, 64), 64)
        normal, _ = norm_stats(resid[0, rows, :])
        half = i // 2
        scaled = normal.reshape(4, 2, 8, D) * (1.0 + quadrant_rows(mods, 4, half))
        value = scaled + quadrant_rows(mods, 3, half)
        second[0, rows, :] = value.reshape(64, D).astype(BF)
        return 0

    lax.fori_loop(0, 4, rows_norm, 0)


def group_spec(*shape):
    return pl.BlockSpec((1,) + shape, lambda g: (g,) + (0,) * len(shape))


def unit_spec(units, start):
    shape = (NJ, NK, units, UR, UC)
    return pl.BlockSpec(
        shape, lambda g: (0, 0, start // units, 0, 0), pipeline_mode=pl.Buffered(1)
    )


def attend(tag, conv_in, tokens, mods, packed):
    return pl.pallas_call(
        attend_kernel,
        grid=(4,),
        in_specs=[
            SMEM_SPEC,
            group_spec(GROUP, D),
            group_spec(GROUP, D),
            whole((6, 4, 8, D)),
            unit_spec(3, 0),
            unit_spec(1, 3),
        ],
        out_specs=[
            group_spec(3 * D, GROUP),
            group_spec(GROUP, D),
            group_spec(GROUP, D),
            group_spec(GROUP, D),
            group_spec(GROUP, D),
            group_spec(16, GROUP),
            whole((D, D)),
        ],
        out_shape=[
            jax.ShapeDtypeStruct((4, 3 * D, GROUP), BF),
            jax.ShapeDtypeStruct((4, GROUP, D), BF),
            jax.ShapeDtypeStruct((4, GROUP, D), BF),
            jax.ShapeDtypeStruct((4, GROUP, D), F32),
            jax.ShapeDtypeStruct((4, GROUP, D), BF),
            jax.ShapeDtypeStruct((4, 16, GROUP), F32),
            jax.ShapeDtypeStruct((D, D), BF),
        ],
        scratch_shapes=[
            pltpu.VMEM((3 * D, D), BF),
            pltpu.VMEM((D, D), BF),
            pltpu.VMEM((GROUP, GROUP), F32),
            pltpu.VMEM((D, GROUP), BF),
        ],
        compiler_params=params(),
        cost_estimate=cost(38),
        name="attend",
    )(tag, conv_in, tokens, mods, packed, packed)


def feed_kernel(
    tag_ref, second, gradient, mods, w_expand, w_shrink, kernel, *rest,
):
    (
        shrunk, d_second, keep_expand, send_expand, keep_shrink, send_shrink, g_kernel,
        d_shrunk, d_shrunk_t, expand, shrink, field, slope, hidden, d_field,
    ) = rest[-15:]
    step = pl.program_id(0)
    tag, core = tag_ref[0], tag_ref[1]

    @pl.when(step == 0)
    def _():
        gate = mods[5].reshape(1, 2, 1, 2, 8, D)
        value = gradient[...].astype(F32).reshape(4, 2, 8, 2, 8, D) * gate
        d_shrunk[...] = value.reshape(TOK, D).astype(BF)
        d_shrunk_t[...] = d_shrunk[...].T
        if len(rest) > 15:
            shrunk[...] = rest[0][...]
            d_second[...] = rest[1][...]
        else:
            shrunk[...] = jnp.zeros_like(shrunk)
            d_second[...] = jnp.zeros_like(d_second)

    join_rows(w_expand, expand)
    for q in range(2):
        shrink[:, q * UC : (q + 1) * UC] = w_shrink[:, 0, q].reshape(D, UC)
    left, right = edge_columns(tag)
    keep = 1.0 - tag.astype(F32)
    field[...] = dot(second[...].reshape(TOK, D), expand[...], 1, 1).reshape(4, GROUP, CHUNK)
    slope[...] = dot(d_shrunk[...], shrink[...], 1, 0).reshape(4, GROUP, CHUNK)

    def lanes(i, _):
        cols = pl.ds(pl.multiple_of(i * 128, 128), 128)
        taps = [jnp.broadcast_to(kernel[t : t + 1, cols], (16, 128)) for t in range(9)]

        def load(g, p):
            return field[g, p * 16 : p * 16 + 16, cols]

        def load_slope(g, p):
            return slope[g, p * 16 : p * 16 + 16, cols]

        def emit(g, p, value):
            square = value * value
            half = 0.5 + 0.5 * jnp.tanh(value * (GELU_A + GELU_B * square))
            out = value * half
            hidden[g, p * 16 : p * 16 + 16, cols] = out.astype(BF)
            rate = half + (out - out * half) * (2.0 * GELU_A + 6.0 * GELU_B * square)
            slope[g, p * 16 : p * 16 + 16, cols] = load_slope(g, p) * rate

        conv_rows(load, taps, left, right, keep, emit)

        def emit_back(g, p, value):
            d_field[g, p * 16 : p * 16 + 16, cols] = value.astype(BF)

        sums = conv_back_rows(load_slope, load, taps, left, right, keep, emit_back)
        for t in range(9):
            g_kernel[t : t + 1, cols] = jnp.sum(sums[t], axis=0, keepdims=True)
        return 0

    lax.fori_loop(0, CHUNK // 128, lanes, 0)
    hid = hidden[...].reshape(TOK, CHUNK)
    d_fld = d_field[...].reshape(TOK, CHUNK)
    grad = dot(d_shrunk_t[...], hid, 1, 0).astype(BF)
    for q in range(2):
        part = grad[:, q * UC : (q + 1) * UC].reshape(NJ // 2, 2, UR, UC)
        keep_shrink[:, 0, q] = jnp.where(core == 0, part[:, 0], part[:, 1])
        send_shrink[:, 0, q] = jnp.where(core == 0, part[:, 1], part[:, 0])
    share_out(dot(d_fld, second[...].reshape(TOK, D), 0, 0), core, (0, 4), keep_expand, send_expand)
    shrunk[...] += dot(hid, shrink[...], 1, 1).reshape(4, GROUP, D)
    d_second[...] += dot(d_fld, expand[...], 1, 0).reshape(4, GROUP, D)


def packed_half(units):
    return jax.ShapeDtypeStruct((NJ // 2, NK, units, UR, UC), BF)


def feed(part, tag, second, gradient, mods, packed, kernel, before=()):
    half = NJ // 2
    expand_spec = pl.BlockSpec((2, NK, 4, UR, UC), lambda c: (c, 0, 0, 0, 0))
    shrink_spec = pl.BlockSpec((half, 1, 2, UR, UC), lambda c: (0, c, 0, 0, 0))
    expand_shape = jax.ShapeDtypeStruct((half // 2, NK, 4, UR, UC), BF)
    return pl.pallas_call(
        feed_kernel,
        grid=(2,),
        in_specs=[
            SMEM_SPEC,
            whole((4, GROUP, D)),
            whole((4, GROUP, D)),
            whole((6, 4, 8, D)),
            pl.BlockSpec((4, NK, 4, UR, UC), lambda c: (2 * c + part, 0, 1, 0, 0)),
            pl.BlockSpec((NJ, 1, 2, UR, UC), lambda c: (0, c, 4 + part, 0, 0)),
            pl.BlockSpec((9, CHUNK), lambda c: (0, 2 * c + part)),
        ]
        + [whole((4, GROUP, D)) for _ in before],
        out_specs=[
            whole((4, GROUP, D)),
            whole((4, GROUP, D)),
            expand_spec,
            expand_spec,
            shrink_spec,
            shrink_spec,
            pl.BlockSpec((9, CHUNK), lambda c: (0, c)),
        ],
        out_shape=[
            jax.ShapeDtypeStruct((4, GROUP, D), F32),
            jax.ShapeDtypeStruct((4, GROUP, D), F32),
            expand_shape,
            expand_shape,
            packed_half(2),
            packed_half(2),
            jax.ShapeDtypeStruct((9, FF // 2), F32),
        ],
        scratch_shapes=[
            pltpu.VMEM((TOK, D), BF),
            pltpu.VMEM((D, TOK), BF),
            pltpu.VMEM((CHUNK, D), BF),
            pltpu.VMEM((D, CHUNK), BF),
            pltpu.VMEM((4, GROUP, CHUNK), F32),
            pltpu.VMEM((4, GROUP, CHUNK), F32),
            pltpu.VMEM((4, GROUP, CHUNK), BF),
            pltpu.VMEM((4, GROUP, CHUNK), BF),
        ],
        compiler_params=params(60),
        cost_estimate=cost(38),
        name=f"feed_{part}",
    )(tag, second, gradient, mods, packed, packed, kernel, *before)


def attend_back_kernel(
    tag_ref, resid, shrunk, d_second, gradient, attn, mods, qkv, lse, proj_t,
    output, d_resid, d_qkv, d_attn_t, sums,
    bias, d_mixed, d_attn,
):
    @pl.when(pl.program_id(0) == 0)
    def _():
        bias[...] = item_bias(tag_ref[0])
        sums[...] = jnp.zeros_like(sums)

    def rows_norm(i, _):
        rows = pl.ds(pl.multiple_of(i * 64, 64), 64)
        half = i // 2
        base = resid[0, rows, :]
        normal, factor = norm_stats(base)
        shrunk_rows = shrunk[0, rows, :]
        outward = gradient[0, rows, :].astype(F32)
        d_sec = d_second[0, rows, :]

        def by_item(value):
            return value.reshape(4, 2, 8, D)

        def add(index, value):
            sums[index, pl.ds(2 * half, 2)] += jnp.sum(by_item(value), axis=0)

        gated = (by_item(shrunk_rows) * quadrant_rows(mods, 5, half)).reshape(64, D)
        output[0, rows, :] = (base + gated).astype(BF)
        add(3, outward * shrunk_rows)
        add(1, d_sec)
        add(2, d_sec * normal)
        inner = (by_item(d_sec) * (1.0 + quadrant_rows(mods, 4, half))).reshape(64, D)
        mean = jnp.mean(inner, axis=-1, keepdims=True)
        along = jnp.mean(inner * normal, axis=-1, keepdims=True)
        back = outward + (inner - mean - normal * along) * factor
        d_resid[0, rows, :] = back
        add(0, back * attn[0, rows, :].astype(F32))
        gated = (by_item(back) * quadrant_rows(mods, 2, half)).reshape(64, D)
        d_attn[rows, :] = gated.astype(BF)
        return 0

    lax.fori_loop(0, 4, rows_norm, 0)
    d_attn_t[...] = d_attn[...].T
    d_mixed[...] = dot(proj_t[...], d_attn[...], 1, 1).astype(BF)

    def head(h, _):
        rows = pl.ds(pl.multiple_of(h * HD, HD), HD)
        key_rows = pl.ds(pl.multiple_of(D + h * HD, HD), HD)
        value_rows = pl.ds(pl.multiple_of(2 * D + h * HD, HD), HD)
        queries = qkv[0, rows, :] * jnp.asarray(HD**-0.5, BF)
        keys = qkv[0, key_rows, :]
        values = qkv[0, value_rows, :]
        d_mix = d_mixed[rows, :]
        probs = jnp.exp(dot(keys, queries, 0, 0) + (bias[...] - lse[0, pl.ds(h, 1), :]))
        d_probs = dot(values, d_mix, 0, 0)
        d_qkv[value_rows, :] = dot(d_mix, probs.astype(BF), 1, 1).astype(BF)
        weighted = probs * d_probs
        inner = jnp.sum(weighted, axis=0, keepdims=True)
        d_scores = (weighted - probs * inner).astype(BF)
        d_qkv[rows, :] = (dot(keys, d_scores, 1, 0) * HD**-0.5).astype(BF)
        d_qkv[key_rows, :] = dot(queries, d_scores, 1, 1).astype(BF)
        return 0

    lax.fori_loop(0, H, head, 0, unroll=6)


def attend_back(part, tag, resid, shrunk, d_second, gradient, attn, mods, qkv, lse, proj_t):
    def pick_group(*shape):
        return pl.BlockSpec((1,) + shape, lambda g: (2 * part + g,) + (0,) * len(shape))

    return pl.pallas_call(
        attend_back_kernel,
        grid=(2,),
        in_specs=[
            SMEM_SPEC,
            pick_group(GROUP, D),
            pick_group(GROUP, D),
            pick_group(GROUP, D),
            pick_group(GROUP, D),
            pick_group(GROUP, D),
            whole((6, 4, 8, D)),
            pick_group(3 * D, GROUP),
            pick_group(16, GROUP),
            whole((D, D)),
        ],
        out_specs=[
            group_spec(GROUP, D),
            group_spec(GROUP, D),
            pl.BlockSpec((3 * D, GROUP), lambda g: (0, g)),
            pl.BlockSpec((D, GROUP), lambda g: (0, g)),
            whole((4, 4, 8, D)),
        ],
        out_shape=[
            jax.ShapeDtypeStruct((2, GROUP, D), BF),
            jax.ShapeDtypeStruct((2, GROUP, D), F32),
            jax.ShapeDtypeStruct((3 * D, 2 * GROUP), BF),
            jax.ShapeDtypeStruct((D, 2 * GROUP), BF),
            jax.ShapeDtypeStruct((4, 4, 8, D), F32),
        ],
        scratch_shapes=[
            pltpu.VMEM((GROUP, GROUP), F32),
            pltpu.VMEM((D, GROUP), BF),
            pltpu.VMEM((GROUP, D), BF),
        ],
        compiler_params=params(),
        cost_estimate=cost(16),
        name=f"attend_back_{part}",
    )(tag, resid, shrunk, d_second, gradient, attn, mods, qkv, lse, proj_t)


PAIRS = 2
ROWS = 288 * PAIRS


def project_grads_kernel(
    tag_ref, d_qkv0, d_qkv1, d_attn0, d_attn1, conv_in, merged, keep_a, send_a, keep_b, send_b
):
    core = tag_ref[1]

    def against(low, high, field):
        return dot(low[...], field[0:2].reshape(2 * GROUP, D), 1, 0) + dot(
            high[...], field[2:4].reshape(2 * GROUP, D), 1, 0
        )

    grad = against(d_qkv0, d_qkv1, conv_in)
    share_out(grad, core, (0, 2), keep_a, send_a)
    share_out(grad, core, (2, 1), keep_b.at[:, :, 0:1], send_b.at[:, :, 0:1])
    grad = against(d_attn0, d_attn1, merged)
    share_out(grad, core, (0, 1), keep_b.at[:, :, 1:2], send_b.at[:, :, 1:2])


def project_grads(tag, d_qkv, d_attn, conv_in, merged):
    packed_spec = pl.BlockSpec((PAIRS, NK, 2, UR, UC), lambda i: (i, 0, 0, 0, 0))
    tall = pl.BlockSpec((ROWS, 2 * GROUP), lambda i: (i, 0))
    short = pl.BlockSpec((96 * PAIRS, 2 * GROUP), lambda i: (i, 0))
    return pl.pallas_call(
        project_grads_kernel,
        grid=(8 // PAIRS,),
        in_specs=[SMEM_SPEC, tall, tall, short, short, whole((4, GROUP, D)), whole((4, GROUP, D))],
        out_specs=[packed_spec] * 4,
        out_shape=[packed_half(2)] * 4,
        compiler_params=params(),
        cost_estimate=cost(8),
        name="project_grads",
    )(tag, *d_qkv, *d_attn, conv_in, merged)


def conv_back_kernel(
    tag_ref, d_qkv0, d_qkv1, w_qkv, norm, mods, kernel, d_first, g_kernel, weight, d_conv
):
    step = pl.program_id(0)

    @pl.when(step == 0)
    def _():
        d_conv[...] = jnp.zeros_like(d_conv)

    join_rows(w_qkv, weight)
    d_conv[0:2] += dot(d_qkv0[...], weight[...], 0, 0).reshape(2, GROUP, D)
    d_conv[2:4] += dot(d_qkv1[...], weight[...], 0, 0).reshape(2, GROUP, D)

    @pl.when(step == pl.num_programs(0) - 1)
    def _():
        tag = tag_ref[0]
        left, right = edge_columns(tag)
        keep = 1.0 - tag.astype(F32)

        def lanes(i, _):
            cols = pl.ds(pl.multiple_of(i * 128, 128), 128)
            taps = [jnp.broadcast_to(kernel[t : t + 1, cols], (16, 128)) for t in range(9)]

            def load_grad(g, p):
                return d_conv[g, p * 16 : p * 16 + 16, cols]

            def load_field(g, p):
                q = 2 * (p // 8)
                shift = mods[0, q : q + 2, :, cols].reshape(16, 128)
                scale = mods[1, q : q + 2, :, cols].reshape(16, 128)
                return norm[g, p * 16 : p * 16 + 16, cols] * (1.0 + scale) + shift

            def emit(g, p, value):
                d_first[g, p * 16 : p * 16 + 16, cols] = value

            grads = conv_back_rows(load_grad, load_field, taps, left, right, keep, emit)
            for t in range(9):
                g_kernel[t : t + 1, cols] = jnp.sum(grads[t], axis=0, keepdims=True)
            return 0

        lax.fori_loop(0, D // 128, lanes, 0)


def conv_back(tag, d_qkv, packed, norm, mods, kernel):
    tall = pl.BlockSpec((ROWS, 2 * GROUP), lambda i: (i, 0))
    return pl.pallas_call(
        conv_back_kernel,
        grid=(8 // PAIRS,),
        in_specs=[
            SMEM_SPEC,
            tall,
            tall,
            pl.BlockSpec((2 * PAIRS, NK, 3, UR, UC), lambda i: (i, 0, 0, 0, 0)),
            whole((4, GROUP, D)),
            whole((6, 4, 8, D)),
            whole((9, D)),
        ],
        out_specs=[whole((4, GROUP, D)), whole((9, D))],
        out_shape=[
            jax.ShapeDtypeStruct((4, GROUP, D), F32),
            jax.ShapeDtypeStruct((9, D), F32),
        ],
        scratch_shapes=[pltpu.VMEM((ROWS, D), BF), pltpu.VMEM((4, GROUP, D), F32)],
        compiler_params=params(),
        cost_estimate=cost(15),
        name="conv_back",
    )(tag, *d_qkv, packed, norm, mods, kernel)


def finish_kernel(
    d_first, norm, factor, d_resid0, d_resid1, output0, output1, mods,
    block_output, input_grad, sums, total,
):
    half = pl.program_id(0) // 2

    @pl.when(pl.program_id(0) == 0)
    def _():
        sums[...] = jnp.zeros_like(sums)

    for g in range(4):
        base = (d_resid0, d_resid1)[g // 2]
        value = d_first[g]
        normal = norm[g]
        sums[0, pl.ds(2 * half, 2)] += jnp.sum(value.reshape(4, 2, 8, D), axis=0)
        sums[1, pl.ds(2 * half, 2)] += jnp.sum((value * normal).reshape(4, 2, 8, D), axis=0)
        inner = (value.reshape(4, 2, 8, D) * (1.0 + quadrant_rows(mods, 1, half))).reshape(64, D)
        mean = jnp.mean(inner, axis=-1, keepdims=True)
        along = jnp.mean(inner * normal, axis=-1, keepdims=True)
        total[g] = base[g % 2] + (inner - mean - normal * along) * factor[g]
    order = ungroup_matrix()
    grouped = total[...].reshape(256, D)
    high = grouped.astype(BF)
    rest = (grouped - high.astype(F32)).astype(BF)
    input_grad[...] = dot(order, high, 1, 0) + dot(order, rest, 1, 0)
    low_half = dot(order[:, 0:128], output0[...].reshape(128, D), 1, 0)
    high_half = dot(order[:, 128:256], output1[...].reshape(128, D), 1, 0)
    block_output[...] = (low_half + high_half).astype(BF)


def finish(d_first, norm, factor, d_resid, output, mods):
    def split(groups, width):
        return pl.BlockSpec((groups, 64, width), lambda i: (0, i, 0))

    flat = pl.BlockSpec((256, D), lambda i: (i, 0))
    return pl.pallas_call(
        finish_kernel,
        grid=(4,),
        in_specs=[split(4, D), split(4, D), split(4, 1)] + [split(2, D)] * 4 + [whole((6, 4, 8, D))],
        out_specs=[flat, flat, whole((2, 4, 8, D))],
        out_shape=[
            jax.ShapeDtypeStruct((TOK, D), BF),
            jax.ShapeDtypeStruct((TOK, D), F32),
            jax.ShapeDtypeStruct((2, 4, 8, D), F32),
        ],
        scratch_shapes=[pltpu.VMEM((4, 64, D), F32)],
        compiler_params=params(),
        cost_estimate=cost(8),
        name="finish",
    )(d_first, norm, factor, *d_resid, *output, mods)


BOTH = ("dp", "fsdp")


def exchange(pieces):
    return lax.all_to_all(pieces, BOTH, 0, 0, tiled=True)


def pack_shards(qkv, proj, expand, shrink):
    low = shrink.T.reshape(UR, 4, UC).transpose(1, 0, 2).reshape(4 * UR, UC)
    return jnp.concatenate([qkv.T, proj.T, expand.T, low], axis=0)


def gather_packed(nd, nf, qkv, proj, expand, shrink):
    if (nd, nf) == (NJ, NK):
        rows = lax.all_gather(pack_shards(qkv, proj, expand, shrink), BOTH)
        return rows.reshape(NJ, NK, UNITS, UR, UC)

    def full(shard):
        rows = lax.all_gather(shard.T, "fsdp", axis=1, tiled=True)
        return lax.all_gather(rows, "dp", axis=0, tiled=True)

    def split(weight, units):
        return weight.reshape(NJ, units, UR, NK, UC).transpose(0, 3, 1, 2, 4)

    low = full(shrink).reshape(NJ, UR, NK, 4, UC).transpose(0, 2, 3, 1, 4)
    return jnp.concatenate(
        [split(full(qkv), 3), split(full(proj), 1), split(full(expand), 4), low], axis=2
    )


def pick(grads, index, axis):
    return lax.dynamic_index_in_dim(grads, index, axis, keepdims=False)


def swap(value, bit):
    if bit is None:
        return lax.ppermute(value, "fsdp", [(0, 1), (1, 0)])
    return lax.ppermute(value, "dp", [(i, i ^ bit) for i in range(NJ)])


def halve(keep, got, axis, bit):
    mine = lax.axis_index("fsdp") if bit is None else (lax.axis_index("dp") // bit) % 2
    kept = pick(keep, mine, axis) + pick(got, mine, axis)
    return kept, pick(keep, 1 - mine, axis) + pick(got, 1 - mine, axis)


def last_sends(total):
    place = lax.axis_index("dp") // 4
    return [pick(total, (place + step) % 4, 0) for step in range(1, 4)]


def last_sum(total, sends):
    own = pick(total, lax.axis_index("dp") // 4, 0).astype(F32)
    for step, sent in enumerate(sends, 1):
        moved = [(i, (i + 4 * step) % NJ) for i in range(NJ)]
        own = own + lax.ppermute(sent, "dp", moved).astype(F32)
    return own


def tie(value, *others):
    return lax.optimization_barrier((value,) + others)


def own_shard(nd, nf, kind, units):
    if (nd, nf) == (NJ, NK):
        if kind == "shrink":
            return units.transpose(1, 0, 2).reshape(UR, 4 * UC).T
        return units.reshape(-1, UC).T
    if kind == "shrink":
        weight = units.transpose(0, 3, 1, 2, 4).reshape(NJ * UR, -1)
    else:
        weight = units.transpose(0, 2, 3, 1, 4).reshape(-1, NK * UC)
    columns = lax.psum_scatter(weight, "dp", scatter_dimension=0, tiled=True)
    piece = lax.psum_scatter(columns, "fsdp", scatter_dimension=1, tiled=True)
    return piece.astype(F32).T


def both_cores(keep, send):
    return jnp.stack([keep, send], axis=1).reshape((-1,) + keep.shape[1:])


def condition(nd, nf, timesteps, classes, step_table, class_table, attn_kernel, ffn_kernel):
    slots = nd * nf
    mine = jnp.concatenate([timesteps[0], classes[0]])[None]
    ids = exchange(jnp.broadcast_to(mine, (slots, 8)))
    first_row = lax.axis_index("fsdp") * step_table.shape[0]
    own = first_row + jnp.arange(step_table.shape[0], dtype=jnp.int32)
    step_hot = (ids[:, :4].reshape(-1, 1) == own[None, :]).astype(BF)
    class_hot = (ids[:, 4:].reshape(-1, 1) == own[None, :]).astype(BF)
    part = jnp.dot(step_hot, step_table, preferred_element_type=F32) + jnp.dot(
        class_hot, class_table, preferred_element_type=F32
    )
    cond = lax.psum(part, "fsdp")
    act = jax.nn.silu(cond).astype(BF)
    items, width = act.shape
    filters = jnp.concatenate([attn_kernel, ffn_kernel], axis=1).reshape(-1, width)
    sent = lax.all_gather(jnp.concatenate([act, filters], axis=0), "dp")
    act_all = sent[:, :items].transpose(1, 0, 2).reshape(items, nd * width)
    filters = sent[:, items:].reshape(nd, 9, -1).astype(F32)
    attn_full = filters[:, :, : attn_kernel.shape[1]].transpose(1, 0, 2).reshape(9, -1)
    ffn_full = filters[:, :, attn_kernel.shape[1] :].transpose(1, 0, 2).reshape(9, -1)
    return step_hot, class_hot, cond, act_all, attn_full, ffn_full


def body(
    latents, size_tags, timesteps, classes, step_table, class_table, modulation_weight,
    attn_kernel, qkv_weight, proj_weight, expand_weight, ffn_kernel, shrink_weight, cotangent,
    *, nd, nf,
):
    slots = nd * nf
    tag = size_tags[0]
    core = lax.axis_index("dp") % 2 if (nd, nf) == (NJ, NK) else jnp.int32(0)
    where = jnp.stack([tag, core])
    packed = gather_packed(nd, nf, qkv_weight, proj_weight, expand_weight, shrink_weight)
    tokens, gradient, norm, factor = prepare(latents, cotangent)
    step_hot, class_hot, cond, act_all, attn_full, ffn_full = condition(
        nd, nf, timesteps, classes, step_table, class_table, attn_kernel, ffn_kernel
    )
    height, width = modulation_weight.shape
    act_rows = lax.dynamic_slice_in_dim(
        act_all, lax.axis_index("fsdp") * height, height, axis=1
    )
    part = jnp.dot(act_rows, modulation_weight, preferred_element_type=F32)
    part = exchange(part.reshape(slots, 4, width)).reshape(nd, nf, 4, width)
    mod_rows = part.sum(axis=1).transpose(1, 0, 2).reshape(4, nd * width)
    chosen = jnp.where(tag == 1, mod_rows, mod_rows[:1])
    mods = jnp.broadcast_to(chosen.reshape(4, 6, 1, D).transpose(1, 0, 2, 3), (6, 4, 8, D))

    conv_in = first_conv(size_tags, norm, mods, attn_full)
    qkv, merged, attn, resid, second, lse, proj_t = attend(
        size_tags, conv_in, tokens, mods, packed
    )
    common = (second, gradient, mods, packed, ffn_full)
    square = (nd, nf) == (NJ, NK)
    shrunk, d_second, keep_e0, send_e0, keep_s0, send_s0, g_ffn0 = feed(0, where, *common)
    if square:
        got_e0, got_s0 = swap(send_e0, 1), swap(send_s0, 1)
    shrunk, d_second, keep_e1, send_e1, keep_s1, send_s1, g_ffn1 = feed(
        1, where, *common, (shrunk, d_second)
    )
    g_ffn = jnp.stack([g_ffn0.reshape(9, 2, -1), g_ffn1.reshape(9, 2, -1)], axis=2).reshape(9, FF)
    if square:
        got_e1, got_s1 = swap(send_e1, 1), swap(send_s1, 1)

        def grid(value, outer):
            return value.reshape((outer, 2) + value.shape[1:])

        keep_e0, out_e0 = halve(grid(keep_e0, 2), grid(got_e0, 2), 2, None)
        keep_s0, out_s0 = halve(grid(keep_s0, 4), grid(got_s0, 4), 1, 2)
        d_second, out_e0, out_s0 = tie(d_second, out_e0, out_s0)
        got_e0, got_s0 = swap(out_e0, None), swap(out_s0, 2)
    back = (gradient, attn, mods, qkv, lse)
    output0, d_resid0, d_qkv0, d_attn0, later0 = attend_back(
        0, where, resid, shrunk, d_second, *back, proj_t
    )
    if square:
        d_qkv0, got_e0, got_s0, got_e1, got_s1 = tie(d_qkv0, got_e0, got_s0, got_e1, got_s1)
        keep_e0, out_e0 = halve(keep_e0, got_e0, 1, 2)
        keep_s0, out_s0 = halve(keep_s0, got_s0, 1, None)
        keep_e1, out_e1 = halve(grid(keep_e1, 2), grid(got_e1, 2), 2, None)
        keep_s1, out_s1 = halve(grid(keep_s1, 4), grid(got_s1, 4), 1, 2)
        d_second, d_qkv0, out_e0, out_s0, out_e1, out_s1 = tie(
            d_second, d_qkv0, out_e0, out_s0, out_e1, out_s1
        )
        got_e0, got_s0 = swap(out_e0, 2), swap(out_s0, None)
        got_e1, got_s1 = swap(out_e1, None), swap(out_s1, 2)
    output1, d_resid1, d_qkv1, d_attn1, later1 = attend_back(
        1, where, resid, shrunk, d_second, *back, proj_t
    )
    d_qkv = (d_qkv0, d_qkv1)
    keep_a, send_a, keep_b, send_b = project_grads(
        where, d_qkv, (d_attn0, d_attn1), conv_in, merged
    )
    if square:
        got_a, got_b = swap(send_a, 1), swap(send_b, 1)
        keep_a, got_e1, got_s1 = tie(keep_a, got_e1, got_s1)
        keep_e1, out_e1 = halve(keep_e1, got_e1, 1, 2)
        keep_s1, out_s1 = halve(keep_s1, got_s1, 1, None)
        norm, out_e1, out_s1 = tie(norm, out_e1, out_s1)
        got_e1, got_s1 = swap(out_e1, 2), swap(out_s1, None)
    d_first, g_attn = conv_back(where, d_qkv, packed, norm, mods, attn_full)
    if square:
        d_first, got_e1, got_s1, got_a, got_b = tie(d_first, got_e1, got_s1, got_a, got_b)
        expand = jnp.stack([keep_e0 + got_e0, keep_e1 + got_e1], axis=1).reshape(4, 4, UR, UC)
        total = jnp.concatenate([expand, keep_s0 + got_s0, keep_s1 + got_s1], axis=1)
        sends = last_sends(total)
        keep_a, out_a = halve(grid(keep_a, 4), grid(got_a, 4), 2, None)
        keep_b, out_b = halve(grid(keep_b, 4), grid(got_b, 4), 1, 2)
        d_first, out_a, out_b, *sends = tie(d_first, out_a, out_b, *sends)
        feeding = last_sum(total, sends)
        got_a, got_b = swap(out_a, None), swap(out_b, 2)
    block_output, input_grad, early = finish(
        d_first, norm, factor, (d_resid0, d_resid1), (output0, output1), mods
    )
    later = later0 + later1
    if square:
        keep_a, out_a = halve(keep_a, got_a, 1, 2)
        keep_b, out_b = halve(keep_b, got_b, 1, None)
        got_a, got_b = swap(out_a, 2), swap(out_b, None)
        total = jnp.concatenate([keep_a + got_a, keep_b + got_b], axis=1)
        packed_grads = (last_sum(total, last_sends(total)), feeding)
        packed_grads = jnp.concatenate(packed_grads, axis=0)
        cuts = [packed_grads[i:j] for i, j in ((0, 3), (3, 4), (4, 8), (8, 12))]
    else:
        first, rest = both_cores(keep_a, send_a), both_cores(keep_b, send_b)
        expand = jnp.stack(
            [both_cores(k, s).reshape((2, 4, NK, 4, UR, UC)) for k, s in
             ((keep_e0, send_e0), (keep_e1, send_e1))],
            axis=1,
        ).reshape(NJ, NK, 4, UR, UC)
        shrink = [both_cores(keep_s0, send_s0), both_cores(keep_s1, send_s1)]
        cuts = [
            jnp.concatenate([first, rest[:, :, :1]], axis=2),
            rest[:, :, 1:],
            expand,
            jnp.concatenate(shrink, axis=2),
        ]
    shards = [
        own_shard(nd, nf, kind, cut)
        for kind, cut in zip(("qkv", "proj", "expand", "shrink"), cuts)
    ]
    rows = jnp.concatenate([early, later], axis=0).sum(axis=2)
    rows = rows.transpose(1, 0, 2).reshape(4, 6 * D)
    alone = jnp.concatenate([rows.sum(axis=0, keepdims=True), jnp.zeros((3, 6 * D), F32)])
    d_mod = jnp.where(tag == 1, rows, alone).astype(BF)
    filters = jnp.concatenate([g_attn.reshape(9, nd, -1), g_ffn.reshape(9, nd, -1)], axis=2)
    pieces = jnp.concatenate(
        [
            d_mod.astype(F32).reshape(4, nd, width).transpose(1, 0, 2).reshape(nd, -1),
            filters.transpose(1, 0, 2).reshape(nd, -1),
        ],
        axis=1,
    )
    pieces = jnp.broadcast_to(pieces[:, None], (nd, nf, pieces.shape[1])).reshape(slots, 1, -1)
    got = exchange(pieces)[:, 0]
    d_mod_all = got[:, : 4 * width].reshape(slots * 4, width).astype(BF)
    filters = got[:, 4 * width :].sum(axis=0).reshape(9, -1)
    modulation_grad = dot(act_rows, d_mod_all, 0, 0)
    d_act = dot(d_mod_all, modulation_weight, 1, 1)
    spread = lax.dynamic_update_slice_in_dim(
        jnp.zeros((slots * 4, D), F32), d_act, lax.axis_index("fsdp") * height, axis=1
    )
    spread = spread.reshape(slots * 4, nd, 1, -1).transpose(1, 2, 0, 3)
    spread = jnp.broadcast_to(spread, (nd, nf) + spread.shape[2:])
    d_act = exchange(spread.reshape((slots,) + spread.shape[2:])).sum(axis=0)
    gate = jax.nn.sigmoid(cond)
    d_cond = d_act * (gate * (1.0 + cond * (1.0 - gate)))

    def table_grad(hot):
        return lax.dot_general(
            hot.astype(F32), d_cond, (((0,), (0,)), ((), ())), precision=lax.Precision.HIGHEST
        )

    cut = attn_kernel.shape[1]
    return (
        block_output,
        input_grad,
        table_grad(step_hot),
        table_grad(class_hot),
        modulation_grad,
        filters[:, :cut],
        shards[0],
        shards[1],
        shards[2],
        filters[:, cut:],
        shards[3],
    )


def solution(mesh):
    matrix = P("fsdp", "dp")
    rows = P(BOTH, None)
    filters = P(None, "dp")
    in_specs = (
        rows, P(BOTH), rows, rows, matrix, matrix, matrix, filters, matrix, matrix, matrix,
        filters, matrix, rows,
    )
    out_specs = (
        rows, rows, matrix, matrix, matrix, filters, matrix, matrix, matrix, filters, matrix,
    )
    run = functools.partial(body, nd=mesh.shape["dp"], nf=mesh.shape["fsdp"])
    return jax.shard_map(run, mesh=mesh, in_specs=in_specs, out_specs=out_specs, check_vma=False)
```

```python
import functools

import jax
import jax.numpy as jnp
from jax import lax
from jax.experimental import pallas as pl
from jax.experimental.pallas import tpu as pltpu
from jax.sharding import PartitionSpec as P

D = 768
H = 12
HD = 64
FF = 3072
SIDE = 32
GROUP = 256
TOK = SIDE * SIDE
EPS = 1e-06
NJ, NK, UR, UC = 16, 2, 48, 384
CHUNK = 768
MIB = 1024 * 1024
BF = jnp.bfloat16
F32 = jnp.float32
GELU_A = 0.7978845608028654
GELU_B = GELU_A * 0.044715


def dot(left, right, left_dim, right_dim):
    return lax.dot_general(
        left, right, (((left_dim,), (right_dim,)), ((), ())), preferred_element_type=F32
    )


def params(limit=56):
    return pltpu.CompilerParams(vmem_limit_bytes=limit * MIB)


def cost(micros):
    return pl.CostEstimate(flops=int(micros * 1e8), transcendentals=0, bytes_accessed=4 * MIB)


def whole(shape):
    zeros = (0,) * len(shape)
    return pl.BlockSpec(shape, lambda *ids: zeros, pipeline_mode=pl.Buffered(1))


SMEM_SPEC = pl.BlockSpec(memory_space=pltpu.SMEM)


def group_place(natural):
    pair, odd_row = natural // 64, (natural // 32) % 2
    column, odd_column = (natural % 32) // 2, natural % 2
    return (2 * odd_row + odd_column) * 64 + pair * 16 + column


def ungroup_matrix():
    natural = lax.broadcasted_iota(jnp.int32, (256, 256), 0)
    grouped = lax.broadcasted_iota(jnp.int32, (256, 256), 1)
    return jnp.where(group_place(natural) == grouped, 1.0, 0.0).astype(BF)


def group_matrix():
    natural = lax.broadcasted_iota(jnp.int32, (256, 256), 1)
    grouped = lax.broadcasted_iota(jnp.int32, (256, 256), 0)
    return jnp.where(group_place(natural) == grouped, 1.0, 0.0).astype(BF)


def norm_stats(values):
    centre = values - jnp.mean(values, axis=-1, keepdims=True)
    variance = jnp.mean(centre * centre, axis=-1, keepdims=True)
    scale = lax.rsqrt(variance + EPS)
    return centre * scale, scale


def prepare_kernel(latents, cotangent, tokens, gradient, norm, scale):
    order = group_matrix()
    gathered = dot(order, latents[...], 1, 0)
    gradient[...] = dot(order, cotangent[...], 1, 0).reshape(4, 64, D).astype(BF)
    tokens[...] = gathered.reshape(4, 64, D).astype(BF)
    normal, factor = norm_stats(gathered)
    norm[...] = normal.reshape(4, 64, D)
    scale[...] = factor.reshape(4, 64, 1)


def prepare(latents, cotangent):
    flat = pl.BlockSpec((256, D), lambda i: (i, 0))
    split = pl.BlockSpec((4, 64, D), lambda i: (0, i, 0))
    return pl.pallas_call(
        prepare_kernel,
        grid=(4,),
        in_specs=[flat, flat],
        out_specs=[split, split, split, pl.BlockSpec((4, 64, 1), lambda i: (0, i, 0))],
        out_shape=[
            jax.ShapeDtypeStruct((4, GROUP, D), BF),
            jax.ShapeDtypeStruct((4, GROUP, D), BF),
            jax.ShapeDtypeStruct((4, GROUP, D), F32),
            jax.ShapeDtypeStruct((4, GROUP, 1), F32),
        ],
        compiler_params=params(),
        cost_estimate=cost(6),
        name="prepare",
    )(latents, cotangent)


def edge_columns(tag):
    place = lax.broadcasted_iota(jnp.int32, (16, 128), 0)
    left = jnp.where((place == 0) | ((place == 8) & (tag == 1)), 0.0, 1.0)
    right = jnp.where((place == 15) | ((place == 7) & (tag == 1)), 0.0, 1.0)
    return left, right


def neighbours(even, odd, left, right):
    return pltpu.roll(odd, 1, 0) * left, pltpu.roll(even, 15, 0) * right


def conv_rows(load, kernel, left, right, keep, emit):
    above = None
    partial = None
    for row in range(SIDE + 1):
        taps = None
        if row < SIDE:
            a, p = row % 2, row // 2
            even, odd = load(2 * a, p), load(2 * a + 1, p)
            odd_left, even_right = neighbours(even, odd, left, right)
            taps = []
            for tap in range(3):
                k = [kernel[3 * tap + b] for b in range(3)]
                taps.append(
                    (
                        k[0] * odd_left + k[1] * even + k[2] * odd,
                        k[0] * even + k[1] * odd + k[2] * even_right,
                    )
                )
        crossing = row == SIDE // 2
        if partial is not None:
            a, p = (row - 1) % 2, (row - 1) // 2
            for b in range(2):
                value = partial[b]
                if taps is not None:
                    below = taps[2][b]
                    value = value + (below * keep if crossing else below)
                emit(2 * a + b, p, value)
        if taps is not None:
            partial = []
            for b in range(2):
                value = taps[1][b]
                if above is not None:
                    value = value + (above[b] * keep if crossing else above[b])
                partial.append(value)
            above = taps[0]


def conv_back_rows(load_grad, load_field, kernel, left, right, keep, emit):
    sums = [jnp.zeros((16, 128), F32) for _ in range(9)]
    from_above = None
    partial = None
    field_above = None
    field = (load_field(0, 0), load_field(1, 0))
    for row in range(SIDE + 1):
        crossing = row == SIDE // 2
        taps = None
        if row < SIDE:
            a, p = row % 2, row // 2
            even, odd = load_grad(2 * a, p), load_grad(2 * a + 1, p)
            odd_left, even_right = neighbours(even, odd, left, right)
            picks = ((odd, even, odd_left), (even_right, odd, even))
            taps = []
            for tap in range(3):
                k = [kernel[3 * tap + b] for b in range(3)]
                taps.append(
                    tuple(k[0] * x[0] + k[1] * x[1] + k[2] * x[2] for x in picks)
                )
            field_below = None
            if row + 1 < SIDE:
                a, p = (row + 1) % 2, (row + 1) // 2
                field_below = (load_field(2 * a, p), load_field(2 * a + 1, p))
            for tap, rows in enumerate((field_above, field, field_below)):
                if rows is None:
                    continue
                if (tap == 0 and crossing) or (tap == 2 and row + 1 == SIDE // 2):
                    rows = (rows[0] * keep, rows[1] * keep)
                for b in range(3):
                    sums[3 * tap + b] = (
                        sums[3 * tap + b] + rows[0] * picks[0][b] + rows[1] * picks[1][b]
                    )
            field_above, field = field, field_below
        if partial is not None:
            a, p = (row - 1) % 2, (row - 1) // 2
            for b in range(2):
                value = partial[b]
                if taps is not None:
                    value = value + (taps[0][b] * keep if crossing else taps[0][b])
                emit(2 * a + b, p, value)
        if taps is not None:
            partial = []
            for b in range(2):
                value = taps[1][b]
                if from_above is not None:
                    value = value + (from_above[b] * keep if crossing else from_above[b])
                partial.append(value)
            from_above = taps[2]
    return sums


def first_conv_kernel(tag_ref, norm, mods, kernel, out):
    tag = tag_ref[0]
    left, right = edge_columns(tag)
    keep = 1.0 - tag.astype(F32)
    taps = [jnp.broadcast_to(kernel[i : i + 1, :], (16, 128)) for i in range(9)]

    def load(g, p):
        q = 2 * (p // 8)
        shift = mods[0, q : q + 2].reshape(16, 128)
        scale = mods[1, q : q + 2].reshape(16, 128)
        return norm[g, p * 16 : p * 16 + 16, :] * (1.0 + scale) + shift

    def emit(g, p, value):
        out[g, p * 16 : p * 16 + 16, :] = value.astype(BF)

    conv_rows(load, taps, left, right, keep, emit)


def first_conv(tag, norm, mods, kernel):
    return pl.pallas_call(
        first_conv_kernel,
        grid=(D // 128,),
        in_specs=[
            SMEM_SPEC,
            pl.BlockSpec((4, GROUP, 128), lambda i: (0, 0, i)),
            pl.BlockSpec((6, 4, 8, 128), lambda i: (0, 0, 0, i)),
            pl.BlockSpec((9, 128), lambda i: (0, i)),
        ],
        out_specs=pl.BlockSpec((4, GROUP, 128), lambda i: (0, 0, i)),
        out_shape=jax.ShapeDtypeStruct((4, GROUP, D), BF),
        compiler_params=params(),
        cost_estimate=cost(6),
        name="first_conv",
    )(tag, norm, mods, kernel)


def join_rows(block, target):
    rows = block.shape[0] * block.shape[2] * UR
    for k in range(NK):
        target[:, k * UC : (k + 1) * UC] = block[:, k].reshape(rows, UC)


def share_out(rows, core, units, keep, send):
    first, count = units
    for k in range(NK):
        part = rows[:, k * UC : (k + 1) * UC].astype(BF)
        part = part.reshape(-1, 2, part.shape[0] // (keep.shape[0] * 2), UC)
        even, odd = part[:, 0], part[:, 1]
        for target, value in (
            (keep, jnp.where(core == 0, even, odd)),
            (send, jnp.where(core == 0, odd, even)),
        ):
            whole_units = value.reshape(value.shape[0], -1, UR, UC)
            target[:, k] = whole_units[:, first : first + count]


def quadrant_rows(mods, index, half):
    return mods[index, pl.ds(2 * half, 2)].reshape(1, 2, 8, D)


def item_bias(tag):
    def label(dim):
        place = lax.broadcasted_iota(jnp.int32, (GROUP, GROUP), dim)
        return 2 * (place // 128) + (place % 16) // 8

    return jnp.where((label(0) == label(1)) | (tag == 0), 0.0, -1e30)


def attend_kernel(
    where, conv_in, tokens, mods, own_a, own_b, peer_a, peer_b,
    qkv, merged, attn, resid, second, lse, proj_t, full_qkv,
    full_proj, bias, mixed_t,
):
    @pl.when(pl.program_id(0) == 0)
    def _():
        core, z, y, x = (where[i] for i in range(1, 5))
        for owner in range(NJ):
            step = (owner // 4 - z + 4) % 4
            side = (owner // 2) % 2 ^ y
            mine = core == owner % 2
            for k in range(NK):
                cols = slice(k * UC, (k + 1) * UC)
                a = jnp.where(mine, own_a[k ^ x, side, step], peer_a[k ^ x, side, step])
                b = jnp.where(mine, own_b[side, k ^ x, step], peer_b[side, k ^ x, step])
                start = owner * 3 * UR
                full_qkv[start : start + 2 * UR, cols] = a.reshape(2 * UR, UC)
                full_qkv[start + 2 * UR : start + 3 * UR, cols] = b[0]
                full_proj[owner * UR : (owner + 1) * UR, cols] = b[1]
        proj_t[...] = full_proj[...].T
        bias[...] = item_bias(where[0])

    qkv[0] = dot(full_qkv[...], conv_in[0], 1, 1).astype(BF)

    def head(h, _):
        rows = pl.ds(pl.multiple_of(h * HD, HD), HD)
        queries = qkv[0, rows, :] * jnp.asarray(HD**-0.5, BF)
        keys = qkv[0, pl.ds(pl.multiple_of(D + h * HD, HD), HD), :]
        values = qkv[0, pl.ds(pl.multiple_of(2 * D + h * HD, HD), HD), :]
        scores = dot(keys, queries, 0, 0) + bias[...]
        highest = jnp.max(scores, axis=0, keepdims=True)
        raised = jnp.exp(scores - highest)
        total = jnp.sum(raised, axis=0, keepdims=True)
        probs = (raised * (1.0 / total)).astype(BF)
        lse[0, pl.ds(h, 1), :] = highest + jnp.log(total)
        mixed_t[rows, :] = dot(values, probs, 1, 0).astype(BF)
        return 0

    lax.fori_loop(0, H, head, 0, unroll=6)
    merged[0] = mixed_t[...].T
    projected = dot(merged[0], full_proj[...], 1, 1)
    attn[0] = projected.astype(BF)
    gate = mods[2].reshape(2, 1, 2, 8, D)
    resid[0] = (
        tokens[0].astype(F32) + (projected.reshape(2, 8, 2, 8, D) * gate).reshape(GROUP, D)
    )

    def rows_norm(i, _):
        rows = pl.ds(pl.multiple_of(i * 64, 64), 64)
        normal, _ = norm_stats(resid[0, rows, :])
        half = i // 2
        scaled = normal.reshape(4, 2, 8, D) * (1.0 + quadrant_rows(mods, 4, half))
        value = scaled + quadrant_rows(mods, 3, half)
        second[0, rows, :] = value.reshape(64, D).astype(BF)
        return 0

    lax.fori_loop(0, 4, rows_norm, 0)


def group_spec(*shape):
    return pl.BlockSpec((1,) + shape, lambda g: (g,) + (0,) * len(shape))


def attend(where, conv_in, tokens, mods, projections):
    relative = (2, 2, 4, 2, UR, UC)
    return pl.pallas_call(
        attend_kernel,
        grid=(4,),
        in_specs=[
            SMEM_SPEC,
            group_spec(GROUP, D),
            group_spec(GROUP, D),
            whole((6, 4, 8, D)),
        ]
        + [whole(relative)] * 4,
        out_specs=[
            group_spec(3 * D, GROUP),
            group_spec(GROUP, D),
            group_spec(GROUP, D),
            group_spec(GROUP, D),
            group_spec(GROUP, D),
            group_spec(16, GROUP),
            whole((D, D)),
            whole((3 * D, D)),
        ],
        out_shape=[
            jax.ShapeDtypeStruct((4, 3 * D, GROUP), BF),
            jax.ShapeDtypeStruct((4, GROUP, D), BF),
            jax.ShapeDtypeStruct((4, GROUP, D), BF),
            jax.ShapeDtypeStruct((4, GROUP, D), F32),
            jax.ShapeDtypeStruct((4, GROUP, D), BF),
            jax.ShapeDtypeStruct((4, 16, GROUP), F32),
            jax.ShapeDtypeStruct((D, D), BF),
            jax.ShapeDtypeStruct((3 * D, D), BF),
        ],
        scratch_shapes=[
            pltpu.VMEM((D, D), BF),
            pltpu.VMEM((GROUP, GROUP), F32),
            pltpu.VMEM((D, GROUP), BF),
        ],
        compiler_params=params(),
        cost_estimate=cost(38),
        name="attend",
    )(where, conv_in, tokens, mods, *projections)


def feed_kernel(
    tag_ref, second, gradient, mods, w_expand, w_shrink, kernel,
    shrunk, d_second, keep_expand, send_expand, keep_shrink, send_shrink, g_kernel,
    d_shrunk, d_shrunk_t, expand, shrink, field, slope, hidden, d_field,
):
    step = pl.program_id(0)
    tag, core = tag_ref[0], tag_ref[1]

    @pl.when(step == 0)
    def _():
        gate = mods[5].reshape(1, 2, 1, 2, 8, D)
        value = gradient[...].astype(F32).reshape(4, 2, 8, 2, 8, D) * gate
        d_shrunk[...] = value.reshape(TOK, D).astype(BF)
        d_shrunk_t[...] = d_shrunk[...].T
        shrunk[...] = jnp.zeros_like(shrunk)
        d_second[...] = jnp.zeros_like(d_second)

    join_rows(w_expand, expand)
    for q in range(2):
        shrink[:, q * UC : (q + 1) * UC] = w_shrink[:, 0, q].reshape(D, UC)
    left, right = edge_columns(tag)
    keep = 1.0 - tag.astype(F32)
    field[...] = dot(second[...].reshape(TOK, D), expand[...], 1, 1).reshape(4, GROUP, CHUNK)
    slope[...] = dot(d_shrunk[...], shrink[...], 1, 0).reshape(4, GROUP, CHUNK)

    def lanes(i, _):
        cols = pl.ds(pl.multiple_of(i * 128, 128), 128)
        taps = [jnp.broadcast_to(kernel[t : t + 1, cols], (16, 128)) for t in range(9)]

        def load(g, p):
            return field[g, p * 16 : p * 16 + 16, cols]

        def load_slope(g, p):
            return slope[g, p * 16 : p * 16 + 16, cols]

        def emit(g, p, value):
            square = value * value
            half = 0.5 + 0.5 * jnp.tanh(value * (GELU_A + GELU_B * square))
            out = value * half
            hidden[g, p * 16 : p * 16 + 16, cols] = out.astype(BF)
            rate = half + (out - out * half) * (2.0 * GELU_A + 6.0 * GELU_B * square)
            slope[g, p * 16 : p * 16 + 16, cols] = load_slope(g, p) * rate

        conv_rows(load, taps, left, right, keep, emit)

        def emit_back(g, p, value):
            d_field[g, p * 16 : p * 16 + 16, cols] = value.astype(BF)

        sums = conv_back_rows(load_slope, load, taps, left, right, keep, emit_back)
        for t in range(9):
            g_kernel[t : t + 1, cols] = jnp.sum(sums[t], axis=0, keepdims=True)
        return 0

    lax.fori_loop(0, CHUNK // 128, lanes, 0)
    hid = hidden[...].reshape(TOK, CHUNK)
    d_fld = d_field[...].reshape(TOK, CHUNK)
    grad = dot(d_shrunk_t[...], hid, 1, 0).astype(BF)
    for q in range(2):
        part = grad[:, q * UC : (q + 1) * UC].reshape(NJ // 2, 2, UR, UC)
        keep_shrink[:, 0, q] = jnp.where(core == 0, part[:, 0], part[:, 1])
        send_shrink[:, 0, q] = jnp.where(core == 0, part[:, 1], part[:, 0])
    share_out(dot(d_fld, second[...].reshape(TOK, D), 0, 0), core, (0, 4), keep_expand, send_expand)
    shrunk[...] += dot(hid, shrink[...], 1, 1).reshape(4, GROUP, D)
    d_second[...] += dot(d_fld, expand[...], 1, 0).reshape(4, GROUP, D)


def packed_half(units):
    return jax.ShapeDtypeStruct((NJ // 2, NK, units, UR, UC), BF)


def feed(tag, second, gradient, mods, packed, kernel):
    half = NJ // 2
    expand_spec = pl.BlockSpec((2, NK, 4, UR, UC), lambda c: (c, 0, 0, 0, 0))
    shrink_spec = pl.BlockSpec((half, 1, 2, UR, UC), lambda c: (0, c // 2, c % 2, 0, 0))
    return pl.pallas_call(
        feed_kernel,
        grid=(FF // CHUNK,),
        in_specs=[
            SMEM_SPEC,
            whole((4, GROUP, D)),
            whole((4, GROUP, D)),
            whole((6, 4, 8, D)),
            pl.BlockSpec((4, NK, 4, UR, UC), lambda c: (c, 0, 0, 0, 0)),
            pl.BlockSpec((NJ, 1, 2, UR, UC), lambda c: (0, c // 2, 2 + c % 2, 0, 0)),
            pl.BlockSpec((9, CHUNK), lambda c: (0, c)),
        ],
        out_specs=[
            whole((4, GROUP, D)),
            whole((4, GROUP, D)),
            expand_spec,
            expand_spec,
            shrink_spec,
            shrink_spec,
            pl.BlockSpec((9, CHUNK), lambda c: (0, c)),
        ],
        out_shape=[
            jax.ShapeDtypeStruct((4, GROUP, D), F32),
            jax.ShapeDtypeStruct((4, GROUP, D), F32),
            packed_half(4),
            packed_half(4),
            packed_half(4),
            packed_half(4),
            jax.ShapeDtypeStruct((9, FF), F32),
        ],
        scratch_shapes=[
            pltpu.VMEM((TOK, D), BF),
            pltpu.VMEM((D, TOK), BF),
            pltpu.VMEM((CHUNK, D), BF),
            pltpu.VMEM((D, CHUNK), BF),
            pltpu.VMEM((4, GROUP, CHUNK), F32),
            pltpu.VMEM((4, GROUP, CHUNK), F32),
            pltpu.VMEM((4, GROUP, CHUNK), BF),
            pltpu.VMEM((4, GROUP, CHUNK), BF),
        ],
        compiler_params=params(60),
        cost_estimate=cost(38),
        name="feed",
    )(tag, second, gradient, mods, packed, packed, kernel)


def attend_back_kernel(
    tag_ref, resid, shrunk, d_second, gradient, attn, mods, qkv, lse, proj_t,
    output, d_resid, d_qkv, d_attn_t, sums,
    bias, d_mixed, d_attn,
):
    @pl.when(pl.program_id(0) == 0)
    def _():
        bias[...] = item_bias(tag_ref[0])
        sums[...] = jnp.zeros_like(sums)

    def rows_norm(i, _):
        rows = pl.ds(pl.multiple_of(i * 64, 64), 64)
        half = i // 2
        base = resid[0, rows, :]
        normal, factor = norm_stats(base)
        shrunk_rows = shrunk[0, rows, :]
        outward = gradient[0, rows, :].astype(F32)
        d_sec = d_second[0, rows, :]

        def by_item(value):
            return value.reshape(4, 2, 8, D)

        def add(index, value):
            sums[index, pl.ds(2 * half, 2)] += jnp.sum(by_item(value), axis=0)

        gated = (by_item(shrunk_rows) * quadrant_rows(mods, 5, half)).reshape(64, D)
        output[0, rows, :] = (base + gated).astype(BF)
        add(3, outward * shrunk_rows)
        add(1, d_sec)
        add(2, d_sec * normal)
        inner = (by_item(d_sec) * (1.0 + quadrant_rows(mods, 4, half))).reshape(64, D)
        mean = jnp.mean(inner, axis=-1, keepdims=True)
        along = jnp.mean(inner * normal, axis=-1, keepdims=True)
        back = outward + (inner - mean - normal * along) * factor
        d_resid[0, rows, :] = back
        add(0, back * attn[0, rows, :].astype(F32))
        gated = (by_item(back) * quadrant_rows(mods, 2, half)).reshape(64, D)
        d_attn[rows, :] = gated.astype(BF)
        return 0

    lax.fori_loop(0, 4, rows_norm, 0)
    d_attn_t[...] = d_attn[...].T
    d_mixed[...] = dot(proj_t[...], d_attn[...], 1, 1).astype(BF)

    def head(h, _):
        rows = pl.ds(pl.multiple_of(h * HD, HD), HD)
        key_rows = pl.ds(pl.multiple_of(D + h * HD, HD), HD)
        value_rows = pl.ds(pl.multiple_of(2 * D + h * HD, HD), HD)
        queries = qkv[0, rows, :] * jnp.asarray(HD**-0.5, BF)
        keys = qkv[0, key_rows, :]
        values = qkv[0, value_rows, :]
        d_mix = d_mixed[rows, :]
        probs = jnp.exp(dot(keys, queries, 0, 0) + (bias[...] - lse[0, pl.ds(h, 1), :]))
        d_probs = dot(values, d_mix, 0, 0)
        d_qkv[value_rows, :] = dot(d_mix, probs.astype(BF), 1, 1).astype(BF)
        weighted = probs * d_probs
        inner = jnp.sum(weighted, axis=0, keepdims=True)
        d_scores = (weighted - probs * inner).astype(BF)
        d_qkv[rows, :] = (dot(keys, d_scores, 1, 0) * HD**-0.5).astype(BF)
        d_qkv[key_rows, :] = dot(queries, d_scores, 1, 1).astype(BF)
        return 0

    lax.fori_loop(0, H, head, 0, unroll=6)


def attend_back(part, tag, resid, shrunk, d_second, gradient, attn, mods, qkv, lse, proj_t):
    def pick_group(*shape):
        return pl.BlockSpec((1,) + shape, lambda g: (2 * part + g,) + (0,) * len(shape))

    return pl.pallas_call(
        attend_back_kernel,
        grid=(2,),
        in_specs=[
            SMEM_SPEC,
            pick_group(GROUP, D),
            pick_group(GROUP, D),
            pick_group(GROUP, D),
            pick_group(GROUP, D),
            pick_group(GROUP, D),
            whole((6, 4, 8, D)),
            pick_group(3 * D, GROUP),
            pick_group(16, GROUP),
            whole((D, D)),
        ],
        out_specs=[
            group_spec(GROUP, D),
            group_spec(GROUP, D),
            pl.BlockSpec((3 * D, GROUP), lambda g: (0, g)),
            pl.BlockSpec((D, GROUP), lambda g: (0, g)),
            whole((4, 4, 8, D)),
        ],
        out_shape=[
            jax.ShapeDtypeStruct((2, GROUP, D), BF),
            jax.ShapeDtypeStruct((2, GROUP, D), F32),
            jax.ShapeDtypeStruct((3 * D, 2 * GROUP), BF),
            jax.ShapeDtypeStruct((D, 2 * GROUP), BF),
            jax.ShapeDtypeStruct((4, 4, 8, D), F32),
        ],
        scratch_shapes=[
            pltpu.VMEM((GROUP, GROUP), F32),
            pltpu.VMEM((D, GROUP), BF),
            pltpu.VMEM((GROUP, D), BF),
        ],
        compiler_params=params(),
        cost_estimate=cost(16),
        name=f"attend_back_{part}",
    )(tag, resid, shrunk, d_second, gradient, attn, mods, qkv, lse, proj_t)


PAIRS = 2
ROWS = 288 * PAIRS


def project_grads_kernel(
    tag_ref, d_qkv0, d_qkv1, d_attn0, d_attn1, conv_in, merged, keep_a, send_a, keep_b, send_b
):
    core = tag_ref[1]

    def against(low, high, field):
        return dot(low[...], field[0:2].reshape(2 * GROUP, D), 1, 0) + dot(
            high[...], field[2:4].reshape(2 * GROUP, D), 1, 0
        )

    grad = against(d_qkv0, d_qkv1, conv_in)
    share_out(grad, core, (0, 2), keep_a, send_a)
    share_out(grad, core, (2, 1), keep_b.at[:, :, 0:1], send_b.at[:, :, 0:1])
    grad = against(d_attn0, d_attn1, merged)
    share_out(grad, core, (0, 1), keep_b.at[:, :, 1:2], send_b.at[:, :, 1:2])


def project_grads(tag, d_qkv, d_attn, conv_in, merged):
    packed_spec = pl.BlockSpec((PAIRS, NK, 2, UR, UC), lambda i: (i, 0, 0, 0, 0))
    tall = pl.BlockSpec((ROWS, 2 * GROUP), lambda i: (i, 0))
    short = pl.BlockSpec((96 * PAIRS, 2 * GROUP), lambda i: (i, 0))
    return pl.pallas_call(
        project_grads_kernel,
        grid=(8 // PAIRS,),
        in_specs=[SMEM_SPEC, tall, tall, short, short, whole((4, GROUP, D)), whole((4, GROUP, D))],
        out_specs=[packed_spec] * 4,
        out_shape=[packed_half(2)] * 4,
        compiler_params=params(),
        cost_estimate=cost(8),
        name="project_grads",
    )(tag, *d_qkv, *d_attn, conv_in, merged)


def conv_back_kernel(
    tag_ref, d_qkv0, d_qkv1, weight, norm, mods, kernel, d_first, g_kernel, d_conv
):
    step = pl.program_id(0)

    @pl.when(step == 0)
    def _():
        d_conv[...] = jnp.zeros_like(d_conv)

    d_conv[0:2] += dot(d_qkv0[...], weight[...], 0, 0).reshape(2, GROUP, D)
    d_conv[2:4] += dot(d_qkv1[...], weight[...], 0, 0).reshape(2, GROUP, D)

    @pl.when(step == pl.num_programs(0) - 1)
    def _():
        tag = tag_ref[0]
        left, right = edge_columns(tag)
        keep = 1.0 - tag.astype(F32)

        def lanes(i, _):
            cols = pl.ds(pl.multiple_of(i * 128, 128), 128)
            taps = [jnp.broadcast_to(kernel[t : t + 1, cols], (16, 128)) for t in range(9)]

            def load_grad(g, p):
                return d_conv[g, p * 16 : p * 16 + 16, cols]

            def load_field(g, p):
                q = 2 * (p // 8)
                shift = mods[0, q : q + 2, :, cols].reshape(16, 128)
                scale = mods[1, q : q + 2, :, cols].reshape(16, 128)
                return norm[g, p * 16 : p * 16 + 16, cols] * (1.0 + scale) + shift

            def emit(g, p, value):
                d_first[g, p * 16 : p * 16 + 16, cols] = value

            grads = conv_back_rows(load_grad, load_field, taps, left, right, keep, emit)
            for t in range(9):
                g_kernel[t : t + 1, cols] = jnp.sum(grads[t], axis=0, keepdims=True)
            return 0

        lax.fori_loop(0, D // 128, lanes, 0)


def conv_back(tag, d_qkv, weight, norm, mods, kernel):
    tall = pl.BlockSpec((ROWS, 2 * GROUP), lambda i: (i, 0))
    return pl.pallas_call(
        conv_back_kernel,
        grid=(8 // PAIRS,),
        in_specs=[
            SMEM_SPEC,
            tall,
            tall,
            pl.BlockSpec((ROWS, D), lambda i: (i, 0)),
            whole((4, GROUP, D)),
            whole((6, 4, 8, D)),
            whole((9, D)),
        ],
        out_specs=[whole((4, GROUP, D)), whole((9, D))],
        out_shape=[
            jax.ShapeDtypeStruct((4, GROUP, D), F32),
            jax.ShapeDtypeStruct((9, D), F32),
        ],
        scratch_shapes=[pltpu.VMEM((4, GROUP, D), F32)],
        compiler_params=params(),
        cost_estimate=cost(15),
        name="conv_back",
    )(tag, *d_qkv, weight, norm, mods, kernel)


def finish_kernel(
    d_first, norm, factor, d_resid0, d_resid1, output0, output1, mods,
    block_output, input_grad, sums, total,
):
    half = pl.program_id(0) // 2

    @pl.when(pl.program_id(0) == 0)
    def _():
        sums[...] = jnp.zeros_like(sums)

    for g in range(4):
        base = (d_resid0, d_resid1)[g // 2]
        value = d_first[g]
        normal = norm[g]
        sums[0, pl.ds(2 * half, 2)] += jnp.sum(value.reshape(4, 2, 8, D), axis=0)
        sums[1, pl.ds(2 * half, 2)] += jnp.sum((value * normal).reshape(4, 2, 8, D), axis=0)
        inner = (value.reshape(4, 2, 8, D) * (1.0 + quadrant_rows(mods, 1, half))).reshape(64, D)
        mean = jnp.mean(inner, axis=-1, keepdims=True)
        along = jnp.mean(inner * normal, axis=-1, keepdims=True)
        total[g] = base[g % 2] + (inner - mean - normal * along) * factor[g]
    order = ungroup_matrix()
    grouped = total[...].reshape(256, D)
    high = grouped.astype(BF)
    rest = (grouped - high.astype(F32)).astype(BF)
    input_grad[...] = dot(order, high, 1, 0) + dot(order, rest, 1, 0)
    low_half = dot(order[:, 0:128], output0[...].reshape(128, D), 1, 0)
    high_half = dot(order[:, 128:256], output1[...].reshape(128, D), 1, 0)
    block_output[...] = (low_half + high_half).astype(BF)


def finish(d_first, norm, factor, d_resid, output, mods):
    def split(groups, width):
        return pl.BlockSpec((groups, 64, width), lambda i: (0, i, 0))

    flat = pl.BlockSpec((256, D), lambda i: (i, 0))
    return pl.pallas_call(
        finish_kernel,
        grid=(4,),
        in_specs=[split(4, D), split(4, D), split(4, 1)] + [split(2, D)] * 4 + [whole((6, 4, 8, D))],
        out_specs=[flat, flat, whole((2, 4, 8, D))],
        out_shape=[
            jax.ShapeDtypeStruct((TOK, D), BF),
            jax.ShapeDtypeStruct((TOK, D), F32),
            jax.ShapeDtypeStruct((2, 4, 8, D), F32),
        ],
        scratch_shapes=[pltpu.VMEM((4, 64, D), F32)],
        compiler_params=params(),
        cost_estimate=cost(8),
        name="finish",
    )(d_first, norm, factor, *d_resid, *output, mods)


BOTH = ("dp", "fsdp")


def exchange(pieces):
    return lax.all_to_all(pieces, BOTH, 0, 0, tiled=True)


def units_of(weight):
    return weight.T.reshape(-1, UR, UC)


def low_units(shrink):
    return shrink.T.reshape(UR, 4, UC).transpose(1, 0, 2)


def gather_feed(nd, nf, expand, shrink):
    if (nd, nf) == (NJ, NK):
        rows = jnp.concatenate([units_of(expand), low_units(shrink)]).reshape(8 * UR, UC)
        return lax.all_gather(rows, BOTH).reshape(NJ, NK, 8, UR, UC)
    low = full_rows(shrink).reshape(NJ, UR, NK, 4, UC).transpose(0, 2, 3, 1, 4)
    return jnp.concatenate([all_units(full_rows(expand), 4), low], axis=2)


def full_rows(shard):
    rows = lax.all_gather(shard.T, "fsdp", axis=1, tiled=True)
    return lax.all_gather(rows, "dp", axis=0, tiled=True)


def all_units(weight, units):
    return weight.reshape(NJ, units, UR, NK, UC).transpose(0, 3, 1, 2, 4)


def gather_projections(nd, nf, qkv, proj):
    if (nd, nf) == (NJ, NK):
        own = jnp.concatenate([units_of(qkv), units_of(proj)])
        turns = [
            lax.ppermute(own, "dp", [(i, (i - 4 * step) % NJ) for i in range(NJ)])
            for step in range(1, 4)
        ]
        a = jnp.stack([own[:2]] + [turn[:2] for turn in turns])
        b = jnp.stack([own[2:]] + [turn[2:] for turn in turns])
        a, b = jnp.stack([a, swap(a, 2)]), jnp.stack([b, swap(b, None)])
        a, b = jnp.stack([a, swap(a, None)]), jnp.stack([b, swap(b, 2)])
        return a, b, swap(a, 1), swap(b, 1)
    units = jnp.concatenate([all_units(full_rows(qkv), 3), all_units(full_rows(proj), 1)], axis=2)
    units = units.reshape((4, 2, 2) + units.shape[1:])
    first, rest = units[:, :, :, :, :2], units[:, :, :, :, 2:]
    a, b = first.transpose(2, 3, 1, 0, 4, 5, 6), rest.transpose(2, 1, 3, 0, 4, 5, 6)
    return a[0], b[0], a[1], b[1]


def pick(grads, index, axis):
    return lax.dynamic_index_in_dim(grads, index, axis, keepdims=False)


def swap(value, bit):
    if bit is None:
        return lax.ppermute(value, "fsdp", [(0, 1), (1, 0)])
    return lax.ppermute(value, "dp", [(i, i ^ bit) for i in range(NJ)])


def halve(keep, got, axis, bit):
    mine = lax.axis_index("fsdp") if bit is None else (lax.axis_index("dp") // bit) % 2
    kept = pick(keep, mine, axis) + pick(got, mine, axis)
    return kept, pick(keep, 1 - mine, axis) + pick(got, 1 - mine, axis)


def last_sends(total):
    place = lax.axis_index("dp") // 4
    return [pick(total, (place + step) % 4, 0) for step in range(1, 4)]


def last_swaps(sends):
    return [
        lax.ppermute(sent, "dp", [(i, (i + 4 * step) % NJ) for i in range(NJ)])
        for step, sent in enumerate(sends, 1)
    ]


def last_sum(total, got):
    own = pick(total, lax.axis_index("dp") // 4, 0).astype(F32)
    for value in got:
        own = own + value.astype(F32)
    return own


def tie(value, *others):
    return lax.optimization_barrier((value,) + others)


def own_shard(nd, nf, kind, units):
    if (nd, nf) == (NJ, NK):
        if kind == "shrink":
            return units.transpose(1, 0, 2).reshape(UR, 4 * UC).T
        return units.reshape(-1, UC).T
    if kind == "shrink":
        weight = units.transpose(0, 3, 1, 2, 4).reshape(NJ * UR, -1)
    else:
        weight = units.transpose(0, 2, 3, 1, 4).reshape(-1, NK * UC)
    columns = lax.psum_scatter(weight, "dp", scatter_dimension=0, tiled=True)
    piece = lax.psum_scatter(columns, "fsdp", scatter_dimension=1, tiled=True)
    return piece.astype(F32).T


def both_cores(keep, send):
    return jnp.stack([keep, send], axis=1).reshape((-1,) + keep.shape[1:])


def condition(nd, nf, timesteps, classes, step_table, class_table, attn_kernel, ffn_kernel):
    slots = nd * nf
    mine = jnp.concatenate([timesteps[0], classes[0]])[None]
    ids = exchange(jnp.broadcast_to(mine, (slots, 8)))
    first_row = lax.axis_index("fsdp") * step_table.shape[0]
    own = first_row + jnp.arange(step_table.shape[0], dtype=jnp.int32)
    step_hot = (ids[:, :4].reshape(-1, 1) == own[None, :]).astype(BF)
    class_hot = (ids[:, 4:].reshape(-1, 1) == own[None, :]).astype(BF)
    part = jnp.dot(step_hot, step_table, preferred_element_type=F32) + jnp.dot(
        class_hot, class_table, preferred_element_type=F32
    )
    cond = lax.psum(part, "fsdp")
    act = jax.nn.silu(cond).astype(BF)
    items, width = act.shape
    filters = jnp.concatenate([attn_kernel, ffn_kernel], axis=1).reshape(-1, width)
    sent = lax.all_gather(jnp.concatenate([act, filters], axis=0), "dp")
    act_all = sent[:, :items].transpose(1, 0, 2).reshape(items, nd * width)
    filters = sent[:, items:].reshape(nd, 9, -1).astype(F32)
    attn_full = filters[:, :, : attn_kernel.shape[1]].transpose(1, 0, 2).reshape(9, -1)
    ffn_full = filters[:, :, attn_kernel.shape[1] :].transpose(1, 0, 2).reshape(9, -1)
    return step_hot, class_hot, cond, act_all, attn_full, ffn_full


def body(
    latents, size_tags, timesteps, classes, step_table, class_table, modulation_weight,
    attn_kernel, qkv_weight, proj_weight, expand_weight, ffn_kernel, shrink_weight, cotangent,
    *, nd, nf,
):
    slots = nd * nf
    tag = size_tags[0]
    square = (nd, nf) == (NJ, NK)
    if square:
        place = lax.axis_index("dp")
        where = [tag, place % 2, place // 4, (place // 2) % 2, lax.axis_index("fsdp")]
        where = jnp.stack(where).astype(jnp.int32)
    else:
        where = jnp.stack([tag] + [jnp.int32(0)] * 4)
    projections = gather_projections(nd, nf, qkv_weight, proj_weight)
    packed = gather_feed(nd, nf, expand_weight, shrink_weight)
    tokens, gradient, norm, factor = prepare(latents, cotangent)
    step_hot, class_hot, cond, act_all, attn_full, ffn_full = condition(
        nd, nf, timesteps, classes, step_table, class_table, attn_kernel, ffn_kernel
    )
    height, width = modulation_weight.shape
    act_rows = lax.dynamic_slice_in_dim(
        act_all, lax.axis_index("fsdp") * height, height, axis=1
    )
    part = jnp.dot(act_rows, modulation_weight, preferred_element_type=F32)
    part = exchange(part.reshape(slots, 4, width)).reshape(nd, nf, 4, width)
    mod_rows = part.sum(axis=1).transpose(1, 0, 2).reshape(4, nd * width)
    chosen = jnp.where(tag == 1, mod_rows, mod_rows[:1])
    mods = jnp.broadcast_to(chosen.reshape(4, 6, 1, D).transpose(1, 0, 2, 3), (6, 4, 8, D))

    conv_in = first_conv(size_tags, norm, mods, attn_full)
    qkv, merged, attn, resid, second, lse, proj_t, full_qkv = attend(
        where, conv_in, tokens, mods, projections
    )
    shrunk, d_second, keep_e, send_e, keep_s, send_s, g_ffn = feed(
        where, second, gradient, mods, packed, ffn_full
    )
    back = (gradient, attn, mods, qkv, lse)
    if square:
        got_e, got_s = swap(send_e, 1), swap(send_s, 1)
    output0, d_resid0, d_qkv0, d_attn0, later0 = attend_back(
        0, where, resid, shrunk, d_second, *back, proj_t
    )

    def grid(value):
        return value.reshape((4, 2) + value.shape[1:])

    if square:
        d_qkv0, got_e, got_s = tie(d_qkv0, got_e, got_s)
        keep_e, out_e = halve(grid(keep_e), grid(got_e), 2, None)
        keep_s, out_s = halve(grid(keep_s), grid(got_s), 1, 2)
        d_second, d_qkv0, out_e, out_s = tie(d_second, d_qkv0, out_e, out_s)
        got_e, got_s = swap(out_e, None), swap(out_s, 2)
    output1, d_resid1, d_qkv1, d_attn1, later1 = attend_back(
        1, where, resid, shrunk, d_second, *back, proj_t
    )
    d_qkv = (d_qkv0, d_qkv1)
    keep_a, send_a, keep_b, send_b = project_grads(
        where, d_qkv, (d_attn0, d_attn1), conv_in, merged
    )
    if square:
        got_a, got_b = swap(send_a, 1), swap(send_b, 1)
        keep_a, got_e, got_s = tie(keep_a, got_e, got_s)
        keep_e, out_e = halve(keep_e, got_e, 1, 2)
        keep_s, out_s = halve(keep_s, got_s, 1, None)
        norm, out_e, out_s = tie(norm, out_e, out_s)
        got_e, got_s = swap(out_e, 2), swap(out_s, None)
    d_first, g_attn = conv_back(where, d_qkv, full_qkv, norm, mods, attn_full)
    if square:
        d_first, got_e, got_s, got_a, got_b = tie(d_first, got_e, got_s, got_a, got_b)
        keep_a, out_a = halve(grid(keep_a), grid(got_a), 2, None)
        keep_b, out_b = halve(grid(keep_b), grid(got_b), 1, 2)
        feeding = jnp.concatenate([keep_e + got_e, keep_s + got_s], axis=1)
        sends = last_sends(feeding)
        d_first, out_a, out_b, *sends = tie(d_first, out_a, out_b, *sends)
        got_a, got_b = swap(out_a, None), swap(out_b, 2)
        got_feeding = last_swaps(sends)
    block_output, input_grad, early = finish(
        d_first, norm, factor, (d_resid0, d_resid1), (output0, output1), mods
    )
    later = later0 + later1
    if square:
        later, got_a, got_b = tie(later, got_a, got_b)
        keep_a, out_a = halve(keep_a, got_a, 1, 2)
        keep_b, out_b = halve(keep_b, got_b, 1, None)
        got_a, got_b = swap(out_a, 2), swap(out_b, None)
        total = jnp.concatenate([keep_a + got_a, keep_b + got_b], axis=1)
        sends = last_sends(total)
        sends[0], *got_feeding = tie(sends[0], *got_feeding)
        feeding = last_sum(feeding, got_feeding)
        total = last_sum(total, last_swaps(sends))
        cuts = [total[:3], total[3:], feeding[:4], feeding[4:]]
    else:
        first, rest = both_cores(keep_a, send_a), both_cores(keep_b, send_b)
        cuts = [
            jnp.concatenate([first, rest[:, :, :1]], axis=2),
            rest[:, :, 1:],
            both_cores(keep_e, send_e),
            both_cores(keep_s, send_s),
        ]
    shards = [
        own_shard(nd, nf, kind, cut)
        for kind, cut in zip(("qkv", "proj", "expand", "shrink"), cuts)
    ]
    rows = jnp.concatenate([early, later], axis=0).sum(axis=2)
    rows = rows.transpose(1, 0, 2).reshape(4, 6 * D)
    alone = jnp.concatenate([rows.sum(axis=0, keepdims=True), jnp.zeros((3, 6 * D), F32)])
    d_mod = jnp.where(tag == 1, rows, alone).astype(BF)
    filters = jnp.concatenate([g_attn.reshape(9, nd, -1), g_ffn.reshape(9, nd, -1)], axis=2)
    pieces = jnp.concatenate(
        [
            d_mod.astype(F32).reshape(4, nd, width).transpose(1, 0, 2).reshape(nd, -1),
            filters.transpose(1, 0, 2).reshape(nd, -1),
        ],
        axis=1,
    )
    pieces = jnp.broadcast_to(pieces[:, None], (nd, nf, pieces.shape[1])).reshape(slots, 1, -1)
    got = exchange(pieces)[:, 0]
    d_mod_all = got[:, : 4 * width].reshape(slots * 4, width).astype(BF)
    filters = got[:, 4 * width :].sum(axis=0).reshape(9, -1)
    modulation_grad = dot(act_rows, d_mod_all, 0, 0)
    d_act = dot(d_mod_all, modulation_weight, 1, 1)
    spread = lax.dynamic_update_slice_in_dim(
        jnp.zeros((slots * 4, D), F32), d_act, lax.axis_index("fsdp") * height, axis=1
    )
    spread = spread.reshape(slots * 4, nd, 1, -1).transpose(1, 2, 0, 3)
    spread = jnp.broadcast_to(spread, (nd, nf) + spread.shape[2:])
    d_act = exchange(spread.reshape((slots,) + spread.shape[2:])).sum(axis=0)
    gate = jax.nn.sigmoid(cond)
    d_cond = d_act * (gate * (1.0 + cond * (1.0 - gate)))

    def table_grad(hot):
        return lax.dot_general(
            hot.astype(F32), d_cond, (((0,), (0,)), ((), ())), precision=lax.Precision.HIGHEST
        )

    cut = attn_kernel.shape[1]
    return (
        block_output,
        input_grad,
        table_grad(step_hot),
        table_grad(class_hot),
        modulation_grad,
        filters[:, :cut],
        shards[0],
        shards[1],
        shards[2],
        filters[:, cut:],
        shards[3],
    )


def solution(mesh):
    matrix = P("fsdp", "dp")
    rows = P(BOTH, None)
    filters = P(None, "dp")
    in_specs = (
        rows, P(BOTH), rows, rows, matrix, matrix, matrix, filters, matrix, matrix, matrix,
        filters, matrix, rows,
    )
    out_specs = (
        rows, rows, matrix, matrix, matrix, filters, matrix, matrix, matrix, filters, matrix,
    )
    run = functools.partial(body, nd=mesh.shape["dp"], nf=mesh.shape["fsdp"])
    return jax.shard_map(run, mesh=mesh, in_specs=in_specs, out_specs=out_specs, check_vma=False)
```

```python
import functools

import jax
import jax.numpy as jnp
from jax import lax
from jax.experimental import pallas as pl
from jax.experimental.pallas import tpu as pltpu
from jax.sharding import PartitionSpec as P

D = 768
H = 12
HD = 64
FF = 3072
SIDE = 32
GROUP = 256
TOK = SIDE * SIDE
EPS = 1e-06
NJ, NK, UR, UC = 16, 2, 48, 384
CHUNK = 768
HEADS = 3
MIB = 1024 * 1024
BF = jnp.bfloat16
F32 = jnp.float32
GELU_A = 0.7978845608028654
GELU_B = GELU_A * 0.044715


def dot(left, right, left_dim, right_dim):
    return lax.dot_general(
        left, right, (((left_dim,), (right_dim,)), ((), ())), preferred_element_type=F32
    )


def params(limit=56):
    return pltpu.CompilerParams(vmem_limit_bytes=limit * MIB)


def cost(micros):
    return pl.CostEstimate(flops=int(micros * 1e8), transcendentals=0, bytes_accessed=4 * MIB)


def whole(shape):
    zeros = (0,) * len(shape)
    return pl.BlockSpec(shape, lambda *ids: zeros, pipeline_mode=pl.Buffered(1))


SMEM_SPEC = pl.BlockSpec(memory_space=pltpu.SMEM)


def group_place(natural):
    pair, odd_row = natural // 64, (natural // 32) % 2
    column, odd_column = (natural % 32) // 2, natural % 2
    return (2 * odd_row + odd_column) * 64 + pair * 16 + column


def ungroup_matrix():
    natural = lax.broadcasted_iota(jnp.int32, (256, 256), 0)
    grouped = lax.broadcasted_iota(jnp.int32, (256, 256), 1)
    return jnp.where(group_place(natural) == grouped, 1.0, 0.0).astype(BF)


def group_matrix():
    natural = lax.broadcasted_iota(jnp.int32, (256, 256), 1)
    grouped = lax.broadcasted_iota(jnp.int32, (256, 256), 0)
    return jnp.where(group_place(natural) == grouped, 1.0, 0.0).astype(BF)


def norm_stats(values):
    centre = values - jnp.mean(values, axis=-1, keepdims=True)
    variance = jnp.mean(centre * centre, axis=-1, keepdims=True)
    scale = lax.rsqrt(variance + EPS)
    return centre * scale, scale


def prepare_kernel(latents, cotangent, tokens, gradient, norm, scale):
    order = group_matrix()
    gathered = dot(order, latents[...], 1, 0)
    gradient[...] = dot(order, cotangent[...], 1, 0).reshape(4, 64, D).astype(BF)
    tokens[...] = gathered.reshape(4, 64, D).astype(BF)
    normal, factor = norm_stats(gathered)
    norm[...] = normal.reshape(4, 64, D)
    scale[...] = factor.reshape(4, 64, 1)


def prepare(latents, cotangent):
    flat = pl.BlockSpec((256, D), lambda i: (i, 0))
    split = pl.BlockSpec((4, 64, D), lambda i: (0, i, 0))
    return pl.pallas_call(
        prepare_kernel,
        grid=(4,),
        in_specs=[flat, flat],
        out_specs=[split, split, split, pl.BlockSpec((4, 64, 1), lambda i: (0, i, 0))],
        out_shape=[
            jax.ShapeDtypeStruct((4, GROUP, D), BF),
            jax.ShapeDtypeStruct((4, GROUP, D), BF),
            jax.ShapeDtypeStruct((4, GROUP, D), F32),
            jax.ShapeDtypeStruct((4, GROUP, 1), F32),
        ],
        compiler_params=params(),
        cost_estimate=cost(6),
        name="prepare",
    )(latents, cotangent)


def edge_columns(tag):
    place = lax.broadcasted_iota(jnp.int32, (16, 128), 0)
    left = jnp.where((place == 0) | ((place == 8) & (tag == 1)), 0.0, 1.0)
    right = jnp.where((place == 15) | ((place == 7) & (tag == 1)), 0.0, 1.0)
    return left, right


def neighbours(even, odd, left, right):
    return pltpu.roll(odd, 1, 0) * left, pltpu.roll(even, 15, 0) * right


def conv_rows(load, kernel, left, right, keep, emit):
    above = None
    partial = None
    for row in range(SIDE + 1):
        taps = None
        if row < SIDE:
            a, p = row % 2, row // 2
            even, odd = load(2 * a, p), load(2 * a + 1, p)
            odd_left, even_right = neighbours(even, odd, left, right)
            taps = []
            for tap in range(3):
                k = [kernel[3 * tap + b] for b in range(3)]
                taps.append(
                    (
                        k[0] * odd_left + k[1] * even + k[2] * odd,
                        k[0] * even + k[1] * odd + k[2] * even_right,
                    )
                )
        crossing = row == SIDE // 2
        if partial is not None:
            a, p = (row - 1) % 2, (row - 1) // 2
            for b in range(2):
                value = partial[b]
                if taps is not None:
                    below = taps[2][b]
                    value = value + (below * keep if crossing else below)
                emit(2 * a + b, p, value)
        if taps is not None:
            partial = []
            for b in range(2):
                value = taps[1][b]
                if above is not None:
                    value = value + (above[b] * keep if crossing else above[b])
                partial.append(value)
            above = taps[0]


def conv_back_rows(load_grad, load_field, kernel, left, right, keep, emit):
    sums = [jnp.zeros((16, 128), F32) for _ in range(9)]
    from_above = None
    partial = None
    field_above = None
    field = (load_field(0, 0), load_field(1, 0))
    for row in range(SIDE + 1):
        crossing = row == SIDE // 2
        taps = None
        if row < SIDE:
            a, p = row % 2, row // 2
            even, odd = load_grad(2 * a, p), load_grad(2 * a + 1, p)
            odd_left, even_right = neighbours(even, odd, left, right)
            picks = ((odd, even, odd_left), (even_right, odd, even))
            taps = []
            for tap in range(3):
                k = [kernel[3 * tap + b] for b in range(3)]
                taps.append(
                    tuple(k[0] * x[0] + k[1] * x[1] + k[2] * x[2] for x in picks)
                )
            field_below = None
            if row + 1 < SIDE:
                a, p = (row + 1) % 2, (row + 1) // 2
                field_below = (load_field(2 * a, p), load_field(2 * a + 1, p))
            for tap, rows in enumerate((field_above, field, field_below)):
                if rows is None:
                    continue
                if (tap == 0 and crossing) or (tap == 2 and row + 1 == SIDE // 2):
                    rows = (rows[0] * keep, rows[1] * keep)
                for b in range(3):
                    sums[3 * tap + b] = (
                        sums[3 * tap + b] + rows[0] * picks[0][b] + rows[1] * picks[1][b]
                    )
            field_above, field = field, field_below
        if partial is not None:
            a, p = (row - 1) % 2, (row - 1) // 2
            for b in range(2):
                value = partial[b]
                if taps is not None:
                    value = value + (taps[0][b] * keep if crossing else taps[0][b])
                emit(2 * a + b, p, value)
        if taps is not None:
            partial = []
            for b in range(2):
                value = taps[1][b]
                if from_above is not None:
                    value = value + (from_above[b] * keep if crossing else from_above[b])
                partial.append(value)
            from_above = taps[2]
    return sums


def first_conv_kernel(tag_ref, norm, mods, kernel, out):
    tag = tag_ref[0]
    left, right = edge_columns(tag)
    keep = 1.0 - tag.astype(F32)
    taps = [jnp.broadcast_to(kernel[i : i + 1, :], (16, 128)) for i in range(9)]

    def load(g, p):
        q = 2 * (p // 8)
        shift = mods[0, q : q + 2].reshape(16, 128)
        scale = mods[1, q : q + 2].reshape(16, 128)
        return norm[g, p * 16 : p * 16 + 16, :] * (1.0 + scale) + shift

    def emit(g, p, value):
        out[g, p * 16 : p * 16 + 16, :] = value.astype(BF)

    conv_rows(load, taps, left, right, keep, emit)


def first_conv(tag, norm, mods, kernel):
    return pl.pallas_call(
        first_conv_kernel,
        grid=(D // 128,),
        in_specs=[
            SMEM_SPEC,
            pl.BlockSpec((4, GROUP, 128), lambda i: (0, 0, i)),
            pl.BlockSpec((6, 4, 8, 128), lambda i: (0, 0, 0, i)),
            pl.BlockSpec((9, 128), lambda i: (0, i)),
        ],
        out_specs=pl.BlockSpec((4, GROUP, 128), lambda i: (0, 0, i)),
        out_shape=jax.ShapeDtypeStruct((4, GROUP, D), BF),
        compiler_params=params(),
        cost_estimate=cost(6),
        name="first_conv",
    )(tag, norm, mods, kernel)


def join_rows(block, target):
    rows = block.shape[0] * block.shape[2] * UR
    for k in range(NK):
        target[:, k * UC : (k + 1) * UC] = block[:, k].reshape(rows, UC)


def share_out(rows, core, units, keep, send):
    first, count = units
    for k in range(NK):
        part = rows[:, k * UC : (k + 1) * UC].astype(BF)
        part = part.reshape(-1, 2, part.shape[0] // (keep.shape[0] * 2), UC)
        even, odd = part[:, 0], part[:, 1]
        for target, value in (
            (keep, jnp.where(core == 0, even, odd)),
            (send, jnp.where(core == 0, odd, even)),
        ):
            whole_units = value.reshape(value.shape[0], -1, UR, UC)
            target[:, k] = whole_units[:, first : first + count]


def quadrant_rows(mods, index, half):
    return mods[index, pl.ds(2 * half, 2)].reshape(1, 2, 8, D)


def item_bias(tag):
    def label(dim):
        place = lax.broadcasted_iota(jnp.int32, (GROUP, GROUP), dim)
        return 2 * (place // 128) + (place % 16) // 8

    return jnp.where((label(0) == label(1)) | (tag == 0), 0.0, -1e30)


def attend_kernel(
    where, conv_in, tokens, mods, own_a, own_b, peer_a, peer_b,
    qkv, merged, attn, resid, second, lse, proj_t, full_qkv,
    full_proj, bias, mixed_t,
):
    @pl.when(pl.program_id(0) == 0)
    def _():
        core, z, y, x = (where[i] for i in range(1, 5))
        for owner in range(NJ):
            step = (owner // 4 - z + 4) % 4
            side = (owner // 2) % 2 ^ y
            mine = core == owner % 2
            for k in range(NK):
                cols = slice(k * UC, (k + 1) * UC)
                a = jnp.where(mine, own_a[k ^ x, side, step], peer_a[k ^ x, side, step])
                b = jnp.where(mine, own_b[side, k ^ x, step], peer_b[side, k ^ x, step])
                start = owner * 3 * UR
                full_qkv[start : start + 2 * UR, cols] = a.reshape(2 * UR, UC)
                full_qkv[start + 2 * UR : start + 3 * UR, cols] = b[0]
                full_proj[owner * UR : (owner + 1) * UR, cols] = b[1]
        proj_t[...] = full_proj[...].T
        bias[...] = item_bias(where[0])

    qkv[0] = dot(full_qkv[...], conv_in[0], 1, 1).astype(BF)

    def head(h, _):
        rows = pl.ds(pl.multiple_of(h * HD, HD), HD)
        queries = qkv[0, rows, :] * jnp.asarray(HD**-0.5, BF)
        keys = qkv[0, pl.ds(pl.multiple_of(D + h * HD, HD), HD), :]
        values = qkv[0, pl.ds(pl.multiple_of(2 * D + h * HD, HD), HD), :]
        scores = dot(keys, queries, 0, 0) + bias[...]
        highest = jnp.max(scores, axis=0, keepdims=True)
        raised = jnp.exp(scores - highest)
        total = jnp.sum(raised, axis=0, keepdims=True)
        probs = (raised * (1.0 / total)).astype(BF)
        lse[0, pl.ds(h, 1), :] = highest + jnp.log(total)
        mixed_t[rows, :] = dot(values, probs, 1, 0).astype(BF)
        return 0

    lax.fori_loop(0, H, head, 0, unroll=HEADS)
    merged[0] = mixed_t[...].T
    projected = dot(merged[0], full_proj[...], 1, 1)
    attn[0] = projected.astype(BF)
    gate = mods[2].reshape(2, 1, 2, 8, D)
    resid[0] = (
        tokens[0].astype(F32) + (projected.reshape(2, 8, 2, 8, D) * gate).reshape(GROUP, D)
    )

    def rows_norm(i, _):
        rows = pl.ds(pl.multiple_of(i * 64, 64), 64)
        normal, _ = norm_stats(resid[0, rows, :])
        half = i // 2
        scaled = normal.reshape(4, 2, 8, D) * (1.0 + quadrant_rows(mods, 4, half))
        value = scaled + quadrant_rows(mods, 3, half)
        second[0, rows, :] = value.reshape(64, D).astype(BF)
        return 0

    lax.fori_loop(0, 4, rows_norm, 0)


def group_spec(*shape):
    return pl.BlockSpec((1,) + shape, lambda g: (g,) + (0,) * len(shape))


def attend(where, conv_in, tokens, mods, projections):
    relative = (2, 2, 4, 2, UR, UC)
    return pl.pallas_call(
        attend_kernel,
        grid=(4,),
        in_specs=[
            SMEM_SPEC,
            group_spec(GROUP, D),
            group_spec(GROUP, D),
            whole((6, 4, 8, D)),
        ]
        + [whole(relative)] * 4,
        out_specs=[
            group_spec(3 * D, GROUP),
            group_spec(GROUP, D),
            group_spec(GROUP, D),
            group_spec(GROUP, D),
            group_spec(GROUP, D),
            group_spec(16, GROUP),
            whole((D, D)),
            whole((3 * D, D)),
        ],
        out_shape=[
            jax.ShapeDtypeStruct((4, 3 * D, GROUP), BF),
            jax.ShapeDtypeStruct((4, GROUP, D), BF),
            jax.ShapeDtypeStruct((4, GROUP, D), BF),
            jax.ShapeDtypeStruct((4, GROUP, D), F32),
            jax.ShapeDtypeStruct((4, GROUP, D), BF),
            jax.ShapeDtypeStruct((4, 16, GROUP), F32),
            jax.ShapeDtypeStruct((D, D), BF),
            jax.ShapeDtypeStruct((3 * D, D), BF),
        ],
        scratch_shapes=[
            pltpu.VMEM((D, D), BF),
            pltpu.VMEM((GROUP, GROUP), F32),
            pltpu.VMEM((D, GROUP), BF),
        ],
        compiler_params=params(),
        cost_estimate=cost(38),
        name="attend",
    )(where, conv_in, tokens, mods, *projections)


def feed_kernel(
    tag_ref, second, gradient, mods, w_expand, w_shrink, kernel,
    shrunk, d_second, keep_expand, send_expand, keep_shrink, send_shrink, g_kernel,
    d_shrunk, d_shrunk_t, expand, shrink, field, slope, hidden, d_field,
):
    step = pl.program_id(0)
    tag, core = tag_ref[0], tag_ref[1]

    @pl.when(step == 0)
    def _():
        gate = mods[5].reshape(1, 2, 1, 2, 8, D)
        value = gradient[...].astype(F32).reshape(4, 2, 8, 2, 8, D) * gate
        d_shrunk[...] = value.reshape(TOK, D).astype(BF)
        d_shrunk_t[...] = d_shrunk[...].T
        shrunk[...] = jnp.zeros_like(shrunk)
        d_second[...] = jnp.zeros_like(d_second)

    join_rows(w_expand, expand)
    for q in range(2):
        shrink[:, q * UC : (q + 1) * UC] = w_shrink[:, 0, q].reshape(D, UC)
    left, right = edge_columns(tag)
    keep = 1.0 - tag.astype(F32)
    field[...] = dot(second[...].reshape(TOK, D), expand[...], 1, 1).reshape(4, GROUP, CHUNK)
    slope[...] = dot(d_shrunk[...], shrink[...], 1, 0).reshape(4, GROUP, CHUNK)

    def lanes(i, _):
        cols = pl.ds(pl.multiple_of(i * 128, 128), 128)
        taps = [jnp.broadcast_to(kernel[t : t + 1, cols], (16, 128)) for t in range(9)]

        def load(g, p):
            return field[g, p * 16 : p * 16 + 16, cols]

        def load_slope(g, p):
            return slope[g, p * 16 : p * 16 + 16, cols]

        def emit(g, p, value):
            square = value * value
            half = 0.5 + 0.5 * jnp.tanh(value * (GELU_A + GELU_B * square))
            out = value * half
            hidden[g, p * 16 : p * 16 + 16, cols] = out.astype(BF)
            rate = half + (out - out * half) * (2.0 * GELU_A + 6.0 * GELU_B * square)
            slope[g, p * 16 : p * 16 + 16, cols] = load_slope(g, p) * rate

        conv_rows(load, taps, left, right, keep, emit)

        def emit_back(g, p, value):
            d_field[g, p * 16 : p * 16 + 16, cols] = value.astype(BF)

        sums = conv_back_rows(load_slope, load, taps, left, right, keep, emit_back)
        for t in range(9):
            g_kernel[t : t + 1, cols] = jnp.sum(sums[t], axis=0, keepdims=True)
        return 0

    lax.fori_loop(0, CHUNK // 128, lanes, 0)
    hid = hidden[...].reshape(TOK, CHUNK)
    d_fld = d_field[...].reshape(TOK, CHUNK)
    grad = dot(d_shrunk_t[...], hid, 1, 0).astype(BF)
    for q in range(2):
        part = grad[:, q * UC : (q + 1) * UC].reshape(NJ // 2, 2, UR, UC)
        keep_shrink[:, 0, q] = jnp.where(core == 0, part[:, 0], part[:, 1])
        send_shrink[:, 0, q] = jnp.where(core == 0, part[:, 1], part[:, 0])
    share_out(dot(d_fld, second[...].reshape(TOK, D), 0, 0), core, (0, 4), keep_expand, send_expand)
    shrunk[...] += dot(hid, shrink[...], 1, 1).reshape(4, GROUP, D)
    d_second[...] += dot(d_fld, expand[...], 1, 0).reshape(4, GROUP, D)


def packed_half(units):
    return jax.ShapeDtypeStruct((NJ // 2, NK, units, UR, UC), BF)


def feed(tag, second, gradient, mods, packed, kernel):
    half = NJ // 2
    expand_spec = pl.BlockSpec((2, NK, 4, UR, UC), lambda c: (c, 0, 0, 0, 0))
    shrink_spec = pl.BlockSpec((half, 1, 2, UR, UC), lambda c: (0, c // 2, c % 2, 0, 0))
    return pl.pallas_call(
        feed_kernel,
        grid=(FF // CHUNK,),
        in_specs=[
            SMEM_SPEC,
            whole((4, GROUP, D)),
            whole((4, GROUP, D)),
            whole((6, 4, 8, D)),
            pl.BlockSpec((4, NK, 4, UR, UC), lambda c: (c, 0, 0, 0, 0)),
            pl.BlockSpec((NJ, 1, 2, UR, UC), lambda c: (0, c // 2, 2 + c % 2, 0, 0)),
            pl.BlockSpec((9, CHUNK), lambda c: (0, c)),
        ],
        out_specs=[
            whole((4, GROUP, D)),
            whole((4, GROUP, D)),
            expand_spec,
            expand_spec,
            shrink_spec,
            shrink_spec,
            pl.BlockSpec((9, CHUNK), lambda c: (0, c)),
        ],
        out_shape=[
            jax.ShapeDtypeStruct((4, GROUP, D), F32),
            jax.ShapeDtypeStruct((4, GROUP, D), F32),
            packed_half(4),
            packed_half(4),
            packed_half(4),
            packed_half(4),
            jax.ShapeDtypeStruct((9, FF), F32),
        ],
        scratch_shapes=[
            pltpu.VMEM((TOK, D), BF),
            pltpu.VMEM((D, TOK), BF),
            pltpu.VMEM((CHUNK, D), BF),
            pltpu.VMEM((D, CHUNK), BF),
            pltpu.VMEM((4, GROUP, CHUNK), F32),
            pltpu.VMEM((4, GROUP, CHUNK), F32),
            pltpu.VMEM((4, GROUP, CHUNK), BF),
            pltpu.VMEM((4, GROUP, CHUNK), BF),
        ],
        compiler_params=params(60),
        cost_estimate=cost(38),
        name="feed",
    )(tag, second, gradient, mods, packed, packed, kernel)


def attend_back_kernel(
    tag_ref, resid, shrunk, d_second, gradient, attn, mods, qkv, lse, proj_t,
    output, d_resid, d_qkv, d_attn_t, item_sums,
    bias, d_mixed, d_attn, sums,
):
    @pl.when(pl.program_id(0) == 0)
    def _():
        bias[...] = item_bias(tag_ref[0])
        sums[...] = jnp.zeros_like(sums)

    def rows_norm(i, _):
        rows = pl.ds(pl.multiple_of(i * 64, 64), 64)
        half = i // 2
        base = resid[0, rows, :]
        normal, factor = norm_stats(base)
        shrunk_rows = shrunk[0, rows, :]
        outward = gradient[0, rows, :].astype(F32)
        d_sec = d_second[0, rows, :]

        def by_item(value):
            return value.reshape(4, 2, 8, D)

        def add(index, value):
            sums[index, pl.ds(2 * half, 2)] += jnp.sum(by_item(value), axis=0)

        gated = (by_item(shrunk_rows) * quadrant_rows(mods, 5, half)).reshape(64, D)
        output[0, rows, :] = (base + gated).astype(BF)
        add(3, outward * shrunk_rows)
        add(1, d_sec)
        add(2, d_sec * normal)
        inner = (by_item(d_sec) * (1.0 + quadrant_rows(mods, 4, half))).reshape(64, D)
        mean = jnp.mean(inner, axis=-1, keepdims=True)
        along = jnp.mean(inner * normal, axis=-1, keepdims=True)
        back = outward + (inner - mean - normal * along) * factor
        d_resid[0, rows, :] = back
        add(0, back * attn[0, rows, :].astype(F32))
        gated = (by_item(back) * quadrant_rows(mods, 2, half)).reshape(64, D)
        d_attn[rows, :] = gated.astype(BF)
        return 0

    lax.fori_loop(0, 4, rows_norm, 0)
    d_attn_t[...] = d_attn[...].T
    d_mixed[...] = dot(proj_t[...], d_attn[...], 1, 1).astype(BF)

    def head(h, _):
        rows = pl.ds(pl.multiple_of(h * HD, HD), HD)
        key_rows = pl.ds(pl.multiple_of(D + h * HD, HD), HD)
        value_rows = pl.ds(pl.multiple_of(2 * D + h * HD, HD), HD)
        queries = qkv[0, rows, :] * jnp.asarray(HD**-0.5, BF)
        keys = qkv[0, key_rows, :]
        values = qkv[0, value_rows, :]
        d_mix = d_mixed[rows, :]
        probs = jnp.exp(dot(keys, queries, 0, 0) + (bias[...] - lse[0, pl.ds(h, 1), :]))
        d_probs = dot(values, d_mix, 0, 0)
        d_qkv[value_rows, :] = dot(d_mix, probs.astype(BF), 1, 1).astype(BF)
        weighted = probs * d_probs
        inner = jnp.sum(weighted, axis=0, keepdims=True)
        d_scores = (weighted - probs * inner).astype(BF)
        d_qkv[rows, :] = (dot(keys, d_scores, 1, 0) * HD**-0.5).astype(BF)
        d_qkv[key_rows, :] = dot(queries, d_scores, 1, 1).astype(BF)
        return 0

    lax.fori_loop(0, H, head, 0, unroll=HEADS)

    @pl.when(pl.program_id(0) == pl.num_programs(0) - 1)
    def _():
        item_sums[...] = jnp.sum(sums[...], axis=2)


def attend_back(part, tag, resid, shrunk, d_second, gradient, attn, mods, qkv, lse, proj_t):
    def pick_group(*shape):
        return pl.BlockSpec((1,) + shape, lambda g: (2 * part + g,) + (0,) * len(shape))

    return pl.pallas_call(
        attend_back_kernel,
        grid=(2,),
        in_specs=[
            SMEM_SPEC,
            pick_group(GROUP, D),
            pick_group(GROUP, D),
            pick_group(GROUP, D),
            pick_group(GROUP, D),
            pick_group(GROUP, D),
            whole((6, 4, 8, D)),
            pick_group(3 * D, GROUP),
            pick_group(16, GROUP),
            whole((D, D)),
        ],
        out_specs=[
            group_spec(GROUP, D),
            group_spec(GROUP, D),
            pl.BlockSpec((3 * D, GROUP), lambda g: (0, g)),
            pl.BlockSpec((D, GROUP), lambda g: (0, g)),
            whole((4, 4, D)),
        ],
        out_shape=[
            jax.ShapeDtypeStruct((2, GROUP, D), BF),
            jax.ShapeDtypeStruct((2, GROUP, D), F32),
            jax.ShapeDtypeStruct((3 * D, 2 * GROUP), BF),
            jax.ShapeDtypeStruct((D, 2 * GROUP), BF),
            jax.ShapeDtypeStruct((4, 4, D), F32),
        ],
        scratch_shapes=[
            pltpu.VMEM((GROUP, GROUP), F32),
            pltpu.VMEM((D, GROUP), BF),
            pltpu.VMEM((GROUP, D), BF),
            pltpu.VMEM((4, 4, 8, D), F32),
        ],
        compiler_params=params(),
        cost_estimate=cost(16),
        name=f"attend_back_{part}",
    )(tag, resid, shrunk, d_second, gradient, attn, mods, qkv, lse, proj_t)


PAIRS = 2
ROWS = 288 * PAIRS


def project_grads_kernel(
    tag_ref, d_qkv0, d_qkv1, d_attn0, d_attn1, conv_in, merged, keep_a, send_a, keep_b, send_b
):
    core = tag_ref[1]

    def against(low, high, field):
        return dot(low[...], field[0:2].reshape(2 * GROUP, D), 1, 0) + dot(
            high[...], field[2:4].reshape(2 * GROUP, D), 1, 0
        )

    grad = against(d_qkv0, d_qkv1, conv_in)
    share_out(grad, core, (0, 2), keep_a, send_a)
    share_out(grad, core, (2, 1), keep_b.at[:, :, 0:1], send_b.at[:, :, 0:1])
    grad = against(d_attn0, d_attn1, merged)
    share_out(grad, core, (0, 1), keep_b.at[:, :, 1:2], send_b.at[:, :, 1:2])


def project_grads(tag, d_qkv, d_attn, conv_in, merged):
    packed_spec = pl.BlockSpec((PAIRS, NK, 2, UR, UC), lambda i: (i, 0, 0, 0, 0))
    tall = pl.BlockSpec((ROWS, 2 * GROUP), lambda i: (i, 0))
    short = pl.BlockSpec((96 * PAIRS, 2 * GROUP), lambda i: (i, 0))
    return pl.pallas_call(
        project_grads_kernel,
        grid=(8 // PAIRS,),
        in_specs=[SMEM_SPEC, tall, tall, short, short, whole((4, GROUP, D)), whole((4, GROUP, D))],
        out_specs=[packed_spec] * 4,
        out_shape=[packed_half(2)] * 4,
        compiler_params=params(),
        cost_estimate=cost(8),
        name="project_grads",
    )(tag, *d_qkv, *d_attn, conv_in, merged)


def conv_back_kernel(
    tag_ref, d_qkv0, d_qkv1, weight, norm, mods, kernel, d_first, g_kernel, item_sums, d_conv
):
    step = pl.program_id(0)

    @pl.when(step == 0)
    def _():
        d_conv[...] = jnp.zeros_like(d_conv)

    d_conv[0:2] += dot(d_qkv0[...], weight[...], 0, 0).reshape(2, GROUP, D)
    d_conv[2:4] += dot(d_qkv1[...], weight[...], 0, 0).reshape(2, GROUP, D)

    @pl.when(step == pl.num_programs(0) - 1)
    def _():
        tag = tag_ref[0]
        left, right = edge_columns(tag)
        keep = 1.0 - tag.astype(F32)

        def lanes(i, _):
            cols = pl.ds(pl.multiple_of(i * 128, 128), 128)
            taps = [jnp.broadcast_to(kernel[t : t + 1, cols], (16, 128)) for t in range(9)]
            sums = [[jnp.zeros((16, 128), F32) for _ in range(2)] for _ in range(2)]

            def load_grad(g, p):
                return d_conv[g, p * 16 : p * 16 + 16, cols]

            def load_field(g, p):
                q = 2 * (p // 8)
                shift = mods[0, q : q + 2, :, cols].reshape(16, 128)
                scale = mods[1, q : q + 2, :, cols].reshape(16, 128)
                return norm[g, p * 16 : p * 16 + 16, cols] * (1.0 + scale) + shift

            def emit(g, p, value):
                rows = slice(p * 16, p * 16 + 16)
                d_first[g, rows, cols] = value
                sums[0][p // 8] += value
                sums[1][p // 8] += value * norm[g, rows, cols]

            grads = conv_back_rows(load_grad, load_field, taps, left, right, keep, emit)
            for t in range(9):
                g_kernel[t : t + 1, cols] = jnp.sum(grads[t], axis=0, keepdims=True)
            for kind in range(2):
                for item in range(4):
                    part = sums[kind][item // 2][8 * (item % 2) : 8 * (item % 2) + 8]
                    item_sums[kind, item : item + 1, cols] = jnp.sum(part, axis=0, keepdims=True)
            return 0

        lax.fori_loop(0, D // 128, lanes, 0)


def conv_back(tag, d_qkv, weight, norm, mods, kernel):
    tall = pl.BlockSpec((ROWS, 2 * GROUP), lambda i: (i, 0))
    return pl.pallas_call(
        conv_back_kernel,
        grid=(8 // PAIRS,),
        in_specs=[
            SMEM_SPEC,
            tall,
            tall,
            pl.BlockSpec((ROWS, D), lambda i: (i, 0)),
            whole((4, GROUP, D)),
            whole((6, 4, 8, D)),
            whole((9, D)),
        ],
        out_specs=[whole((4, GROUP, D)), whole((9, D)), whole((2, 4, D))],
        out_shape=[
            jax.ShapeDtypeStruct((4, GROUP, D), F32),
            jax.ShapeDtypeStruct((9, D), F32),
            jax.ShapeDtypeStruct((2, 4, D), F32),
        ],
        scratch_shapes=[pltpu.VMEM((4, GROUP, D), F32)],
        compiler_params=params(),
        cost_estimate=cost(15),
        name="conv_back",
    )(tag, *d_qkv, weight, norm, mods, kernel)


def finish_kernel(
    d_first, norm, factor, d_resid0, d_resid1, output0, output1, mods,
    block_output, input_grad, total,
):
    half = pl.program_id(0) // 2

    for g in range(4):
        base = (d_resid0, d_resid1)[g // 2]
        value = d_first[g]
        normal = norm[g]
        inner = (value.reshape(4, 2, 8, D) * (1.0 + quadrant_rows(mods, 1, half))).reshape(64, D)
        mean = jnp.mean(inner, axis=-1, keepdims=True)
        along = jnp.mean(inner * normal, axis=-1, keepdims=True)
        total[g] = base[g % 2] + (inner - mean - normal * along) * factor[g]
    order = ungroup_matrix()
    grouped = total[...].reshape(256, D)
    high = grouped.astype(BF)
    rest = (grouped - high.astype(F32)).astype(BF)
    input_grad[...] = dot(order, high, 1, 0) + dot(order, rest, 1, 0)
    low_half = dot(order[:, 0:128], output0[...].reshape(128, D), 1, 0)
    high_half = dot(order[:, 128:256], output1[...].reshape(128, D), 1, 0)
    block_output[...] = (low_half + high_half).astype(BF)


def finish(d_first, norm, factor, d_resid, output, mods):
    def split(groups, width):
        return pl.BlockSpec((groups, 64, width), lambda i: (0, i, 0))

    flat = pl.BlockSpec((256, D), lambda i: (i, 0))
    return pl.pallas_call(
        finish_kernel,
        grid=(4,),
        in_specs=[split(4, D), split(4, D), split(4, 1)] + [split(2, D)] * 4 + [whole((6, 4, 8, D))],
        out_specs=[flat, flat],
        out_shape=[
            jax.ShapeDtypeStruct((TOK, D), BF),
            jax.ShapeDtypeStruct((TOK, D), F32),
        ],
        scratch_shapes=[pltpu.VMEM((4, 64, D), F32)],
        compiler_params=params(),
        cost_estimate=cost(8),
        name="finish",
    )(d_first, norm, factor, *d_resid, *output, mods)


BOTH = ("dp", "fsdp")


def exchange(pieces):
    return lax.all_to_all(pieces, BOTH, 0, 0, tiled=True)


def units_of(weight):
    return weight.T.reshape(-1, UR, UC)


def low_units(shrink):
    return shrink.T.reshape(UR, 4, UC).transpose(1, 0, 2)


def gather_feed(nd, nf, expand, shrink):
    if (nd, nf) == (NJ, NK):
        rows = jnp.concatenate([units_of(expand), low_units(shrink)]).reshape(8 * UR, UC)
        return lax.all_gather(rows, BOTH).reshape(NJ, NK, 8, UR, UC)
    low = full_rows(shrink).reshape(NJ, UR, NK, 4, UC).transpose(0, 2, 3, 1, 4)
    return jnp.concatenate([all_units(full_rows(expand), 4), low], axis=2)


def full_rows(shard):
    rows = lax.all_gather(shard.T, "fsdp", axis=1, tiled=True)
    return lax.all_gather(rows, "dp", axis=0, tiled=True)


def all_units(weight, units):
    return weight.reshape(NJ, units, UR, NK, UC).transpose(0, 3, 1, 2, 4)


def project_turns(own):
    turns = [
        lax.ppermute(own, "dp", [(i, (i - 4 * step) % NJ) for i in range(NJ)])
        for step in range(1, 4)
    ]
    return turns


def widen(a, b, bit_a, bit_b):
    return jnp.stack([a, swap(a, bit_a)]), jnp.stack([b, swap(b, bit_b)])


def all_projections(qkv, proj):
    units = jnp.concatenate([all_units(full_rows(qkv), 3), all_units(full_rows(proj), 1)], axis=2)
    units = units.reshape((4, 2, 2) + units.shape[1:])
    first, rest = units[:, :, :, :, :2], units[:, :, :, :, 2:]
    a, b = first.transpose(2, 3, 1, 0, 4, 5, 6), rest.transpose(2, 1, 3, 0, 4, 5, 6)
    return a[0], b[0], a[1], b[1]


def pick(grads, index, axis):
    return lax.dynamic_index_in_dim(grads, index, axis, keepdims=False)


def swap(value, bit):
    if bit is None:
        return lax.ppermute(value, "fsdp", [(0, 1), (1, 0)])
    return lax.ppermute(value, "dp", [(i, i ^ bit) for i in range(NJ)])


def halve(keep, got, axis, bit):
    mine = lax.axis_index("fsdp") if bit is None else (lax.axis_index("dp") // bit) % 2
    kept = pick(keep, mine, axis) + pick(got, mine, axis)
    return kept, pick(keep, 1 - mine, axis) + pick(got, 1 - mine, axis)


def last_sends(total):
    place = lax.axis_index("dp") // 4
    return [pick(total, (place + step) % 4, 0) for step in range(1, 4)]


def last_swaps(sends):
    return [
        lax.ppermute(sent, "dp", [(i, (i + 4 * step) % NJ) for i in range(NJ)])
        for step, sent in enumerate(sends, 1)
    ]


def last_sum(total, got):
    own = pick(total, lax.axis_index("dp") // 4, 0).astype(F32)
    for value in got:
        own = own + value.astype(F32)
    return own


def after(value, *others):
    return lax.optimization_barrier((value,) + others)[0]


def own_shard(nd, nf, kind, units):
    if (nd, nf) == (NJ, NK):
        if kind == "shrink":
            return units.transpose(1, 0, 2).reshape(UR, 4 * UC).T
        return units.reshape(-1, UC).T
    if kind == "shrink":
        weight = units.transpose(0, 3, 1, 2, 4).reshape(NJ * UR, -1)
    else:
        weight = units.transpose(0, 2, 3, 1, 4).reshape(-1, NK * UC)
    columns = lax.psum_scatter(weight, "dp", scatter_dimension=0, tiled=True)
    piece = lax.psum_scatter(columns, "fsdp", scatter_dimension=1, tiled=True)
    return piece.astype(F32).T


def both_cores(keep, send):
    return jnp.stack([keep, send], axis=1).reshape((-1,) + keep.shape[1:])


def look_up(ids, step_table, class_table):
    first_row = lax.axis_index("fsdp") * step_table.shape[0]
    own = first_row + jnp.arange(step_table.shape[0], dtype=jnp.int32)
    step_hot = (ids[:, :4].reshape(-1, 1) == own[None, :]).astype(BF)
    class_hot = (ids[:, 4:].reshape(-1, 1) == own[None, :]).astype(BF)
    return step_hot, class_hot, dot(step_hot, step_table, 1, 0) + dot(class_hot, class_table, 1, 0)


def share_act(nd, cond, attn_kernel, ffn_kernel):
    items, width = cond.shape
    act = jax.nn.silu(cond).astype(BF)
    filters = jnp.concatenate([attn_kernel, ffn_kernel], axis=1).reshape(-1, width)
    sent = lax.all_gather(jnp.concatenate([act, filters], axis=0), "dp")
    act_all = sent[:, :items].transpose(1, 0, 2).reshape(items, nd * width)
    filters = sent[:, items:].reshape(nd, 9, -1).astype(F32)
    attn_full = filters[:, :, : attn_kernel.shape[1]].transpose(1, 0, 2).reshape(9, -1)
    ffn_full = filters[:, :, attn_kernel.shape[1] :].transpose(1, 0, 2).reshape(9, -1)
    return act_all, attn_full, ffn_full


def exchange_columns(nd, nf, d_act):
    rows, items = d_act.shape
    if (nd, nf) == (NJ, NK):
        return lax.all_to_all(d_act.reshape(nd, rows // nd, items), "dp", 0, 0, tiled=True)
    spread = lax.dynamic_update_slice_in_dim(
        jnp.zeros((rows * nf, items), F32), d_act, lax.axis_index("fsdp") * rows, axis=0
    )
    spread = spread.reshape(nd, 1, -1, items)
    spread = jnp.broadcast_to(spread, (nd, nf) + spread.shape[2:])
    return exchange(spread.reshape((nd * nf,) + spread.shape[2:]))


def own_columns(nd, nf, terms):
    part = terms.sum(axis=0)
    if (nd, nf) != (NJ, NK):
        return part
    order = [(j * NK + k, k * NJ + j) for j in range(NJ) for k in range(NK)]
    own = lax.ppermute(part, BOTH, order)
    other = lax.ppermute(part, BOTH, [(i, o ^ 1) for i, o in order])
    first = lax.axis_index("fsdp") == 0
    return jnp.concatenate([jnp.where(first, own, other), jnp.where(first, other, own)])


def body(
    latents, size_tags, timesteps, classes, step_table, class_table, modulation_weight,
    attn_kernel, qkv_weight, proj_weight, expand_weight, ffn_kernel, shrink_weight, cotangent,
    *, nd, nf,
):
    slots = nd * nf
    tag = size_tags[0]
    square = (nd, nf) == (NJ, NK)
    if square:
        place = lax.axis_index("dp")
        where = [tag, place % 2, place // 4, (place // 2) % 2, lax.axis_index("fsdp")]
        where = jnp.stack(where).astype(jnp.int32)
    else:
        where = jnp.stack([tag] + [jnp.int32(0)] * 4)
    packed = gather_feed(nd, nf, expand_weight, shrink_weight)
    tokens, gradient, norm, factor = prepare(latents, cotangent)
    mine = jnp.concatenate([timesteps[0], classes[0]])[None]
    mine = jnp.broadcast_to(mine, (slots, 8))
    if square:
        own = jnp.concatenate([units_of(qkv_weight), units_of(proj_weight)])
        own = after(own, mine)
        turns = project_turns(own)
    ids = exchange(mine)
    if square:
        ids = after(ids, norm)
    step_hot, class_hot, part = look_up(ids, step_table, class_table)
    if square:
        cond = part + swap(part, None)
        a = jnp.stack([own[:2]] + [turn[:2] for turn in turns])
        b = jnp.stack([own[2:]] + [turn[2:] for turn in turns])
        a, b = widen(a, b, 2, None)
        cond = after(cond, a, b)
        next_a, next_b = swap(a, None), swap(b, 2)
    else:
        cond = lax.psum(part, "fsdp")
    act_all, attn_full, ffn_full = share_act(nd, cond, attn_kernel, ffn_kernel)
    if square:
        next_a, next_b = after(next_a, act_all), after(next_b, act_all)
    height, width = modulation_weight.shape
    act_rows = lax.dynamic_slice_in_dim(
        act_all, lax.axis_index("fsdp") * height, height, axis=1
    )
    terms = dot(act_rows, modulation_weight, 1, 0)
    terms = exchange(terms.reshape(slots, 1, 4 * width)).reshape(nd, nf, 4, width)
    if square:
        a, b = jnp.stack([a, next_a]), jnp.stack([b, next_b])
        projections = (a, b, swap(a, 1), swap(b, 1))
    else:
        projections = all_projections(qkv_weight, proj_weight)
    mod_rows = terms.sum(axis=1).transpose(1, 0, 2).reshape(4, nd * width)
    chosen = jnp.where(tag == 1, mod_rows, mod_rows[:1])
    mods = jnp.broadcast_to(chosen.reshape(4, 6, 1, D).transpose(1, 0, 2, 3), (6, 4, 8, D))

    conv_in = first_conv(size_tags, norm, mods, attn_full)
    qkv, merged, attn, resid, second, lse, proj_t, full_qkv = attend(
        where, conv_in, tokens, mods, projections
    )
    shrunk, d_second, keep_e, send_e, keep_s, send_s, g_ffn = feed(
        where, second, gradient, mods, packed, ffn_full
    )
    back = (gradient, attn, mods, qkv, lse)
    if square:
        got_e, got_s = swap(send_e, 1), swap(send_s, 1)
    output0, d_resid0, d_qkv0, d_attn0, later0 = attend_back(
        0, where, resid, shrunk, d_second, *back, proj_t
    )

    def grid(value):
        return value.reshape((4, 2) + value.shape[1:])

    if square:
        got_e, got_s = after(got_e, d_qkv0), after(got_s, d_qkv0)
        keep_e, out_e = halve(grid(keep_e), grid(got_e), 2, None)
        keep_s, out_s = halve(grid(keep_s), grid(got_s), 1, 2)
        d_second = after(d_second, out_e, out_s)
        got_e, got_s = swap(out_e, None), swap(out_s, 2)
    output1, d_resid1, d_qkv1, d_attn1, later1 = attend_back(
        1, where, resid, shrunk, d_second, *back, proj_t
    )
    d_qkv = (d_qkv0, d_qkv1)
    keep_a, send_a, keep_b, send_b = project_grads(
        where, d_qkv, (d_attn0, d_attn1), conv_in, merged
    )
    if square:
        got_a, got_b = swap(send_a, 1), swap(send_b, 1)
        got_e, got_s = after(got_e, keep_a), after(got_s, keep_a)
        keep_e, out_e = halve(keep_e, got_e, 1, 2)
        keep_s, out_s = halve(keep_s, got_s, 1, None)
        full_qkv = after(full_qkv, out_e, out_s)
        got_e, got_s = swap(out_e, 2), swap(out_s, None)
    d_first, g_attn, early = conv_back(where, d_qkv, full_qkv, norm, mods, attn_full)
    if square:
        got_e, got_s, got_a, got_b = (after(x, d_first) for x in (got_e, got_s, got_a, got_b))
        early, g_attn = after(early, got_e, got_s), after(g_attn, got_e, got_s)
    later = later0 + later1
    rows = jnp.concatenate([early, later], axis=0)
    rows = rows.transpose(1, 0, 2).reshape(4, 6 * D)
    alone = jnp.concatenate([rows.sum(axis=0, keepdims=True), jnp.zeros((3, 6 * D), F32)])
    d_mod = jnp.where(tag == 1, rows, alone).astype(BF)
    filters = jnp.concatenate([g_attn.reshape(9, nd, -1), g_ffn.reshape(9, nd, -1)], axis=2)
    pieces = jnp.concatenate(
        [
            d_mod.reshape(4, nd, width).transpose(1, 0, 2).reshape(nd, -1),
            filters.astype(BF).transpose(1, 0, 2).reshape(nd, -1),
        ],
        axis=1,
    )
    pieces = jnp.broadcast_to(pieces[:, None], (nd, nf, pieces.shape[1])).reshape(slots, 1, -1)
    if square:
        keep_a, out_a = halve(grid(keep_a), grid(got_a), 2, None)
        keep_b, out_b = halve(grid(keep_b), grid(got_b), 1, 2)
        e = halve(keep_e.reshape((2, 2) + keep_e.shape[1:]), got_e.reshape((2, 2) + got_e.shape[1:]), 1, 4)
        s = halve(keep_s.reshape((2, 2) + keep_s.shape[1:]), got_s.reshape((2, 2) + got_s.shape[1:]), 1, 4)
        feeding, out_f = (jnp.concatenate(pair, axis=1) for pair in zip(e, s))
        d_first = after(d_first, out_a, out_b, out_f, pieces)
        got_a, got_b = swap(out_a, None), swap(out_b, 2)
        got_f = swap(out_f, 4)
    got = exchange(pieces)[:, 0]
    block_output, input_grad = finish(
        d_first, norm, factor, (d_resid0, d_resid1), (output0, output1), mods
    )
    if square:
        got = after(got, input_grad)
        got_a, got_b, got_f = (after(x, got) for x in (got_a, got_b, got_f))
        keep_a, out_a = halve(keep_a, got_a, 1, 2)
        keep_b, out_b = halve(keep_b, got_b, 1, None)
        got_a, got_b = swap(out_a, 2), swap(out_b, None)
    d_mod_all = got[:, : 4 * width].reshape(slots * 4, width)
    d_act = dot(modulation_weight, d_mod_all, 1, 1)
    own_act = exchange_columns(nd, nf, d_act)
    if square:
        feeding, out_f = halve(feeding, got_f, 0, 8)
        total = jnp.concatenate([keep_a + got_a, keep_b + got_b], axis=1)
        sends = last_sends(total)
        sends[1] = jnp.concatenate([sends[1], out_f])
        own_act = after(own_act, *sends)
        last = last_swaps(sends)
        last[1], got_f = last[1][:4], last[1][4:]
        total = last_sum(total, last)
        feeding = feeding.astype(F32) + got_f.astype(F32)
        cuts = [total[:3], total[3:], feeding[:4], feeding[4:]]
    else:
        first, rest = both_cores(keep_a, send_a), both_cores(keep_b, send_b)
        cuts = [
            jnp.concatenate([first, rest[:, :, :1]], axis=2),
            rest[:, :, 1:],
            both_cores(keep_e, send_e),
            both_cores(keep_s, send_s),
        ]
    shards = [
        own_shard(nd, nf, kind, cut)
        for kind, cut in zip(("qkv", "proj", "expand", "shrink"), cuts)
    ]
    filters = got[:, 4 * width :].astype(F32).sum(axis=0).reshape(9, -1)
    modulation_grad = dot(act_rows, d_mod_all, 0, 0)
    gate = jax.nn.sigmoid(cond)
    d_cond = own_columns(nd, nf, own_act)
    d_cond = d_cond * (gate * (1.0 + cond * (1.0 - gate))).T

    def table_grad(hot):
        return lax.dot_general(
            hot.astype(F32), d_cond, (((0,), (1,)), ((), ())), precision=lax.Precision.HIGHEST
        )

    cut = attn_kernel.shape[1]
    return (
        block_output,
        input_grad,
        table_grad(step_hot),
        table_grad(class_hot),
        modulation_grad,
        filters[:, :cut],
        shards[0],
        shards[1],
        shards[2],
        filters[:, cut:],
        shards[3],
    )


def solution(mesh):
    matrix = P("fsdp", "dp")
    rows = P(BOTH, None)
    filters = P(None, "dp")
    in_specs = (
        rows, P(BOTH), rows, rows, matrix, matrix, matrix, filters, matrix, matrix, matrix,
        filters, matrix, rows,
    )
    out_specs = (
        rows, rows, matrix, matrix, matrix, filters, matrix, matrix, matrix, filters, matrix,
    )
    run = functools.partial(body, nd=mesh.shape["dp"], nf=mesh.shape["fsdp"])
    return jax.shard_map(run, mesh=mesh, in_specs=in_specs, out_specs=out_specs, check_vma=False)
```

```python
import functools

import jax
import jax.numpy as jnp
from jax import lax
from jax.experimental import pallas as pl
from jax.experimental.pallas import tpu as pltpu
from jax.sharding import PartitionSpec as P

D = 768
H = 12
HD = 64
FF = 3072
SIDE = 32
GROUP = 256
TOK = SIDE * SIDE
EPS = 1e-06
NJ, NK, UR, UC = 16, 2, 48, 384
CHUNK = 768
HEADS = 6
PARTS = ((0, 1), (1, 3))
MIB = 1024 * 1024
BF = jnp.bfloat16
F32 = jnp.float32
GELU_A = 0.7978845608028654
GELU_B = GELU_A * 0.044715


def dot(left, right, left_dim, right_dim):
    return lax.dot_general(
        left, right, (((left_dim,), (right_dim,)), ((), ())), preferred_element_type=F32
    )


def params(limit=56):
    return pltpu.CompilerParams(vmem_limit_bytes=limit * MIB)


def cost(micros):
    return pl.CostEstimate(flops=int(micros * 1e8), transcendentals=0, bytes_accessed=4 * MIB)


def whole(shape):
    zeros = (0,) * len(shape)
    return pl.BlockSpec(shape, lambda *ids: zeros, pipeline_mode=pl.Buffered(1))


SMEM_SPEC = pl.BlockSpec(memory_space=pltpu.SMEM)


def group_place(natural):
    pair, odd_row = natural // 64, (natural // 32) % 2
    column, odd_column = (natural % 32) // 2, natural % 2
    return (2 * odd_row + odd_column) * 64 + pair * 16 + column


def ungroup_matrix():
    natural = lax.broadcasted_iota(jnp.int32, (256, 256), 0)
    grouped = lax.broadcasted_iota(jnp.int32, (256, 256), 1)
    return jnp.where(group_place(natural) == grouped, 1.0, 0.0).astype(BF)


def group_matrix():
    natural = lax.broadcasted_iota(jnp.int32, (256, 256), 1)
    grouped = lax.broadcasted_iota(jnp.int32, (256, 256), 0)
    return jnp.where(group_place(natural) == grouped, 1.0, 0.0).astype(BF)


def norm_stats(values):
    centre = values - jnp.mean(values, axis=-1, keepdims=True)
    variance = jnp.mean(centre * centre, axis=-1, keepdims=True)
    scale = lax.rsqrt(variance + EPS)
    return centre * scale, scale


def prepare_kernel(latents, cotangent, tokens, gradient, norm, scale):
    order = group_matrix()
    gathered = dot(order, latents[...], 1, 0)
    gradient[...] = dot(order, cotangent[...], 1, 0).reshape(4, 64, D).astype(BF)
    tokens[...] = gathered.reshape(4, 64, D).astype(BF)
    normal, factor = norm_stats(gathered)
    norm[...] = normal.reshape(4, 64, D)
    scale[...] = factor.reshape(4, 64, 1)


def prepare(latents, cotangent):
    flat = pl.BlockSpec((256, D), lambda i: (i, 0))
    split = pl.BlockSpec((4, 64, D), lambda i: (0, i, 0))
    return pl.pallas_call(
        prepare_kernel,
        grid=(4,),
        in_specs=[flat, flat],
        out_specs=[split, split, split, pl.BlockSpec((4, 64, 1), lambda i: (0, i, 0))],
        out_shape=[
            jax.ShapeDtypeStruct((4, GROUP, D), BF),
            jax.ShapeDtypeStruct((4, GROUP, D), BF),
            jax.ShapeDtypeStruct((4, GROUP, D), F32),
            jax.ShapeDtypeStruct((4, GROUP, 1), F32),
        ],
        compiler_params=params(),
        cost_estimate=cost(6),
        name="prepare",
    )(latents, cotangent)


def edge_columns(tag):
    place = lax.broadcasted_iota(jnp.int32, (16, 128), 0)
    left = jnp.where((place == 0) | ((place == 8) & (tag == 1)), 0.0, 1.0)
    right = jnp.where((place == 15) | ((place == 7) & (tag == 1)), 0.0, 1.0)
    return left, right


def neighbours(even, odd, left, right):
    return pltpu.roll(odd, 1, 0) * left, pltpu.roll(even, 15, 0) * right


def conv_rows(load, kernel, left, right, keep, emit):
    above = None
    partial = None
    for row in range(SIDE + 1):
        taps = None
        if row < SIDE:
            a, p = row % 2, row // 2
            even, odd = load(2 * a, p), load(2 * a + 1, p)
            odd_left, even_right = neighbours(even, odd, left, right)
            taps = []
            for tap in range(3):
                k = [kernel[3 * tap + b] for b in range(3)]
                taps.append(
                    (
                        k[0] * odd_left + k[1] * even + k[2] * odd,
                        k[0] * even + k[1] * odd + k[2] * even_right,
                    )
                )
        crossing = row == SIDE // 2
        if partial is not None:
            a, p = (row - 1) % 2, (row - 1) // 2
            for b in range(2):
                value = partial[b]
                if taps is not None:
                    below = taps[2][b]
                    value = value + (below * keep if crossing else below)
                emit(2 * a + b, p, value)
        if taps is not None:
            partial = []
            for b in range(2):
                value = taps[1][b]
                if above is not None:
                    value = value + (above[b] * keep if crossing else above[b])
                partial.append(value)
            above = taps[0]


def conv_back_rows(load_grad, load_field, kernel, left, right, keep, emit):
    sums = [jnp.zeros((16, 128), F32) for _ in range(9)]
    from_above = None
    partial = None
    field_above = None
    field = (load_field(0, 0), load_field(1, 0))
    for row in range(SIDE + 1):
        crossing = row == SIDE // 2
        taps = None
        if row < SIDE:
            a, p = row % 2, row // 2
            even, odd = load_grad(2 * a, p), load_grad(2 * a + 1, p)
            odd_left, even_right = neighbours(even, odd, left, right)
            picks = ((odd, even, odd_left), (even_right, odd, even))
            taps = []
            for tap in range(3):
                k = [kernel[3 * tap + b] for b in range(3)]
                taps.append(
                    tuple(k[0] * x[0] + k[1] * x[1] + k[2] * x[2] for x in picks)
                )
            field_below = None
            if row + 1 < SIDE:
                a, p = (row + 1) % 2, (row + 1) // 2
                field_below = (load_field(2 * a, p), load_field(2 * a + 1, p))
            for tap, rows in enumerate((field_above, field, field_below)):
                if rows is None:
                    continue
                if (tap == 0 and crossing) or (tap == 2 and row + 1 == SIDE // 2):
                    rows = (rows[0] * keep, rows[1] * keep)
                for b in range(3):
                    sums[3 * tap + b] = (
                        sums[3 * tap + b] + rows[0] * picks[0][b] + rows[1] * picks[1][b]
                    )
            field_above, field = field, field_below
        if partial is not None:
            a, p = (row - 1) % 2, (row - 1) // 2
            for b in range(2):
                value = partial[b]
                if taps is not None:
                    value = value + (taps[0][b] * keep if crossing else taps[0][b])
                emit(2 * a + b, p, value)
        if taps is not None:
            partial = []
            for b in range(2):
                value = taps[1][b]
                if from_above is not None:
                    value = value + (from_above[b] * keep if crossing else from_above[b])
                partial.append(value)
            from_above = taps[2]
    return sums


def first_conv_kernel(tag_ref, norm, mods, kernel, out):
    tag = tag_ref[0]
    left, right = edge_columns(tag)
    keep = 1.0 - tag.astype(F32)
    taps = [jnp.broadcast_to(kernel[i : i + 1, :], (16, 128)) for i in range(9)]

    def load(g, p):
        q = 2 * (p // 8)
        shift = mods[0, q : q + 2].reshape(16, 128)
        scale = mods[1, q : q + 2].reshape(16, 128)
        return norm[g, p * 16 : p * 16 + 16, :] * (1.0 + scale) + shift

    def emit(g, p, value):
        out[g, p * 16 : p * 16 + 16, :] = value.astype(BF)

    conv_rows(load, taps, left, right, keep, emit)


def first_conv(tag, norm, mods, kernel):
    return pl.pallas_call(
        first_conv_kernel,
        grid=(D // 128,),
        in_specs=[
            SMEM_SPEC,
            pl.BlockSpec((4, GROUP, 128), lambda i: (0, 0, i)),
            pl.BlockSpec((6, 4, 8, 128), lambda i: (0, 0, 0, i)),
            pl.BlockSpec((9, 128), lambda i: (0, i)),
        ],
        out_specs=pl.BlockSpec((4, GROUP, 128), lambda i: (0, 0, i)),
        out_shape=jax.ShapeDtypeStruct((4, GROUP, D), BF),
        compiler_params=params(),
        cost_estimate=cost(6),
        name="first_conv",
    )(tag, norm, mods, kernel)


def join_rows(block, target):
    rows = block.shape[0] * block.shape[2] * UR
    for k in range(NK):
        target[:, k * UC : (k + 1) * UC] = block[:, k].reshape(rows, UC)


def share_out(rows, core, units, keep, send):
    first, count = units
    for k in range(NK):
        part = rows[:, k * UC : (k + 1) * UC].astype(BF)
        part = part.reshape(-1, 2, part.shape[0] // (keep.shape[0] * 2), UC)
        even, odd = part[:, 0], part[:, 1]
        for target, value in (
            (keep, jnp.where(core == 0, even, odd)),
            (send, jnp.where(core == 0, odd, even)),
        ):
            whole_units = value.reshape(value.shape[0], -1, UR, UC)
            target[:, k] = whole_units[:, first : first + count]


def quadrant_rows(mods, index, half):
    return mods[index, pl.ds(2 * half, 2)].reshape(1, 2, 8, D)


def item_bias(tag):
    def label(dim):
        place = lax.broadcasted_iota(jnp.int32, (GROUP, GROUP), dim)
        return 2 * (place // 128) + (place % 16) // 8

    return jnp.where((label(0) == label(1)) | (tag == 0), 0.0, -1e30)


def attend_kernel(
    where, conv_in, tokens, mods, own_a, own_b, peer_a, peer_b,
    qkv, merged, attn, resid, second, lse, proj_t, full_qkv,
    full_proj, bias, mixed_t,
):
    @pl.when(pl.program_id(0) == 0)
    def _():
        core, z, y, x = (where[i] for i in range(1, 5))
        for owner in range(NJ):
            step = (owner // 4 - z + 4) % 4
            side = (owner // 2) % 2 ^ y
            mine = core == owner % 2
            for k in range(NK):
                cols = slice(k * UC, (k + 1) * UC)
                a = jnp.where(mine, own_a[k ^ x, side, step], peer_a[k ^ x, side, step])
                b = jnp.where(mine, own_b[side, k ^ x, step], peer_b[side, k ^ x, step])
                start = owner * 3 * UR
                full_qkv[start : start + 2 * UR, cols] = a.reshape(2 * UR, UC)
                full_qkv[start + 2 * UR : start + 3 * UR, cols] = b[0]
                full_proj[owner * UR : (owner + 1) * UR, cols] = b[1]
        proj_t[...] = full_proj[...].T
        bias[...] = item_bias(where[0])

    qkv[0] = dot(full_qkv[...], conv_in[0], 1, 1).astype(BF)

    def head(h, _):
        rows = pl.ds(pl.multiple_of(h * HD, HD), HD)
        queries = qkv[0, rows, :] * jnp.asarray(HD**-0.5, BF)
        keys = qkv[0, pl.ds(pl.multiple_of(D + h * HD, HD), HD), :]
        values = qkv[0, pl.ds(pl.multiple_of(2 * D + h * HD, HD), HD), :]
        scores = dot(keys, queries, 0, 0) + bias[...]
        highest = jnp.max(scores, axis=0, keepdims=True)
        raised = jnp.exp(scores - highest)
        total = jnp.sum(raised, axis=0, keepdims=True)
        probs = (raised * (1.0 / total)).astype(BF)
        lse[0, pl.ds(h, 1), :] = highest + jnp.log(total)
        mixed_t[rows, :] = dot(values, probs, 1, 0).astype(BF)
        return 0

    lax.fori_loop(0, H, head, 0, unroll=HEADS)
    merged[0] = mixed_t[...].T
    projected = dot(merged[0], full_proj[...], 1, 1)
    attn[0] = projected.astype(BF)
    gate = mods[2].reshape(2, 1, 2, 8, D)
    resid[0] = (
        tokens[0].astype(F32) + (projected.reshape(2, 8, 2, 8, D) * gate).reshape(GROUP, D)
    )

    def rows_norm(i, _):
        rows = pl.ds(pl.multiple_of(i * 64, 64), 64)
        normal, _ = norm_stats(resid[0, rows, :])
        half = i // 2
        scaled = normal.reshape(4, 2, 8, D) * (1.0 + quadrant_rows(mods, 4, half))
        value = scaled + quadrant_rows(mods, 3, half)
        second[0, rows, :] = value.reshape(64, D).astype(BF)
        return 0

    lax.fori_loop(0, 4, rows_norm, 0)


def group_spec(*shape):
    return pl.BlockSpec((1,) + shape, lambda g: (g,) + (0,) * len(shape))


def attend(where, conv_in, tokens, mods, projections):
    relative = (2, 2, 4, 2, UR, UC)
    return pl.pallas_call(
        attend_kernel,
        grid=(4,),
        in_specs=[
            SMEM_SPEC,
            group_spec(GROUP, D),
            group_spec(GROUP, D),
            whole((6, 4, 8, D)),
        ]
        + [whole(relative)] * 4,
        out_specs=[
            group_spec(3 * D, GROUP),
            group_spec(GROUP, D),
            group_spec(GROUP, D),
            group_spec(GROUP, D),
            group_spec(GROUP, D),
            group_spec(16, GROUP),
            whole((D, D)),
            whole((3 * D, D)),
        ],
        out_shape=[
            jax.ShapeDtypeStruct((4, 3 * D, GROUP), BF),
            jax.ShapeDtypeStruct((4, GROUP, D), BF),
            jax.ShapeDtypeStruct((4, GROUP, D), BF),
            jax.ShapeDtypeStruct((4, GROUP, D), F32),
            jax.ShapeDtypeStruct((4, GROUP, D), BF),
            jax.ShapeDtypeStruct((4, 16, GROUP), F32),
            jax.ShapeDtypeStruct((D, D), BF),
            jax.ShapeDtypeStruct((3 * D, D), BF),
        ],
        scratch_shapes=[
            pltpu.VMEM((D, D), BF),
            pltpu.VMEM((GROUP, GROUP), F32),
            pltpu.VMEM((D, GROUP), BF),
        ],
        compiler_params=params(),
        cost_estimate=cost(38),
        name="attend",
    )(where, conv_in, tokens, mods, *projections)


def feed_kernel(
    tag_ref, second, gradient, mods, w_expand, w_shrink, kernel,
    shrunk, d_second, keep_expand, send_expand, keep_shrink, send_shrink, g_kernel,
    d_shrunk, d_shrunk_t, expand, shrink, field, slope, hidden, d_field,
):
    step = pl.program_id(0)
    tag, core = tag_ref[0], tag_ref[1]

    @pl.when(step == 0)
    def _():
        gate = mods[5].reshape(1, 2, 1, 2, 8, D)
        value = gradient[...].astype(F32).reshape(4, 2, 8, 2, 8, D) * gate
        d_shrunk[...] = value.reshape(TOK, D).astype(BF)
        d_shrunk_t[...] = d_shrunk[...].T
        shrunk[...] = jnp.zeros_like(shrunk)
        d_second[...] = jnp.zeros_like(d_second)

    join_rows(w_expand, expand)
    for q in range(2):
        shrink[:, q * UC : (q + 1) * UC] = w_shrink[:, 0, q].reshape(D, UC)
    left, right = edge_columns(tag)
    keep = 1.0 - tag.astype(F32)
    field[...] = dot(second[...].reshape(TOK, D), expand[...], 1, 1).reshape(4, GROUP, CHUNK)
    slope[...] = dot(d_shrunk[...], shrink[...], 1, 0).reshape(4, GROUP, CHUNK)

    def lanes(i, _):
        cols = pl.ds(pl.multiple_of(i * 128, 128), 128)
        taps = [jnp.broadcast_to(kernel[t : t + 1, cols], (16, 128)) for t in range(9)]

        def load(g, p):
            return field[g, p * 16 : p * 16 + 16, cols]

        def load_slope(g, p):
            return slope[g, p * 16 : p * 16 + 16, cols]

        def emit(g, p, value):
            square = value * value
            half = 0.5 + 0.5 * jnp.tanh(value * (GELU_A + GELU_B * square))
            out = value * half
            hidden[g, p * 16 : p * 16 + 16, cols] = out.astype(BF)
            rate = half + (out - out * half) * (2.0 * GELU_A + 6.0 * GELU_B * square)
            slope[g, p * 16 : p * 16 + 16, cols] = load_slope(g, p) * rate

        conv_rows(load, taps, left, right, keep, emit)

        def emit_back(g, p, value):
            d_field[g, p * 16 : p * 16 + 16, cols] = value.astype(BF)

        sums = conv_back_rows(load_slope, load, taps, left, right, keep, emit_back)
        for t in range(9):
            g_kernel[t : t + 1, cols] = jnp.sum(sums[t], axis=0, keepdims=True)
        return 0

    lax.fori_loop(0, CHUNK // 128, lanes, 0)
    hid = hidden[...].reshape(TOK, CHUNK)
    d_fld = d_field[...].reshape(TOK, CHUNK)
    grad = dot(d_shrunk_t[...], hid, 1, 0).astype(BF)
    for q in range(2):
        part = grad[:, q * UC : (q + 1) * UC].reshape(NJ // 2, 2, UR, UC)
        keep_shrink[:, 0, q] = jnp.where(core == 0, part[:, 0], part[:, 1])
        send_shrink[:, 0, q] = jnp.where(core == 0, part[:, 1], part[:, 0])
    share_out(dot(d_fld, second[...].reshape(TOK, D), 0, 0), core, (0, 4), keep_expand, send_expand)
    shrunk[...] += dot(hid, shrink[...], 1, 1).reshape(4, GROUP, D)
    d_second[...] += dot(d_fld, expand[...], 1, 0).reshape(4, GROUP, D)


def packed_half(units):
    return jax.ShapeDtypeStruct((NJ // 2, NK, units, UR, UC), BF)


def feed(tag, second, gradient, mods, packed, kernel):
    half = NJ // 2
    expand_spec = pl.BlockSpec((2, NK, 4, UR, UC), lambda c: (c, 0, 0, 0, 0))
    shrink_spec = pl.BlockSpec((half, 1, 2, UR, UC), lambda c: (0, c // 2, c % 2, 0, 0))
    return pl.pallas_call(
        feed_kernel,
        grid=(FF // CHUNK,),
        in_specs=[
            SMEM_SPEC,
            whole((4, GROUP, D)),
            whole((4, GROUP, D)),
            whole((6, 4, 8, D)),
            pl.BlockSpec((4, NK, 4, UR, UC), lambda c: (c, 0, 0, 0, 0)),
            pl.BlockSpec((NJ, 1, 2, UR, UC), lambda c: (0, c // 2, 2 + c % 2, 0, 0)),
            pl.BlockSpec((9, CHUNK), lambda c: (0, c)),
        ],
        out_specs=[
            whole((4, GROUP, D)),
            whole((4, GROUP, D)),
            expand_spec,
            expand_spec,
            shrink_spec,
            shrink_spec,
            pl.BlockSpec((9, CHUNK), lambda c: (0, c)),
        ],
        out_shape=[
            jax.ShapeDtypeStruct((4, GROUP, D), F32),
            jax.ShapeDtypeStruct((4, GROUP, D), F32),
            packed_half(4),
            packed_half(4),
            packed_half(4),
            packed_half(4),
            jax.ShapeDtypeStruct((9, FF), F32),
        ],
        scratch_shapes=[
            pltpu.VMEM((TOK, D), BF),
            pltpu.VMEM((D, TOK), BF),
            pltpu.VMEM((CHUNK, D), BF),
            pltpu.VMEM((D, CHUNK), BF),
            pltpu.VMEM((4, GROUP, CHUNK), F32),
            pltpu.VMEM((4, GROUP, CHUNK), F32),
            pltpu.VMEM((4, GROUP, CHUNK), BF),
            pltpu.VMEM((4, GROUP, CHUNK), BF),
        ],
        compiler_params=params(60),
        cost_estimate=cost(38),
        name="feed",
    )(tag, second, gradient, mods, packed, packed, kernel)


def attend_back_kernel(
    tag_ref, resid, shrunk, d_second, gradient, attn, mods, qkv, lse, proj_t,
    output, d_resid, d_qkv, d_attn_t, item_sums,
    bias, d_mixed, d_attn, sums,
):
    @pl.when(pl.program_id(0) == 0)
    def _():
        bias[...] = item_bias(tag_ref[0])
        sums[...] = jnp.zeros_like(sums)

    def rows_norm(i, _):
        rows = pl.ds(pl.multiple_of(i * 64, 64), 64)
        half = i // 2
        base = resid[0, rows, :]
        normal, factor = norm_stats(base)
        shrunk_rows = shrunk[0, rows, :]
        outward = gradient[0, rows, :].astype(F32)
        d_sec = d_second[0, rows, :]

        def by_item(value):
            return value.reshape(4, 2, 8, D)

        def add(index, value):
            sums[index, pl.ds(2 * half, 2)] += jnp.sum(by_item(value), axis=0)

        gated = (by_item(shrunk_rows) * quadrant_rows(mods, 5, half)).reshape(64, D)
        output[0, rows, :] = (base + gated).astype(BF)
        add(3, outward * shrunk_rows)
        add(1, d_sec)
        add(2, d_sec * normal)
        inner = (by_item(d_sec) * (1.0 + quadrant_rows(mods, 4, half))).reshape(64, D)
        mean = jnp.mean(inner, axis=-1, keepdims=True)
        along = jnp.mean(inner * normal, axis=-1, keepdims=True)
        back = outward + (inner - mean - normal * along) * factor
        d_resid[0, rows, :] = back
        add(0, back * attn[0, rows, :].astype(F32))
        gated = (by_item(back) * quadrant_rows(mods, 2, half)).reshape(64, D)
        d_attn[rows, :] = gated.astype(BF)
        return 0

    lax.fori_loop(0, 4, rows_norm, 0)
    d_attn_t[...] = d_attn[...].T
    d_mixed[...] = dot(proj_t[...], d_attn[...], 1, 1).astype(BF)

    def head(h, _):
        rows = pl.ds(pl.multiple_of(h * HD, HD), HD)
        key_rows = pl.ds(pl.multiple_of(D + h * HD, HD), HD)
        value_rows = pl.ds(pl.multiple_of(2 * D + h * HD, HD), HD)
        queries = qkv[0, rows, :] * jnp.asarray(HD**-0.5, BF)
        keys = qkv[0, key_rows, :]
        values = qkv[0, value_rows, :]
        d_mix = d_mixed[rows, :]
        probs = jnp.exp(dot(keys, queries, 0, 0) + (bias[...] - lse[0, pl.ds(h, 1), :]))
        d_probs = dot(values, d_mix, 0, 0)
        d_qkv[value_rows, :] = dot(d_mix, probs.astype(BF), 1, 1).astype(BF)
        weighted = probs * d_probs
        inner = jnp.sum(weighted, axis=0, keepdims=True)
        d_scores = (weighted - probs * inner).astype(BF)
        d_qkv[rows, :] = (dot(keys, d_scores, 1, 0) * HD**-0.5).astype(BF)
        d_qkv[key_rows, :] = dot(queries, d_scores, 1, 1).astype(BF)
        return 0

    lax.fori_loop(0, H, head, 0, unroll=HEADS)

    @pl.when(pl.program_id(0) == pl.num_programs(0) - 1)
    def _():
        item_sums[...] = jnp.sum(sums[...], axis=2)


def attend_back(part, tag, resid, shrunk, d_second, gradient, attn, mods, qkv, lse, proj_t):
    first, count = PARTS[part]

    def pick_group(*shape):
        return pl.BlockSpec((1,) + shape, lambda g: (first + g,) + (0,) * len(shape))

    return pl.pallas_call(
        attend_back_kernel,
        grid=(count,),
        in_specs=[
            SMEM_SPEC,
            pick_group(GROUP, D),
            pick_group(GROUP, D),
            pick_group(GROUP, D),
            pick_group(GROUP, D),
            pick_group(GROUP, D),
            whole((6, 4, 8, D)),
            pick_group(3 * D, GROUP),
            pick_group(16, GROUP),
            whole((D, D)),
        ],
        out_specs=[
            group_spec(GROUP, D),
            group_spec(GROUP, D),
            pl.BlockSpec((3 * D, GROUP), lambda g: (0, g)),
            pl.BlockSpec((D, GROUP), lambda g: (0, g)),
            whole((4, 4, D)),
        ],
        out_shape=[
            jax.ShapeDtypeStruct((count, GROUP, D), BF),
            jax.ShapeDtypeStruct((count, GROUP, D), F32),
            jax.ShapeDtypeStruct((3 * D, count * GROUP), BF),
            jax.ShapeDtypeStruct((D, count * GROUP), BF),
            jax.ShapeDtypeStruct((4, 4, D), F32),
        ],
        scratch_shapes=[
            pltpu.VMEM((GROUP, GROUP), F32),
            pltpu.VMEM((D, GROUP), BF),
            pltpu.VMEM((GROUP, D), BF),
            pltpu.VMEM((4, 4, 8, D), F32),
        ],
        compiler_params=params(),
        cost_estimate=cost(9 * count),
        name=f"attend_back_{part}",
    )(tag, resid, shrunk, d_second, gradient, attn, mods, qkv, lse, proj_t)


PAIRS = 2
ROWS = 288 * PAIRS


def project_grads_kernel(
    tag_ref, d_qkv0, d_qkv1, d_attn0, d_attn1, conv_in, merged, keep_a, send_a, keep_b, send_b
):
    core = tag_ref[1]

    def against(low, high, field):
        return dot(low[...], field[0], 1, 0) + dot(
            high[...], field[1:4].reshape(3 * GROUP, D), 1, 0
        )

    grad = against(d_qkv0, d_qkv1, conv_in)
    share_out(grad, core, (0, 2), keep_a, send_a)
    share_out(grad, core, (2, 1), keep_b.at[:, :, 0:1], send_b.at[:, :, 0:1])
    grad = against(d_attn0, d_attn1, merged)
    share_out(grad, core, (0, 1), keep_b.at[:, :, 1:2], send_b.at[:, :, 1:2])


def column_specs(rows):
    return [pl.BlockSpec((rows, count * GROUP), lambda i: (i, 0)) for _, count in PARTS]


def project_grads(tag, d_qkv, d_attn, conv_in, merged):
    packed_spec = pl.BlockSpec((PAIRS, NK, 2, UR, UC), lambda i: (i, 0, 0, 0, 0))
    tall = column_specs(ROWS)
    short = column_specs(96 * PAIRS)
    return pl.pallas_call(
        project_grads_kernel,
        grid=(8 // PAIRS,),
        in_specs=[SMEM_SPEC, *tall, *short, whole((4, GROUP, D)), whole((4, GROUP, D))],
        out_specs=[packed_spec] * 4,
        out_shape=[packed_half(2)] * 4,
        compiler_params=params(),
        cost_estimate=cost(8),
        name="project_grads",
    )(tag, *d_qkv, *d_attn, conv_in, merged)


def conv_back_kernel(
    tag_ref, d_qkv0, d_qkv1, weight, norm, mods, kernel, later0, later1, g_ffn,
    d_first, pieces, d_conv, g_kernel, item_sums,
):
    step = pl.program_id(0)

    @pl.when(step == 0)
    def _():
        d_conv[...] = jnp.zeros_like(d_conv)

    d_conv[0] += dot(d_qkv0[...], weight[...], 0, 0)
    d_conv[1:4] += dot(d_qkv1[...], weight[...], 0, 0).reshape(3, GROUP, D)

    @pl.when(step == pl.num_programs(0) - 1)
    def _():
        tag = tag_ref[0]
        left, right = edge_columns(tag)
        keep = 1.0 - tag.astype(F32)

        def lanes(i, _):
            cols = pl.ds(pl.multiple_of(i * 128, 128), 128)
            taps = [jnp.broadcast_to(kernel[t : t + 1, cols], (16, 128)) for t in range(9)]
            sums = [[jnp.zeros((16, 128), F32) for _ in range(2)] for _ in range(2)]

            def load_grad(g, p):
                return d_conv[g, p * 16 : p * 16 + 16, cols]

            def load_field(g, p):
                q = 2 * (p // 8)
                shift = mods[0, q : q + 2, :, cols].reshape(16, 128)
                scale = mods[1, q : q + 2, :, cols].reshape(16, 128)
                return norm[g, p * 16 : p * 16 + 16, cols] * (1.0 + scale) + shift

            def emit(g, p, value):
                rows = slice(p * 16, p * 16 + 16)
                d_first[g, rows, cols] = value
                sums[0][p // 8] += value
                sums[1][p // 8] += value * norm[g, rows, cols]

            grads = conv_back_rows(load_grad, load_field, taps, left, right, keep, emit)
            for t in range(9):
                g_kernel[t : t + 1, cols] = jnp.sum(grads[t], axis=0, keepdims=True)
            for kind in range(2):
                for item in range(4):
                    part = sums[kind][item // 2][8 * (item % 2) : 8 * (item % 2) + 8]
                    item_sums[kind, item : item + 1, cols] = jnp.sum(part, axis=0, keepdims=True)
            return 0

        lax.fori_loop(0, D // 128, lanes, 0)
        later = later0[...] + later1[...]
        rows = [item_sums[i] for i in range(2)] + [later[i] for i in range(4)]
        rows = jnp.concatenate(rows, axis=1)
        alone = jnp.concatenate([jnp.sum(rows, axis=0, keepdims=True), jnp.zeros((3, 6 * D), F32)])
        rows = jnp.where(tag == 1, rows, alone)
        slots, _, width = pieces.shape
        owners = 6 * D // width
        short, long = D // owners, FF // owners
        for j in range(owners):
            filters = jnp.concatenate(
                [
                    g_kernel[:, j * short : (j + 1) * short],
                    g_ffn[:, j * long : (j + 1) * long],
                    jnp.zeros((9, width - short - long), F32),
                ],
                axis=1,
            )
            part = [rows[:, j * width : (j + 1) * width], filters, jnp.zeros((3, width), F32)]
            part = jnp.concatenate(part, axis=0).astype(BF)
            for copy in range(slots // owners):
                pieces[j * (slots // owners) + copy] = part


def conv_back(slots, width, tag, d_qkv, weight, norm, mods, kernel, later, g_ffn):
    return pl.pallas_call(
        conv_back_kernel,
        grid=(8 // PAIRS,),
        in_specs=[
            SMEM_SPEC,
            *column_specs(ROWS),
            pl.BlockSpec((ROWS, D), lambda i: (i, 0)),
            whole((4, GROUP, D)),
            whole((6, 4, 8, D)),
            whole((9, D)),
            whole((4, 4, D)),
            whole((4, 4, D)),
            whole((9, FF)),
        ],
        out_specs=[whole((4, GROUP, D)), whole((slots, 16, width))],
        out_shape=[
            jax.ShapeDtypeStruct((4, GROUP, D), F32),
            jax.ShapeDtypeStruct((slots, 16, width), BF),
        ],
        scratch_shapes=[
            pltpu.VMEM((4, GROUP, D), F32),
            pltpu.VMEM((9, D), F32),
            pltpu.VMEM((2, 4, D), F32),
        ],
        compiler_params=params(),
        cost_estimate=cost(15),
        name="conv_back",
    )(tag, *d_qkv, weight, norm, mods, kernel, *later, g_ffn)


def finish_kernel(
    d_first, norm, factor, d_resid0, d_resid1, output0, output1, mods,
    block_output, input_grad, total,
):
    half = pl.program_id(0) // 2

    for g in range(4):
        base = d_resid1[g - 1] if g else d_resid0[0]
        value = d_first[g]
        normal = norm[g]
        inner = (value.reshape(4, 2, 8, D) * (1.0 + quadrant_rows(mods, 1, half))).reshape(64, D)
        mean = jnp.mean(inner, axis=-1, keepdims=True)
        along = jnp.mean(inner * normal, axis=-1, keepdims=True)
        total[g] = base + (inner - mean - normal * along) * factor[g]
    order = ungroup_matrix()
    grouped = total[...].reshape(256, D)
    high = grouped.astype(BF)
    rest = (grouped - high.astype(F32)).astype(BF)
    input_grad[...] = dot(order, high, 1, 0) + dot(order, rest, 1, 0)
    grouped = jnp.concatenate([output0[...], output1[...]], axis=0).reshape(256, D)
    block_output[...] = dot(order, grouped, 1, 0).astype(BF)


def finish(d_first, norm, factor, d_resid, output, mods):
    def split(groups, width):
        return pl.BlockSpec((groups, 64, width), lambda i: (0, i, 0))

    flat = pl.BlockSpec((256, D), lambda i: (i, 0))
    return pl.pallas_call(
        finish_kernel,
        grid=(4,),
        in_specs=[split(4, D), split(4, D), split(4, 1)]
        + [split(count, D) for _, count in PARTS] * 2
        + [whole((6, 4, 8, D))],
        out_specs=[flat, flat],
        out_shape=[
            jax.ShapeDtypeStruct((TOK, D), BF),
            jax.ShapeDtypeStruct((TOK, D), F32),
        ],
        scratch_shapes=[pltpu.VMEM((4, 64, D), F32)],
        compiler_params=params(),
        cost_estimate=cost(8),
        name="finish",
    )(d_first, norm, factor, *d_resid, *output, mods)


BOTH = ("dp", "fsdp")


def exchange(pieces):
    return lax.all_to_all(pieces, BOTH, 0, 0, tiled=True)


def units_of(weight):
    return weight.T.reshape(-1, UR, UC)


def low_units(shrink):
    return shrink.T.reshape(UR, 4, UC).transpose(1, 0, 2)


def gather_feed(nd, nf, expand, shrink):
    if (nd, nf) == (NJ, NK):
        rows = jnp.concatenate([units_of(expand), low_units(shrink)]).reshape(8 * UR, UC)
        return lax.all_gather(rows, BOTH).reshape(NJ, NK, 8, UR, UC)
    low = full_rows(shrink).reshape(NJ, UR, NK, 4, UC).transpose(0, 2, 3, 1, 4)
    return jnp.concatenate([all_units(full_rows(expand), 4), low], axis=2)


def full_rows(shard):
    rows = lax.all_gather(shard.T, "fsdp", axis=1, tiled=True)
    return lax.all_gather(rows, "dp", axis=0, tiled=True)


def all_units(weight, units):
    return weight.reshape(NJ, units, UR, NK, UC).transpose(0, 3, 1, 2, 4)


def project_turns(own):
    turns = [
        lax.ppermute(own, "dp", [(i, (i - 4 * step) % NJ) for i in range(NJ)])
        for step in range(1, 4)
    ]
    return turns


def widen(a, b, bit_a, bit_b):
    return jnp.stack([a, swap(a, bit_a)]), jnp.stack([b, swap(b, bit_b)])


def all_projections(qkv, proj):
    units = jnp.concatenate([all_units(full_rows(qkv), 3), all_units(full_rows(proj), 1)], axis=2)
    units = units.reshape((4, 2, 2) + units.shape[1:])
    first, rest = units[:, :, :, :, :2], units[:, :, :, :, 2:]
    a, b = first.transpose(2, 3, 1, 0, 4, 5, 6), rest.transpose(2, 1, 3, 0, 4, 5, 6)
    return a[0], b[0], a[1], b[1]


def pick(grads, index, axis):
    return lax.dynamic_index_in_dim(grads, index, axis, keepdims=False)


def swap(value, bit):
    if bit is None:
        return lax.ppermute(value, "fsdp", [(0, 1), (1, 0)])
    return lax.ppermute(value, "dp", [(i, i ^ bit) for i in range(NJ)])


def halve(keep, got, axis, bit):
    mine = lax.axis_index("fsdp") if bit is None else (lax.axis_index("dp") // bit) % 2
    kept = pick(keep, mine, axis) + pick(got, mine, axis)
    return kept, pick(keep, 1 - mine, axis) + pick(got, 1 - mine, axis)


def last_sends(total):
    place = lax.axis_index("dp") // 4
    return [pick(total, (place + step) % 4, 0) for step in range(1, 4)]


def last_swaps(sends):
    return [
        lax.ppermute(sent, "dp", [(i, (i + 4 * step) % NJ) for i in range(NJ)])
        for step, sent in enumerate(sends, 1)
    ]


def last_sum(total, got):
    own = pick(total, lax.axis_index("dp") // 4, 0).astype(F32)
    for value in got:
        own = own + value.astype(F32)
    return own


def after(value, *others):
    return lax.optimization_barrier((value,) + others)[0]


def own_shard(nd, nf, kind, units):
    if (nd, nf) == (NJ, NK):
        if kind == "shrink":
            return units.transpose(1, 0, 2).reshape(UR, 4 * UC).T
        return units.reshape(-1, UC).T
    if kind == "shrink":
        weight = units.transpose(0, 3, 1, 2, 4).reshape(NJ * UR, -1)
    else:
        weight = units.transpose(0, 2, 3, 1, 4).reshape(-1, NK * UC)
    columns = lax.psum_scatter(weight, "dp", scatter_dimension=0, tiled=True)
    piece = lax.psum_scatter(columns, "fsdp", scatter_dimension=1, tiled=True)
    return piece.astype(F32).T


def both_cores(keep, send):
    return jnp.stack([keep, send], axis=1).reshape((-1,) + keep.shape[1:])


def look_up(ids, step_table, class_table):
    first_row = lax.axis_index("fsdp") * step_table.shape[0]
    own = first_row + jnp.arange(step_table.shape[0], dtype=jnp.int32)
    step_hot = (ids[:, :4].reshape(-1, 1) == own[None, :]).astype(BF)
    class_hot = (ids[:, 4:].reshape(-1, 1) == own[None, :]).astype(BF)
    return step_hot, class_hot, dot(step_hot, step_table, 1, 0) + dot(class_hot, class_table, 1, 0)


def share_act(nd, cond, attn_kernel, ffn_kernel):
    items, width = cond.shape
    act = jax.nn.silu(cond).astype(BF)
    filters = jnp.concatenate([attn_kernel, ffn_kernel], axis=1).reshape(-1, width)
    sent = jnp.concatenate([act, filters], axis=0)[None]
    sent = lax.all_to_all(jnp.broadcast_to(sent, (nd,) + sent.shape[1:]), "dp", 0, 0, tiled=True)
    act_all = sent[:, :items].transpose(1, 0, 2).reshape(items, nd * width)
    filters = sent[:, items:].reshape(nd, 9, -1).astype(F32)
    attn_full = filters[:, :, : attn_kernel.shape[1]].transpose(1, 0, 2).reshape(9, -1)
    ffn_full = filters[:, :, attn_kernel.shape[1] :].transpose(1, 0, 2).reshape(9, -1)
    return act_all, attn_full, ffn_full


def exchange_columns(nd, nf, d_act):
    rows, items = d_act.shape
    if (nd, nf) == (NJ, NK):
        return lax.all_to_all(d_act.reshape(nd, rows // nd, items), "dp", 0, 0, tiled=True)
    spread = lax.dynamic_update_slice_in_dim(
        jnp.zeros((rows * nf, items), F32), d_act, lax.axis_index("fsdp") * rows, axis=0
    )
    spread = spread.reshape(nd, 1, -1, items)
    spread = jnp.broadcast_to(spread, (nd, nf) + spread.shape[2:])
    return exchange(spread.reshape((nd * nf,) + spread.shape[2:]))


def own_columns(nd, nf, terms):
    part = terms.sum(axis=0)
    if (nd, nf) != (NJ, NK):
        return part
    order = [(j * NK + k, k * NJ + j) for j in range(NJ) for k in range(NK)]
    own = lax.ppermute(part, BOTH, order)
    other = lax.ppermute(part, BOTH, [(i, o ^ 1) for i, o in order])
    first = lax.axis_index("fsdp") == 0
    return jnp.concatenate([jnp.where(first, own, other), jnp.where(first, other, own)])


def body(
    latents, size_tags, timesteps, classes, step_table, class_table, modulation_weight,
    attn_kernel, qkv_weight, proj_weight, expand_weight, ffn_kernel, shrink_weight, cotangent,
    *, nd, nf,
):
    slots = nd * nf
    tag = size_tags[0]
    square = (nd, nf) == (NJ, NK)
    if square:
        place = lax.axis_index("dp")
        where = [tag, place % 2, place // 4, (place // 2) % 2, lax.axis_index("fsdp")]
        where = jnp.stack(where).astype(jnp.int32)
    else:
        where = jnp.stack([tag] + [jnp.int32(0)] * 4)
    packed = gather_feed(nd, nf, expand_weight, shrink_weight)
    tokens, gradient, norm, factor = prepare(latents, cotangent)
    mine = jnp.concatenate([timesteps[0], classes[0]])[None]
    mine = jnp.broadcast_to(mine, (slots, 8))
    if square:
        own = jnp.concatenate([units_of(qkv_weight), units_of(proj_weight)])
        own = after(own, mine)
        turns = project_turns(own)
    ids = exchange(mine)
    if square:
        ids = after(ids, norm)
    step_hot, class_hot, part = look_up(ids, step_table, class_table)
    if square:
        cond = part + swap(part, None)
        a = jnp.stack([own[:2]] + [turn[:2] for turn in turns])
        b = jnp.stack([own[2:]] + [turn[2:] for turn in turns])
        a, b = widen(a, b, 2, None)
        cond = after(cond, a, b)
        next_a, next_b = swap(a, None), swap(b, 2)
    else:
        cond = lax.psum(part, "fsdp")
    act_all, attn_full, ffn_full = share_act(nd, cond, attn_kernel, ffn_kernel)
    if square:
        next_a, next_b = after(next_a, act_all), after(next_b, act_all)
    height, width = modulation_weight.shape
    act_rows = lax.dynamic_slice_in_dim(
        act_all, lax.axis_index("fsdp") * height, height, axis=1
    )
    terms = dot(act_rows, modulation_weight, 1, 0)
    terms = exchange(terms.reshape(slots, 1, 4 * width)).reshape(nd, nf, 4, width)
    if square:
        a, b = jnp.stack([a, next_a]), jnp.stack([b, next_b])
        projections = (a, b, swap(a, 1), swap(b, 1))
    else:
        projections = all_projections(qkv_weight, proj_weight)
    mod_rows = terms.sum(axis=1).transpose(1, 0, 2).reshape(4, nd * width)
    chosen = jnp.where(tag == 1, mod_rows, mod_rows[:1])
    mods = jnp.broadcast_to(chosen.reshape(4, 6, 1, D).transpose(1, 0, 2, 3), (6, 4, 8, D))

    conv_in = first_conv(size_tags, norm, mods, attn_full)
    qkv, merged, attn, resid, second, lse, proj_t, full_qkv = attend(
        where, conv_in, tokens, mods, projections
    )
    shrunk, d_second, keep_e, send_e, keep_s, send_s, g_ffn = feed(
        where, second, gradient, mods, packed, ffn_full
    )
    back = (gradient, attn, mods, qkv, lse)
    if square:
        got_e, got_s = swap(send_e, 1), swap(send_s, 1)
    output0, d_resid0, d_qkv0, d_attn0, later0 = attend_back(
        0, where, resid, shrunk, d_second, *back, proj_t
    )

    def grid(value):
        return value.reshape((4, 2) + value.shape[1:])

    if square:
        got_e, got_s = after(got_e, d_qkv0), after(got_s, d_qkv0)
        keep_e, out_e = halve(grid(keep_e), grid(got_e), 2, None)
        keep_s, out_s = halve(grid(keep_s), grid(got_s), 1, 2)
        d_second = after(d_second, out_e, out_s)
        got_e, got_s = swap(out_e, None), swap(out_s, 2)
    output1, d_resid1, d_qkv1, d_attn1, later1 = attend_back(
        1, where, resid, shrunk, d_second, *back, proj_t
    )
    if square:
        got_e, got_s = after(got_e, d_attn1), after(got_s, d_attn1)
        keep_e, out_e = halve(keep_e, got_e, 1, 2)
        keep_s, out_s = halve(keep_s, got_s, 1, None)
        d_attn0 = after(d_attn0, out_e, out_s)
        got_e, got_s = swap(out_e, 2), swap(out_s, None)
    d_qkv = (d_qkv0, d_qkv1)
    keep_a, send_a, keep_b, send_b = project_grads(
        where, d_qkv, (d_attn0, d_attn1), conv_in, merged
    )
    if square:
        got_e, got_s = after(got_e, keep_a), after(got_s, keep_a)
        got_a, got_b = swap(send_a, 1), swap(send_b, 1)
        e = halve(keep_e.reshape((2, 2) + keep_e.shape[1:]), got_e.reshape((2, 2) + got_e.shape[1:]), 1, 4)
        s = halve(keep_s.reshape((2, 2) + keep_s.shape[1:]), got_s.reshape((2, 2) + got_s.shape[1:]), 1, 4)
        feeding, out_f = (jnp.concatenate(pair, axis=1) for pair in zip(e, s))
        keep_a, out_a = halve(grid(keep_a), grid(got_a), 2, None)
        keep_b, out_b = halve(grid(keep_b), grid(got_b), 1, 2)
        full_qkv = after(full_qkv, out_a, out_b, out_f)
        got_a, got_b, got_f = swap(out_a, None), swap(out_b, 2), swap(out_f, 4)
    d_first, pieces = conv_back(
        slots, width, where, d_qkv, full_qkv, norm, mods, attn_full, (later0, later1), g_ffn
    )
    if square:
        got_a, got_b, got_f = (after(x, d_first) for x in (got_a, got_b, got_f))
        keep_a, out_a = halve(keep_a, got_a, 1, 2)
        keep_b, out_b = halve(keep_b, got_b, 1, None)
        feeding, out_f = halve(feeding, got_f, 0, 8)
    if square:
        d_first = after(d_first, out_a, out_b, out_f, pieces)
        got_a, got_b, got_f = swap(out_a, 2), swap(out_b, None), swap(out_f, 8)
    got = exchange(pieces)
    block_output, input_grad = finish(
        d_first, norm, factor, (d_resid0, d_resid1), (output0, output1), mods
    )
    if square:
        got = after(got, input_grad)
    d_mod_all = got[:, :4].reshape(slots * 4, width)
    d_act = dot(modulation_weight, d_mod_all, 1, 1)
    if square:
        got_a, got_b = after(got_a, d_act), after(got_b, d_act)
        total = jnp.concatenate([keep_a + got_a, keep_b + got_b], axis=1)
        sends = last_sends(total)
        last = last_swaps(sends)
    own_act = exchange_columns(nd, nf, d_act)
    if square:
        got_f = after(got_f, own_act)
        total = last_sum(total, last)
        feeding = feeding.astype(F32) + got_f.astype(F32)
        cuts = [total[:3], total[3:], feeding[:4], feeding[4:]]
    else:
        first, rest = both_cores(keep_a, send_a), both_cores(keep_b, send_b)
        cuts = [
            jnp.concatenate([first, rest[:, :, :1]], axis=2),
            rest[:, :, 1:],
            both_cores(keep_e, send_e),
            both_cores(keep_s, send_s),
        ]
    shards = [
        own_shard(nd, nf, kind, cut)
        for kind, cut in zip(("qkv", "proj", "expand", "shrink"), cuts)
    ]
    cut = attn_kernel.shape[1]
    filters = got[:, 4:13, : cut + ffn_kernel.shape[1]].astype(F32).sum(axis=0)
    modulation_grad = dot(act_rows, d_mod_all, 0, 0)
    gate = jax.nn.sigmoid(cond)
    d_cond = own_columns(nd, nf, own_act)
    d_cond = d_cond * (gate * (1.0 + cond * (1.0 - gate))).T

    def table_grad(hot):
        return lax.dot_general(
            hot.astype(F32), d_cond, (((0,), (1,)), ((), ())), precision=lax.Precision.HIGHEST
        )

    return (
        block_output,
        input_grad,
        table_grad(step_hot),
        table_grad(class_hot),
        modulation_grad,
        filters[:, :cut],
        shards[0],
        shards[1],
        shards[2],
        filters[:, cut:],
        shards[3],
    )


def solution(mesh):
    matrix = P("fsdp", "dp")
    rows = P(BOTH, None)
    filters = P(None, "dp")
    in_specs = (
        rows, P(BOTH), rows, rows, matrix, matrix, matrix, filters, matrix, matrix, matrix,
        filters, matrix, rows,
    )
    out_specs = (
        rows, rows, matrix, matrix, matrix, filters, matrix, matrix, matrix, filters, matrix,
    )
    run = functools.partial(body, nd=mesh.shape["dp"], nf=mesh.shape["fsdp"])
    return jax.shard_map(run, mesh=mesh, in_specs=in_specs, out_specs=out_specs, check_vma=False)
```

```python
import functools

import jax
import jax.numpy as jnp
from jax import lax
from jax.experimental import pallas as pl
from jax.experimental.pallas import tpu as pltpu
from jax.sharding import PartitionSpec as P

D = 768
H = 12
HD = 64
FF = 3072
SIDE = 32
GROUP = 256
TOK = SIDE * SIDE
EPS = 1e-06
NJ, NK, UR, UC = 16, 2, 48, 384
CHUNK = 768
HEADS = 6
PARTS = ((0, 1), (1, 3))
MIB = 1024 * 1024
BF = jnp.bfloat16
F32 = jnp.float32
GELU_A = 0.7978845608028654
GELU_B = GELU_A * 0.044715


def dot(left, right, left_dim, right_dim):
    return lax.dot_general(
        left, right, (((left_dim,), (right_dim,)), ((), ())), preferred_element_type=F32
    )


def params(limit=56):
    return pltpu.CompilerParams(vmem_limit_bytes=limit * MIB)


def cost(micros):
    return pl.CostEstimate(flops=int(micros * 1e8), transcendentals=0, bytes_accessed=4 * MIB)


def whole(shape):
    zeros = (0,) * len(shape)
    return pl.BlockSpec(shape, lambda *ids: zeros, pipeline_mode=pl.Buffered(1))


SMEM_SPEC = pl.BlockSpec(memory_space=pltpu.SMEM)


def group_place(natural):
    pair, odd_row = natural // 64, (natural // 32) % 2
    column, odd_column = (natural % 32) // 2, natural % 2
    return (2 * odd_row + odd_column) * 64 + pair * 16 + column


def ungroup_matrix():
    natural = lax.broadcasted_iota(jnp.int32, (256, 256), 0)
    grouped = lax.broadcasted_iota(jnp.int32, (256, 256), 1)
    return jnp.where(group_place(natural) == grouped, 1.0, 0.0).astype(BF)


def group_matrix():
    natural = lax.broadcasted_iota(jnp.int32, (256, 256), 1)
    grouped = lax.broadcasted_iota(jnp.int32, (256, 256), 0)
    return jnp.where(group_place(natural) == grouped, 1.0, 0.0).astype(BF)


def norm_stats(values):
    centre = values - jnp.mean(values, axis=-1, keepdims=True)
    variance = jnp.mean(centre * centre, axis=-1, keepdims=True)
    scale = lax.rsqrt(variance + EPS)
    return centre * scale, scale


def prepare_kernel(latents, cotangent, tokens, gradient, norm, scale):
    order = group_matrix()
    gathered = dot(order, latents[...], 1, 0)
    gradient[...] = dot(order, cotangent[...], 1, 0).reshape(4, 64, D).astype(BF)
    tokens[...] = gathered.reshape(4, 64, D).astype(BF)
    normal, factor = norm_stats(gathered)
    norm[...] = normal.reshape(4, 64, D)
    scale[...] = factor.reshape(4, 64, 1)


def prepare(latents, cotangent):
    flat = pl.BlockSpec((256, D), lambda i: (i, 0))
    split = pl.BlockSpec((4, 64, D), lambda i: (0, i, 0))
    return pl.pallas_call(
        prepare_kernel,
        grid=(4,),
        in_specs=[flat, flat],
        out_specs=[split, split, split, pl.BlockSpec((4, 64, 1), lambda i: (0, i, 0))],
        out_shape=[
            jax.ShapeDtypeStruct((4, GROUP, D), BF),
            jax.ShapeDtypeStruct((4, GROUP, D), BF),
            jax.ShapeDtypeStruct((4, GROUP, D), F32),
            jax.ShapeDtypeStruct((4, GROUP, 1), F32),
        ],
        compiler_params=params(),
        cost_estimate=cost(6),
        name="prepare",
    )(latents, cotangent)


def edge_columns(tag):
    place = lax.broadcasted_iota(jnp.int32, (16, 128), 0)
    left = jnp.where((place == 0) | ((place == 8) & (tag == 1)), 0.0, 1.0)
    right = jnp.where((place == 15) | ((place == 7) & (tag == 1)), 0.0, 1.0)
    return left, right


def neighbours(even, odd, left, right):
    return pltpu.roll(odd, 1, 0) * left, pltpu.roll(even, 15, 0) * right


def conv_rows(load, kernel, left, right, keep, emit):
    above = None
    partial = None
    for row in range(SIDE + 1):
        taps = None
        if row < SIDE:
            a, p = row % 2, row // 2
            even, odd = load(2 * a, p), load(2 * a + 1, p)
            odd_left, even_right = neighbours(even, odd, left, right)
            taps = []
            for tap in range(3):
                k = [kernel[3 * tap + b] for b in range(3)]
                taps.append(
                    (
                        k[0] * odd_left + k[1] * even + k[2] * odd,
                        k[0] * even + k[1] * odd + k[2] * even_right,
                    )
                )
        crossing = row == SIDE // 2
        if partial is not None:
            a, p = (row - 1) % 2, (row - 1) // 2
            for b in range(2):
                value = partial[b]
                if taps is not None:
                    below = taps[2][b]
                    value = value + (below * keep if crossing else below)
                emit(2 * a + b, p, value)
        if taps is not None:
            partial = []
            for b in range(2):
                value = taps[1][b]
                if above is not None:
                    value = value + (above[b] * keep if crossing else above[b])
                partial.append(value)
            above = taps[0]


def conv_back_rows(load_grad, load_field, kernel, left, right, keep, emit):
    sums = [jnp.zeros((16, 128), F32) for _ in range(9)]
    from_above = None
    partial = None
    field_above = None
    field = (load_field(0, 0), load_field(1, 0))
    for row in range(SIDE + 1):
        crossing = row == SIDE // 2
        taps = None
        if row < SIDE:
            a, p = row % 2, row // 2
            even, odd = load_grad(2 * a, p), load_grad(2 * a + 1, p)
            odd_left, even_right = neighbours(even, odd, left, right)
            picks = ((odd, even, odd_left), (even_right, odd, even))
            taps = []
            for tap in range(3):
                k = [kernel[3 * tap + b] for b in range(3)]
                taps.append(
                    tuple(k[0] * x[0] + k[1] * x[1] + k[2] * x[2] for x in picks)
                )
            field_below = None
            if row + 1 < SIDE:
                a, p = (row + 1) % 2, (row + 1) // 2
                field_below = (load_field(2 * a, p), load_field(2 * a + 1, p))
            for tap, rows in enumerate((field_above, field, field_below)):
                if rows is None:
                    continue
                if (tap == 0 and crossing) or (tap == 2 and row + 1 == SIDE // 2):
                    rows = (rows[0] * keep, rows[1] * keep)
                for b in range(3):
                    sums[3 * tap + b] = (
                        sums[3 * tap + b] + rows[0] * picks[0][b] + rows[1] * picks[1][b]
                    )
            field_above, field = field, field_below
        if partial is not None:
            a, p = (row - 1) % 2, (row - 1) // 2
            for b in range(2):
                value = partial[b]
                if taps is not None:
                    value = value + (taps[0][b] * keep if crossing else taps[0][b])
                emit(2 * a + b, p, value)
        if taps is not None:
            partial = []
            for b in range(2):
                value = taps[1][b]
                if from_above is not None:
                    value = value + (from_above[b] * keep if crossing else from_above[b])
                partial.append(value)
            from_above = taps[2]
    return sums


def first_conv_kernel(tag_ref, norm, mods, kernel, out):
    tag = tag_ref[0]
    left, right = edge_columns(tag)
    keep = 1.0 - tag.astype(F32)
    taps = [jnp.broadcast_to(kernel[i : i + 1, :], (16, 128)) for i in range(9)]

    def load(g, p):
        q = 2 * (p // 8)
        shift = mods[0, q : q + 2].reshape(16, 128)
        scale = mods[1, q : q + 2].reshape(16, 128)
        return norm[g, p * 16 : p * 16 + 16, :] * (1.0 + scale) + shift

    def emit(g, p, value):
        out[g, p * 16 : p * 16 + 16, :] = value.astype(BF)

    conv_rows(load, taps, left, right, keep, emit)


def first_conv(tag, norm, mods, kernel):
    return pl.pallas_call(
        first_conv_kernel,
        grid=(D // 128,),
        in_specs=[
            SMEM_SPEC,
            pl.BlockSpec((4, GROUP, 128), lambda i: (0, 0, i)),
            pl.BlockSpec((6, 4, 8, 128), lambda i: (0, 0, 0, i)),
            pl.BlockSpec((9, 128), lambda i: (0, i)),
        ],
        out_specs=pl.BlockSpec((4, GROUP, 128), lambda i: (0, 0, i)),
        out_shape=jax.ShapeDtypeStruct((4, GROUP, D), BF),
        compiler_params=params(),
        cost_estimate=cost(6),
        name="first_conv",
    )(tag, norm, mods, kernel)


def join_rows(block, target):
    rows = block.shape[0] * block.shape[2] * UR
    for k in range(NK):
        target[:, k * UC : (k + 1) * UC] = block[:, k].reshape(rows, UC)


def share_out(rows, core, units, keep, send):
    first, count = units
    for k in range(NK):
        part = rows[:, k * UC : (k + 1) * UC].astype(BF)
        part = part.reshape(-1, 2, part.shape[0] // (keep.shape[0] * 2), UC)
        even, odd = part[:, 0], part[:, 1]
        for target, value in (
            (keep, jnp.where(core == 0, even, odd)),
            (send, jnp.where(core == 0, odd, even)),
        ):
            whole_units = value.reshape(value.shape[0], -1, UR, UC)
            target[:, k] = whole_units[:, first : first + count]


def quadrant_rows(mods, index, half):
    return mods[index, pl.ds(2 * half, 2)].reshape(1, 2, 8, D)


def item_bias(tag):
    def label(dim):
        place = lax.broadcasted_iota(jnp.int32, (GROUP, GROUP), dim)
        return 2 * (place // 128) + (place % 16) // 8

    return jnp.where((label(0) == label(1)) | (tag == 0), 0.0, -1e30)


def attend_kernel(
    where, conv_in, tokens, mods, own_a, own_b, peer_a, peer_b,
    qkv, merged, attn, resid, second, lse, proj_t, full_qkv,
    full_proj, bias, mixed_t,
):
    @pl.when(pl.program_id(0) == 0)
    def _():
        core, z, y, x = (where[i] for i in range(1, 5))
        for owner in range(NJ):
            step = (owner // 4 - z + 4) % 4
            side = (owner // 2) % 2 ^ y
            mine = core == owner % 2
            for k in range(NK):
                cols = slice(k * UC, (k + 1) * UC)
                a = jnp.where(mine, own_a[k ^ x, side, step], peer_a[k ^ x, side, step])
                b = jnp.where(mine, own_b[side, k ^ x, step], peer_b[side, k ^ x, step])
                start = owner * 3 * UR
                full_qkv[start : start + 2 * UR, cols] = a.reshape(2 * UR, UC)
                full_qkv[start + 2 * UR : start + 3 * UR, cols] = b[0]
                full_proj[owner * UR : (owner + 1) * UR, cols] = b[1]
        proj_t[...] = full_proj[...].T
        bias[...] = item_bias(where[0])

    qkv[0] = dot(full_qkv[...], conv_in[0], 1, 1).astype(BF)

    def head(h, _):
        rows = pl.ds(pl.multiple_of(h * HD, HD), HD)
        queries = qkv[0, rows, :] * jnp.asarray(HD**-0.5, BF)
        keys = qkv[0, pl.ds(pl.multiple_of(D + h * HD, HD), HD), :]
        values = qkv[0, pl.ds(pl.multiple_of(2 * D + h * HD, HD), HD), :]
        scores = dot(keys, queries, 0, 0) + bias[...]
        highest = jnp.max(scores, axis=0, keepdims=True)
        raised = jnp.exp(scores - highest)
        total = jnp.sum(raised, axis=0, keepdims=True)
        probs = (raised * (1.0 / total)).astype(BF)
        lse[0, pl.ds(h, 1), :] = highest + jnp.log(total)
        mixed_t[rows, :] = dot(values, probs, 1, 0).astype(BF)
        return 0

    lax.fori_loop(0, H, head, 0, unroll=HEADS)
    merged[0] = mixed_t[...].T
    projected = dot(merged[0], full_proj[...], 1, 1)
    attn[0] = projected.astype(BF)
    gate = mods[2].reshape(2, 1, 2, 8, D)
    resid[0] = (
        tokens[0].astype(F32) + (projected.reshape(2, 8, 2, 8, D) * gate).reshape(GROUP, D)
    )

    def rows_norm(i, _):
        rows = pl.ds(pl.multiple_of(i * 64, 64), 64)
        normal, _ = norm_stats(resid[0, rows, :])
        half = i // 2
        scaled = normal.reshape(4, 2, 8, D) * (1.0 + quadrant_rows(mods, 4, half))
        value = scaled + quadrant_rows(mods, 3, half)
        second[0, rows, :] = value.reshape(64, D).astype(BF)
        return 0

    lax.fori_loop(0, 4, rows_norm, 0)


def group_spec(*shape):
    return pl.BlockSpec((1,) + shape, lambda g: (g,) + (0,) * len(shape))


def attend(where, conv_in, tokens, mods, projections):
    relative = (2, 2, 4, 2, UR, UC)
    return pl.pallas_call(
        attend_kernel,
        grid=(4,),
        in_specs=[
            SMEM_SPEC,
            group_spec(GROUP, D),
            group_spec(GROUP, D),
            whole((6, 4, 8, D)),
        ]
        + [whole(relative)] * 4,
        out_specs=[
            group_spec(3 * D, GROUP),
            group_spec(GROUP, D),
            group_spec(GROUP, D),
            group_spec(GROUP, D),
            group_spec(GROUP, D),
            group_spec(16, GROUP),
            whole((D, D)),
            whole((3 * D, D)),
        ],
        out_shape=[
            jax.ShapeDtypeStruct((4, 3 * D, GROUP), BF),
            jax.ShapeDtypeStruct((4, GROUP, D), BF),
            jax.ShapeDtypeStruct((4, GROUP, D), BF),
            jax.ShapeDtypeStruct((4, GROUP, D), F32),
            jax.ShapeDtypeStruct((4, GROUP, D), BF),
            jax.ShapeDtypeStruct((4, 16, GROUP), F32),
            jax.ShapeDtypeStruct((D, D), BF),
            jax.ShapeDtypeStruct((3 * D, D), BF),
        ],
        scratch_shapes=[
            pltpu.VMEM((D, D), BF),
            pltpu.VMEM((GROUP, GROUP), F32),
            pltpu.VMEM((D, GROUP), BF),
        ],
        compiler_params=params(),
        cost_estimate=cost(38),
        name="attend",
    )(where, conv_in, tokens, mods, *projections)


def feed_kernel(
    tag_ref, second, gradient, mods, w_expand, w_shrink, kernel,
    shrunk, d_second, keep_expand, send_expand, keep_shrink, send_shrink, g_kernel,
    d_shrunk, d_shrunk_t, expand, shrink, field, slope, hidden, d_field,
):
    step = pl.program_id(0)
    tag, core = tag_ref[0], tag_ref[1]

    @pl.when(step == 0)
    def _():
        gate = mods[5].reshape(1, 2, 1, 2, 8, D)
        value = gradient[...].astype(F32).reshape(4, 2, 8, 2, 8, D) * gate
        d_shrunk[...] = value.reshape(TOK, D).astype(BF)
        d_shrunk_t[...] = d_shrunk[...].T
        shrunk[...] = jnp.zeros_like(shrunk)
        d_second[...] = jnp.zeros_like(d_second)

    join_rows(w_expand, expand)
    for q in range(2):
        shrink[:, q * UC : (q + 1) * UC] = w_shrink[:, 0, q].reshape(D, UC)
    left, right = edge_columns(tag)
    keep = 1.0 - tag.astype(F32)
    field[...] = dot(second[...].reshape(TOK, D), expand[...], 1, 1).reshape(4, GROUP, CHUNK)
    slope[...] = dot(d_shrunk[...], shrink[...], 1, 0).reshape(4, GROUP, CHUNK)

    def lanes(i, _):
        cols = pl.ds(pl.multiple_of(i * 128, 128), 128)
        taps = [jnp.broadcast_to(kernel[t : t + 1, cols], (16, 128)) for t in range(9)]

        def load(g, p):
            return field[g, p * 16 : p * 16 + 16, cols]

        def load_slope(g, p):
            return slope[g, p * 16 : p * 16 + 16, cols]

        def emit(g, p, value):
            square = value * value
            half = 0.5 + 0.5 * jnp.tanh(value * (GELU_A + GELU_B * square))
            out = value * half
            hidden[g, p * 16 : p * 16 + 16, cols] = out.astype(BF)
            rate = half + (out - out * half) * (2.0 * GELU_A + 6.0 * GELU_B * square)
            slope[g, p * 16 : p * 16 + 16, cols] = load_slope(g, p) * rate

        conv_rows(load, taps, left, right, keep, emit)

        def emit_back(g, p, value):
            d_field[g, p * 16 : p * 16 + 16, cols] = value.astype(BF)

        sums = conv_back_rows(load_slope, load, taps, left, right, keep, emit_back)
        for t in range(9):
            g_kernel[t : t + 1, cols] = jnp.sum(sums[t], axis=0, keepdims=True)
        return 0

    lax.fori_loop(0, CHUNK // 128, lanes, 0)
    hid = hidden[...].reshape(TOK, CHUNK)
    d_fld = d_field[...].reshape(TOK, CHUNK)
    grad = dot(d_shrunk_t[...], hid, 1, 0).astype(BF)
    for q in range(2):
        part = grad[:, q * UC : (q + 1) * UC].reshape(NJ // 2, 2, UR, UC)
        keep_shrink[:, 0, q] = jnp.where(core == 0, part[:, 0], part[:, 1])
        send_shrink[:, 0, q] = jnp.where(core == 0, part[:, 1], part[:, 0])
    share_out(dot(d_fld, second[...].reshape(TOK, D), 0, 0), core, (0, 4), keep_expand, send_expand)
    shrunk[...] += dot(hid, shrink[...], 1, 1).reshape(4, GROUP, D)
    d_second[...] += dot(d_fld, expand[...], 1, 0).reshape(4, GROUP, D)


def packed_half(units):
    return jax.ShapeDtypeStruct((NJ // 2, NK, units, UR, UC), BF)


def feed(tag, second, gradient, mods, packed, kernel):
    half = NJ // 2
    expand_spec = pl.BlockSpec((2, NK, 4, UR, UC), lambda c: (c, 0, 0, 0, 0))
    shrink_spec = pl.BlockSpec((half, 1, 2, UR, UC), lambda c: (0, c // 2, c % 2, 0, 0))
    return pl.pallas_call(
        feed_kernel,
        grid=(FF // CHUNK,),
        in_specs=[
            SMEM_SPEC,
            whole((4, GROUP, D)),
            whole((4, GROUP, D)),
            whole((6, 4, 8, D)),
            pl.BlockSpec((4, NK, 4, UR, UC), lambda c: (c, 0, 0, 0, 0)),
            pl.BlockSpec((NJ, 1, 2, UR, UC), lambda c: (0, c // 2, 2 + c % 2, 0, 0)),
            pl.BlockSpec((9, CHUNK), lambda c: (0, c)),
        ],
        out_specs=[
            whole((4, GROUP, D)),
            whole((4, GROUP, D)),
            expand_spec,
            expand_spec,
            shrink_spec,
            shrink_spec,
            pl.BlockSpec((9, CHUNK), lambda c: (0, c)),
        ],
        out_shape=[
            jax.ShapeDtypeStruct((4, GROUP, D), F32),
            jax.ShapeDtypeStruct((4, GROUP, D), F32),
            packed_half(4),
            packed_half(4),
            packed_half(4),
            packed_half(4),
            jax.ShapeDtypeStruct((9, FF), F32),
        ],
        scratch_shapes=[
            pltpu.VMEM((TOK, D), BF),
            pltpu.VMEM((D, TOK), BF),
            pltpu.VMEM((CHUNK, D), BF),
            pltpu.VMEM((D, CHUNK), BF),
            pltpu.VMEM((4, GROUP, CHUNK), F32),
            pltpu.VMEM((4, GROUP, CHUNK), F32),
            pltpu.VMEM((4, GROUP, CHUNK), BF),
            pltpu.VMEM((4, GROUP, CHUNK), BF),
        ],
        compiler_params=params(60),
        cost_estimate=cost(38),
        name="feed",
    )(tag, second, gradient, mods, packed, packed, kernel)


def attend_back_kernel(
    tag_ref, resid, shrunk, d_second, gradient, attn, mods, qkv, lse, proj_t,
    output, d_resid, d_qkv, d_attn_t, item_sums,
    bias, d_mixed, d_attn, sums,
):
    @pl.when(pl.program_id(0) == 0)
    def _():
        bias[...] = item_bias(tag_ref[0])
        sums[...] = jnp.zeros_like(sums)

    def rows_norm(i, _):
        rows = pl.ds(pl.multiple_of(i * 64, 64), 64)
        half = i // 2
        base = resid[0, rows, :]
        normal, factor = norm_stats(base)
        shrunk_rows = shrunk[0, rows, :]
        outward = gradient[0, rows, :].astype(F32)
        d_sec = d_second[0, rows, :]

        def by_item(value):
            return value.reshape(4, 2, 8, D)

        def add(index, value):
            sums[index, pl.ds(2 * half, 2)] += jnp.sum(by_item(value), axis=0)

        gated = (by_item(shrunk_rows) * quadrant_rows(mods, 5, half)).reshape(64, D)
        output[0, rows, :] = (base + gated).astype(BF)
        add(3, outward * shrunk_rows)
        add(1, d_sec)
        add(2, d_sec * normal)
        inner = (by_item(d_sec) * (1.0 + quadrant_rows(mods, 4, half))).reshape(64, D)
        mean = jnp.mean(inner, axis=-1, keepdims=True)
        along = jnp.mean(inner * normal, axis=-1, keepdims=True)
        back = outward + (inner - mean - normal * along) * factor
        d_resid[0, rows, :] = back
        add(0, back * attn[0, rows, :].astype(F32))
        gated = (by_item(back) * quadrant_rows(mods, 2, half)).reshape(64, D)
        d_attn[rows, :] = gated.astype(BF)
        return 0

    lax.fori_loop(0, 4, rows_norm, 0)
    d_attn_t[...] = d_attn[...].T
    d_mixed[...] = dot(proj_t[...], d_attn[...], 1, 1).astype(BF)

    def head(h, _):
        rows = pl.ds(pl.multiple_of(h * HD, HD), HD)
        key_rows = pl.ds(pl.multiple_of(D + h * HD, HD), HD)
        value_rows = pl.ds(pl.multiple_of(2 * D + h * HD, HD), HD)
        queries = qkv[0, rows, :] * jnp.asarray(HD**-0.5, BF)
        keys = qkv[0, key_rows, :]
        values = qkv[0, value_rows, :]
        d_mix = d_mixed[rows, :]
        probs = jnp.exp(dot(keys, queries, 0, 0) + (bias[...] - lse[0, pl.ds(h, 1), :]))
        d_probs = dot(values, d_mix, 0, 0)
        d_qkv[value_rows, :] = dot(d_mix, probs.astype(BF), 1, 1).astype(BF)
        weighted = probs * d_probs
        inner = jnp.sum(weighted, axis=0, keepdims=True)
        d_scores = (weighted - probs * inner).astype(BF)
        d_qkv[rows, :] = (dot(keys, d_scores, 1, 0) * HD**-0.5).astype(BF)
        d_qkv[key_rows, :] = dot(queries, d_scores, 1, 1).astype(BF)
        return 0

    lax.fori_loop(0, H, head, 0, unroll=HEADS)

    @pl.when(pl.program_id(0) == pl.num_programs(0) - 1)
    def _():
        item_sums[...] = jnp.sum(sums[...], axis=2)


def attend_back(part, tag, resid, shrunk, d_second, gradient, attn, mods, qkv, lse, proj_t):
    first, count = PARTS[part]

    def pick_group(*shape):
        return pl.BlockSpec((1,) + shape, lambda g: (first + g,) + (0,) * len(shape))

    return pl.pallas_call(
        attend_back_kernel,
        grid=(count,),
        in_specs=[
            SMEM_SPEC,
            pick_group(GROUP, D),
            pick_group(GROUP, D),
            pick_group(GROUP, D),
            pick_group(GROUP, D),
            pick_group(GROUP, D),
            whole((6, 4, 8, D)),
            pick_group(3 * D, GROUP),
            pick_group(16, GROUP),
            whole((D, D)),
        ],
        out_specs=[
            group_spec(GROUP, D),
            group_spec(GROUP, D),
            pl.BlockSpec((3 * D, GROUP), lambda g: (0, g)),
            pl.BlockSpec((D, GROUP), lambda g: (0, g)),
            whole((4, 4, D)),
        ],
        out_shape=[
            jax.ShapeDtypeStruct((count, GROUP, D), BF),
            jax.ShapeDtypeStruct((count, GROUP, D), F32),
            jax.ShapeDtypeStruct((3 * D, count * GROUP), BF),
            jax.ShapeDtypeStruct((D, count * GROUP), BF),
            jax.ShapeDtypeStruct((4, 4, D), F32),
        ],
        scratch_shapes=[
            pltpu.VMEM((GROUP, GROUP), F32),
            pltpu.VMEM((D, GROUP), BF),
            pltpu.VMEM((GROUP, D), BF),
            pltpu.VMEM((4, 4, 8, D), F32),
        ],
        compiler_params=params(),
        cost_estimate=cost(9 * count),
        name=f"attend_back_{part}",
    )(tag, resid, shrunk, d_second, gradient, attn, mods, qkv, lse, proj_t)


PAIRS = 2
ROWS = 288 * PAIRS


def project_grads_kernel(
    tag_ref, d_qkv0, d_qkv1, d_attn0, d_attn1, conv_in, merged, keep_a, send_a, keep_b, send_b
):
    core = tag_ref[1]

    def against(low, high, field):
        return dot(low[...], field[0], 1, 0) + dot(
            high[...], field[1:4].reshape(3 * GROUP, D), 1, 0
        )

    grad = against(d_qkv0, d_qkv1, conv_in)
    share_out(grad, core, (0, 2), keep_a, send_a)
    share_out(grad, core, (2, 1), keep_b.at[:, :, 0:1], send_b.at[:, :, 0:1])
    grad = against(d_attn0, d_attn1, merged)
    share_out(grad, core, (0, 1), keep_b.at[:, :, 1:2], send_b.at[:, :, 1:2])


def column_specs(rows):
    return [pl.BlockSpec((rows, count * GROUP), lambda i: (i, 0)) for _, count in PARTS]


def project_grads(tag, d_qkv, d_attn, conv_in, merged):
    packed_spec = pl.BlockSpec((PAIRS, NK, 2, UR, UC), lambda i: (i, 0, 0, 0, 0))
    tall = column_specs(ROWS)
    short = column_specs(96 * PAIRS)
    return pl.pallas_call(
        project_grads_kernel,
        grid=(8 // PAIRS,),
        in_specs=[SMEM_SPEC, *tall, *short, whole((4, GROUP, D)), whole((4, GROUP, D))],
        out_specs=[packed_spec] * 4,
        out_shape=[packed_half(2)] * 4,
        compiler_params=params(),
        cost_estimate=cost(8),
        name="project_grads",
    )(tag, *d_qkv, *d_attn, conv_in, merged)


def conv_back_kernel(
    tag_ref, d_qkv0, d_qkv1, weight, norm, mods, kernel, later0, later1, g_ffn,
    d_first, pieces, d_conv, g_kernel, item_sums,
):
    step = pl.program_id(0)

    @pl.when(step == 0)
    def _():
        d_conv[...] = jnp.zeros_like(d_conv)

    d_conv[0] += dot(d_qkv0[...], weight[...], 0, 0)
    d_conv[1:4] += dot(d_qkv1[...], weight[...], 0, 0).reshape(3, GROUP, D)

    @pl.when(step == pl.num_programs(0) - 1)
    def _():
        tag = tag_ref[0]
        left, right = edge_columns(tag)
        keep = 1.0 - tag.astype(F32)

        def lanes(i, _):
            cols = pl.ds(pl.multiple_of(i * 128, 128), 128)
            taps = [jnp.broadcast_to(kernel[t : t + 1, cols], (16, 128)) for t in range(9)]
            sums = [[jnp.zeros((16, 128), F32) for _ in range(2)] for _ in range(2)]

            def load_grad(g, p):
                return d_conv[g, p * 16 : p * 16 + 16, cols]

            def load_field(g, p):
                q = 2 * (p // 8)
                shift = mods[0, q : q + 2, :, cols].reshape(16, 128)
                scale = mods[1, q : q + 2, :, cols].reshape(16, 128)
                return norm[g, p * 16 : p * 16 + 16, cols] * (1.0 + scale) + shift

            def emit(g, p, value):
                rows = slice(p * 16, p * 16 + 16)
                d_first[g, rows, cols] = value
                sums[0][p // 8] += value
                sums[1][p // 8] += value * norm[g, rows, cols]

            grads = conv_back_rows(load_grad, load_field, taps, left, right, keep, emit)
            for t in range(9):
                g_kernel[t : t + 1, cols] = jnp.sum(grads[t], axis=0, keepdims=True)
            for kind in range(2):
                for item in range(4):
                    part = sums[kind][item // 2][8 * (item % 2) : 8 * (item % 2) + 8]
                    item_sums[kind, item : item + 1, cols] = jnp.sum(part, axis=0, keepdims=True)
            return 0

        lax.fori_loop(0, D // 128, lanes, 0)
        later = later0[...] + later1[...]
        rows = [item_sums[i] for i in range(2)] + [later[i] for i in range(4)]
        rows = jnp.concatenate(rows, axis=1)
        alone = jnp.concatenate([jnp.sum(rows, axis=0, keepdims=True), jnp.zeros((3, 6 * D), F32)])
        rows = jnp.where(tag == 1, rows, alone)
        slots, _, width = pieces.shape
        owners = 6 * D // width
        short, long = D // owners, FF // owners
        for j in range(owners):
            filters = jnp.concatenate(
                [
                    g_kernel[:, j * short : (j + 1) * short],
                    g_ffn[:, j * long : (j + 1) * long],
                    jnp.zeros((9, width - short - long), F32),
                ],
                axis=1,
            )
            part = [rows[:, j * width : (j + 1) * width], filters, jnp.zeros((3, width), F32)]
            part = jnp.concatenate(part, axis=0).astype(BF)
            for copy in range(slots // owners):
                pieces[j * (slots // owners) + copy] = part


def conv_back(slots, width, tag, d_qkv, weight, norm, mods, kernel, later, g_ffn):
    return pl.pallas_call(
        conv_back_kernel,
        grid=(8 // PAIRS,),
        in_specs=[
            SMEM_SPEC,
            *column_specs(ROWS),
            pl.BlockSpec((ROWS, D), lambda i: (i, 0)),
            whole((4, GROUP, D)),
            whole((6, 4, 8, D)),
            whole((9, D)),
            whole((4, 4, D)),
            whole((4, 4, D)),
            whole((9, FF)),
        ],
        out_specs=[whole((4, GROUP, D)), whole((slots, 16, width))],
        out_shape=[
            jax.ShapeDtypeStruct((4, GROUP, D), F32),
            jax.ShapeDtypeStruct((slots, 16, width), BF),
        ],
        scratch_shapes=[
            pltpu.VMEM((4, GROUP, D), F32),
            pltpu.VMEM((9, D), F32),
            pltpu.VMEM((2, 4, D), F32),
        ],
        compiler_params=params(),
        cost_estimate=cost(15),
        name="conv_back",
    )(tag, *d_qkv, weight, norm, mods, kernel, *later, g_ffn)


def finish_kernel(
    d_first, norm, factor, d_resid0, d_resid1, output0, output1, mods,
    block_output, input_grad, total,
):
    half = pl.program_id(0) // 2

    for g in range(4):
        base = d_resid1[g - 1] if g else d_resid0[0]
        value = d_first[g]
        normal = norm[g]
        inner = (value.reshape(4, 2, 8, D) * (1.0 + quadrant_rows(mods, 1, half))).reshape(64, D)
        mean = jnp.mean(inner, axis=-1, keepdims=True)
        along = jnp.mean(inner * normal, axis=-1, keepdims=True)
        total[g] = base + (inner - mean - normal * along) * factor[g]
    order = ungroup_matrix()
    grouped = total[...].reshape(256, D)
    high = grouped.astype(BF)
    rest = (grouped - high.astype(F32)).astype(BF)
    input_grad[...] = dot(order, high, 1, 0) + dot(order, rest, 1, 0)
    grouped = jnp.concatenate([output0[...], output1[...]], axis=0).reshape(256, D)
    block_output[...] = dot(order, grouped, 1, 0).astype(BF)


def finish(d_first, norm, factor, d_resid, output, mods):
    def split(groups, width):
        return pl.BlockSpec((groups, 64, width), lambda i: (0, i, 0))

    flat = pl.BlockSpec((256, D), lambda i: (i, 0))
    return pl.pallas_call(
        finish_kernel,
        grid=(4,),
        in_specs=[split(4, D), split(4, D), split(4, 1)]
        + [split(count, D) for _, count in PARTS] * 2
        + [whole((6, 4, 8, D))],
        out_specs=[flat, flat],
        out_shape=[
            jax.ShapeDtypeStruct((TOK, D), BF),
            jax.ShapeDtypeStruct((TOK, D), F32),
        ],
        scratch_shapes=[pltpu.VMEM((4, 64, D), F32)],
        compiler_params=params(),
        cost_estimate=cost(8),
        name="finish",
    )(d_first, norm, factor, *d_resid, *output, mods)


BOTH = ("dp", "fsdp")


def exchange(pieces):
    return lax.all_to_all(pieces, BOTH, 0, 0, tiled=True)


def units_of(weight):
    return weight.T.reshape(-1, UR, UC)


def low_units(shrink):
    return shrink.T.reshape(UR, 4, UC).transpose(1, 0, 2)


def gather_feed(nd, nf, expand, shrink):
    if (nd, nf) == (NJ, NK):
        rows = jnp.concatenate([units_of(expand), low_units(shrink)]).reshape(8 * UR, UC)
        return lax.all_gather(rows, BOTH).reshape(NJ, NK, 8, UR, UC)
    low = full_rows(shrink).reshape(NJ, UR, NK, 4, UC).transpose(0, 2, 3, 1, 4)
    return jnp.concatenate([all_units(full_rows(expand), 4), low], axis=2)


def full_rows(shard):
    rows = lax.all_gather(shard.T, "fsdp", axis=1, tiled=True)
    return lax.all_gather(rows, "dp", axis=0, tiled=True)


def all_units(weight, units):
    return weight.reshape(NJ, units, UR, NK, UC).transpose(0, 3, 1, 2, 4)


def project_turns(own):
    turns = [
        lax.ppermute(own, "dp", [(i, (i - 4 * step) % NJ) for i in range(NJ)])
        for step in range(1, 4)
    ]
    return turns


def widen(a, b, bit_a, bit_b):
    return jnp.stack([a, swap(a, bit_a)]), jnp.stack([b, swap(b, bit_b)])


def all_projections(qkv, proj):
    units = jnp.concatenate([all_units(full_rows(qkv), 3), all_units(full_rows(proj), 1)], axis=2)
    units = units.reshape((4, 2, 2) + units.shape[1:])
    first, rest = units[:, :, :, :, :2], units[:, :, :, :, 2:]
    a, b = first.transpose(2, 3, 1, 0, 4, 5, 6), rest.transpose(2, 1, 3, 0, 4, 5, 6)
    return a[0], b[0], a[1], b[1]


def pick(grads, index, axis):
    return lax.dynamic_index_in_dim(grads, index, axis, keepdims=False)


def swap(value, bit):
    if bit is None:
        return lax.ppermute(value, "fsdp", [(0, 1), (1, 0)])
    return lax.ppermute(value, "dp", [(i, i ^ bit) for i in range(NJ)])


def halve(keep, got, axis, bit):
    mine = lax.axis_index("fsdp") if bit is None else (lax.axis_index("dp") // bit) % 2
    kept = pick(keep, mine, axis) + pick(got, mine, axis)
    return kept, pick(keep, 1 - mine, axis) + pick(got, 1 - mine, axis)


def last_sends(total):
    place = lax.axis_index("dp") // 4
    return [pick(total, (place + step) % 4, 0) for step in range(1, 4)]


def last_swaps(sends):
    return [
        lax.ppermute(sent, "dp", [(i, (i + 4 * step) % NJ) for i in range(NJ)])
        for step, sent in enumerate(sends, 1)
    ]


def last_sum(total, got):
    own = pick(total, lax.axis_index("dp") // 4, 0).astype(F32)
    for value in got:
        own = own + value.astype(F32)
    return own


def after(value, *others):
    return lax.optimization_barrier((value,) + others)[0]


def own_shard(nd, nf, kind, units):
    if (nd, nf) == (NJ, NK):
        if kind == "shrink":
            return units.transpose(1, 0, 2).reshape(UR, 4 * UC).T
        return units.reshape(-1, UC).T
    if kind == "shrink":
        weight = units.transpose(0, 3, 1, 2, 4).reshape(NJ * UR, -1)
    else:
        weight = units.transpose(0, 2, 3, 1, 4).reshape(-1, NK * UC)
    columns = lax.psum_scatter(weight, "dp", scatter_dimension=0, tiled=True)
    piece = lax.psum_scatter(columns, "fsdp", scatter_dimension=1, tiled=True)
    return piece.astype(F32).T


def both_cores(keep, send):
    return jnp.stack([keep, send], axis=1).reshape((-1,) + keep.shape[1:])


def look_up(ids, step_table, class_table):
    first_row = lax.axis_index("fsdp") * step_table.shape[0]
    own = first_row + jnp.arange(step_table.shape[0], dtype=jnp.int32)
    step_hot = (ids[:, :4].reshape(-1, 1) == own[None, :]).astype(BF)
    class_hot = (ids[:, 4:].reshape(-1, 1) == own[None, :]).astype(BF)
    return step_hot, class_hot, dot(step_table, step_hot, 0, 1) + dot(class_table, class_hot, 0, 1)


def share_act(nd, cond, attn_kernel, ffn_kernel):
    width, items = cond.shape
    act = jax.nn.silu(cond).astype(BF)
    filters = jnp.concatenate([attn_kernel, ffn_kernel], axis=1).reshape(-1)
    size = filters.shape[0]
    filters = jnp.pad(filters, (0, -size % items)).reshape(-1, items)
    sent = jnp.concatenate([act, filters], axis=0)[None]
    sent = lax.all_to_all(jnp.broadcast_to(sent, (nd,) + sent.shape[1:]), "dp", 0, 0, tiled=True)
    act_all = sent[:, :width].reshape(nd * width, items)
    filters = sent[:, width:].reshape(nd, -1)[:, :size]
    filters = filters.reshape(nd, 9, -1).astype(F32)
    attn_full = filters[:, :, : attn_kernel.shape[1]].transpose(1, 0, 2).reshape(9, -1)
    ffn_full = filters[:, :, attn_kernel.shape[1] :].transpose(1, 0, 2).reshape(9, -1)
    return act_all, attn_full, ffn_full


def exchange_columns(nd, nf, d_act):
    rows, items = d_act.shape
    if (nd, nf) == (NJ, NK):
        return lax.all_to_all(d_act.reshape(nd, rows // nd, items), "dp", 0, 0, tiled=True)
    spread = lax.dynamic_update_slice_in_dim(
        jnp.zeros((rows * nf, items), F32), d_act, lax.axis_index("fsdp") * rows, axis=0
    )
    spread = spread.reshape(nd, 1, -1, items)
    spread = jnp.broadcast_to(spread, (nd, nf) + spread.shape[2:])
    return exchange(spread.reshape((nd * nf,) + spread.shape[2:]))


def own_columns(nd, nf, terms):
    part = terms.sum(axis=0)
    if (nd, nf) != (NJ, NK):
        return part
    order = [(j * NK + k, k * NJ + j) for j in range(NJ) for k in range(NK)]
    own = lax.ppermute(part, BOTH, order)
    other = lax.ppermute(part, BOTH, [(i, o ^ 1) for i, o in order])
    first = lax.axis_index("fsdp") == 0
    return jnp.concatenate([jnp.where(first, own, other), jnp.where(first, other, own)])


def body(
    latents, size_tags, timesteps, classes, step_table, class_table, modulation_weight,
    attn_kernel, qkv_weight, proj_weight, expand_weight, ffn_kernel, shrink_weight, cotangent,
    *, nd, nf,
):
    slots = nd * nf
    tag = size_tags[0]
    square = (nd, nf) == (NJ, NK)
    if square:
        place = lax.axis_index("dp")
        where = [tag, place % 2, place // 4, (place // 2) % 2, lax.axis_index("fsdp")]
        where = jnp.stack(where).astype(jnp.int32)
    else:
        where = jnp.stack([tag] + [jnp.int32(0)] * 4)
    packed = gather_feed(nd, nf, expand_weight, shrink_weight)
    tokens, gradient, norm, factor = prepare(latents, cotangent)
    mine = jnp.concatenate([timesteps[0], classes[0]])[None]
    mine = jnp.broadcast_to(mine, (slots, 8))
    if square:
        own = jnp.concatenate([units_of(qkv_weight), units_of(proj_weight)])
        own = after(own, mine)
        turns = project_turns(own)
    ids = exchange(mine)
    if square:
        ids = after(ids, norm)
    step_hot, class_hot, part = look_up(ids, step_table, class_table)
    if square:
        cond = part + swap(part, None)
        a = jnp.stack([own[:2]] + [turn[:2] for turn in turns])
        b = jnp.stack([own[2:]] + [turn[2:] for turn in turns])
        a, b = widen(a, b, 2, None)
        cond = after(cond, a, b)
        next_a, next_b = swap(a, None), swap(b, 2)
    else:
        cond = lax.psum(part, "fsdp")
    act_all, attn_full, ffn_full = share_act(nd, cond, attn_kernel, ffn_kernel)
    if square:
        next_a, next_b = after(next_a, act_all), after(next_b, act_all)
    height, width = modulation_weight.shape
    act_rows = lax.dynamic_slice_in_dim(
        act_all, lax.axis_index("fsdp") * height, height, axis=0
    )
    terms = dot(act_rows, modulation_weight, 0, 0)
    terms = exchange(terms.reshape(slots, 1, 4 * width)).reshape(nd, nf, 4, width)
    if square:
        a, b = jnp.stack([a, next_a]), jnp.stack([b, next_b])
        projections = (a, b, swap(a, 1), swap(b, 1))
    else:
        projections = all_projections(qkv_weight, proj_weight)
    mod_rows = terms.sum(axis=1).transpose(1, 0, 2).reshape(4, nd * width)
    chosen = jnp.where(tag == 1, mod_rows, mod_rows[:1])
    mods = jnp.broadcast_to(chosen.reshape(4, 6, 1, D).transpose(1, 0, 2, 3), (6, 4, 8, D))

    conv_in = first_conv(size_tags, norm, mods, attn_full)
    qkv, merged, attn, resid, second, lse, proj_t, full_qkv = attend(
        where, conv_in, tokens, mods, projections
    )
    shrunk, d_second, keep_e, send_e, keep_s, send_s, g_ffn = feed(
        where, second, gradient, mods, packed, ffn_full
    )
    back = (gradient, attn, mods, qkv, lse)
    if square:
        got_e, got_s = swap(send_e, 1), swap(send_s, 1)
    output0, d_resid0, d_qkv0, d_attn0, later0 = attend_back(
        0, where, resid, shrunk, d_second, *back, proj_t
    )

    def grid(value):
        return value.reshape((4, 2) + value.shape[1:])

    if square:
        got_e, got_s = after(got_e, d_qkv0), after(got_s, d_qkv0)
        keep_e, out_e = halve(grid(keep_e), grid(got_e), 2, None)
        keep_s, out_s = halve(grid(keep_s), grid(got_s), 1, 2)
        d_second = after(d_second, out_e, out_s)
        got_e, got_s = swap(out_e, None), swap(out_s, 2)
    output1, d_resid1, d_qkv1, d_attn1, later1 = attend_back(
        1, where, resid, shrunk, d_second, *back, proj_t
    )
    if square:
        got_e, got_s = after(got_e, d_attn1), after(got_s, d_attn1)
        keep_e, out_e = halve(keep_e, got_e, 1, 2)
        keep_s, out_s = halve(keep_s, got_s, 1, None)
        d_attn0 = after(d_attn0, out_e, out_s)
        got_e, got_s = swap(out_e, 2), swap(out_s, None)
    d_qkv = (d_qkv0, d_qkv1)
    keep_a, send_a, keep_b, send_b = project_grads(
        where, d_qkv, (d_attn0, d_attn1), conv_in, merged
    )
    if square:
        got_e, got_s = after(got_e, keep_a), after(got_s, keep_a)
        got_a, got_b = swap(send_a, 1), swap(send_b, 1)
        e = halve(keep_e.reshape((2, 2) + keep_e.shape[1:]), got_e.reshape((2, 2) + got_e.shape[1:]), 1, 4)
        s = halve(keep_s.reshape((2, 2) + keep_s.shape[1:]), got_s.reshape((2, 2) + got_s.shape[1:]), 1, 4)
        feeding, out_f = (jnp.concatenate(pair, axis=1) for pair in zip(e, s))
        keep_a, out_a = halve(grid(keep_a), grid(got_a), 2, None)
        keep_b, out_b = halve(grid(keep_b), grid(got_b), 1, 2)
        full_qkv = after(full_qkv, out_a, out_b, out_f)
        got_a, got_b, got_f = swap(out_a, None), swap(out_b, 2), swap(out_f, 4)
    d_first, pieces = conv_back(
        slots, width, where, d_qkv, full_qkv, norm, mods, attn_full, (later0, later1), g_ffn
    )
    if square:
        got_a, got_b, got_f = (after(x, d_first) for x in (got_a, got_b, got_f))
        keep_a, out_a = halve(keep_a, got_a, 1, 2)
        keep_b, out_b = halve(keep_b, got_b, 1, None)
        feeding, out_f = halve(feeding, got_f, 0, 8)
    if square:
        d_first = after(d_first, out_a, out_b, out_f, pieces)
        got_a, got_b, got_f = swap(out_a, 2), swap(out_b, None), swap(out_f, 8)
    got = exchange(pieces)
    block_output, input_grad = finish(
        d_first, norm, factor, (d_resid0, d_resid1), (output0, output1), mods
    )
    if square:
        got = after(got, input_grad)
    d_mod_all = got[:, :4].reshape(slots * 4, width)
    d_act = dot(modulation_weight, d_mod_all, 1, 1)
    if square:
        got_a, got_b = after(got_a, d_act), after(got_b, d_act)
        total = jnp.concatenate([keep_a + got_a, keep_b + got_b], axis=1)
        sends = last_sends(total)
        last = last_swaps(sends)
    own_act = exchange_columns(nd, nf, d_act)
    if square:
        got_f = after(got_f, own_act)
        total = last_sum(total, last)
        feeding = feeding.astype(F32) + got_f.astype(F32)
        cuts = [total[:3], total[3:], feeding[:4], feeding[4:]]
    else:
        first, rest = both_cores(keep_a, send_a), both_cores(keep_b, send_b)
        cuts = [
            jnp.concatenate([first, rest[:, :, :1]], axis=2),
            rest[:, :, 1:],
            both_cores(keep_e, send_e),
            both_cores(keep_s, send_s),
        ]
    shards = [
        own_shard(nd, nf, kind, cut)
        for kind, cut in zip(("qkv", "proj", "expand", "shrink"), cuts)
    ]
    cut = attn_kernel.shape[1]
    filters = got[:, 4:13, : cut + ffn_kernel.shape[1]].astype(F32).sum(axis=0)
    modulation_grad = dot(act_rows, d_mod_all, 1, 0)
    gate = jax.nn.sigmoid(cond)
    d_cond = own_columns(nd, nf, own_act)
    d_cond = d_cond * (gate * (1.0 + cond * (1.0 - gate)))

    def table_grad(hot):
        return lax.dot_general(
            hot.astype(F32), d_cond, (((0,), (1,)), ((), ())), precision=lax.Precision.HIGHEST
        )

    return (
        block_output,
        input_grad,
        table_grad(step_hot),
        table_grad(class_hot),
        modulation_grad,
        filters[:, :cut],
        shards[0],
        shards[1],
        shards[2],
        filters[:, cut:],
        shards[3],
    )


def solution(mesh):
    matrix = P("fsdp", "dp")
    rows = P(BOTH, None)
    filters = P(None, "dp")
    in_specs = (
        rows, P(BOTH), rows, rows, matrix, matrix, matrix, filters, matrix, matrix, matrix,
        filters, matrix, rows,
    )
    out_specs = (
        rows, rows, matrix, matrix, matrix, filters, matrix, matrix, matrix, filters, matrix,
    )
    run = functools.partial(body, nd=mesh.shape["dp"], nf=mesh.shape["fsdp"])
    return jax.shard_map(run, mesh=mesh, in_specs=in_specs, out_specs=out_specs, check_vma=False)
```

```python
import functools

import jax
import jax.numpy as jnp
from jax import lax
from jax.experimental import pallas as pl
from jax.experimental.pallas import tpu as pltpu
from jax.sharding import PartitionSpec as P

D = 768
H = 12
HD = 64
FF = 3072
SIDE = 32
GROUP = 256
TOK = SIDE * SIDE
EPS = 1e-06
NJ, NK, UR, UC = 16, 2, 48, 384
CHUNK = 768
HEADS = 6
PARTS = ((0, 1), (1, 3))
MIB = 1024 * 1024
BF = jnp.bfloat16
F32 = jnp.float32
GELU_A = 0.7978845608028654
GELU_B = GELU_A * 0.044715


def dot(left, right, left_dim, right_dim):
    return lax.dot_general(
        left, right, (((left_dim,), (right_dim,)), ((), ())), preferred_element_type=F32
    )


def params(limit=56):
    return pltpu.CompilerParams(vmem_limit_bytes=limit * MIB)


def cost(micros):
    return pl.CostEstimate(flops=int(micros * 1e8), transcendentals=0, bytes_accessed=4 * MIB)


def whole(shape):
    zeros = (0,) * len(shape)
    return pl.BlockSpec(shape, lambda *ids: zeros, pipeline_mode=pl.Buffered(1))


SMEM_SPEC = pl.BlockSpec(memory_space=pltpu.SMEM)


def group_place(natural):
    pair, odd_row = natural // 64, (natural // 32) % 2
    column, odd_column = (natural % 32) // 2, natural % 2
    return (2 * odd_row + odd_column) * 64 + pair * 16 + column


def ungroup_matrix():
    natural = lax.broadcasted_iota(jnp.int32, (256, 256), 0)
    grouped = lax.broadcasted_iota(jnp.int32, (256, 256), 1)
    return jnp.where(group_place(natural) == grouped, 1.0, 0.0).astype(BF)


def group_matrix():
    natural = lax.broadcasted_iota(jnp.int32, (256, 256), 1)
    grouped = lax.broadcasted_iota(jnp.int32, (256, 256), 0)
    return jnp.where(group_place(natural) == grouped, 1.0, 0.0).astype(BF)


def norm_stats(values):
    centre = values - jnp.mean(values, axis=-1, keepdims=True)
    variance = jnp.mean(centre * centre, axis=-1, keepdims=True)
    scale = lax.rsqrt(variance + EPS)
    return centre * scale, scale


def prepare_kernel(latents, cotangent, tokens, gradient, norm, scale):
    order = group_matrix()
    gathered = dot(order, latents[...], 1, 0)
    gradient[...] = dot(order, cotangent[...], 1, 0).reshape(4, 64, D).astype(BF)
    tokens[...] = gathered.reshape(4, 64, D).astype(BF)
    normal, factor = norm_stats(gathered)
    norm[...] = normal.reshape(4, 64, D)
    scale[...] = factor.reshape(4, 64, 1)


def prepare(latents, cotangent):
    flat = pl.BlockSpec((256, D), lambda i: (i, 0))
    split = pl.BlockSpec((4, 64, D), lambda i: (0, i, 0))
    return pl.pallas_call(
        prepare_kernel,
        grid=(4,),
        in_specs=[flat, flat],
        out_specs=[split, split, split, pl.BlockSpec((4, 64, 1), lambda i: (0, i, 0))],
        out_shape=[
            jax.ShapeDtypeStruct((4, GROUP, D), BF),
            jax.ShapeDtypeStruct((4, GROUP, D), BF),
            jax.ShapeDtypeStruct((4, GROUP, D), F32),
            jax.ShapeDtypeStruct((4, GROUP, 1), F32),
        ],
        compiler_params=params(),
        cost_estimate=cost(6),
        name="prepare",
    )(latents, cotangent)


def edge_columns(tag):
    place = lax.broadcasted_iota(jnp.int32, (16, 128), 0)
    left = jnp.where((place == 0) | ((place == 8) & (tag == 1)), 0.0, 1.0)
    right = jnp.where((place == 15) | ((place == 7) & (tag == 1)), 0.0, 1.0)
    return left, right


def neighbours(even, odd, left, right):
    return pltpu.roll(odd, 1, 0) * left, pltpu.roll(even, 15, 0) * right


def conv_rows(load, kernel, left, right, keep, emit):
    above = None
    partial = None
    for row in range(SIDE + 1):
        taps = None
        if row < SIDE:
            a, p = row % 2, row // 2
            even, odd = load(2 * a, p), load(2 * a + 1, p)
            odd_left, even_right = neighbours(even, odd, left, right)
            taps = []
            for tap in range(3):
                k = [kernel[3 * tap + b] for b in range(3)]
                taps.append(
                    (
                        k[0] * odd_left + k[1] * even + k[2] * odd,
                        k[0] * even + k[1] * odd + k[2] * even_right,
                    )
                )
        crossing = row == SIDE // 2
        if partial is not None:
            a, p = (row - 1) % 2, (row - 1) // 2
            for b in range(2):
                value = partial[b]
                if taps is not None:
                    below = taps[2][b]
                    value = value + (below * keep if crossing else below)
                emit(2 * a + b, p, value)
        if taps is not None:
            partial = []
            for b in range(2):
                value = taps[1][b]
                if above is not None:
                    value = value + (above[b] * keep if crossing else above[b])
                partial.append(value)
            above = taps[0]


def conv_back_rows(load_grad, load_field, kernel, left, right, keep, emit):
    sums = [jnp.zeros((16, 128), F32) for _ in range(9)]
    from_above = None
    partial = None
    field_above = None
    field = (load_field(0, 0), load_field(1, 0))
    for row in range(SIDE + 1):
        crossing = row == SIDE // 2
        taps = None
        if row < SIDE:
            a, p = row % 2, row // 2
            even, odd = load_grad(2 * a, p), load_grad(2 * a + 1, p)
            odd_left, even_right = neighbours(even, odd, left, right)
            picks = ((odd, even, odd_left), (even_right, odd, even))
            taps = []
            for tap in range(3):
                k = [kernel[3 * tap + b] for b in range(3)]
                taps.append(
                    tuple(k[0] * x[0] + k[1] * x[1] + k[2] * x[2] for x in picks)
                )
            field_below = None
            if row + 1 < SIDE:
                a, p = (row + 1) % 2, (row + 1) // 2
                field_below = (load_field(2 * a, p), load_field(2 * a + 1, p))
            for tap, rows in enumerate((field_above, field, field_below)):
                if rows is None:
                    continue
                if (tap == 0 and crossing) or (tap == 2 and row + 1 == SIDE // 2):
                    rows = (rows[0] * keep, rows[1] * keep)
                for b in range(3):
                    sums[3 * tap + b] = (
                        sums[3 * tap + b] + rows[0] * picks[0][b] + rows[1] * picks[1][b]
                    )
            field_above, field = field, field_below
        if partial is not None:
            a, p = (row - 1) % 2, (row - 1) // 2
            for b in range(2):
                value = partial[b]
                if taps is not None:
                    value = value + (taps[0][b] * keep if crossing else taps[0][b])
                emit(2 * a + b, p, value)
        if taps is not None:
            partial = []
            for b in range(2):
                value = taps[1][b]
                if from_above is not None:
                    value = value + (from_above[b] * keep if crossing else from_above[b])
                partial.append(value)
            from_above = taps[2]
    return sums


def first_conv_kernel(tag_ref, norm, mods, kernel, out):
    tag = tag_ref[0]
    left, right = edge_columns(tag)
    keep = 1.0 - tag.astype(F32)
    taps = [jnp.broadcast_to(kernel[i : i + 1, :], (16, 128)) for i in range(9)]

    def load(g, p):
        q = 2 * (p // 8)
        shift = mods[0, q : q + 2].reshape(16, 128)
        scale = mods[1, q : q + 2].reshape(16, 128)
        return norm[g, p * 16 : p * 16 + 16, :] * (1.0 + scale) + shift

    def emit(g, p, value):
        out[g, p * 16 : p * 16 + 16, :] = value.astype(BF)

    conv_rows(load, taps, left, right, keep, emit)


def first_conv(tag, norm, mods, kernel):
    return pl.pallas_call(
        first_conv_kernel,
        grid=(D // 128,),
        in_specs=[
            SMEM_SPEC,
            pl.BlockSpec((4, GROUP, 128), lambda i: (0, 0, i)),
            pl.BlockSpec((6, 4, 8, 128), lambda i: (0, 0, 0, i)),
            pl.BlockSpec((9, 128), lambda i: (0, i)),
        ],
        out_specs=pl.BlockSpec((4, GROUP, 128), lambda i: (0, 0, i)),
        out_shape=jax.ShapeDtypeStruct((4, GROUP, D), BF),
        compiler_params=params(),
        cost_estimate=cost(6),
        name="first_conv",
    )(tag, norm, mods, kernel)


def join_rows(block, target):
    rows = block.shape[0] * block.shape[2] * UR
    for k in range(NK):
        target[:, k * UC : (k + 1) * UC] = block[:, k].reshape(rows, UC)


def share_out(rows, core, units, keep, send):
    first, count = units
    for k in range(NK):
        part = rows[:, k * UC : (k + 1) * UC].astype(BF)
        part = part.reshape(-1, 2, part.shape[0] // (keep.shape[0] * 2), UC)
        even, odd = part[:, 0], part[:, 1]
        for target, value in (
            (keep, jnp.where(core == 0, even, odd)),
            (send, jnp.where(core == 0, odd, even)),
        ):
            whole_units = value.reshape(value.shape[0], -1, UR, UC)
            target[:, k] = whole_units[:, first : first + count]


def quadrant_rows(mods, index, half):
    return mods[index, pl.ds(2 * half, 2)].reshape(1, 2, 8, D)


def item_bias(tag):
    def label(dim):
        place = lax.broadcasted_iota(jnp.int32, (GROUP, GROUP), dim)
        return 2 * (place // 128) + (place % 16) // 8

    return jnp.where((label(0) == label(1)) | (tag == 0), 0.0, -1e30)


def attend_kernel(
    where, conv_in, tokens, mods, own_a, own_b, peer_a, peer_b,
    qkv, merged, attn, resid, second, lse, proj_t, full_qkv,
    full_proj, bias, mixed_t,
):
    @pl.when(pl.program_id(0) == 0)
    def _():
        core, z, y, x = (where[i] for i in range(1, 5))
        for owner in range(NJ):
            step = (owner // 4 - z + 4) % 4
            side = (owner // 2) % 2 ^ y
            mine = core == owner % 2
            for k in range(NK):
                cols = slice(k * UC, (k + 1) * UC)
                a = jnp.where(mine, own_a[k ^ x, side, step], peer_a[k ^ x, side, step])
                b = jnp.where(mine, own_b[side, k ^ x, step], peer_b[side, k ^ x, step])
                start = owner * 3 * UR
                full_qkv[start : start + 2 * UR, cols] = a.reshape(2 * UR, UC)
                full_qkv[start + 2 * UR : start + 3 * UR, cols] = b[0]
                full_proj[owner * UR : (owner + 1) * UR, cols] = b[1]
        proj_t[...] = full_proj[...].T
        bias[...] = item_bias(where[0])

    qkv[0] = dot(full_qkv[...], conv_in[0], 1, 1).astype(BF)

    def head(h, _):
        rows = pl.ds(pl.multiple_of(h * HD, HD), HD)
        queries = qkv[0, rows, :] * jnp.asarray(HD**-0.5, BF)
        keys = qkv[0, pl.ds(pl.multiple_of(D + h * HD, HD), HD), :]
        values = qkv[0, pl.ds(pl.multiple_of(2 * D + h * HD, HD), HD), :]
        scores = dot(keys, queries, 0, 0) + bias[...]
        highest = jnp.max(scores, axis=0, keepdims=True)
        raised = jnp.exp(scores - highest)
        total = jnp.sum(raised, axis=0, keepdims=True)
        probs = (raised * (1.0 / total)).astype(BF)
        lse[0, pl.ds(h, 1), :] = highest + jnp.log(total)
        mixed_t[rows, :] = dot(values, probs, 1, 0).astype(BF)
        return 0

    lax.fori_loop(0, H, head, 0, unroll=HEADS)
    merged[0] = mixed_t[...].T
    projected = dot(merged[0], full_proj[...], 1, 1)
    attn[0] = projected.astype(BF)
    gate = mods[2].reshape(2, 1, 2, 8, D)
    resid[0] = (
        tokens[0].astype(F32) + (projected.reshape(2, 8, 2, 8, D) * gate).reshape(GROUP, D)
    )

    def rows_norm(i, _):
        rows = pl.ds(pl.multiple_of(i * 64, 64), 64)
        normal, _ = norm_stats(resid[0, rows, :])
        half = i // 2
        scaled = normal.reshape(4, 2, 8, D) * (1.0 + quadrant_rows(mods, 4, half))
        value = scaled + quadrant_rows(mods, 3, half)
        second[0, rows, :] = value.reshape(64, D).astype(BF)
        return 0

    lax.fori_loop(0, 4, rows_norm, 0)


def group_spec(*shape):
    return pl.BlockSpec((1,) + shape, lambda g: (g,) + (0,) * len(shape))


def attend(where, conv_in, tokens, mods, projections):
    relative = (2, 2, 4, 2, UR, UC)
    return pl.pallas_call(
        attend_kernel,
        grid=(4,),
        in_specs=[
            SMEM_SPEC,
            group_spec(GROUP, D),
            group_spec(GROUP, D),
            whole((6, 4, 8, D)),
        ]
        + [whole(relative)] * 4,
        out_specs=[
            group_spec(3 * D, GROUP),
            group_spec(GROUP, D),
            group_spec(GROUP, D),
            group_spec(GROUP, D),
            group_spec(GROUP, D),
            group_spec(16, GROUP),
            whole((D, D)),
            whole((3 * D, D)),
        ],
        out_shape=[
            jax.ShapeDtypeStruct((4, 3 * D, GROUP), BF),
            jax.ShapeDtypeStruct((4, GROUP, D), BF),
            jax.ShapeDtypeStruct((4, GROUP, D), BF),
            jax.ShapeDtypeStruct((4, GROUP, D), F32),
            jax.ShapeDtypeStruct((4, GROUP, D), BF),
            jax.ShapeDtypeStruct((4, 16, GROUP), F32),
            jax.ShapeDtypeStruct((D, D), BF),
            jax.ShapeDtypeStruct((3 * D, D), BF),
        ],
        scratch_shapes=[
            pltpu.VMEM((D, D), BF),
            pltpu.VMEM((GROUP, GROUP), F32),
            pltpu.VMEM((D, GROUP), BF),
        ],
        compiler_params=params(),
        cost_estimate=cost(38),
        name="attend",
    )(where, conv_in, tokens, mods, *projections)


def feed_kernel(
    tag_ref, second, gradient, mods, w_expand, w_shrink, kernel,
    shrunk, d_second, keep_expand, send_expand, keep_shrink, send_shrink, g_kernel,
    d_shrunk, d_shrunk_t, expand, shrink, field, slope, hidden, d_field,
):
    step = pl.program_id(0)
    tag, core = tag_ref[0], tag_ref[1]

    @pl.when(step == 0)
    def _():
        gate = mods[5].reshape(1, 2, 1, 2, 8, D)
        value = gradient[...].astype(F32).reshape(4, 2, 8, 2, 8, D) * gate
        d_shrunk[...] = value.reshape(TOK, D).astype(BF)
        d_shrunk_t[...] = d_shrunk[...].T
        shrunk[...] = jnp.zeros_like(shrunk)
        d_second[...] = jnp.zeros_like(d_second)

    join_rows(w_expand, expand)
    for q in range(2):
        shrink[:, q * UC : (q + 1) * UC] = w_shrink[:, 0, q].reshape(D, UC)
    left, right = edge_columns(tag)
    keep = 1.0 - tag.astype(F32)
    field[...] = dot(second[...].reshape(TOK, D), expand[...], 1, 1).reshape(4, GROUP, CHUNK)
    slope[...] = dot(d_shrunk[...], shrink[...], 1, 0).reshape(4, GROUP, CHUNK)

    def lanes(i, _):
        cols = pl.ds(pl.multiple_of(i * 128, 128), 128)
        taps = [jnp.broadcast_to(kernel[t : t + 1, cols], (16, 128)) for t in range(9)]

        def load(g, p):
            return field[g, p * 16 : p * 16 + 16, cols]

        def load_slope(g, p):
            return slope[g, p * 16 : p * 16 + 16, cols]

        def emit(g, p, value):
            square = value * value
            half = 0.5 + 0.5 * jnp.tanh(value * (GELU_A + GELU_B * square))
            out = value * half
            hidden[g, p * 16 : p * 16 + 16, cols] = out.astype(BF)
            rate = half + (out - out * half) * (2.0 * GELU_A + 6.0 * GELU_B * square)
            slope[g, p * 16 : p * 16 + 16, cols] = load_slope(g, p) * rate

        conv_rows(load, taps, left, right, keep, emit)

        def emit_back(g, p, value):
            d_field[g, p * 16 : p * 16 + 16, cols] = value.astype(BF)

        sums = conv_back_rows(load_slope, load, taps, left, right, keep, emit_back)
        for t in range(9):
            g_kernel[t : t + 1, cols] = jnp.sum(sums[t], axis=0, keepdims=True)
        return 0

    lax.fori_loop(0, CHUNK // 128, lanes, 0)
    hid = hidden[...].reshape(TOK, CHUNK)
    d_fld = d_field[...].reshape(TOK, CHUNK)
    grad = dot(d_shrunk_t[...], hid, 1, 0).astype(BF)
    for q in range(2):
        part = grad[:, q * UC : (q + 1) * UC].reshape(NJ // 2, 2, UR, UC)
        keep_shrink[:, 0, q] = jnp.where(core == 0, part[:, 0], part[:, 1])
        send_shrink[:, 0, q] = jnp.where(core == 0, part[:, 1], part[:, 0])
    share_out(dot(d_fld, second[...].reshape(TOK, D), 0, 0), core, (0, 4), keep_expand, send_expand)
    shrunk[...] += dot(hid, shrink[...], 1, 1).reshape(4, GROUP, D)
    d_second[...] += dot(d_fld, expand[...], 1, 0).reshape(4, GROUP, D)


def packed_half(units):
    return jax.ShapeDtypeStruct((NJ // 2, NK, units, UR, UC), BF)


def feed(tag, second, gradient, mods, packed, kernel):
    half = NJ // 2
    expand_spec = pl.BlockSpec((2, NK, 4, UR, UC), lambda c: (c, 0, 0, 0, 0))
    shrink_spec = pl.BlockSpec((half, 1, 2, UR, UC), lambda c: (0, c // 2, c % 2, 0, 0))
    return pl.pallas_call(
        feed_kernel,
        grid=(FF // CHUNK,),
        in_specs=[
            SMEM_SPEC,
            whole((4, GROUP, D)),
            whole((4, GROUP, D)),
            whole((6, 4, 8, D)),
            pl.BlockSpec((4, NK, 4, UR, UC), lambda c: (c, 0, 0, 0, 0)),
            pl.BlockSpec((NJ, 1, 2, UR, UC), lambda c: (0, c // 2, 2 + c % 2, 0, 0)),
            pl.BlockSpec((9, CHUNK), lambda c: (0, c)),
        ],
        out_specs=[
            whole((4, GROUP, D)),
            whole((4, GROUP, D)),
            expand_spec,
            expand_spec,
            shrink_spec,
            shrink_spec,
            pl.BlockSpec((9, CHUNK), lambda c: (0, c)),
        ],
        out_shape=[
            jax.ShapeDtypeStruct((4, GROUP, D), F32),
            jax.ShapeDtypeStruct((4, GROUP, D), F32),
            packed_half(4),
            packed_half(4),
            packed_half(4),
            packed_half(4),
            jax.ShapeDtypeStruct((9, FF), F32),
        ],
        scratch_shapes=[
            pltpu.VMEM((TOK, D), BF),
            pltpu.VMEM((D, TOK), BF),
            pltpu.VMEM((CHUNK, D), BF),
            pltpu.VMEM((D, CHUNK), BF),
            pltpu.VMEM((4, GROUP, CHUNK), F32),
            pltpu.VMEM((4, GROUP, CHUNK), F32),
            pltpu.VMEM((4, GROUP, CHUNK), BF),
            pltpu.VMEM((4, GROUP, CHUNK), BF),
        ],
        compiler_params=params(60),
        cost_estimate=cost(38),
        name="feed",
    )(tag, second, gradient, mods, packed, packed, kernel)


def attend_back_kernel(
    tag_ref, resid, shrunk, d_second, gradient, attn, mods, qkv, lse, proj_t,
    output, d_resid, d_qkv, d_attn_t, item_sums,
    bias, d_mixed, d_attn, sums,
):
    @pl.when(pl.program_id(0) == 0)
    def _():
        bias[...] = item_bias(tag_ref[0])
        sums[...] = jnp.zeros_like(sums)

    def rows_norm(i, _):
        rows = pl.ds(pl.multiple_of(i * 64, 64), 64)
        half = i // 2
        base = resid[0, rows, :]
        normal, factor = norm_stats(base)
        shrunk_rows = shrunk[0, rows, :]
        outward = gradient[0, rows, :].astype(F32)
        d_sec = d_second[0, rows, :]

        def by_item(value):
            return value.reshape(4, 2, 8, D)

        def add(index, value):
            sums[index, pl.ds(2 * half, 2)] += jnp.sum(by_item(value), axis=0)

        gated = (by_item(shrunk_rows) * quadrant_rows(mods, 5, half)).reshape(64, D)
        output[0, rows, :] = (base + gated).astype(BF)
        add(3, outward * shrunk_rows)
        add(1, d_sec)
        add(2, d_sec * normal)
        inner = (by_item(d_sec) * (1.0 + quadrant_rows(mods, 4, half))).reshape(64, D)
        mean = jnp.mean(inner, axis=-1, keepdims=True)
        along = jnp.mean(inner * normal, axis=-1, keepdims=True)
        back = outward + (inner - mean - normal * along) * factor
        d_resid[0, rows, :] = back
        add(0, back * attn[0, rows, :].astype(F32))
        gated = (by_item(back) * quadrant_rows(mods, 2, half)).reshape(64, D)
        d_attn[rows, :] = gated.astype(BF)
        return 0

    lax.fori_loop(0, 4, rows_norm, 0)
    d_attn_t[...] = d_attn[...].T
    d_mixed[...] = dot(proj_t[...], d_attn[...], 1, 1).astype(BF)

    def head(h, _):
        rows = pl.ds(pl.multiple_of(h * HD, HD), HD)
        key_rows = pl.ds(pl.multiple_of(D + h * HD, HD), HD)
        value_rows = pl.ds(pl.multiple_of(2 * D + h * HD, HD), HD)
        queries = qkv[0, rows, :] * jnp.asarray(HD**-0.5, BF)
        keys = qkv[0, key_rows, :]
        values = qkv[0, value_rows, :]
        d_mix = d_mixed[rows, :]
        probs = jnp.exp(dot(keys, queries, 0, 0) + (bias[...] - lse[0, pl.ds(h, 1), :]))
        d_probs = dot(values, d_mix, 0, 0)
        d_qkv[value_rows, :] = dot(d_mix, probs.astype(BF), 1, 1).astype(BF)
        weighted = probs * d_probs
        inner = jnp.sum(weighted, axis=0, keepdims=True)
        d_scores = (weighted - probs * inner).astype(BF)
        d_qkv[rows, :] = (dot(keys, d_scores, 1, 0) * HD**-0.5).astype(BF)
        d_qkv[key_rows, :] = dot(queries, d_scores, 1, 1).astype(BF)
        return 0

    lax.fori_loop(0, H, head, 0, unroll=HEADS)

    @pl.when(pl.program_id(0) == pl.num_programs(0) - 1)
    def _():
        item_sums[...] = jnp.sum(sums[...], axis=2)


def attend_back(part, tag, resid, shrunk, d_second, gradient, attn, mods, qkv, lse, proj_t):
    first, count = PARTS[part]

    def pick_group(*shape):
        return pl.BlockSpec((1,) + shape, lambda g: (first + g,) + (0,) * len(shape))

    return pl.pallas_call(
        attend_back_kernel,
        grid=(count,),
        in_specs=[
            SMEM_SPEC,
            pick_group(GROUP, D),
            pick_group(GROUP, D),
            pick_group(GROUP, D),
            pick_group(GROUP, D),
            pick_group(GROUP, D),
            whole((6, 4, 8, D)),
            pick_group(3 * D, GROUP),
            pick_group(16, GROUP),
            whole((D, D)),
        ],
        out_specs=[
            group_spec(GROUP, D),
            group_spec(GROUP, D),
            pl.BlockSpec((3 * D, GROUP), lambda g: (0, g)),
            pl.BlockSpec((D, GROUP), lambda g: (0, g)),
            whole((4, 4, D)),
        ],
        out_shape=[
            jax.ShapeDtypeStruct((count, GROUP, D), BF),
            jax.ShapeDtypeStruct((count, GROUP, D), F32),
            jax.ShapeDtypeStruct((3 * D, count * GROUP), BF),
            jax.ShapeDtypeStruct((D, count * GROUP), BF),
            jax.ShapeDtypeStruct((4, 4, D), F32),
        ],
        scratch_shapes=[
            pltpu.VMEM((GROUP, GROUP), F32),
            pltpu.VMEM((D, GROUP), BF),
            pltpu.VMEM((GROUP, D), BF),
            pltpu.VMEM((4, 4, 8, D), F32),
        ],
        compiler_params=params(),
        cost_estimate=cost(9 * count),
        name=f"attend_back_{part}",
    )(tag, resid, shrunk, d_second, gradient, attn, mods, qkv, lse, proj_t)


PAIRS = 2
ROWS = 288 * PAIRS


def project_grads_kernel(
    tag_ref, d_qkv0, d_qkv1, d_attn0, d_attn1, conv_in, merged, keep_a, send_a, keep_b, send_b
):
    core = tag_ref[1]

    def against(low, high, field):
        return dot(low[...], field[0], 1, 0) + dot(
            high[...], field[1:4].reshape(3 * GROUP, D), 1, 0
        )

    grad = against(d_qkv0, d_qkv1, conv_in)
    share_out(grad, core, (0, 2), keep_a, send_a)
    share_out(grad, core, (2, 1), keep_b.at[:, :, 0:1], send_b.at[:, :, 0:1])
    grad = against(d_attn0, d_attn1, merged)
    share_out(grad, core, (0, 1), keep_b.at[:, :, 1:2], send_b.at[:, :, 1:2])


def column_specs(rows):
    return [pl.BlockSpec((rows, count * GROUP), lambda i: (i, 0)) for _, count in PARTS]


def project_grads(tag, d_qkv, d_attn, conv_in, merged):
    packed_spec = pl.BlockSpec((PAIRS, NK, 2, UR, UC), lambda i: (i, 0, 0, 0, 0))
    tall = column_specs(ROWS)
    short = column_specs(96 * PAIRS)
    return pl.pallas_call(
        project_grads_kernel,
        grid=(8 // PAIRS,),
        in_specs=[SMEM_SPEC, *tall, *short, whole((4, GROUP, D)), whole((4, GROUP, D))],
        out_specs=[packed_spec] * 4,
        out_shape=[packed_half(2)] * 4,
        compiler_params=params(),
        cost_estimate=cost(8),
        name="project_grads",
    )(tag, *d_qkv, *d_attn, conv_in, merged)


def conv_back_kernel(
    tag_ref, d_qkv0, d_qkv1, weight, norm, mods, kernel, later0, later1, g_ffn,
    d_first, pieces, d_conv, g_kernel, item_sums,
):
    step = pl.program_id(0)

    @pl.when(step == 0)
    def _():
        d_conv[...] = jnp.zeros_like(d_conv)

    d_conv[0] += dot(d_qkv0[...], weight[...], 0, 0)
    d_conv[1:4] += dot(d_qkv1[...], weight[...], 0, 0).reshape(3, GROUP, D)

    @pl.when(step == pl.num_programs(0) - 1)
    def _():
        tag = tag_ref[0]
        left, right = edge_columns(tag)
        keep = 1.0 - tag.astype(F32)

        def lanes(i, _):
            cols = pl.ds(pl.multiple_of(i * 128, 128), 128)
            taps = [jnp.broadcast_to(kernel[t : t + 1, cols], (16, 128)) for t in range(9)]
            sums = [[jnp.zeros((16, 128), F32) for _ in range(2)] for _ in range(2)]

            def load_grad(g, p):
                return d_conv[g, p * 16 : p * 16 + 16, cols]

            def load_field(g, p):
                q = 2 * (p // 8)
                shift = mods[0, q : q + 2, :, cols].reshape(16, 128)
                scale = mods[1, q : q + 2, :, cols].reshape(16, 128)
                return norm[g, p * 16 : p * 16 + 16, cols] * (1.0 + scale) + shift

            def emit(g, p, value):
                rows = slice(p * 16, p * 16 + 16)
                d_first[g, rows, cols] = value
                sums[0][p // 8] += value
                sums[1][p // 8] += value * norm[g, rows, cols]

            grads = conv_back_rows(load_grad, load_field, taps, left, right, keep, emit)
            for t in range(9):
                g_kernel[t : t + 1, cols] = jnp.sum(grads[t], axis=0, keepdims=True)
            for kind in range(2):
                for item in range(4):
                    part = sums[kind][item // 2][8 * (item % 2) : 8 * (item % 2) + 8]
                    item_sums[kind, item : item + 1, cols] = jnp.sum(part, axis=0, keepdims=True)
            return 0

        lax.fori_loop(0, D // 128, lanes, 0)
        later = later0[...] + later1[...]
        rows = [item_sums[i] for i in range(2)] + [later[i] for i in range(4)]
        rows = jnp.concatenate(rows, axis=1)
        alone = jnp.concatenate([jnp.sum(rows, axis=0, keepdims=True), jnp.zeros((3, 6 * D), F32)])
        rows = jnp.where(tag == 1, rows, alone)
        slots, _, width = pieces.shape
        owners = 6 * D // width
        short, long = D // owners, FF // owners
        for j in range(owners):
            filters = jnp.concatenate(
                [
                    g_kernel[:, j * short : (j + 1) * short],
                    g_ffn[:, j * long : (j + 1) * long],
                    jnp.zeros((9, width - short - long), F32),
                ],
                axis=1,
            )
            part = [rows[:, j * width : (j + 1) * width], filters, jnp.zeros((3, width), F32)]
            part = jnp.concatenate(part, axis=0).astype(BF)
            for copy in range(slots // owners):
                pieces[j * (slots // owners) + copy] = part


def conv_back(slots, width, tag, d_qkv, weight, norm, mods, kernel, later, g_ffn):
    return pl.pallas_call(
        conv_back_kernel,
        grid=(8 // PAIRS,),
        in_specs=[
            SMEM_SPEC,
            *column_specs(ROWS),
            pl.BlockSpec((ROWS, D), lambda i: (i, 0)),
            whole((4, GROUP, D)),
            whole((6, 4, 8, D)),
            whole((9, D)),
            whole((4, 4, D)),
            whole((4, 4, D)),
            whole((9, FF)),
        ],
        out_specs=[whole((4, GROUP, D)), whole((slots, 16, width))],
        out_shape=[
            jax.ShapeDtypeStruct((4, GROUP, D), F32),
            jax.ShapeDtypeStruct((slots, 16, width), BF),
        ],
        scratch_shapes=[
            pltpu.VMEM((4, GROUP, D), F32),
            pltpu.VMEM((9, D), F32),
            pltpu.VMEM((2, 4, D), F32),
        ],
        compiler_params=params(),
        cost_estimate=cost(15),
        name="conv_back",
    )(tag, *d_qkv, weight, norm, mods, kernel, *later, g_ffn)


def finish_kernel(
    d_first, norm, factor, d_resid0, d_resid1, output0, output1, mods,
    block_output, input_grad, total,
):
    half = pl.program_id(0) // 2

    for g in range(4):
        base = d_resid1[g - 1] if g else d_resid0[0]
        value = d_first[g]
        normal = norm[g]
        inner = (value.reshape(4, 2, 8, D) * (1.0 + quadrant_rows(mods, 1, half))).reshape(64, D)
        mean = jnp.mean(inner, axis=-1, keepdims=True)
        along = jnp.mean(inner * normal, axis=-1, keepdims=True)
        total[g] = base + (inner - mean - normal * along) * factor[g]
    order = ungroup_matrix()
    grouped = total[...].reshape(256, D)
    high = grouped.astype(BF)
    rest = (grouped - high.astype(F32)).astype(BF)
    input_grad[...] = dot(order, high, 1, 0) + dot(order, rest, 1, 0)
    grouped = jnp.concatenate([output0[...], output1[...]], axis=0).reshape(256, D)
    block_output[...] = dot(order, grouped, 1, 0).astype(BF)


def finish(d_first, norm, factor, d_resid, output, mods):
    def split(groups, width):
        return pl.BlockSpec((groups, 64, width), lambda i: (0, i, 0))

    flat = pl.BlockSpec((256, D), lambda i: (i, 0))
    return pl.pallas_call(
        finish_kernel,
        grid=(4,),
        in_specs=[split(4, D), split(4, D), split(4, 1)]
        + [split(count, D) for _, count in PARTS] * 2
        + [whole((6, 4, 8, D))],
        out_specs=[flat, flat],
        out_shape=[
            jax.ShapeDtypeStruct((TOK, D), BF),
            jax.ShapeDtypeStruct((TOK, D), F32),
        ],
        scratch_shapes=[pltpu.VMEM((4, 64, D), F32)],
        compiler_params=params(),
        cost_estimate=cost(8),
        name="finish",
    )(d_first, norm, factor, *d_resid, *output, mods)


BOTH = ("dp", "fsdp")


def exchange(pieces):
    return lax.all_to_all(pieces, BOTH, 0, 0, tiled=True)


def units_of(weight):
    return weight.T.reshape(-1, UR, UC)


def low_units(shrink):
    return shrink.T.reshape(UR, 4, UC).transpose(1, 0, 2)


def gather_feed(nd, nf, expand, shrink):
    if (nd, nf) == (NJ, NK):
        rows = jnp.concatenate([units_of(expand), low_units(shrink)]).reshape(8 * UR, UC)
        return lax.all_gather(rows, BOTH).reshape(NJ, NK, 8, UR, UC)
    low = full_rows(shrink).reshape(NJ, UR, NK, 4, UC).transpose(0, 2, 3, 1, 4)
    return jnp.concatenate([all_units(full_rows(expand), 4), low], axis=2)


def full_rows(shard):
    rows = lax.all_gather(shard.T, "fsdp", axis=1, tiled=True)
    return lax.all_gather(rows, "dp", axis=0, tiled=True)


def all_units(weight, units):
    return weight.reshape(NJ, units, UR, NK, UC).transpose(0, 3, 1, 2, 4)


def project_turns(own):
    turns = [
        lax.ppermute(own, "dp", [(i, (i - 4 * step) % NJ) for i in range(NJ)])
        for step in range(1, 4)
    ]
    return turns


def widen(a, b, bit_a, bit_b):
    return jnp.stack([a, swap(a, bit_a)]), jnp.stack([b, swap(b, bit_b)])


def all_projections(qkv, proj):
    units = jnp.concatenate([all_units(full_rows(qkv), 3), all_units(full_rows(proj), 1)], axis=2)
    units = units.reshape((4, 2, 2) + units.shape[1:])
    first, rest = units[:, :, :, :, :2], units[:, :, :, :, 2:]
    a, b = first.transpose(2, 3, 1, 0, 4, 5, 6), rest.transpose(2, 1, 3, 0, 4, 5, 6)
    return a[0], b[0], a[1], b[1]


def pick(grads, index, axis):
    return lax.dynamic_index_in_dim(grads, index, axis, keepdims=False)


def swap(value, bit):
    if bit is None:
        return lax.ppermute(value, "fsdp", [(0, 1), (1, 0)])
    return lax.ppermute(value, "dp", [(i, i ^ bit) for i in range(NJ)])


def halve(keep, got, axis, bit):
    mine = lax.axis_index("fsdp") if bit is None else (lax.axis_index("dp") // bit) % 2
    kept = pick(keep, mine, axis) + pick(got, mine, axis)
    return kept, pick(keep, 1 - mine, axis) + pick(got, 1 - mine, axis)


def last_sends(total):
    place = lax.axis_index("dp") // 4
    return [pick(total, (place + step) % 4, 0) for step in range(1, 4)]


def last_swaps(sends):
    return [
        lax.ppermute(sent, "dp", [(i, (i + 4 * step) % NJ) for i in range(NJ)])
        for step, sent in enumerate(sends, 1)
    ]


def last_sum(total, got):
    own = pick(total, lax.axis_index("dp") // 4, 0).astype(F32)
    for value in got:
        own = own + value.astype(F32)
    return own


def after(value, *others):
    return lax.optimization_barrier((value,) + others)[0]


def own_shard(nd, nf, kind, units):
    if (nd, nf) == (NJ, NK):
        if kind == "shrink":
            return units.transpose(1, 0, 2).reshape(UR, 4 * UC).T
        return units.reshape(-1, UC).T
    if kind == "shrink":
        weight = units.transpose(0, 3, 1, 2, 4).reshape(NJ * UR, -1)
    else:
        weight = units.transpose(0, 2, 3, 1, 4).reshape(-1, NK * UC)
    columns = lax.psum_scatter(weight, "dp", scatter_dimension=0, tiled=True)
    piece = lax.psum_scatter(columns, "fsdp", scatter_dimension=1, tiled=True)
    return piece.astype(F32).T


def both_cores(keep, send):
    return jnp.stack([keep, send], axis=1).reshape((-1,) + keep.shape[1:])


def look_up(ids, step_table, class_table):
    first_row = lax.axis_index("fsdp") * step_table.shape[0]
    own = first_row + jnp.arange(step_table.shape[0], dtype=jnp.int32)
    step_hot = (ids[:, :4].reshape(-1, 1) == own[None, :]).astype(BF)
    class_hot = (ids[:, 4:].reshape(-1, 1) == own[None, :]).astype(BF)
    return step_hot, class_hot, dot(step_table, step_hot, 0, 1) + dot(class_table, class_hot, 0, 1)


def share_act(nd, cond, attn_kernel, ffn_kernel, beside):
    width, items = cond.shape
    act = jax.nn.silu(cond).astype(BF)
    filters = jnp.concatenate([attn_kernel, ffn_kernel], axis=1).reshape(-1)
    size = filters.shape[0]
    filters = jnp.pad(filters, (0, -size % items)).reshape(-1, items)
    sent = jnp.concatenate([act, filters], axis=0)[None]
    sent = lax.all_to_all(jnp.broadcast_to(sent, (nd,) + sent.shape[1:]), "dp", 0, 0, tiled=True)
    sent = after(sent, *beside)
    act_all = sent[:, :width].reshape(nd * width, items)
    filters = sent[:, width:].reshape(nd, -1)[:, :size]
    filters = filters.reshape(nd, 9, -1).astype(F32)
    attn_full = filters[:, :, : attn_kernel.shape[1]].transpose(1, 0, 2).reshape(9, -1)
    ffn_full = filters[:, :, attn_kernel.shape[1] :].transpose(1, 0, 2).reshape(9, -1)
    return act_all, attn_full, ffn_full


def exchange_columns(nd, nf, d_act):
    rows, items = d_act.shape
    if (nd, nf) == (NJ, NK):
        return lax.all_to_all(d_act.reshape(nd, rows // nd, items), "dp", 0, 0, tiled=True)
    spread = lax.dynamic_update_slice_in_dim(
        jnp.zeros((rows * nf, items), F32), d_act, lax.axis_index("fsdp") * rows, axis=0
    )
    spread = spread.reshape(nd, 1, -1, items)
    spread = jnp.broadcast_to(spread, (nd, nf) + spread.shape[2:])
    return exchange(spread.reshape((nd * nf,) + spread.shape[2:]))


def own_columns(nd, nf, terms):
    part = terms.sum(axis=0)
    if (nd, nf) != (NJ, NK):
        return part
    order = [(j * NK + k, k * NJ + j) for j in range(NJ) for k in range(NK)]
    own = lax.ppermute(part, BOTH, order)
    other = lax.ppermute(part, BOTH, [(i, o ^ 1) for i, o in order])
    first = lax.axis_index("fsdp") == 0
    return jnp.concatenate([jnp.where(first, own, other), jnp.where(first, other, own)])


def body(
    latents, size_tags, timesteps, classes, step_table, class_table, modulation_weight,
    attn_kernel, qkv_weight, proj_weight, expand_weight, ffn_kernel, shrink_weight, cotangent,
    *, nd, nf,
):
    slots = nd * nf
    tag = size_tags[0]
    square = (nd, nf) == (NJ, NK)
    if square:
        place = lax.axis_index("dp")
        where = [tag, place % 2, place // 4, (place // 2) % 2, lax.axis_index("fsdp")]
        where = jnp.stack(where).astype(jnp.int32)
    else:
        where = jnp.stack([tag] + [jnp.int32(0)] * 4)
    packed = gather_feed(nd, nf, expand_weight, shrink_weight)
    tokens, gradient, norm, factor = prepare(latents, cotangent)
    mine = jnp.concatenate([timesteps[0], classes[0]])[None]
    mine = jnp.broadcast_to(mine, (slots, 8))
    if square:
        own = jnp.concatenate([units_of(qkv_weight), units_of(proj_weight)])
        own = after(own, mine)
        turns = project_turns(own)
    ids = exchange(mine)
    if square:
        ids = after(ids, norm)
    step_hot, class_hot, part = look_up(ids, step_table, class_table)
    if square:
        cond = part + swap(part, None)
        own, *turns = (after(x, cond) for x in (own, *turns))
        a = jnp.stack([own[:2]] + [turn[:2] for turn in turns])
        b = jnp.stack([own[2:]] + [turn[2:] for turn in turns])
        next_a, next_b = swap(a, 2), swap(b, None)
        a, b = jnp.stack([a, next_a]), jnp.stack([b, next_b])
        beside = (a, b)
    else:
        beside = ()
        cond = lax.psum(part, "fsdp")
    act_all, attn_full, ffn_full = share_act(nd, cond, attn_kernel, ffn_kernel, beside)
    if square:
        next_a, next_b = swap(a, None), swap(b, 2)
        next_a, next_b = after(next_a, act_all), after(next_b, act_all)
    height, width = modulation_weight.shape
    act_rows = lax.dynamic_slice_in_dim(
        act_all, lax.axis_index("fsdp") * height, height, axis=0
    )
    terms = dot(act_rows, modulation_weight, 0, 0)
    terms = exchange(terms.reshape(slots, 1, 4 * width)).reshape(nd, nf, 4, width)
    if square:
        a, b = jnp.stack([a, next_a]), jnp.stack([b, next_b])
        projections = (a, b, swap(a, 1), swap(b, 1))
    else:
        projections = all_projections(qkv_weight, proj_weight)
    mod_rows = terms.sum(axis=1).transpose(1, 0, 2).reshape(4, nd * width)
    chosen = jnp.where(tag == 1, mod_rows, mod_rows[:1])
    mods = jnp.broadcast_to(chosen.reshape(4, 6, 1, D).transpose(1, 0, 2, 3), (6, 4, 8, D))

    conv_in = first_conv(size_tags, norm, mods, attn_full)
    qkv, merged, attn, resid, second, lse, proj_t, full_qkv = attend(
        where, conv_in, tokens, mods, projections
    )
    shrunk, d_second, keep_e, send_e, keep_s, send_s, g_ffn = feed(
        where, second, gradient, mods, packed, ffn_full
    )
    back = (gradient, attn, mods, qkv, lse)
    if square:
        got_e, got_s = swap(send_e, 1), swap(send_s, 1)
    output0, d_resid0, d_qkv0, d_attn0, later0 = attend_back(
        0, where, resid, shrunk, d_second, *back, proj_t
    )

    def grid(value):
        return value.reshape((4, 2) + value.shape[1:])

    if square:
        got_e, got_s = after(got_e, d_qkv0), after(got_s, d_qkv0)
        keep_e, out_e = halve(grid(keep_e), grid(got_e), 2, None)
        keep_s, out_s = halve(grid(keep_s), grid(got_s), 1, 2)
        d_second = after(d_second, out_e, out_s)
        got_e, got_s = swap(out_e, None), swap(out_s, 2)
    output1, d_resid1, d_qkv1, d_attn1, later1 = attend_back(
        1, where, resid, shrunk, d_second, *back, proj_t
    )
    if square:
        got_e, got_s = after(got_e, d_attn1), after(got_s, d_attn1)
        keep_e, out_e = halve(keep_e, got_e, 1, 2)
        keep_s, out_s = halve(keep_s, got_s, 1, None)
        d_attn0 = after(d_attn0, out_e, out_s)
        got_e, got_s = swap(out_e, 2), swap(out_s, None)
    d_qkv = (d_qkv0, d_qkv1)
    keep_a, send_a, keep_b, send_b = project_grads(
        where, d_qkv, (d_attn0, d_attn1), conv_in, merged
    )
    if square:
        got_e, got_s = after(got_e, keep_a), after(got_s, keep_a)
        got_a, got_b = swap(send_a, 1), swap(send_b, 1)
        e = halve(keep_e.reshape((2, 2) + keep_e.shape[1:]), got_e.reshape((2, 2) + got_e.shape[1:]), 1, 4)
        s = halve(keep_s.reshape((2, 2) + keep_s.shape[1:]), got_s.reshape((2, 2) + got_s.shape[1:]), 1, 4)
        feeding, out_f = (jnp.concatenate(pair, axis=1) for pair in zip(e, s))
        keep_a, out_a = halve(grid(keep_a), grid(got_a), 2, None)
        keep_b, out_b = halve(grid(keep_b), grid(got_b), 1, 2)
        full_qkv = after(full_qkv, out_a, out_b, out_f)
        got_a, got_b, got_f = swap(out_a, None), swap(out_b, 2), swap(out_f, 4)
    d_first, pieces = conv_back(
        slots, width, where, d_qkv, full_qkv, norm, mods, attn_full, (later0, later1), g_ffn
    )
    if square:
        got_a, got_b, got_f = (after(x, d_first) for x in (got_a, got_b, got_f))
        keep_a, out_a = halve(keep_a, got_a, 1, 2)
        keep_b, out_b = halve(keep_b, got_b, 1, None)
        feeding, out_f = halve(feeding, got_f, 0, 8)
    if square:
        d_first = after(d_first, out_a, out_b, out_f, pieces)
        got_a, got_b, got_f = swap(out_a, 2), swap(out_b, None), swap(out_f, 8)
    got = exchange(pieces)
    block_output, input_grad = finish(
        d_first, norm, factor, (d_resid0, d_resid1), (output0, output1), mods
    )
    if square:
        got = after(got, input_grad)
    d_mod_all = got[:, :4].reshape(slots * 4, width)
    d_act = dot(modulation_weight, d_mod_all, 1, 1)
    if square:
        got_a, got_b = after(got_a, d_act), after(got_b, d_act)
        total = jnp.concatenate([keep_a + got_a, keep_b + got_b], axis=1)
        sends = last_sends(total)
        last = last_swaps(sends)
    own_act = exchange_columns(nd, nf, d_act)
    if square:
        got_f = after(got_f, own_act)
        total = last_sum(total, last)
        feeding = feeding.astype(F32) + got_f.astype(F32)
        cuts = [total[:3], total[3:], feeding[:4], feeding[4:]]
    else:
        first, rest = both_cores(keep_a, send_a), both_cores(keep_b, send_b)
        cuts = [
            jnp.concatenate([first, rest[:, :, :1]], axis=2),
            rest[:, :, 1:],
            both_cores(keep_e, send_e),
            both_cores(keep_s, send_s),
        ]
    shards = [
        own_shard(nd, nf, kind, cut)
        for kind, cut in zip(("qkv", "proj", "expand", "shrink"), cuts)
    ]
    cut = attn_kernel.shape[1]
    filters = got[:, 4:13, : cut + ffn_kernel.shape[1]].astype(F32).sum(axis=0)
    modulation_grad = dot(act_rows, d_mod_all, 1, 0)
    gate = jax.nn.sigmoid(cond)
    d_cond = own_columns(nd, nf, own_act)
    d_cond = d_cond * (gate * (1.0 + cond * (1.0 - gate)))

    def table_grad(hot):
        return lax.dot_general(
            hot.astype(F32), d_cond, (((0,), (1,)), ((), ())), precision=lax.Precision.HIGHEST
        )

    return (
        block_output,
        input_grad,
        table_grad(step_hot),
        table_grad(class_hot),
        modulation_grad,
        filters[:, :cut],
        shards[0],
        shards[1],
        shards[2],
        filters[:, cut:],
        shards[3],
    )


def solution(mesh):
    matrix = P("fsdp", "dp")
    rows = P(BOTH, None)
    filters = P(None, "dp")
    in_specs = (
        rows, P(BOTH), rows, rows, matrix, matrix, matrix, filters, matrix, matrix, matrix,
        filters, matrix, rows,
    )
    out_specs = (
        rows, rows, matrix, matrix, matrix, filters, matrix, matrix, matrix, filters, matrix,
    )
    run = functools.partial(body, nd=mesh.shape["dp"], nf=mesh.shape["fsdp"])
    return jax.shard_map(run, mesh=mesh, in_specs=in_specs, out_specs=out_specs, check_vma=False)
```

```python
import functools

import jax
import jax.numpy as jnp
from jax import lax
from jax.experimental import pallas as pl
from jax.experimental.pallas import tpu as pltpu
from jax.sharding import PartitionSpec as P

D = 768
H = 12
HD = 64
FF = 3072
SIDE = 32
GROUP = 256
TOK = SIDE * SIDE
EPS = 1e-06
NJ, NK, UR, UC = 16, 2, 48, 384
CHUNK = 768
HEADS = 6
PARTS = ((0, 1), (1, 3))
MIB = 1024 * 1024
BF = jnp.bfloat16
F32 = jnp.float32
GELU_A = 0.7978845608028654
GELU_B = GELU_A * 0.044715


def dot(left, right, left_dim, right_dim):
    return lax.dot_general(
        left, right, (((left_dim,), (right_dim,)), ((), ())), preferred_element_type=F32
    )


def params(limit=56):
    return pltpu.CompilerParams(vmem_limit_bytes=limit * MIB)


def cost(micros):
    return pl.CostEstimate(flops=int(micros * 1e8), transcendentals=0, bytes_accessed=4 * MIB)


def whole(shape):
    zeros = (0,) * len(shape)
    return pl.BlockSpec(shape, lambda *ids: zeros, pipeline_mode=pl.Buffered(1))


SMEM_SPEC = pl.BlockSpec(memory_space=pltpu.SMEM)


def group_place(natural):
    pair, odd_row = natural // 64, (natural // 32) % 2
    column, odd_column = (natural % 32) // 2, natural % 2
    return (2 * odd_row + odd_column) * 64 + pair * 16 + column


def ungroup_matrix():
    natural = lax.broadcasted_iota(jnp.int32, (256, 256), 0)
    grouped = lax.broadcasted_iota(jnp.int32, (256, 256), 1)
    return jnp.where(group_place(natural) == grouped, 1.0, 0.0).astype(BF)


def group_matrix():
    natural = lax.broadcasted_iota(jnp.int32, (256, 256), 1)
    grouped = lax.broadcasted_iota(jnp.int32, (256, 256), 0)
    return jnp.where(group_place(natural) == grouped, 1.0, 0.0).astype(BF)


def norm_stats(values):
    centre = values - jnp.mean(values, axis=-1, keepdims=True)
    variance = jnp.mean(centre * centre, axis=-1, keepdims=True)
    scale = lax.rsqrt(variance + EPS)
    return centre * scale, scale


def prepare_kernel(latents, cotangent, tokens, gradient, norm, scale):
    order = group_matrix()
    gathered = dot(order, latents[...], 1, 0)
    gradient[...] = dot(order, cotangent[...], 1, 0).reshape(4, 64, D).astype(BF)
    tokens[...] = gathered.reshape(4, 64, D).astype(BF)
    normal, factor = norm_stats(gathered)
    norm[...] = normal.reshape(4, 64, D)
    scale[...] = factor.reshape(4, 64, 1)


def prepare(latents, cotangent):
    flat = pl.BlockSpec((256, D), lambda i: (i, 0))
    split = pl.BlockSpec((4, 64, D), lambda i: (0, i, 0))
    return pl.pallas_call(
        prepare_kernel,
        grid=(4,),
        in_specs=[flat, flat],
        out_specs=[split, split, split, pl.BlockSpec((4, 64, 1), lambda i: (0, i, 0))],
        out_shape=[
            jax.ShapeDtypeStruct((4, GROUP, D), BF),
            jax.ShapeDtypeStruct((4, GROUP, D), BF),
            jax.ShapeDtypeStruct((4, GROUP, D), F32),
            jax.ShapeDtypeStruct((4, GROUP, 1), F32),
        ],
        compiler_params=params(),
        cost_estimate=cost(6),
        name="prepare",
    )(latents, cotangent)


def edge_columns(tag):
    place = lax.broadcasted_iota(jnp.int32, (16, 128), 0)
    left = jnp.where((place == 0) | ((place == 8) & (tag == 1)), 0.0, 1.0)
    right = jnp.where((place == 15) | ((place == 7) & (tag == 1)), 0.0, 1.0)
    return left, right


def neighbours(even, odd, left, right):
    return pltpu.roll(odd, 1, 0) * left, pltpu.roll(even, 15, 0) * right


def conv_rows(load, kernel, left, right, keep, emit):
    above = None
    partial = None
    for row in range(SIDE + 1):
        taps = None
        if row < SIDE:
            a, p = row % 2, row // 2
            even, odd = load(2 * a, p), load(2 * a + 1, p)
            odd_left, even_right = neighbours(even, odd, left, right)
            taps = []
            for tap in range(3):
                k = [kernel[3 * tap + b] for b in range(3)]
                taps.append(
                    (
                        k[0] * odd_left + k[1] * even + k[2] * odd,
                        k[0] * even + k[1] * odd + k[2] * even_right,
                    )
                )
        crossing = row == SIDE // 2
        if partial is not None:
            a, p = (row - 1) % 2, (row - 1) // 2
            for b in range(2):
                value = partial[b]
                if taps is not None:
                    below = taps[2][b]
                    value = value + (below * keep if crossing else below)
                emit(2 * a + b, p, value)
        if taps is not None:
            partial = []
            for b in range(2):
                value = taps[1][b]
                if above is not None:
                    value = value + (above[b] * keep if crossing else above[b])
                partial.append(value)
            above = taps[0]


def conv_back_rows(load_grad, load_field, kernel, left, right, keep, emit):
    sums = [jnp.zeros((16, 128), F32) for _ in range(9)]
    from_above = None
    partial = None
    field_above = None
    field = (load_field(0, 0), load_field(1, 0))
    for row in range(SIDE + 1):
        crossing = row == SIDE // 2
        taps = None
        if row < SIDE:
            a, p = row % 2, row // 2
            even, odd = load_grad(2 * a, p), load_grad(2 * a + 1, p)
            odd_left, even_right = neighbours(even, odd, left, right)
            picks = ((odd, even, odd_left), (even_right, odd, even))
            taps = []
            for tap in range(3):
                k = [kernel[3 * tap + b] for b in range(3)]
                taps.append(
                    tuple(k[0] * x[0] + k[1] * x[1] + k[2] * x[2] for x in picks)
                )
            field_below = None
            if row + 1 < SIDE:
                a, p = (row + 1) % 2, (row + 1) // 2
                field_below = (load_field(2 * a, p), load_field(2 * a + 1, p))
            for tap, rows in enumerate((field_above, field, field_below)):
                if rows is None:
                    continue
                if (tap == 0 and crossing) or (tap == 2 and row + 1 == SIDE // 2):
                    rows = (rows[0] * keep, rows[1] * keep)
                for b in range(3):
                    sums[3 * tap + b] = (
                        sums[3 * tap + b] + rows[0] * picks[0][b] + rows[1] * picks[1][b]
                    )
            field_above, field = field, field_below
        if partial is not None:
            a, p = (row - 1) % 2, (row - 1) // 2
            for b in range(2):
                value = partial[b]
                if taps is not None:
                    value = value + (taps[0][b] * keep if crossing else taps[0][b])
                emit(2 * a + b, p, value)
        if taps is not None:
            partial = []
            for b in range(2):
                value = taps[1][b]
                if from_above is not None:
                    value = value + (from_above[b] * keep if crossing else from_above[b])
                partial.append(value)
            from_above = taps[2]
    return sums


def first_conv_kernel(tag_ref, norm, mods, kernel, out):
    tag = tag_ref[0]
    left, right = edge_columns(tag)
    keep = 1.0 - tag.astype(F32)
    taps = [jnp.broadcast_to(kernel[i : i + 1, :], (16, 128)) for i in range(9)]

    def load(g, p):
        q = 2 * (p // 8)
        shift = mods[0, q : q + 2].reshape(16, 128)
        scale = mods[1, q : q + 2].reshape(16, 128)
        return norm[g, p * 16 : p * 16 + 16, :] * (1.0 + scale) + shift

    def emit(g, p, value):
        out[g, p * 16 : p * 16 + 16, :] = value.astype(BF)

    conv_rows(load, taps, left, right, keep, emit)


def first_conv(tag, norm, mods, kernel):
    return pl.pallas_call(
        first_conv_kernel,
        grid=(D // 128,),
        in_specs=[
            SMEM_SPEC,
            pl.BlockSpec((4, GROUP, 128), lambda i: (0, 0, i)),
            pl.BlockSpec((6, 4, 8, 128), lambda i: (0, 0, 0, i)),
            pl.BlockSpec((9, 128), lambda i: (0, i)),
        ],
        out_specs=pl.BlockSpec((4, GROUP, 128), lambda i: (0, 0, i)),
        out_shape=jax.ShapeDtypeStruct((4, GROUP, D), BF),
        compiler_params=params(),
        cost_estimate=cost(6),
        name="first_conv",
    )(tag, norm, mods, kernel)


def join_rows(block, target):
    rows = block.shape[0] * block.shape[2] * UR
    for k in range(NK):
        target[:, k * UC : (k + 1) * UC] = block[:, k].reshape(rows, UC)


def share_out(rows, core, units, keep, send):
    first, count = units
    for k in range(NK):
        part = rows[:, k * UC : (k + 1) * UC].astype(BF)
        part = part.reshape(-1, 2, part.shape[0] // (keep.shape[0] * 2), UC)
        even, odd = part[:, 0], part[:, 1]
        for target, value in (
            (keep, jnp.where(core == 0, even, odd)),
            (send, jnp.where(core == 0, odd, even)),
        ):
            whole_units = value.reshape(value.shape[0], -1, UR, UC)
            target[:, k] = whole_units[:, first : first + count]


def quadrant_rows(mods, index, half):
    return mods[index, pl.ds(2 * half, 2)].reshape(1, 2, 8, D)


def item_bias(tag):
    def label(dim):
        place = lax.broadcasted_iota(jnp.int32, (GROUP, GROUP), dim)
        return 2 * (place // 128) + (place % 16) // 8

    return jnp.where((label(0) == label(1)) | (tag == 0), 0.0, -1e30)


def attend_kernel(
    where, conv_in, tokens, mods, own_a, own_b, peer_a, peer_b,
    qkv, merged, attn, resid, second, lse, proj_t, full_qkv,
    full_proj, bias, mixed_t,
):
    @pl.when(pl.program_id(0) == 0)
    def _():
        core, z, y, x = (where[i] for i in range(1, 5))
        for owner in range(NJ):
            step = (owner // 4 - z + 4) % 4
            side = (owner // 2) % 2 ^ y
            mine = core == owner % 2
            for k in range(NK):
                cols = slice(k * UC, (k + 1) * UC)
                a = jnp.where(mine, own_a[k ^ x, side, step], peer_a[k ^ x, side, step])
                b = jnp.where(mine, own_b[side, k ^ x, step], peer_b[side, k ^ x, step])
                start = owner * 3 * UR
                full_qkv[start : start + 2 * UR, cols] = a.reshape(2 * UR, UC)
                full_qkv[start + 2 * UR : start + 3 * UR, cols] = b[0]
                full_proj[owner * UR : (owner + 1) * UR, cols] = b[1]
        proj_t[...] = full_proj[...].T
        bias[...] = item_bias(where[0])

    qkv[0] = dot(full_qkv[...], conv_in[0], 1, 1).astype(BF)

    def head(h, _):
        rows = pl.ds(pl.multiple_of(h * HD, HD), HD)
        queries = qkv[0, rows, :] * jnp.asarray(HD**-0.5, BF)
        keys = qkv[0, pl.ds(pl.multiple_of(D + h * HD, HD), HD), :]
        values = qkv[0, pl.ds(pl.multiple_of(2 * D + h * HD, HD), HD), :]
        scores = dot(keys, queries, 0, 0) + bias[...]
        highest = jnp.max(scores, axis=0, keepdims=True)
        raised = jnp.exp(scores - highest)
        total = jnp.sum(raised, axis=0, keepdims=True)
        probs = (raised * (1.0 / total)).astype(BF)
        lse[0, pl.ds(h, 1), :] = highest + jnp.log(total)
        mixed_t[rows, :] = dot(values, probs, 1, 0).astype(BF)
        return 0

    lax.fori_loop(0, H, head, 0, unroll=HEADS)
    merged[0] = mixed_t[...].T
    projected = dot(merged[0], full_proj[...], 1, 1)
    attn[0] = projected.astype(BF)
    gate = mods[2].reshape(2, 1, 2, 8, D)
    resid[0] = (
        tokens[0].astype(F32) + (projected.reshape(2, 8, 2, 8, D) * gate).reshape(GROUP, D)
    )

    def rows_norm(i, _):
        rows = pl.ds(pl.multiple_of(i * 64, 64), 64)
        normal, _ = norm_stats(resid[0, rows, :])
        half = i // 2
        scaled = normal.reshape(4, 2, 8, D) * (1.0 + quadrant_rows(mods, 4, half))
        value = scaled + quadrant_rows(mods, 3, half)
        second[0, rows, :] = value.reshape(64, D).astype(BF)
        return 0

    lax.fori_loop(0, 4, rows_norm, 0)


def group_spec(*shape):
    return pl.BlockSpec((1,) + shape, lambda g: (g,) + (0,) * len(shape))


def attend(where, conv_in, tokens, mods, projections):
    relative = (2, 2, 4, 2, UR, UC)
    return pl.pallas_call(
        attend_kernel,
        grid=(4,),
        in_specs=[
            SMEM_SPEC,
            group_spec(GROUP, D),
            group_spec(GROUP, D),
            whole((6, 4, 8, D)),
        ]
        + [whole(relative)] * 4,
        out_specs=[
            group_spec(3 * D, GROUP),
            group_spec(GROUP, D),
            group_spec(GROUP, D),
            group_spec(GROUP, D),
            group_spec(GROUP, D),
            group_spec(16, GROUP),
            whole((D, D)),
            whole((3 * D, D)),
        ],
        out_shape=[
            jax.ShapeDtypeStruct((4, 3 * D, GROUP), BF),
            jax.ShapeDtypeStruct((4, GROUP, D), BF),
            jax.ShapeDtypeStruct((4, GROUP, D), BF),
            jax.ShapeDtypeStruct((4, GROUP, D), F32),
            jax.ShapeDtypeStruct((4, GROUP, D), BF),
            jax.ShapeDtypeStruct((4, 16, GROUP), F32),
            jax.ShapeDtypeStruct((D, D), BF),
            jax.ShapeDtypeStruct((3 * D, D), BF),
        ],
        scratch_shapes=[
            pltpu.VMEM((D, D), BF),
            pltpu.VMEM((GROUP, GROUP), F32),
            pltpu.VMEM((D, GROUP), BF),
        ],
        compiler_params=params(),
        cost_estimate=cost(38),
        name="attend",
    )(where, conv_in, tokens, mods, *projections)


def feed_kernel(
    tag_ref, second, gradient, mods, w_expand, w_shrink, kernel,
    shrunk, d_second, keep_expand, send_expand, keep_shrink, send_shrink, g_kernel,
    d_shrunk, d_shrunk_t, expand, shrink, field, slope, hidden, d_field, shrunk_sum, second_sum,
):
    step = pl.program_id(0)
    tag, core = tag_ref[0], tag_ref[1]

    @pl.when(step == 0)
    def _():
        gate = mods[5].reshape(1, 2, 1, 2, 8, D)
        value = gradient[...].astype(F32).reshape(4, 2, 8, 2, 8, D) * gate
        d_shrunk[...] = value.reshape(TOK, D).astype(BF)
        d_shrunk_t[...] = d_shrunk[...].T
        shrunk_sum[...] = jnp.zeros_like(shrunk_sum)
        second_sum[...] = jnp.zeros_like(second_sum)

    join_rows(w_expand, expand)
    for q in range(2):
        shrink[:, q * UC : (q + 1) * UC] = w_shrink[:, 0, q].reshape(D, UC)
    left, right = edge_columns(tag)
    keep = 1.0 - tag.astype(F32)
    field[...] = dot(second[...].reshape(TOK, D), expand[...], 1, 1).reshape(4, GROUP, CHUNK)
    slope[...] = dot(d_shrunk[...], shrink[...], 1, 0).reshape(4, GROUP, CHUNK)

    def lanes(i, _):
        cols = pl.ds(pl.multiple_of(i * 128, 128), 128)
        taps = [jnp.broadcast_to(kernel[t : t + 1, cols], (16, 128)) for t in range(9)]

        def load(g, p):
            return field[g, p * 16 : p * 16 + 16, cols]

        def load_slope(g, p):
            return slope[g, p * 16 : p * 16 + 16, cols]

        def emit(g, p, value):
            square = value * value
            half = 0.5 + 0.5 * jnp.tanh(value * (GELU_A + GELU_B * square))
            out = value * half
            hidden[g, p * 16 : p * 16 + 16, cols] = out.astype(BF)
            rate = half + (out - out * half) * (2.0 * GELU_A + 6.0 * GELU_B * square)
            slope[g, p * 16 : p * 16 + 16, cols] = load_slope(g, p) * rate

        conv_rows(load, taps, left, right, keep, emit)

        def emit_back(g, p, value):
            d_field[g, p * 16 : p * 16 + 16, cols] = value.astype(BF)

        sums = conv_back_rows(load_slope, load, taps, left, right, keep, emit_back)
        for t in range(9):
            g_kernel[t : t + 1, cols] = jnp.sum(sums[t], axis=0, keepdims=True)
        return 0

    lax.fori_loop(0, CHUNK // 128, lanes, 0)
    hid = hidden[...].reshape(TOK, CHUNK)
    d_fld = d_field[...].reshape(TOK, CHUNK)
    grad = dot(d_shrunk_t[...], hid, 1, 0).astype(BF)
    for q in range(2):
        part = grad[:, q * UC : (q + 1) * UC].reshape(NJ // 2, 2, UR, UC)
        keep_shrink[:, 0, q] = jnp.where(core == 0, part[:, 0], part[:, 1])
        send_shrink[:, 0, q] = jnp.where(core == 0, part[:, 1], part[:, 0])
    share_out(dot(d_fld, second[...].reshape(TOK, D), 0, 0), core, (0, 4), keep_expand, send_expand)
    shrunk_sum[...] += dot(hid, shrink[...], 1, 1).reshape(4, GROUP, D)
    second_sum[...] += dot(d_fld, expand[...], 1, 0).reshape(4, GROUP, D)

    @pl.when(step == pl.num_programs(0) - 1)
    def _():
        shrunk[...] = shrunk_sum[...].astype(BF)
        d_second[...] = second_sum[...].astype(BF)


def packed_half(units):
    return jax.ShapeDtypeStruct((NJ // 2, NK, units, UR, UC), BF)


def feed(tag, second, gradient, mods, packed, kernel):
    half = NJ // 2
    expand_spec = pl.BlockSpec((2, NK, 4, UR, UC), lambda c: (c, 0, 0, 0, 0))
    shrink_spec = pl.BlockSpec((half, 1, 2, UR, UC), lambda c: (0, c // 2, c % 2, 0, 0))
    return pl.pallas_call(
        feed_kernel,
        grid=(FF // CHUNK,),
        in_specs=[
            SMEM_SPEC,
            whole((4, GROUP, D)),
            whole((4, GROUP, D)),
            whole((6, 4, 8, D)),
            pl.BlockSpec((4, NK, 4, UR, UC), lambda c: (c, 0, 0, 0, 0)),
            pl.BlockSpec((NJ, 1, 2, UR, UC), lambda c: (0, c // 2, 2 + c % 2, 0, 0)),
            pl.BlockSpec((9, CHUNK), lambda c: (0, c)),
        ],
        out_specs=[
            whole((4, GROUP, D)),
            whole((4, GROUP, D)),
            expand_spec,
            expand_spec,
            shrink_spec,
            shrink_spec,
            pl.BlockSpec((9, CHUNK), lambda c: (0, c)),
        ],
        out_shape=[
            jax.ShapeDtypeStruct((4, GROUP, D), BF),
            jax.ShapeDtypeStruct((4, GROUP, D), BF),
            packed_half(4),
            packed_half(4),
            packed_half(4),
            packed_half(4),
            jax.ShapeDtypeStruct((9, FF), F32),
        ],
        scratch_shapes=[
            pltpu.VMEM((TOK, D), BF),
            pltpu.VMEM((D, TOK), BF),
            pltpu.VMEM((CHUNK, D), BF),
            pltpu.VMEM((D, CHUNK), BF),
            pltpu.VMEM((4, GROUP, CHUNK), F32),
            pltpu.VMEM((4, GROUP, CHUNK), F32),
            pltpu.VMEM((4, GROUP, CHUNK), BF),
            pltpu.VMEM((4, GROUP, CHUNK), BF),
            pltpu.VMEM((4, GROUP, D), F32),
            pltpu.VMEM((4, GROUP, D), F32),
        ],
        compiler_params=params(60),
        cost_estimate=cost(38),
        name="feed",
    )(tag, second, gradient, mods, packed, packed, kernel)


def attend_back_kernel(
    tag_ref, resid, shrunk, d_second, gradient, attn, mods, qkv, lse, proj_t,
    output, d_resid, d_qkv, d_attn_t, item_sums,
    bias, d_mixed, d_attn, sums,
):
    @pl.when(pl.program_id(0) == 0)
    def _():
        bias[...] = item_bias(tag_ref[0])
        sums[...] = jnp.zeros_like(sums)

    def rows_norm(i, _):
        rows = pl.ds(pl.multiple_of(i * 64, 64), 64)
        half = i // 2
        base = resid[0, rows, :]
        normal, factor = norm_stats(base)
        shrunk_rows = shrunk[0, rows, :].astype(F32)
        outward = gradient[0, rows, :].astype(F32)
        d_sec = d_second[0, rows, :].astype(F32)

        def by_item(value):
            return value.reshape(4, 2, 8, D)

        def add(index, value):
            sums[index, pl.ds(2 * half, 2)] += jnp.sum(by_item(value), axis=0)

        gated = (by_item(shrunk_rows) * quadrant_rows(mods, 5, half)).reshape(64, D)
        output[0, rows, :] = (base + gated).astype(BF)
        add(3, outward * shrunk_rows)
        add(1, d_sec)
        add(2, d_sec * normal)
        inner = (by_item(d_sec) * (1.0 + quadrant_rows(mods, 4, half))).reshape(64, D)
        mean = jnp.mean(inner, axis=-1, keepdims=True)
        along = jnp.mean(inner * normal, axis=-1, keepdims=True)
        back = outward + (inner - mean - normal * along) * factor
        d_resid[0, rows, :] = back
        add(0, back * attn[0, rows, :].astype(F32))
        gated = (by_item(back) * quadrant_rows(mods, 2, half)).reshape(64, D)
        d_attn[rows, :] = gated.astype(BF)
        return 0

    lax.fori_loop(0, 4, rows_norm, 0)
    d_attn_t[...] = d_attn[...].T
    d_mixed[...] = dot(proj_t[...], d_attn[...], 1, 1).astype(BF)

    def head(h, _):
        rows = pl.ds(pl.multiple_of(h * HD, HD), HD)
        key_rows = pl.ds(pl.multiple_of(D + h * HD, HD), HD)
        value_rows = pl.ds(pl.multiple_of(2 * D + h * HD, HD), HD)
        queries = qkv[0, rows, :] * jnp.asarray(HD**-0.5, BF)
        keys = qkv[0, key_rows, :]
        values = qkv[0, value_rows, :]
        d_mix = d_mixed[rows, :]
        probs = jnp.exp(dot(keys, queries, 0, 0) + (bias[...] - lse[0, pl.ds(h, 1), :]))
        d_probs = dot(values, d_mix, 0, 0)
        d_qkv[value_rows, :] = dot(d_mix, probs.astype(BF), 1, 1).astype(BF)
        weighted = probs * d_probs
        inner = jnp.sum(weighted, axis=0, keepdims=True)
        d_scores = (weighted - probs * inner).astype(BF)
        d_qkv[rows, :] = (dot(keys, d_scores, 1, 0) * HD**-0.5).astype(BF)
        d_qkv[key_rows, :] = dot(queries, d_scores, 1, 1).astype(BF)
        return 0

    lax.fori_loop(0, H, head, 0, unroll=HEADS)

    @pl.when(pl.program_id(0) == pl.num_programs(0) - 1)
    def _():
        item_sums[...] = jnp.sum(sums[...], axis=2)


def attend_back(part, tag, resid, shrunk, d_second, gradient, attn, mods, qkv, lse, proj_t):
    first, count = PARTS[part]

    def pick_group(*shape):
        return pl.BlockSpec((1,) + shape, lambda g: (first + g,) + (0,) * len(shape))

    return pl.pallas_call(
        attend_back_kernel,
        grid=(count,),
        in_specs=[
            SMEM_SPEC,
            pick_group(GROUP, D),
            pick_group(GROUP, D),
            pick_group(GROUP, D),
            pick_group(GROUP, D),
            pick_group(GROUP, D),
            whole((6, 4, 8, D)),
            pick_group(3 * D, GROUP),
            pick_group(16, GROUP),
            whole((D, D)),
        ],
        out_specs=[
            group_spec(GROUP, D),
            group_spec(GROUP, D),
            pl.BlockSpec((3 * D, GROUP), lambda g: (0, g)),
            pl.BlockSpec((D, GROUP), lambda g: (0, g)),
            whole((4, 4, D)),
        ],
        out_shape=[
            jax.ShapeDtypeStruct((count, GROUP, D), BF),
            jax.ShapeDtypeStruct((count, GROUP, D), F32),
            jax.ShapeDtypeStruct((3 * D, count * GROUP), BF),
            jax.ShapeDtypeStruct((D, count * GROUP), BF),
            jax.ShapeDtypeStruct((4, 4, D), F32),
        ],
        scratch_shapes=[
            pltpu.VMEM((GROUP, GROUP), F32),
            pltpu.VMEM((D, GROUP), BF),
            pltpu.VMEM((GROUP, D), BF),
            pltpu.VMEM((4, 4, 8, D), F32),
        ],
        compiler_params=params(),
        cost_estimate=cost(9 * count),
        name=f"attend_back_{part}",
    )(tag, resid, shrunk, d_second, gradient, attn, mods, qkv, lse, proj_t)


PAIRS = 2
ROWS = 288 * PAIRS


def project_grads_kernel(
    tag_ref, d_qkv0, d_qkv1, d_attn0, d_attn1, conv_in, merged, keep_a, send_a, keep_b, send_b
):
    core = tag_ref[1]

    def against(low, high, field):
        return dot(low[...], field[0], 1, 0) + dot(
            high[...], field[1:4].reshape(3 * GROUP, D), 1, 0
        )

    grad = against(d_qkv0, d_qkv1, conv_in)
    share_out(grad, core, (0, 2), keep_a, send_a)
    share_out(grad, core, (2, 1), keep_b.at[:, :, 0:1], send_b.at[:, :, 0:1])
    grad = against(d_attn0, d_attn1, merged)
    share_out(grad, core, (0, 1), keep_b.at[:, :, 1:2], send_b.at[:, :, 1:2])


def column_specs(rows):
    return [pl.BlockSpec((rows, count * GROUP), lambda i: (i, 0)) for _, count in PARTS]


def project_grads(tag, d_qkv, d_attn, conv_in, merged):
    packed_spec = pl.BlockSpec((PAIRS, NK, 2, UR, UC), lambda i: (i, 0, 0, 0, 0))
    tall = column_specs(ROWS)
    short = column_specs(96 * PAIRS)
    return pl.pallas_call(
        project_grads_kernel,
        grid=(8 // PAIRS,),
        in_specs=[SMEM_SPEC, *tall, *short, whole((4, GROUP, D)), whole((4, GROUP, D))],
        out_specs=[packed_spec] * 4,
        out_shape=[packed_half(2)] * 4,
        compiler_params=params(),
        cost_estimate=cost(8),
        name="project_grads",
    )(tag, *d_qkv, *d_attn, conv_in, merged)


def conv_back_kernel(
    tag_ref, d_qkv0, d_qkv1, weight, norm, mods, kernel, later0, later1, g_ffn,
    d_first, pieces, d_conv, g_kernel, item_sums,
):
    step = pl.program_id(0)

    @pl.when(step == 0)
    def _():
        d_conv[...] = jnp.zeros_like(d_conv)

    d_conv[0] += dot(d_qkv0[...], weight[...], 0, 0)
    d_conv[1:4] += dot(d_qkv1[...], weight[...], 0, 0).reshape(3, GROUP, D)

    @pl.when(step == pl.num_programs(0) - 1)
    def _():
        tag = tag_ref[0]
        left, right = edge_columns(tag)
        keep = 1.0 - tag.astype(F32)

        def lanes(i, _):
            cols = pl.ds(pl.multiple_of(i * 128, 128), 128)
            taps = [jnp.broadcast_to(kernel[t : t + 1, cols], (16, 128)) for t in range(9)]
            sums = [[jnp.zeros((16, 128), F32) for _ in range(2)] for _ in range(2)]

            def load_grad(g, p):
                return d_conv[g, p * 16 : p * 16 + 16, cols]

            def load_field(g, p):
                q = 2 * (p // 8)
                shift = mods[0, q : q + 2, :, cols].reshape(16, 128)
                scale = mods[1, q : q + 2, :, cols].reshape(16, 128)
                return norm[g, p * 16 : p * 16 + 16, cols] * (1.0 + scale) + shift

            def emit(g, p, value):
                rows = slice(p * 16, p * 16 + 16)
                d_first[g, rows, cols] = value
                sums[0][p // 8] += value
                sums[1][p // 8] += value * norm[g, rows, cols]

            grads = conv_back_rows(load_grad, load_field, taps, left, right, keep, emit)
            for t in range(9):
                g_kernel[t : t + 1, cols] = jnp.sum(grads[t], axis=0, keepdims=True)
            for kind in range(2):
                for item in range(4):
                    part = sums[kind][item // 2][8 * (item % 2) : 8 * (item % 2) + 8]
                    item_sums[kind, item : item + 1, cols] = jnp.sum(part, axis=0, keepdims=True)
            return 0

        lax.fori_loop(0, D // 128, lanes, 0)
        later = later0[...] + later1[...]
        rows = [item_sums[i] for i in range(2)] + [later[i] for i in range(4)]
        rows = jnp.concatenate(rows, axis=1)
        alone = jnp.concatenate([jnp.sum(rows, axis=0, keepdims=True), jnp.zeros((3, 6 * D), F32)])
        rows = jnp.where(tag == 1, rows, alone)
        slots, _, width = pieces.shape
        owners = 6 * D // width
        short, long = D // owners, FF // owners
        for j in range(owners):
            filters = jnp.concatenate(
                [
                    g_kernel[:, j * short : (j + 1) * short],
                    g_ffn[:, j * long : (j + 1) * long],
                    jnp.zeros((9, width - short - long), F32),
                ],
                axis=1,
            )
            part = [rows[:, j * width : (j + 1) * width], filters, jnp.zeros((3, width), F32)]
            part = jnp.concatenate(part, axis=0).astype(BF)
            for copy in range(slots // owners):
                pieces[j * (slots // owners) + copy] = part


def conv_back(slots, width, tag, d_qkv, weight, norm, mods, kernel, later, g_ffn):
    return pl.pallas_call(
        conv_back_kernel,
        grid=(8 // PAIRS,),
        in_specs=[
            SMEM_SPEC,
            *column_specs(ROWS),
            pl.BlockSpec((ROWS, D), lambda i: (i, 0)),
            whole((4, GROUP, D)),
            whole((6, 4, 8, D)),
            whole((9, D)),
            whole((4, 4, D)),
            whole((4, 4, D)),
            whole((9, FF)),
        ],
        out_specs=[whole((4, GROUP, D)), whole((slots, 16, width))],
        out_shape=[
            jax.ShapeDtypeStruct((4, GROUP, D), F32),
            jax.ShapeDtypeStruct((slots, 16, width), BF),
        ],
        scratch_shapes=[
            pltpu.VMEM((4, GROUP, D), F32),
            pltpu.VMEM((9, D), F32),
            pltpu.VMEM((2, 4, D), F32),
        ],
        compiler_params=params(),
        cost_estimate=cost(15),
        name="conv_back",
    )(tag, *d_qkv, weight, norm, mods, kernel, *later, g_ffn)


def finish_kernel(
    d_first, norm, factor, d_resid0, d_resid1, output0, output1, mods,
    block_output, input_grad, total,
):
    half = pl.program_id(0) // 2

    for g in range(4):
        base = d_resid1[g - 1] if g else d_resid0[0]
        value = d_first[g]
        normal = norm[g]
        inner = (value.reshape(4, 2, 8, D) * (1.0 + quadrant_rows(mods, 1, half))).reshape(64, D)
        mean = jnp.mean(inner, axis=-1, keepdims=True)
        along = jnp.mean(inner * normal, axis=-1, keepdims=True)
        total[g] = base + (inner - mean - normal * along) * factor[g]
    order = ungroup_matrix()
    grouped = total[...].reshape(256, D)
    high = grouped.astype(BF)
    rest = (grouped - high.astype(F32)).astype(BF)
    input_grad[...] = dot(order, high, 1, 0) + dot(order, rest, 1, 0)
    grouped = jnp.concatenate([output0[...], output1[...]], axis=0).reshape(256, D)
    block_output[...] = dot(order, grouped, 1, 0).astype(BF)


def finish(d_first, norm, factor, d_resid, output, mods):
    def split(groups, width):
        return pl.BlockSpec((groups, 64, width), lambda i: (0, i, 0))

    flat = pl.BlockSpec((256, D), lambda i: (i, 0))
    return pl.pallas_call(
        finish_kernel,
        grid=(4,),
        in_specs=[split(4, D), split(4, D), split(4, 1)]
        + [split(count, D) for _, count in PARTS] * 2
        + [whole((6, 4, 8, D))],
        out_specs=[flat, flat],
        out_shape=[
            jax.ShapeDtypeStruct((TOK, D), BF),
            jax.ShapeDtypeStruct((TOK, D), F32),
        ],
        scratch_shapes=[pltpu.VMEM((4, 64, D), F32)],
        compiler_params=params(),
        cost_estimate=cost(8),
        name="finish",
    )(d_first, norm, factor, *d_resid, *output, mods)


BOTH = ("dp", "fsdp")


def exchange(pieces):
    return lax.all_to_all(pieces, BOTH, 0, 0, tiled=True)


def units_of(weight):
    return weight.T.reshape(-1, UR, UC)


def low_units(shrink):
    return shrink.T.reshape(UR, 4, UC).transpose(1, 0, 2)


def gather_feed(nd, nf, expand, shrink):
    if (nd, nf) == (NJ, NK):
        rows = jnp.concatenate([units_of(expand), low_units(shrink)]).reshape(8 * UR, UC)
        return lax.all_gather(rows, BOTH).reshape(NJ, NK, 8, UR, UC)
    low = full_rows(shrink).reshape(NJ, UR, NK, 4, UC).transpose(0, 2, 3, 1, 4)
    return jnp.concatenate([all_units(full_rows(expand), 4), low], axis=2)


def full_rows(shard):
    rows = lax.all_gather(shard.T, "fsdp", axis=1, tiled=True)
    return lax.all_gather(rows, "dp", axis=0, tiled=True)


def all_units(weight, units):
    return weight.reshape(NJ, units, UR, NK, UC).transpose(0, 3, 1, 2, 4)


def project_turns(own):
    turns = [
        lax.ppermute(own, "dp", [(i, (i - 4 * step) % NJ) for i in range(NJ)])
        for step in range(1, 4)
    ]
    return turns


def widen(a, b, bit_a, bit_b):
    return jnp.stack([a, swap(a, bit_a)]), jnp.stack([b, swap(b, bit_b)])


def all_projections(qkv, proj):
    units = jnp.concatenate([all_units(full_rows(qkv), 3), all_units(full_rows(proj), 1)], axis=2)
    units = units.reshape((4, 2, 2) + units.shape[1:])
    first, rest = units[:, :, :, :, :2], units[:, :, :, :, 2:]
    a, b = first.transpose(2, 3, 1, 0, 4, 5, 6), rest.transpose(2, 1, 3, 0, 4, 5, 6)
    return a[0], b[0], a[1], b[1]


def pick(grads, index, axis):
    return lax.dynamic_index_in_dim(grads, index, axis, keepdims=False)


def swap(value, bit):
    if bit is None:
        return lax.ppermute(value, "fsdp", [(0, 1), (1, 0)])
    return lax.ppermute(value, "dp", [(i, i ^ bit) for i in range(NJ)])


def halve(keep, got, axis, bit):
    mine = lax.axis_index("fsdp") if bit is None else (lax.axis_index("dp") // bit) % 2
    kept = pick(keep, mine, axis) + pick(got, mine, axis)
    return kept, pick(keep, 1 - mine, axis) + pick(got, 1 - mine, axis)


def last_sends(total):
    place = lax.axis_index("dp") // 4
    return [pick(total, (place + step) % 4, 0) for step in range(1, 4)]


def last_swaps(sends):
    return [
        lax.ppermute(sent, "dp", [(i, (i + 4 * step) % NJ) for i in range(NJ)])
        for step, sent in enumerate(sends, 1)
    ]


def last_sum(total, got):
    own = pick(total, lax.axis_index("dp") // 4, 0).astype(F32)
    for value in got:
        own = own + value.astype(F32)
    return own


def after(value, *others):
    return lax.optimization_barrier((value,) + others)[0]


def own_shard(nd, nf, kind, units):
    if (nd, nf) == (NJ, NK):
        if kind == "shrink":
            return units.transpose(1, 0, 2).reshape(UR, 4 * UC).T
        return units.reshape(-1, UC).T
    if kind == "shrink":
        weight = units.transpose(0, 3, 1, 2, 4).reshape(NJ * UR, -1)
    else:
        weight = units.transpose(0, 2, 3, 1, 4).reshape(-1, NK * UC)
    columns = lax.psum_scatter(weight, "dp", scatter_dimension=0, tiled=True)
    piece = lax.psum_scatter(columns, "fsdp", scatter_dimension=1, tiled=True)
    return piece.astype(F32).T


def both_cores(keep, send):
    return jnp.stack([keep, send], axis=1).reshape((-1,) + keep.shape[1:])


def look_up(ids, step_table, class_table):
    first_row = lax.axis_index("fsdp") * step_table.shape[0]
    own = first_row + jnp.arange(step_table.shape[0], dtype=jnp.int32)
    step_hot = (ids[:, :4].reshape(-1, 1) == own[None, :]).astype(BF)
    class_hot = (ids[:, 4:].reshape(-1, 1) == own[None, :]).astype(BF)
    return step_hot, class_hot, dot(step_table, step_hot, 0, 1) + dot(class_table, class_hot, 0, 1)


def share_act(nd, cond, attn_kernel, ffn_kernel, beside):
    width, items = cond.shape
    act = jax.nn.silu(cond).astype(BF)
    filters = jnp.concatenate([attn_kernel, ffn_kernel], axis=1).reshape(-1)
    size = filters.shape[0]
    filters = jnp.pad(filters, (0, -size % items)).reshape(-1, items)
    sent = jnp.concatenate([act, filters], axis=0)[None]
    sent = lax.all_to_all(jnp.broadcast_to(sent, (nd,) + sent.shape[1:]), "dp", 0, 0, tiled=True)
    sent = after(sent, *beside)
    act_all = sent[:, :width].reshape(nd * width, items)
    filters = sent[:, width:].reshape(nd, -1)[:, :size]
    filters = filters.reshape(nd, 9, -1).astype(F32)
    attn_full = filters[:, :, : attn_kernel.shape[1]].transpose(1, 0, 2).reshape(9, -1)
    ffn_full = filters[:, :, attn_kernel.shape[1] :].transpose(1, 0, 2).reshape(9, -1)
    return act_all, attn_full, ffn_full


def exchange_columns(nd, nf, d_act):
    rows, items = d_act.shape
    half = lax.axis_index("fsdp")
    if (nd, nf) == (NJ, NK):
        spread = jnp.zeros((nd, 2 * rows // nd, items), BF)
        own = d_act.astype(BF).reshape(nd // 2, 2 * rows // nd, items)
        spread = lax.dynamic_update_slice_in_dim(spread, own, half * (nd // 2), axis=0)
        return lax.all_to_all(spread, "dp", 0, 0, tiled=True)
    spread = jnp.zeros((rows * nf, items), F32)
    spread = lax.dynamic_update_slice_in_dim(spread, d_act, half * rows, axis=0)
    spread = spread.reshape(nd, 1, -1, items)
    spread = jnp.broadcast_to(spread, (nd, nf) + spread.shape[2:])
    return exchange(spread.reshape((nd * nf,) + spread.shape[2:]))


def own_columns(nd, nf, terms):
    part = terms.astype(F32).sum(axis=0)
    if (nd, nf) != (NJ, NK):
        return part
    return part + swap(part, None)


def body(
    latents, size_tags, timesteps, classes, step_table, class_table, modulation_weight,
    attn_kernel, qkv_weight, proj_weight, expand_weight, ffn_kernel, shrink_weight, cotangent,
    *, nd, nf,
):
    slots = nd * nf
    tag = size_tags[0]
    square = (nd, nf) == (NJ, NK)
    if square:
        place = lax.axis_index("dp")
        where = [tag, place % 2, place // 4, (place // 2) % 2, lax.axis_index("fsdp")]
        where = jnp.stack(where).astype(jnp.int32)
    else:
        where = jnp.stack([tag] + [jnp.int32(0)] * 4)
    packed = gather_feed(nd, nf, expand_weight, shrink_weight)
    tokens, gradient, norm, factor = prepare(latents, cotangent)
    mine = jnp.concatenate([timesteps[0], classes[0]])[None]
    mine = jnp.broadcast_to(mine, (slots, 8))
    if square:
        own = jnp.concatenate([units_of(qkv_weight), units_of(proj_weight)])
        own = after(own, mine)
        turns = project_turns(own)
    ids = exchange(mine)
    if square:
        ids = after(ids, norm)
    step_hot, class_hot, part = look_up(ids, step_table, class_table)
    if square:
        cond = part + swap(part, None)
        own, *turns = (after(x, cond) for x in (own, *turns))
        a = jnp.stack([own[:2]] + [turn[:2] for turn in turns])
        b = jnp.stack([own[2:]] + [turn[2:] for turn in turns])
        next_a, next_b = swap(a, 2), swap(b, None)
        a, b = jnp.stack([a, next_a]), jnp.stack([b, next_b])
        beside = (a, b)
    else:
        beside = ()
        cond = lax.psum(part, "fsdp")
    act_all, attn_full, ffn_full = share_act(nd, cond, attn_kernel, ffn_kernel, beside)
    if square:
        next_a, next_b = swap(a, None), swap(b, 2)
        next_a, next_b = after(next_a, act_all), after(next_b, act_all)
    height, width = modulation_weight.shape
    act_rows = lax.dynamic_slice_in_dim(
        act_all, lax.axis_index("fsdp") * height, height, axis=0
    )
    terms = dot(act_rows, modulation_weight, 0, 0)
    terms = exchange(terms.reshape(slots, 1, 4 * width)).reshape(nd, nf, 4, width)
    if square:
        a, b = jnp.stack([a, next_a]), jnp.stack([b, next_b])
        projections = (a, b, swap(a, 1), swap(b, 1))
    else:
        projections = all_projections(qkv_weight, proj_weight)
    mod_rows = terms.sum(axis=1).transpose(1, 0, 2).reshape(4, nd * width)
    chosen = jnp.where(tag == 1, mod_rows, mod_rows[:1])
    mods = jnp.broadcast_to(chosen.reshape(4, 6, 1, D).transpose(1, 0, 2, 3), (6, 4, 8, D))

    conv_in = first_conv(size_tags, norm, mods, attn_full)
    qkv, merged, attn, resid, second, lse, proj_t, full_qkv = attend(
        where, conv_in, tokens, mods, projections
    )
    shrunk, d_second, keep_e, send_e, keep_s, send_s, g_ffn = feed(
        where, second, gradient, mods, packed, ffn_full
    )
    back = (gradient, attn, mods, qkv, lse)
    if square:
        got_e, got_s = swap(send_e, 1), swap(send_s, 1)
    output0, d_resid0, d_qkv0, d_attn0, later0 = attend_back(
        0, where, resid, shrunk, d_second, *back, proj_t
    )

    def grid(value):
        return value.reshape((4, 2) + value.shape[1:])

    if square:
        got_e, got_s = after(got_e, d_qkv0), after(got_s, d_qkv0)
        keep_e, out_e = halve(grid(keep_e), grid(got_e), 2, None)
        keep_s, out_s = halve(grid(keep_s), grid(got_s), 1, 2)
        d_second = after(d_second, out_e, out_s)
        got_e, got_s = swap(out_e, None), swap(out_s, 2)
    output1, d_resid1, d_qkv1, d_attn1, later1 = attend_back(
        1, where, resid, shrunk, d_second, *back, proj_t
    )
    if square:
        got_e, got_s = after(got_e, d_attn1), after(got_s, d_attn1)
        keep_e, out_e = halve(keep_e, got_e, 1, 2)
        keep_s, out_s = halve(keep_s, got_s, 1, None)
        d_attn0 = after(d_attn0, out_e, out_s)
        got_e, got_s = swap(out_e, 2), swap(out_s, None)
    d_qkv = (d_qkv0, d_qkv1)
    keep_a, send_a, keep_b, send_b = project_grads(
        where, d_qkv, (d_attn0, d_attn1), conv_in, merged
    )
    if square:
        got_e, got_s = after(got_e, keep_a), after(got_s, keep_a)
        got_a, got_b = swap(send_a, 1), swap(send_b, 1)
        e = halve(keep_e.reshape((2, 2) + keep_e.shape[1:]), got_e.reshape((2, 2) + got_e.shape[1:]), 1, 4)
        s = halve(keep_s.reshape((2, 2) + keep_s.shape[1:]), got_s.reshape((2, 2) + got_s.shape[1:]), 1, 4)
        feeding, out_f = (jnp.concatenate(pair, axis=1) for pair in zip(e, s))
        keep_a, out_a = halve(grid(keep_a), grid(got_a), 2, None)
        keep_b, out_b = halve(grid(keep_b), grid(got_b), 1, 2)
        full_qkv = after(full_qkv, out_a, out_b, out_f)
        got_a, got_b, got_f = swap(out_a, None), swap(out_b, 2), swap(out_f, 4)
    d_first, pieces = conv_back(
        slots, width, where, d_qkv, full_qkv, norm, mods, attn_full, (later0, later1), g_ffn
    )
    if square:
        got_a, got_b, got_f = (after(x, d_first) for x in (got_a, got_b, got_f))
        keep_a, out_a = halve(keep_a, got_a, 1, 2)
        keep_b, out_b = halve(keep_b, got_b, 1, None)
        feeding, out_f = halve(feeding, got_f, 0, 8)
    if square:
        d_first = after(d_first, out_a, out_b, out_f, pieces)
        got_a, got_b, got_f = swap(out_a, 2), swap(out_b, None), swap(out_f, 8)
    got = exchange(pieces)
    block_output, input_grad = finish(
        d_first, norm, factor, (d_resid0, d_resid1), (output0, output1), mods
    )
    if square:
        got = after(got, input_grad)
    d_mod_all = got[:, :4].reshape(slots * 4, width)
    d_act = dot(modulation_weight, d_mod_all, 1, 1)
    if square:
        got_a, got_b = after(got_a, d_act), after(got_b, d_act)
        total = jnp.concatenate([keep_a + got_a, keep_b + got_b], axis=1)
        sends = last_sends(total)
        last = last_swaps(sends)
    own_act = exchange_columns(nd, nf, d_act)
    if square:
        got_f = after(got_f, own_act)
        total = last_sum(total, last)
        feeding = feeding.astype(F32) + got_f.astype(F32)
        cuts = [total[:3], total[3:], feeding[:4], feeding[4:]]
    else:
        first, rest = both_cores(keep_a, send_a), both_cores(keep_b, send_b)
        cuts = [
            jnp.concatenate([first, rest[:, :, :1]], axis=2),
            rest[:, :, 1:],
            both_cores(keep_e, send_e),
            both_cores(keep_s, send_s),
        ]
    shards = [
        own_shard(nd, nf, kind, cut)
        for kind, cut in zip(("qkv", "proj", "expand", "shrink"), cuts)
    ]
    cut = attn_kernel.shape[1]
    filters = got[:, 4:13, : cut + ffn_kernel.shape[1]].astype(F32).sum(axis=0)
    modulation_grad = dot(act_rows, d_mod_all, 1, 0)
    gate = jax.nn.sigmoid(cond)
    d_cond = own_columns(nd, nf, own_act)
    d_cond = d_cond * (gate * (1.0 + cond * (1.0 - gate)))

    def table_grad(hot):
        return lax.dot_general(
            hot.astype(F32), d_cond, (((0,), (1,)), ((), ())), precision=lax.Precision.HIGHEST
        )

    return (
        block_output,
        input_grad,
        table_grad(step_hot),
        table_grad(class_hot),
        modulation_grad,
        filters[:, :cut],
        shards[0],
        shards[1],
        shards[2],
        filters[:, cut:],
        shards[3],
    )


def solution(mesh):
    matrix = P("fsdp", "dp")
    rows = P(BOTH, None)
    filters = P(None, "dp")
    in_specs = (
        rows, P(BOTH), rows, rows, matrix, matrix, matrix, filters, matrix, matrix, matrix,
        filters, matrix, rows,
    )
    out_specs = (
        rows, rows, matrix, matrix, matrix, filters, matrix, matrix, matrix, filters, matrix,
    )
    run = functools.partial(body, nd=mesh.shape["dp"], nf=mesh.shape["fsdp"])
    return jax.shard_map(run, mesh=mesh, in_specs=in_specs, out_specs=out_specs, check_vma=False)
```

```python
import functools

import jax
import jax.numpy as jnp
from jax import lax
from jax.experimental import pallas as pl
from jax.experimental.pallas import tpu as pltpu
from jax.sharding import PartitionSpec as P

D = 768
H = 12
HD = 64
FF = 3072
SIDE = 32
GROUP = 256
TOK = SIDE * SIDE
EPS = 1e-06
NJ, NK, UR, UC = 16, 2, 48, 384
CHUNK = 768
HEADS = 6
PARTS = ((0, 1), (1, 3))
MIB = 1024 * 1024
BF = jnp.bfloat16
F32 = jnp.float32
GELU_A = 0.7978845608028654
GELU_B = GELU_A * 0.044715


def dot(left, right, left_dim, right_dim):
    return lax.dot_general(
        left, right, (((left_dim,), (right_dim,)), ((), ())), preferred_element_type=F32
    )


def params(limit=56):
    return pltpu.CompilerParams(vmem_limit_bytes=limit * MIB)


def cost(micros):
    return pl.CostEstimate(flops=int(micros * 1e8), transcendentals=0, bytes_accessed=4 * MIB)


def whole(shape):
    zeros = (0,) * len(shape)
    return pl.BlockSpec(shape, lambda *ids: zeros, pipeline_mode=pl.Buffered(1))


SMEM_SPEC = pl.BlockSpec(memory_space=pltpu.SMEM)


def group_place(natural):
    pair, odd_row = natural // 64, (natural // 32) % 2
    column, odd_column = (natural % 32) // 2, natural % 2
    return (2 * odd_row + odd_column) * 64 + pair * 16 + column


def ungroup_matrix():
    natural = lax.broadcasted_iota(jnp.int32, (256, 256), 0)
    grouped = lax.broadcasted_iota(jnp.int32, (256, 256), 1)
    return jnp.where(group_place(natural) == grouped, 1.0, 0.0).astype(BF)


def group_matrix():
    natural = lax.broadcasted_iota(jnp.int32, (256, 256), 1)
    grouped = lax.broadcasted_iota(jnp.int32, (256, 256), 0)
    return jnp.where(group_place(natural) == grouped, 1.0, 0.0).astype(BF)


def norm_stats(values):
    centre = values - jnp.mean(values, axis=-1, keepdims=True)
    variance = jnp.mean(centre * centre, axis=-1, keepdims=True)
    scale = lax.rsqrt(variance + EPS)
    return centre * scale, scale


def prepare_kernel(latents, cotangent, tokens, gradient, norm, scale):
    order = group_matrix()
    gathered = dot(order, latents[...], 1, 0)
    gradient[...] = dot(order, cotangent[...], 1, 0).reshape(4, 64, D).astype(BF)
    tokens[...] = gathered.reshape(4, 64, D).astype(BF)
    normal, factor = norm_stats(gathered)
    norm[...] = normal.reshape(4, 64, D)
    scale[...] = factor.reshape(4, 64, 1)


def prepare(latents, cotangent):
    flat = pl.BlockSpec((256, D), lambda i: (i, 0))
    split = pl.BlockSpec((4, 64, D), lambda i: (0, i, 0))
    return pl.pallas_call(
        prepare_kernel,
        grid=(4,),
        in_specs=[flat, flat],
        out_specs=[split, split, split, pl.BlockSpec((4, 64, 1), lambda i: (0, i, 0))],
        out_shape=[
            jax.ShapeDtypeStruct((4, GROUP, D), BF),
            jax.ShapeDtypeStruct((4, GROUP, D), BF),
            jax.ShapeDtypeStruct((4, GROUP, D), F32),
            jax.ShapeDtypeStruct((4, GROUP, 1), F32),
        ],
        compiler_params=params(),
        cost_estimate=cost(6),
        name="prepare",
    )(latents, cotangent)


def edge_columns(tag):
    place = lax.broadcasted_iota(jnp.int32, (16, 128), 0)
    left = jnp.where((place == 0) | ((place == 8) & (tag == 1)), 0.0, 1.0)
    right = jnp.where((place == 15) | ((place == 7) & (tag == 1)), 0.0, 1.0)
    return left, right


def neighbours(even, odd, left, right):
    return pltpu.roll(odd, 1, 0) * left, pltpu.roll(even, 15, 0) * right


def conv_rows(load, kernel, left, right, keep, emit):
    above = None
    partial = None
    for row in range(SIDE + 1):
        taps = None
        if row < SIDE:
            a, p = row % 2, row // 2
            even, odd = load(2 * a, p), load(2 * a + 1, p)
            odd_left, even_right = neighbours(even, odd, left, right)
            taps = []
            for tap in range(3):
                k = [kernel[3 * tap + b] for b in range(3)]
                taps.append(
                    (
                        k[0] * odd_left + k[1] * even + k[2] * odd,
                        k[0] * even + k[1] * odd + k[2] * even_right,
                    )
                )
        crossing = row == SIDE // 2
        if partial is not None:
            a, p = (row - 1) % 2, (row - 1) // 2
            for b in range(2):
                value = partial[b]
                if taps is not None:
                    below = taps[2][b]
                    value = value + (below * keep if crossing else below)
                emit(2 * a + b, p, value)
        if taps is not None:
            partial = []
            for b in range(2):
                value = taps[1][b]
                if above is not None:
                    value = value + (above[b] * keep if crossing else above[b])
                partial.append(value)
            above = taps[0]


def conv_back_rows(load_grad, load_field, kernel, left, right, keep, emit):
    sums = [jnp.zeros((16, 128), F32) for _ in range(9)]
    from_above = None
    partial = None
    field_above = None
    field = (load_field(0, 0), load_field(1, 0))
    for row in range(SIDE + 1):
        crossing = row == SIDE // 2
        taps = None
        if row < SIDE:
            a, p = row % 2, row // 2
            even, odd = load_grad(2 * a, p), load_grad(2 * a + 1, p)
            odd_left, even_right = neighbours(even, odd, left, right)
            picks = ((odd, even, odd_left), (even_right, odd, even))
            taps = []
            for tap in range(3):
                k = [kernel[3 * tap + b] for b in range(3)]
                taps.append(
                    tuple(k[0] * x[0] + k[1] * x[1] + k[2] * x[2] for x in picks)
                )
            field_below = None
            if row + 1 < SIDE:
                a, p = (row + 1) % 2, (row + 1) // 2
                field_below = (load_field(2 * a, p), load_field(2 * a + 1, p))
            for tap, rows in enumerate((field_above, field, field_below)):
                if rows is None:
                    continue
                if (tap == 0 and crossing) or (tap == 2 and row + 1 == SIDE // 2):
                    rows = (rows[0] * keep, rows[1] * keep)
                for b in range(3):
                    sums[3 * tap + b] = (
                        sums[3 * tap + b] + rows[0] * picks[0][b] + rows[1] * picks[1][b]
                    )
            field_above, field = field, field_below
        if partial is not None:
            a, p = (row - 1) % 2, (row - 1) // 2
            for b in range(2):
                value = partial[b]
                if taps is not None:
                    value = value + (taps[0][b] * keep if crossing else taps[0][b])
                emit(2 * a + b, p, value)
        if taps is not None:
            partial = []
            for b in range(2):
                value = taps[1][b]
                if from_above is not None:
                    value = value + (from_above[b] * keep if crossing else from_above[b])
                partial.append(value)
            from_above = taps[2]
    return sums


def first_conv_kernel(tag_ref, norm, mods, kernel, out):
    tag = tag_ref[0]
    left, right = edge_columns(tag)
    keep = 1.0 - tag.astype(F32)

    def lanes(i, _):
        cols = pl.ds(pl.multiple_of(i * 128, 128), 128)
        taps = [jnp.broadcast_to(kernel[t : t + 1, cols], (16, 128)) for t in range(9)]

        def load(g, p):
            q = 2 * (p // 8)
            shift = mods[0, q : q + 2, :, cols].reshape(16, 128)
            scale = mods[1, q : q + 2, :, cols].reshape(16, 128)
            return norm[g, p * 16 : p * 16 + 16, cols] * (1.0 + scale) + shift

        def emit(g, p, value):
            out[g, p * 16 : p * 16 + 16, cols] = value.astype(BF)

        conv_rows(load, taps, left, right, keep, emit)
        return 0

    lax.fori_loop(0, 2, lanes, 0)


def first_conv(tag, norm, mods, kernel):
    lanes = pl.BlockSpec((4, GROUP, 256), lambda i: (0, 0, i))
    return pl.pallas_call(
        first_conv_kernel,
        grid=(D // 256,),
        in_specs=[
            SMEM_SPEC,
            lanes,
            pl.BlockSpec((2, 4, 8, 256), lambda i: (0, 0, 0, i)),
            pl.BlockSpec((9, 256), lambda i: (0, i)),
        ],
        out_specs=lanes,
        out_shape=jax.ShapeDtypeStruct((4, GROUP, D), BF),
        compiler_params=params(),
        cost_estimate=cost(6),
        name="first_conv",
    )(tag, norm, mods, kernel)


def join_rows(block, target):
    rows = block.shape[0] * block.shape[2] * UR
    for k in range(NK):
        target[:, k * UC : (k + 1) * UC] = block[:, k].reshape(rows, UC)


def share_out(rows, core, units, keep, send):
    first, count = units
    for k in range(NK):
        part = rows[:, k * UC : (k + 1) * UC].astype(BF)
        part = part.reshape(-1, 2, part.shape[0] // (keep.shape[0] * 2), UC)
        even, odd = part[:, 0], part[:, 1]
        for target, value in (
            (keep, jnp.where(core == 0, even, odd)),
            (send, jnp.where(core == 0, odd, even)),
        ):
            whole_units = value.reshape(value.shape[0], -1, UR, UC)
            target[:, k] = whole_units[:, first : first + count]


def quadrant_rows(mods, index, half):
    return mods[index, pl.ds(2 * half, 2)].reshape(1, 2, 8, D)


def item_bias(tag):
    def label(dim):
        place = lax.broadcasted_iota(jnp.int32, (GROUP, GROUP), dim)
        return 2 * (place // 128) + (place % 16) // 8

    return jnp.where((label(0) == label(1)) | (tag == 0), 0.0, -1e30)


def attend_kernel(
    where, conv_in, tokens, mods, own_a, own_b, peer_a, peer_b,
    qkv, merged, attn, resid, second, lse, proj_t, full_qkv,
    full_proj, bias, mixed_t,
):
    @pl.when(pl.program_id(0) == 0)
    def _():
        core, z, y, x = (where[i] for i in range(1, 5))
        for owner in range(NJ):
            step = (owner // 4 - z + 4) % 4
            side = (owner // 2) % 2 ^ y
            mine = core == owner % 2
            for k in range(NK):
                cols = slice(k * UC, (k + 1) * UC)
                a = jnp.where(mine, own_a[k ^ x, side, step], peer_a[k ^ x, side, step])
                b = jnp.where(mine, own_b[side, k ^ x, step], peer_b[side, k ^ x, step])
                start = owner * 3 * UR
                full_qkv[start : start + 2 * UR, cols] = a.reshape(2 * UR, UC)
                full_qkv[start + 2 * UR : start + 3 * UR, cols] = b[0]
                full_proj[owner * UR : (owner + 1) * UR, cols] = b[1]
        proj_t[...] = full_proj[...].T
        bias[...] = item_bias(where[0])

    qkv[0] = dot(full_qkv[...], conv_in[0], 1, 1).astype(BF)

    def head(h, _):
        rows = pl.ds(pl.multiple_of(h * HD, HD), HD)
        queries = qkv[0, rows, :] * jnp.asarray(HD**-0.5, BF)
        keys = qkv[0, pl.ds(pl.multiple_of(D + h * HD, HD), HD), :]
        values = qkv[0, pl.ds(pl.multiple_of(2 * D + h * HD, HD), HD), :]
        scores = dot(keys, queries, 0, 0) + bias[...]
        highest = jnp.max(scores, axis=0, keepdims=True)
        raised = jnp.exp(scores - highest)
        total = jnp.sum(raised, axis=0, keepdims=True)
        probs = (raised * (1.0 / total)).astype(BF)
        lse[0, pl.ds(h, 1), :] = highest + jnp.log(total)
        mixed_t[rows, :] = dot(values, probs, 1, 0).astype(BF)
        return 0

    lax.fori_loop(0, H, head, 0, unroll=HEADS)
    merged[0] = mixed_t[...].T
    projected = dot(merged[0], full_proj[...], 1, 1)
    attn[0] = projected.astype(BF)
    gate = mods[2].reshape(2, 1, 2, 8, D)
    resid[0] = (
        tokens[0].astype(F32) + (projected.reshape(2, 8, 2, 8, D) * gate).reshape(GROUP, D)
    )

    def rows_norm(i, _):
        rows = pl.ds(pl.multiple_of(i * 64, 64), 64)
        normal, _ = norm_stats(resid[0, rows, :])
        half = i // 2
        scaled = normal.reshape(4, 2, 8, D) * (1.0 + quadrant_rows(mods, 4, half))
        value = scaled + quadrant_rows(mods, 3, half)
        second[0, rows, :] = value.reshape(64, D).astype(BF)
        return 0

    lax.fori_loop(0, 4, rows_norm, 0)


def group_spec(*shape):
    return pl.BlockSpec((1,) + shape, lambda g: (g,) + (0,) * len(shape))


def attend(where, conv_in, tokens, mods, projections):
    relative = (2, 2, 4, 2, UR, UC)
    return pl.pallas_call(
        attend_kernel,
        grid=(4,),
        in_specs=[
            SMEM_SPEC,
            group_spec(GROUP, D),
            group_spec(GROUP, D),
            whole((6, 4, 8, D)),
        ]
        + [whole(relative)] * 4,
        out_specs=[
            group_spec(3 * D, GROUP),
            group_spec(GROUP, D),
            group_spec(GROUP, D),
            group_spec(GROUP, D),
            group_spec(GROUP, D),
            group_spec(16, GROUP),
            whole((D, D)),
            whole((3 * D, D)),
        ],
        out_shape=[
            jax.ShapeDtypeStruct((4, 3 * D, GROUP), BF),
            jax.ShapeDtypeStruct((4, GROUP, D), BF),
            jax.ShapeDtypeStruct((4, GROUP, D), BF),
            jax.ShapeDtypeStruct((4, GROUP, D), F32),
            jax.ShapeDtypeStruct((4, GROUP, D), BF),
            jax.ShapeDtypeStruct((4, 16, GROUP), F32),
            jax.ShapeDtypeStruct((D, D), BF),
            jax.ShapeDtypeStruct((3 * D, D), BF),
        ],
        scratch_shapes=[
            pltpu.VMEM((D, D), BF),
            pltpu.VMEM((GROUP, GROUP), F32),
            pltpu.VMEM((D, GROUP), BF),
        ],
        compiler_params=params(),
        cost_estimate=cost(38),
        name="attend",
    )(where, conv_in, tokens, mods, *projections)


def feed_kernel(
    tag_ref, second, gradient, mods, w_expand, w_shrink, kernel,
    shrunk, d_second, keep_expand, send_expand, keep_shrink, send_shrink, g_kernel,
    d_shrunk, d_shrunk_t, expand, shrink, field, slope, hidden, d_field, shrunk_sum, second_sum,
):
    step = pl.program_id(0)
    tag, core = tag_ref[0], tag_ref[1]

    @pl.when(step == 0)
    def _():
        gate = mods[5].reshape(1, 2, 1, 2, 8, D)
        value = gradient[...].astype(F32).reshape(4, 2, 8, 2, 8, D) * gate
        d_shrunk[...] = value.reshape(TOK, D).astype(BF)
        d_shrunk_t[...] = d_shrunk[...].T
        shrunk_sum[...] = jnp.zeros_like(shrunk_sum)
        second_sum[...] = jnp.zeros_like(second_sum)

    join_rows(w_expand, expand)
    for q in range(2):
        shrink[:, q * UC : (q + 1) * UC] = w_shrink[:, 0, q].reshape(D, UC)
    left, right = edge_columns(tag)
    keep = 1.0 - tag.astype(F32)
    field[...] = dot(second[...].reshape(TOK, D), expand[...], 1, 1).reshape(4, GROUP, CHUNK)
    slope[...] = dot(d_shrunk[...], shrink[...], 1, 0).reshape(4, GROUP, CHUNK)

    def lanes(i, _):
        cols = pl.ds(pl.multiple_of(i * 128, 128), 128)
        taps = [jnp.broadcast_to(kernel[t : t + 1, cols], (16, 128)) for t in range(9)]

        def load(g, p):
            return field[g, p * 16 : p * 16 + 16, cols]

        def load_slope(g, p):
            return slope[g, p * 16 : p * 16 + 16, cols]

        def emit(g, p, value):
            square = value * value
            half = 0.5 + 0.5 * jnp.tanh(value * (GELU_A + GELU_B * square))
            out = value * half
            hidden[g, p * 16 : p * 16 + 16, cols] = out.astype(BF)
            rate = half + (out - out * half) * (2.0 * GELU_A + 6.0 * GELU_B * square)
            slope[g, p * 16 : p * 16 + 16, cols] = load_slope(g, p) * rate

        conv_rows(load, taps, left, right, keep, emit)

        def emit_back(g, p, value):
            d_field[g, p * 16 : p * 16 + 16, cols] = value.astype(BF)

        sums = conv_back_rows(load_slope, load, taps, left, right, keep, emit_back)
        for t in range(9):
            g_kernel[t : t + 1, cols] = jnp.sum(sums[t], axis=0, keepdims=True)
        return 0

    lax.fori_loop(0, CHUNK // 128, lanes, 0)
    hid = hidden[...].reshape(TOK, CHUNK)
    d_fld = d_field[...].reshape(TOK, CHUNK)
    grad = dot(d_shrunk_t[...], hid, 1, 0).astype(BF)
    for q in range(2):
        part = grad[:, q * UC : (q + 1) * UC].reshape(NJ // 2, 2, UR, UC)
        keep_shrink[:, 0, q] = jnp.where(core == 0, part[:, 0], part[:, 1])
        send_shrink[:, 0, q] = jnp.where(core == 0, part[:, 1], part[:, 0])
    share_out(dot(d_fld, second[...].reshape(TOK, D), 0, 0), core, (0, 4), keep_expand, send_expand)
    shrunk_sum[...] += dot(hid, shrink[...], 1, 1).reshape(4, GROUP, D)
    second_sum[...] += dot(d_fld, expand[...], 1, 0).reshape(4, GROUP, D)

    @pl.when(step == pl.num_programs(0) - 1)
    def _():
        shrunk[...] = shrunk_sum[...].astype(BF)
        d_second[...] = second_sum[...].astype(BF)


def packed_half(units):
    return jax.ShapeDtypeStruct((NJ // 2, NK, units, UR, UC), BF)


def feed(tag, second, gradient, mods, packed, kernel):
    half = NJ // 2
    expand_spec = pl.BlockSpec((2, NK, 4, UR, UC), lambda c: (c, 0, 0, 0, 0))
    shrink_spec = pl.BlockSpec((half, 1, 2, UR, UC), lambda c: (0, c // 2, c % 2, 0, 0))
    return pl.pallas_call(
        feed_kernel,
        grid=(FF // CHUNK,),
        in_specs=[
            SMEM_SPEC,
            whole((4, GROUP, D)),
            whole((4, GROUP, D)),
            whole((6, 4, 8, D)),
            pl.BlockSpec((4, NK, 4, UR, UC), lambda c: (c, 0, 0, 0, 0)),
            pl.BlockSpec((NJ, 1, 2, UR, UC), lambda c: (0, c // 2, 2 + c % 2, 0, 0)),
            pl.BlockSpec((9, CHUNK), lambda c: (0, c)),
        ],
        out_specs=[
            whole((4, GROUP, D)),
            whole((4, GROUP, D)),
            expand_spec,
            expand_spec,
            shrink_spec,
            shrink_spec,
            pl.BlockSpec((9, CHUNK), lambda c: (0, c)),
        ],
        out_shape=[
            jax.ShapeDtypeStruct((4, GROUP, D), BF),
            jax.ShapeDtypeStruct((4, GROUP, D), BF),
            packed_half(4),
            packed_half(4),
            packed_half(4),
            packed_half(4),
            jax.ShapeDtypeStruct((9, FF), F32),
        ],
        scratch_shapes=[
            pltpu.VMEM((TOK, D), BF),
            pltpu.VMEM((D, TOK), BF),
            pltpu.VMEM((CHUNK, D), BF),
            pltpu.VMEM((D, CHUNK), BF),
            pltpu.VMEM((4, GROUP, CHUNK), F32),
            pltpu.VMEM((4, GROUP, CHUNK), F32),
            pltpu.VMEM((4, GROUP, CHUNK), BF),
            pltpu.VMEM((4, GROUP, CHUNK), BF),
            pltpu.VMEM((4, GROUP, D), F32),
            pltpu.VMEM((4, GROUP, D), F32),
        ],
        compiler_params=params(60),
        cost_estimate=cost(38),
        name="feed",
    )(tag, second, gradient, mods, packed, packed, kernel)


def attend_back_kernel(
    tag_ref, resid, shrunk, d_second, gradient, attn, mods, qkv, lse, proj_t,
    output, d_resid, d_qkv, d_attn_t, item_sums,
    bias, d_mixed, d_attn, sums,
):
    @pl.when(pl.program_id(0) == 0)
    def _():
        bias[...] = item_bias(tag_ref[0])
        sums[...] = jnp.zeros_like(sums)

    def rows_norm(i, _):
        rows = pl.ds(pl.multiple_of(i * 64, 64), 64)
        half = i // 2
        base = resid[0, rows, :]
        normal, factor = norm_stats(base)
        shrunk_rows = shrunk[0, rows, :].astype(F32)
        outward = gradient[0, rows, :].astype(F32)
        d_sec = d_second[0, rows, :].astype(F32)

        def by_item(value):
            return value.reshape(4, 2, 8, D)

        def add(index, value):
            sums[index, pl.ds(2 * half, 2)] += jnp.sum(by_item(value), axis=0)

        gated = (by_item(shrunk_rows) * quadrant_rows(mods, 5, half)).reshape(64, D)
        output[0, rows, :] = (base + gated).astype(BF)
        add(3, outward * shrunk_rows)
        add(1, d_sec)
        add(2, d_sec * normal)
        inner = (by_item(d_sec) * (1.0 + quadrant_rows(mods, 4, half))).reshape(64, D)
        mean = jnp.mean(inner, axis=-1, keepdims=True)
        along = jnp.mean(inner * normal, axis=-1, keepdims=True)
        back = outward + (inner - mean - normal * along) * factor
        d_resid[0, rows, :] = back.astype(BF)
        add(0, back * attn[0, rows, :].astype(F32))
        gated = (by_item(back) * quadrant_rows(mods, 2, half)).reshape(64, D)
        d_attn[rows, :] = gated.astype(BF)
        return 0

    lax.fori_loop(0, 4, rows_norm, 0)
    d_attn_t[...] = d_attn[...].T
    d_mixed[...] = dot(proj_t[...], d_attn[...], 1, 1).astype(BF)

    def head(h, _):
        rows = pl.ds(pl.multiple_of(h * HD, HD), HD)
        key_rows = pl.ds(pl.multiple_of(D + h * HD, HD), HD)
        value_rows = pl.ds(pl.multiple_of(2 * D + h * HD, HD), HD)
        queries = qkv[0, rows, :] * jnp.asarray(HD**-0.5, BF)
        keys = qkv[0, key_rows, :]
        values = qkv[0, value_rows, :]
        d_mix = d_mixed[rows, :]
        probs = jnp.exp(dot(keys, queries, 0, 0) + (bias[...] - lse[0, pl.ds(h, 1), :]))
        d_probs = dot(values, d_mix, 0, 0)
        d_qkv[value_rows, :] = dot(d_mix, probs.astype(BF), 1, 1).astype(BF)
        weighted = probs * d_probs
        inner = jnp.sum(weighted, axis=0, keepdims=True)
        d_scores = (weighted - probs * inner).astype(BF)
        d_qkv[rows, :] = (dot(keys, d_scores, 1, 0) * HD**-0.5).astype(BF)
        d_qkv[key_rows, :] = dot(queries, d_scores, 1, 1).astype(BF)
        return 0

    lax.fori_loop(0, H, head, 0, unroll=HEADS)

    @pl.when(pl.program_id(0) == pl.num_programs(0) - 1)
    def _():
        item_sums[...] = jnp.sum(sums[...], axis=2)


def attend_back(part, tag, resid, shrunk, d_second, gradient, attn, mods, qkv, lse, proj_t):
    first, count = PARTS[part]

    def pick_group(*shape):
        return pl.BlockSpec((1,) + shape, lambda g: (first + g,) + (0,) * len(shape))

    return pl.pallas_call(
        attend_back_kernel,
        grid=(count,),
        in_specs=[
            SMEM_SPEC,
            pick_group(GROUP, D),
            pick_group(GROUP, D),
            pick_group(GROUP, D),
            pick_group(GROUP, D),
            pick_group(GROUP, D),
            whole((6, 4, 8, D)),
            pick_group(3 * D, GROUP),
            pick_group(16, GROUP),
            whole((D, D)),
        ],
        out_specs=[
            group_spec(GROUP, D),
            group_spec(GROUP, D),
            pl.BlockSpec((3 * D, GROUP), lambda g: (0, g)),
            pl.BlockSpec((D, GROUP), lambda g: (0, g)),
            whole((4, 4, D)),
        ],
        out_shape=[
            jax.ShapeDtypeStruct((count, GROUP, D), BF),
            jax.ShapeDtypeStruct((count, GROUP, D), BF),
            jax.ShapeDtypeStruct((3 * D, count * GROUP), BF),
            jax.ShapeDtypeStruct((D, count * GROUP), BF),
            jax.ShapeDtypeStruct((4, 4, D), F32),
        ],
        scratch_shapes=[
            pltpu.VMEM((GROUP, GROUP), F32),
            pltpu.VMEM((D, GROUP), BF),
            pltpu.VMEM((GROUP, D), BF),
            pltpu.VMEM((4, 4, 8, D), F32),
        ],
        compiler_params=params(),
        cost_estimate=cost(9 * count),
        name=f"attend_back_{part}",
    )(tag, resid, shrunk, d_second, gradient, attn, mods, qkv, lse, proj_t)


PAIRS = 2
ROWS = 288 * PAIRS


def project_grads_kernel(
    tag_ref, d_qkv0, d_qkv1, d_attn0, d_attn1, conv_in, merged, keep_a, send_a, keep_b, send_b
):
    core = tag_ref[1]

    def against(low, high, field):
        return dot(low[...], field[0], 1, 0) + dot(
            high[...], field[1:4].reshape(3 * GROUP, D), 1, 0
        )

    grad = against(d_qkv0, d_qkv1, conv_in)
    share_out(grad, core, (0, 2), keep_a, send_a)
    share_out(grad, core, (2, 1), keep_b.at[:, :, 0:1], send_b.at[:, :, 0:1])
    grad = against(d_attn0, d_attn1, merged)
    share_out(grad, core, (0, 1), keep_b.at[:, :, 1:2], send_b.at[:, :, 1:2])


def column_specs(rows):
    return [pl.BlockSpec((rows, count * GROUP), lambda i: (i, 0)) for _, count in PARTS]


def project_grads(tag, d_qkv, d_attn, conv_in, merged):
    packed_spec = pl.BlockSpec((PAIRS, NK, 2, UR, UC), lambda i: (i, 0, 0, 0, 0))
    tall = column_specs(ROWS)
    short = column_specs(96 * PAIRS)
    return pl.pallas_call(
        project_grads_kernel,
        grid=(8 // PAIRS,),
        in_specs=[SMEM_SPEC, *tall, *short, whole((4, GROUP, D)), whole((4, GROUP, D))],
        out_specs=[packed_spec] * 4,
        out_shape=[packed_half(2)] * 4,
        compiler_params=params(),
        cost_estimate=cost(8),
        name="project_grads",
    )(tag, *d_qkv, *d_attn, conv_in, merged)


def conv_back_kernel(
    tag_ref, d_qkv0, d_qkv1, weight, norm, mods, kernel, later0, later1, g_ffn,
    d_first, pieces, d_conv, g_kernel, item_sums,
):
    step = pl.program_id(0)

    @pl.when(step == 0)
    def _():
        d_conv[...] = jnp.zeros_like(d_conv)

    d_conv[0] += dot(d_qkv0[...], weight[...], 0, 0)
    d_conv[1:4] += dot(d_qkv1[...], weight[...], 0, 0).reshape(3, GROUP, D)

    @pl.when(step == pl.num_programs(0) - 1)
    def _():
        tag = tag_ref[0]
        left, right = edge_columns(tag)
        keep = 1.0 - tag.astype(F32)

        def lanes(i, _):
            cols = pl.ds(pl.multiple_of(i * 128, 128), 128)
            taps = [jnp.broadcast_to(kernel[t : t + 1, cols], (16, 128)) for t in range(9)]
            sums = [[jnp.zeros((16, 128), F32) for _ in range(2)] for _ in range(2)]

            def load_grad(g, p):
                return d_conv[g, p * 16 : p * 16 + 16, cols]

            def load_field(g, p):
                q = 2 * (p // 8)
                shift = mods[0, q : q + 2, :, cols].reshape(16, 128)
                scale = mods[1, q : q + 2, :, cols].reshape(16, 128)
                return norm[g, p * 16 : p * 16 + 16, cols] * (1.0 + scale) + shift

            def emit(g, p, value):
                rows = slice(p * 16, p * 16 + 16)
                d_first[g, rows, cols] = value.astype(BF)
                sums[0][p // 8] += value
                sums[1][p // 8] += value * norm[g, rows, cols]

            grads = conv_back_rows(load_grad, load_field, taps, left, right, keep, emit)
            for t in range(9):
                g_kernel[t : t + 1, cols] = jnp.sum(grads[t], axis=0, keepdims=True)
            for kind in range(2):
                for item in range(4):
                    part = sums[kind][item // 2][8 * (item % 2) : 8 * (item % 2) + 8]
                    item_sums[kind, item : item + 1, cols] = jnp.sum(part, axis=0, keepdims=True)
            return 0

        lax.fori_loop(0, D // 128, lanes, 0)
        later = later0[...] + later1[...]
        rows = [item_sums[i] for i in range(2)] + [later[i] for i in range(4)]
        rows = jnp.concatenate(rows, axis=1)
        alone = jnp.concatenate([jnp.sum(rows, axis=0, keepdims=True), jnp.zeros((3, 6 * D), F32)])
        rows = jnp.where(tag == 1, rows, alone)
        slots, _, width = pieces.shape
        owners = 6 * D // width
        short, long = D // owners, FF // owners
        for j in range(owners):
            filters = jnp.concatenate(
                [
                    g_kernel[:, j * short : (j + 1) * short],
                    g_ffn[:, j * long : (j + 1) * long],
                    jnp.zeros((9, width - short - long), F32),
                ],
                axis=1,
            )
            part = [rows[:, j * width : (j + 1) * width], filters, jnp.zeros((3, width), F32)]
            part = jnp.concatenate(part, axis=0).astype(BF)
            for copy in range(slots // owners):
                pieces[j * (slots // owners) + copy] = part


def conv_back(slots, width, tag, d_qkv, weight, norm, mods, kernel, later, g_ffn):
    return pl.pallas_call(
        conv_back_kernel,
        grid=(8 // PAIRS,),
        in_specs=[
            SMEM_SPEC,
            *column_specs(ROWS),
            pl.BlockSpec((ROWS, D), lambda i: (i, 0)),
            whole((4, GROUP, D)),
            whole((2, 4, 8, D)),
            whole((9, D)),
            whole((4, 4, D)),
            whole((4, 4, D)),
            whole((9, FF)),
        ],
        out_specs=[whole((4, GROUP, D)), whole((slots, 16, width))],
        out_shape=[
            jax.ShapeDtypeStruct((4, GROUP, D), BF),
            jax.ShapeDtypeStruct((slots, 16, width), BF),
        ],
        scratch_shapes=[
            pltpu.VMEM((4, GROUP, D), F32),
            pltpu.VMEM((9, D), F32),
            pltpu.VMEM((2, 4, D), F32),
        ],
        compiler_params=params(),
        cost_estimate=cost(15),
        name="conv_back",
    )(tag, *d_qkv, weight, norm, mods, kernel, *later, g_ffn)


def finish_kernel(
    d_first, norm, factor, d_resid0, d_resid1, output0, output1, mods,
    block_output, input_grad, total,
):
    half = pl.program_id(0) // 2

    for g in range(4):
        base = (d_resid1[g - 1] if g else d_resid0[0]).astype(F32)
        value = d_first[g].astype(F32)
        normal = norm[g]
        inner = (value.reshape(4, 2, 8, D) * (1.0 + quadrant_rows(mods, 1, half))).reshape(64, D)
        mean = jnp.mean(inner, axis=-1, keepdims=True)
        along = jnp.mean(inner * normal, axis=-1, keepdims=True)
        total[g] = base + (inner - mean - normal * along) * factor[g]
    order = ungroup_matrix()
    grouped = total[...].reshape(256, D)
    high = grouped.astype(BF)
    rest = (grouped - high.astype(F32)).astype(BF)
    input_grad[...] = dot(order, high, 1, 0) + dot(order, rest, 1, 0)
    grouped = jnp.concatenate([output0[...], output1[...]], axis=0).reshape(256, D)
    block_output[...] = dot(order, grouped, 1, 0).astype(BF)


def finish(d_first, norm, factor, d_resid, output, mods):
    def split(groups, width):
        return pl.BlockSpec((groups, 64, width), lambda i: (0, i, 0))

    flat = pl.BlockSpec((256, D), lambda i: (i, 0))
    return pl.pallas_call(
        finish_kernel,
        grid=(4,),
        in_specs=[split(4, D), split(4, D), split(4, 1)]
        + [split(count, D) for _, count in PARTS] * 2
        + [whole((2, 4, 8, D))],
        out_specs=[flat, flat],
        out_shape=[
            jax.ShapeDtypeStruct((TOK, D), BF),
            jax.ShapeDtypeStruct((TOK, D), F32),
        ],
        scratch_shapes=[pltpu.VMEM((4, 64, D), F32)],
        compiler_params=params(),
        cost_estimate=cost(8),
        name="finish",
    )(d_first, norm, factor, *d_resid, *output, mods)


BOTH = ("dp", "fsdp")


def exchange(pieces):
    return lax.all_to_all(pieces, BOTH, 0, 0, tiled=True)


def units_of(weight):
    return weight.T.reshape(-1, UR, UC)


def low_units(shrink):
    return shrink.T.reshape(UR, 4, UC).transpose(1, 0, 2)


def gather_feed(nd, nf, expand, shrink):
    if (nd, nf) == (NJ, NK):
        rows = jnp.concatenate([units_of(expand), low_units(shrink)]).reshape(8 * UR, UC)
        return lax.all_gather(rows, BOTH).reshape(NJ, NK, 8, UR, UC)
    low = full_rows(shrink).reshape(NJ, UR, NK, 4, UC).transpose(0, 2, 3, 1, 4)
    return jnp.concatenate([all_units(full_rows(expand), 4), low], axis=2)


def full_rows(shard):
    rows = lax.all_gather(shard.T, "fsdp", axis=1, tiled=True)
    return lax.all_gather(rows, "dp", axis=0, tiled=True)


def all_units(weight, units):
    return weight.reshape(NJ, units, UR, NK, UC).transpose(0, 3, 1, 2, 4)


def project_turns(own):
    turns = [
        lax.ppermute(own, "dp", [(i, (i - 4 * step) % NJ) for i in range(NJ)])
        for step in range(1, 4)
    ]
    return turns


def widen(a, b, bit_a, bit_b):
    return jnp.stack([a, swap(a, bit_a)]), jnp.stack([b, swap(b, bit_b)])


def all_projections(qkv, proj):
    units = jnp.concatenate([all_units(full_rows(qkv), 3), all_units(full_rows(proj), 1)], axis=2)
    units = units.reshape((4, 2, 2) + units.shape[1:])
    first, rest = units[:, :, :, :, :2], units[:, :, :, :, 2:]
    a, b = first.transpose(2, 3, 1, 0, 4, 5, 6), rest.transpose(2, 1, 3, 0, 4, 5, 6)
    return a[0], b[0], a[1], b[1]


def pick(grads, index, axis):
    return lax.dynamic_index_in_dim(grads, index, axis, keepdims=False)


def swap(value, bit):
    if bit is None:
        return lax.ppermute(value, "fsdp", [(0, 1), (1, 0)])
    return lax.ppermute(value, "dp", [(i, i ^ bit) for i in range(NJ)])


def halve(keep, got, axis, bit):
    mine = lax.axis_index("fsdp") if bit is None else (lax.axis_index("dp") // bit) % 2
    kept = pick(keep, mine, axis) + pick(got, mine, axis)
    return kept, pick(keep, 1 - mine, axis) + pick(got, 1 - mine, axis)


def last_sends(total):
    place = lax.axis_index("dp") // 4
    return [pick(total, (place + step) % 4, 0) for step in range(1, 4)]


def last_swaps(sends):
    return [
        lax.ppermute(sent, "dp", [(i, (i + 4 * step) % NJ) for i in range(NJ)])
        for step, sent in enumerate(sends, 1)
    ]


def last_sum(total, got):
    own = pick(total, lax.axis_index("dp") // 4, 0).astype(F32)
    for value in got:
        own = own + value.astype(F32)
    return own


def after(value, *others):
    return lax.optimization_barrier((value,) + others)[0]


def own_shard(nd, nf, kind, units):
    if (nd, nf) == (NJ, NK):
        if kind == "shrink":
            return units.transpose(1, 0, 2).reshape(UR, 4 * UC).T
        return units.reshape(-1, UC).T
    if kind == "shrink":
        weight = units.transpose(0, 3, 1, 2, 4).reshape(NJ * UR, -1)
    else:
        weight = units.transpose(0, 2, 3, 1, 4).reshape(-1, NK * UC)
    columns = lax.psum_scatter(weight, "dp", scatter_dimension=0, tiled=True)
    piece = lax.psum_scatter(columns, "fsdp", scatter_dimension=1, tiled=True)
    return piece.astype(F32).T


def both_cores(keep, send):
    return jnp.stack([keep, send], axis=1).reshape((-1,) + keep.shape[1:])


def look_up(ids, step_table, class_table):
    first_row = lax.axis_index("fsdp") * step_table.shape[0]
    own = first_row + jnp.arange(step_table.shape[0], dtype=jnp.int32)
    step_hot = (ids[:, :4].reshape(-1, 1) == own[None, :]).astype(BF)
    class_hot = (ids[:, 4:].reshape(-1, 1) == own[None, :]).astype(BF)
    return step_hot, class_hot, dot(step_table, step_hot, 0, 1) + dot(class_table, class_hot, 0, 1)


def share_act(nd, cond, attn_kernel, ffn_kernel, beside):
    width, items = cond.shape
    act = jax.nn.silu(cond).astype(BF)
    filters = jnp.concatenate([attn_kernel, ffn_kernel], axis=1).reshape(-1)
    size = filters.shape[0]
    filters = jnp.pad(filters, (0, -size % items)).reshape(-1, items)
    sent = jnp.concatenate([act, filters], axis=0)[None]
    sent = lax.all_to_all(jnp.broadcast_to(sent, (nd,) + sent.shape[1:]), "dp", 0, 0, tiled=True)
    sent = after(sent, *beside)
    act_all = sent[:, :width].reshape(nd * width, items)
    filters = sent[:, width:].reshape(nd, -1)[:, :size]
    filters = filters.reshape(nd, 9, -1).astype(F32)
    attn_full = filters[:, :, : attn_kernel.shape[1]].transpose(1, 0, 2).reshape(9, -1)
    ffn_full = filters[:, :, attn_kernel.shape[1] :].transpose(1, 0, 2).reshape(9, -1)
    return act_all, attn_full, ffn_full


def exchange_columns(nd, nf, d_act):
    rows, items = d_act.shape
    half = lax.axis_index("fsdp")
    if (nd, nf) == (NJ, NK):
        spread = jnp.zeros((nd, 2 * rows // nd, items), BF)
        own = d_act.astype(BF).reshape(nd // 2, 2 * rows // nd, items)
        spread = lax.dynamic_update_slice_in_dim(spread, own, half * (nd // 2), axis=0)
        return lax.all_to_all(spread, "dp", 0, 0, tiled=True)
    spread = jnp.zeros((rows * nf, items), F32)
    spread = lax.dynamic_update_slice_in_dim(spread, d_act, half * rows, axis=0)
    spread = spread.reshape(nd, 1, -1, items)
    spread = jnp.broadcast_to(spread, (nd, nf) + spread.shape[2:])
    return exchange(spread.reshape((nd * nf,) + spread.shape[2:]))


def own_columns(nd, nf, terms):
    part = terms.astype(F32).sum(axis=0)
    if (nd, nf) != (NJ, NK):
        return part
    return part + swap(part, None)


def body(
    latents, size_tags, timesteps, classes, step_table, class_table, modulation_weight,
    attn_kernel, qkv_weight, proj_weight, expand_weight, ffn_kernel, shrink_weight, cotangent,
    *, nd, nf,
):
    slots = nd * nf
    tag = size_tags[0]
    square = (nd, nf) == (NJ, NK)
    if square:
        place = lax.axis_index("dp")
        where = [tag, place % 2, place // 4, (place // 2) % 2, lax.axis_index("fsdp")]
        where = jnp.stack(where).astype(jnp.int32)
    else:
        where = jnp.stack([tag] + [jnp.int32(0)] * 4)
    packed = gather_feed(nd, nf, expand_weight, shrink_weight)
    tokens, gradient, norm, factor = prepare(latents, cotangent)
    mine = jnp.concatenate([timesteps[0], classes[0]])[None]
    mine = jnp.broadcast_to(mine, (slots, 8))
    if square:
        own = jnp.concatenate([units_of(qkv_weight), units_of(proj_weight)])
        own = after(own, mine)
        turns = project_turns(own)
    ids = exchange(mine)
    if square:
        ids = after(ids, norm)
    step_hot, class_hot, part = look_up(ids, step_table, class_table)
    if square:
        cond = part + swap(part, None)
        own, *turns = (after(x, cond) for x in (own, *turns))
        a = jnp.stack([own[:2]] + [turn[:2] for turn in turns])
        b = jnp.stack([own[2:]] + [turn[2:] for turn in turns])
        next_a, next_b = swap(a, 2), swap(b, None)
        a, b = jnp.stack([a, next_a]), jnp.stack([b, next_b])
        beside = (a, b)
    else:
        beside = ()
        cond = lax.psum(part, "fsdp")
    act_all, attn_full, ffn_full = share_act(nd, cond, attn_kernel, ffn_kernel, beside)
    if square:
        next_a, next_b = swap(a, None), swap(b, 2)
        next_a, next_b = after(next_a, act_all), after(next_b, act_all)
    height, width = modulation_weight.shape
    act_rows = lax.dynamic_slice_in_dim(
        act_all, lax.axis_index("fsdp") * height, height, axis=0
    )
    terms = dot(act_rows, modulation_weight, 0, 0)
    terms = exchange(terms.reshape(slots, 1, 4 * width)).reshape(nd, nf, 4, width)
    if square:
        a, b = jnp.stack([a, next_a]), jnp.stack([b, next_b])
        projections = (a, b, swap(a, 1), swap(b, 1))
    else:
        projections = all_projections(qkv_weight, proj_weight)
    mod_rows = terms.sum(axis=1).transpose(1, 0, 2).reshape(4, nd * width)
    chosen = jnp.where(tag == 1, mod_rows, mod_rows[:1])
    mods = jnp.broadcast_to(chosen.reshape(4, 6, 1, D).transpose(1, 0, 2, 3), (6, 4, 8, D))

    conv_in = first_conv(size_tags, norm, mods, attn_full)
    qkv, merged, attn, resid, second, lse, proj_t, full_qkv = attend(
        where, conv_in, tokens, mods, projections
    )
    shrunk, d_second, keep_e, send_e, keep_s, send_s, g_ffn = feed(
        where, second, gradient, mods, packed, ffn_full
    )
    back = (gradient, attn, mods, qkv, lse)
    if square:
        got_e, got_s = swap(send_e, 1), swap(send_s, 1)
    output0, d_resid0, d_qkv0, d_attn0, later0 = attend_back(
        0, where, resid, shrunk, d_second, *back, proj_t
    )

    def grid(value):
        return value.reshape((4, 2) + value.shape[1:])

    if square:
        got_e, got_s = after(got_e, d_qkv0), after(got_s, d_qkv0)
        keep_e, out_e = halve(grid(keep_e), grid(got_e), 2, None)
        keep_s, out_s = halve(grid(keep_s), grid(got_s), 1, 2)
        d_second = after(d_second, out_e, out_s)
        got_e, got_s = swap(out_e, None), swap(out_s, 2)
    output1, d_resid1, d_qkv1, d_attn1, later1 = attend_back(
        1, where, resid, shrunk, d_second, *back, proj_t
    )
    if square:
        got_e, got_s = after(got_e, d_attn1), after(got_s, d_attn1)
        keep_e, out_e = halve(keep_e, got_e, 1, 2)
        keep_s, out_s = halve(keep_s, got_s, 1, None)
        d_attn0 = after(d_attn0, out_e, out_s)
        got_e, got_s = swap(out_e, 2), swap(out_s, None)
    d_qkv = (d_qkv0, d_qkv1)
    keep_a, send_a, keep_b, send_b = project_grads(
        where, d_qkv, (d_attn0, d_attn1), conv_in, merged
    )
    if square:
        got_e, got_s = after(got_e, keep_a), after(got_s, keep_a)
        got_a, got_b = swap(send_a, 1), swap(send_b, 1)
        e = halve(keep_e.reshape((2, 2) + keep_e.shape[1:]), got_e.reshape((2, 2) + got_e.shape[1:]), 1, 4)
        s = halve(keep_s.reshape((2, 2) + keep_s.shape[1:]), got_s.reshape((2, 2) + got_s.shape[1:]), 1, 4)
        feeding, out_f = (jnp.concatenate(pair, axis=1) for pair in zip(e, s))
        keep_a, out_a = halve(grid(keep_a), grid(got_a), 2, None)
        keep_b, out_b = halve(grid(keep_b), grid(got_b), 1, 2)
        full_qkv = after(full_qkv, out_a, out_b, out_f)
        got_a, got_b, got_f = swap(out_a, None), swap(out_b, 2), swap(out_f, 4)
    d_first, pieces = conv_back(
        slots, width, where, d_qkv, full_qkv, norm, mods, attn_full, (later0, later1), g_ffn
    )
    if square:
        got_a, got_b, got_f = (after(x, d_first) for x in (got_a, got_b, got_f))
        keep_a, out_a = halve(keep_a, got_a, 1, 2)
        keep_b, out_b = halve(keep_b, got_b, 1, None)
        feeding, out_f = halve(feeding, got_f, 0, 8)
    if square:
        d_first = after(d_first, out_a, out_b, out_f, pieces)
        got_a, got_b, got_f = swap(out_a, 2), swap(out_b, None), swap(out_f, 8)
    got = exchange(pieces)
    block_output, input_grad = finish(
        d_first, norm, factor, (d_resid0, d_resid1), (output0, output1), mods
    )
    if square:
        got = after(got, input_grad)
    d_mod_all = got[:, :4].reshape(slots * 4, width)
    d_act = dot(modulation_weight, d_mod_all, 1, 1)
    if square:
        got_a, got_b = after(got_a, d_act), after(got_b, d_act)
        total = jnp.concatenate([keep_a + got_a, keep_b + got_b], axis=1)
        sends = last_sends(total)
        last = last_swaps(sends)
    own_act = exchange_columns(nd, nf, d_act)
    if square:
        got_f = after(got_f, own_act)
        total = last_sum(total, last)
        feeding = feeding.astype(F32) + got_f.astype(F32)
        cuts = [total[:3], total[3:], feeding[:4], feeding[4:]]
    else:
        first, rest = both_cores(keep_a, send_a), both_cores(keep_b, send_b)
        cuts = [
            jnp.concatenate([first, rest[:, :, :1]], axis=2),
            rest[:, :, 1:],
            both_cores(keep_e, send_e),
            both_cores(keep_s, send_s),
        ]
    shards = [
        own_shard(nd, nf, kind, cut)
        for kind, cut in zip(("qkv", "proj", "expand", "shrink"), cuts)
    ]
    cut = attn_kernel.shape[1]
    filters = got[:, 4:13, : cut + ffn_kernel.shape[1]].astype(F32).sum(axis=0)
    modulation_grad = dot(act_rows, d_mod_all, 1, 0)
    gate = jax.nn.sigmoid(cond)
    d_cond = own_columns(nd, nf, own_act)
    d_cond = d_cond * (gate * (1.0 + cond * (1.0 - gate)))

    def table_grad(hot):
        return lax.dot_general(
            hot.astype(F32), d_cond, (((0,), (1,)), ((), ())), precision=lax.Precision.HIGHEST
        )

    return (
        block_output,
        input_grad,
        table_grad(step_hot),
        table_grad(class_hot),
        modulation_grad,
        filters[:, :cut],
        shards[0],
        shards[1],
        shards[2],
        filters[:, cut:],
        shards[3],
    )


def solution(mesh):
    matrix = P("fsdp", "dp")
    rows = P(BOTH, None)
    filters = P(None, "dp")
    in_specs = (
        rows, P(BOTH), rows, rows, matrix, matrix, matrix, filters, matrix, matrix, matrix,
        filters, matrix, rows,
    )
    out_specs = (
        rows, rows, matrix, matrix, matrix, filters, matrix, matrix, matrix, filters, matrix,
    )
    run = functools.partial(body, nd=mesh.shape["dp"], nf=mesh.shape["fsdp"])
    return jax.shard_map(run, mesh=mesh, in_specs=in_specs, out_specs=out_specs, check_vma=False)
```

```python
import functools

import jax
import jax.numpy as jnp
from jax import lax
from jax.experimental import pallas as pl
from jax.experimental.pallas import tpu as pltpu
from jax.sharding import PartitionSpec as P

D = 768
H = 12
HD = 64
FF = 3072
SIDE = 32
GROUP = 256
TOK = SIDE * SIDE
EPS = 1e-06
NJ, NK, UR, UC = 16, 2, 48, 384
CHUNK = 768
HEADS = 6
PARTS = ((0, 1), (1, 3))
MIB = 1024 * 1024
BF = jnp.bfloat16
F32 = jnp.float32
GELU_A = 0.7978845608028654
GELU_B = GELU_A * 0.044715


def dot(left, right, left_dim, right_dim):
    return lax.dot_general(
        left, right, (((left_dim,), (right_dim,)), ((), ())), preferred_element_type=F32
    )


def params(limit=56):
    return pltpu.CompilerParams(vmem_limit_bytes=limit * MIB)


def cost(micros):
    return pl.CostEstimate(flops=int(micros * 1e8), transcendentals=0, bytes_accessed=4 * MIB)


def whole(shape):
    zeros = (0,) * len(shape)
    return pl.BlockSpec(shape, lambda *ids: zeros, pipeline_mode=pl.Buffered(1))


SMEM_SPEC = pl.BlockSpec(memory_space=pltpu.SMEM)


def group_place(natural):
    pair, odd_row = natural // 64, (natural // 32) % 2
    column, odd_column = (natural % 32) // 2, natural % 2
    return (2 * odd_row + odd_column) * 64 + pair * 16 + column


def ungroup_matrix():
    natural = lax.broadcasted_iota(jnp.int32, (256, 256), 0)
    grouped = lax.broadcasted_iota(jnp.int32, (256, 256), 1)
    return jnp.where(group_place(natural) == grouped, 1.0, 0.0).astype(BF)


def group_matrix():
    natural = lax.broadcasted_iota(jnp.int32, (256, 256), 1)
    grouped = lax.broadcasted_iota(jnp.int32, (256, 256), 0)
    return jnp.where(group_place(natural) == grouped, 1.0, 0.0).astype(BF)


def norm_stats(values):
    centre = values - jnp.mean(values, axis=-1, keepdims=True)
    variance = jnp.mean(centre * centre, axis=-1, keepdims=True)
    scale = lax.rsqrt(variance + EPS)
    return centre * scale, scale


def prepare_kernel(latents, cotangent, tokens, gradient, norm, scale):
    order = group_matrix()
    gathered = dot(order, latents[...], 1, 0)
    gradient[...] = dot(order, cotangent[...], 1, 0).reshape(4, 64, D).astype(BF)
    tokens[...] = gathered.reshape(4, 64, D).astype(BF)
    normal, factor = norm_stats(gathered)
    norm[...] = normal.reshape(4, 64, D)
    scale[...] = factor.reshape(4, 64, 1)


def prepare(latents, cotangent):
    flat = pl.BlockSpec((256, D), lambda i: (i, 0))
    split = pl.BlockSpec((4, 64, D), lambda i: (0, i, 0))
    return pl.pallas_call(
        prepare_kernel,
        grid=(4,),
        in_specs=[flat, flat],
        out_specs=[split, split, split, pl.BlockSpec((4, 64, 1), lambda i: (0, i, 0))],
        out_shape=[
            jax.ShapeDtypeStruct((4, GROUP, D), BF),
            jax.ShapeDtypeStruct((4, GROUP, D), BF),
            jax.ShapeDtypeStruct((4, GROUP, D), F32),
            jax.ShapeDtypeStruct((4, GROUP, 1), F32),
        ],
        compiler_params=params(),
        cost_estimate=cost(6),
        name="prepare",
    )(latents, cotangent)


def edge_columns(tag):
    place = lax.broadcasted_iota(jnp.int32, (16, 128), 0)
    left = jnp.where((place == 0) | ((place == 8) & (tag == 1)), 0.0, 1.0)
    right = jnp.where((place == 15) | ((place == 7) & (tag == 1)), 0.0, 1.0)
    return left, right


def neighbours(even, odd, left, right):
    return pltpu.roll(odd, 1, 0) * left, pltpu.roll(even, 15, 0) * right


def conv_rows(load, kernel, left, right, keep, emit):
    above = None
    partial = None
    for row in range(SIDE + 1):
        taps = None
        if row < SIDE:
            a, p = row % 2, row // 2
            even, odd = load(2 * a, p), load(2 * a + 1, p)
            odd_left, even_right = neighbours(even, odd, left, right)
            taps = []
            for tap in range(3):
                k = [kernel[3 * tap + b] for b in range(3)]
                taps.append(
                    (
                        k[0] * odd_left + k[1] * even + k[2] * odd,
                        k[0] * even + k[1] * odd + k[2] * even_right,
                    )
                )
        crossing = row == SIDE // 2
        if partial is not None:
            a, p = (row - 1) % 2, (row - 1) // 2
            for b in range(2):
                value = partial[b]
                if taps is not None:
                    below = taps[2][b]
                    value = value + (below * keep if crossing else below)
                emit(2 * a + b, p, value)
        if taps is not None:
            partial = []
            for b in range(2):
                value = taps[1][b]
                if above is not None:
                    value = value + (above[b] * keep if crossing else above[b])
                partial.append(value)
            above = taps[0]


def conv_back_rows(load_grad, load_field, kernel, left, right, keep, emit):
    sums = [jnp.zeros((16, 128), F32) for _ in range(9)]
    from_above = None
    partial = None
    field_above = None
    field = (load_field(0, 0), load_field(1, 0))
    for row in range(SIDE + 1):
        crossing = row == SIDE // 2
        taps = None
        if row < SIDE:
            a, p = row % 2, row // 2
            even, odd = load_grad(2 * a, p), load_grad(2 * a + 1, p)
            odd_left, even_right = neighbours(even, odd, left, right)
            picks = ((odd, even, odd_left), (even_right, odd, even))
            taps = []
            for tap in range(3):
                k = [kernel[3 * tap + b] for b in range(3)]
                taps.append(
                    tuple(k[0] * x[0] + k[1] * x[1] + k[2] * x[2] for x in picks)
                )
            field_below = None
            if row + 1 < SIDE:
                a, p = (row + 1) % 2, (row + 1) // 2
                field_below = (load_field(2 * a, p), load_field(2 * a + 1, p))
            for tap, rows in enumerate((field_above, field, field_below)):
                if rows is None:
                    continue
                if (tap == 0 and crossing) or (tap == 2 and row + 1 == SIDE // 2):
                    rows = (rows[0] * keep, rows[1] * keep)
                for b in range(3):
                    sums[3 * tap + b] = (
                        sums[3 * tap + b] + rows[0] * picks[0][b] + rows[1] * picks[1][b]
                    )
            field_above, field = field, field_below
        if partial is not None:
            a, p = (row - 1) % 2, (row - 1) // 2
            for b in range(2):
                value = partial[b]
                if taps is not None:
                    value = value + (taps[0][b] * keep if crossing else taps[0][b])
                emit(2 * a + b, p, value)
        if taps is not None:
            partial = []
            for b in range(2):
                value = taps[1][b]
                if from_above is not None:
                    value = value + (from_above[b] * keep if crossing else from_above[b])
                partial.append(value)
            from_above = taps[2]
    return sums


def first_conv_kernel(tag_ref, norm, mods, kernel, out):
    tag = tag_ref[0]
    left, right = edge_columns(tag)
    keep = 1.0 - tag.astype(F32)

    def lanes(i, _):
        cols = pl.ds(pl.multiple_of(i * 128, 128), 128)
        taps = [jnp.broadcast_to(kernel[t : t + 1, cols], (16, 128)) for t in range(9)]

        def load(g, p):
            q = 2 * (p // 8)
            shift = mods[0, q : q + 2, :, cols].reshape(16, 128)
            scale = mods[1, q : q + 2, :, cols].reshape(16, 128)
            return norm[g, p * 16 : p * 16 + 16, cols] * (1.0 + scale) + shift

        def emit(g, p, value):
            out[g, p * 16 : p * 16 + 16, cols] = value.astype(BF)

        conv_rows(load, taps, left, right, keep, emit)
        return 0

    lax.fori_loop(0, 2, lanes, 0)


def first_conv(tag, norm, mods, kernel):
    lanes = pl.BlockSpec((4, GROUP, 256), lambda i: (0, 0, i))
    return pl.pallas_call(
        first_conv_kernel,
        grid=(D // 256,),
        in_specs=[
            SMEM_SPEC,
            lanes,
            pl.BlockSpec((2, 4, 8, 256), lambda i: (0, 0, 0, i)),
            pl.BlockSpec((9, 256), lambda i: (0, i)),
        ],
        out_specs=lanes,
        out_shape=jax.ShapeDtypeStruct((4, GROUP, D), BF),
        compiler_params=params(),
        cost_estimate=cost(6),
        name="first_conv",
    )(tag, norm, mods, kernel)


def join_rows(block, target):
    rows = block.shape[0] * block.shape[2] * UR
    for k in range(NK):
        target[:, k * UC : (k + 1) * UC] = block[:, k].reshape(rows, UC)


def share_out(rows, core, units, keep, send):
    first, count = units
    for k in range(NK):
        part = rows[:, k * UC : (k + 1) * UC].astype(BF)
        part = part.reshape(-1, 2, part.shape[0] // (keep.shape[0] * 2), UC)
        even, odd = part[:, 0], part[:, 1]
        for target, value in (
            (keep, jnp.where(core == 0, even, odd)),
            (send, jnp.where(core == 0, odd, even)),
        ):
            whole_units = value.reshape(value.shape[0], -1, UR, UC)
            target[:, k] = whole_units[:, first : first + count]


def quadrant_rows(mods, index, half):
    return mods[index, pl.ds(2 * half, 2)].reshape(1, 2, 8, D)


def item_bias(tag):
    def label(dim):
        place = lax.broadcasted_iota(jnp.int32, (GROUP, GROUP), dim)
        return 2 * (place // 128) + (place % 16) // 8

    return jnp.where((label(0) == label(1)) | (tag == 0), 0.0, -1e30)


def attend_kernel(
    where, conv_in, tokens, mods, own_a, own_b, peer_a, peer_b,
    qkv, merged, attn, resid, second, lse, proj_t, full_qkv,
    full_proj, bias, mixed_t,
):
    @pl.when(pl.program_id(0) == 0)
    def _():
        core, z, y, x = (where[i] for i in range(1, 5))
        for owner in range(NJ):
            step = (owner // 4 - z + 4) % 4
            side = (owner // 2) % 2 ^ y
            mine = core == owner % 2
            for k in range(NK):
                cols = slice(k * UC, (k + 1) * UC)
                a = jnp.where(mine, own_a[k ^ x, side, step], peer_a[k ^ x, side, step])
                b = jnp.where(mine, own_b[side, k ^ x, step], peer_b[side, k ^ x, step])
                start = owner * 3 * UR
                full_qkv[start : start + 2 * UR, cols] = a.reshape(2 * UR, UC)
                full_qkv[start + 2 * UR : start + 3 * UR, cols] = b[0]
                full_proj[owner * UR : (owner + 1) * UR, cols] = b[1]
        proj_t[...] = full_proj[...].T
        bias[...] = item_bias(where[0])

    qkv[0] = dot(full_qkv[...], conv_in[0], 1, 1).astype(BF)

    def head(h, _):
        rows = pl.ds(pl.multiple_of(h * HD, HD), HD)
        queries = qkv[0, rows, :] * jnp.asarray(HD**-0.5, BF)
        keys = qkv[0, pl.ds(pl.multiple_of(D + h * HD, HD), HD), :]
        values = qkv[0, pl.ds(pl.multiple_of(2 * D + h * HD, HD), HD), :]
        scores = dot(keys, queries, 0, 0) + bias[...]
        highest = jnp.max(scores, axis=0, keepdims=True)
        raised = jnp.exp(scores - highest)
        total = jnp.sum(raised, axis=0, keepdims=True)
        probs = (raised * (1.0 / total)).astype(BF)
        lse[0, pl.ds(h, 1), :] = highest + jnp.log(total)
        mixed_t[rows, :] = dot(values, probs, 1, 0).astype(BF)
        return 0

    lax.fori_loop(0, H, head, 0, unroll=HEADS)
    merged[0] = mixed_t[...].T
    projected = dot(merged[0], full_proj[...], 1, 1)
    attn[0] = projected.astype(BF)
    gate = mods[2].reshape(2, 1, 2, 8, D)
    resid[0] = (
        tokens[0].astype(F32) + (projected.reshape(2, 8, 2, 8, D) * gate).reshape(GROUP, D)
    )

    def rows_norm(i, _):
        rows = pl.ds(pl.multiple_of(i * 64, 64), 64)
        normal, _ = norm_stats(resid[0, rows, :])
        half = i // 2
        scaled = normal.reshape(4, 2, 8, D) * (1.0 + quadrant_rows(mods, 4, half))
        value = scaled + quadrant_rows(mods, 3, half)
        second[0, rows, :] = value.reshape(64, D).astype(BF)
        return 0

    lax.fori_loop(0, 4, rows_norm, 0)


def group_spec(*shape):
    return pl.BlockSpec((1,) + shape, lambda g: (g,) + (0,) * len(shape))


def attend(where, conv_in, tokens, mods, projections):
    relative = (2, 2, 4, 2, UR, UC)
    return pl.pallas_call(
        attend_kernel,
        grid=(4,),
        in_specs=[
            SMEM_SPEC,
            group_spec(GROUP, D),
            group_spec(GROUP, D),
            whole((6, 4, 8, D)),
        ]
        + [whole(relative)] * 4,
        out_specs=[
            group_spec(3 * D, GROUP),
            group_spec(GROUP, D),
            group_spec(GROUP, D),
            group_spec(GROUP, D),
            group_spec(GROUP, D),
            group_spec(16, GROUP),
            whole((D, D)),
            whole((3 * D, D)),
        ],
        out_shape=[
            jax.ShapeDtypeStruct((4, 3 * D, GROUP), BF),
            jax.ShapeDtypeStruct((4, GROUP, D), BF),
            jax.ShapeDtypeStruct((4, GROUP, D), BF),
            jax.ShapeDtypeStruct((4, GROUP, D), F32),
            jax.ShapeDtypeStruct((4, GROUP, D), BF),
            jax.ShapeDtypeStruct((4, 16, GROUP), F32),
            jax.ShapeDtypeStruct((D, D), BF),
            jax.ShapeDtypeStruct((3 * D, D), BF),
        ],
        scratch_shapes=[
            pltpu.VMEM((D, D), BF),
            pltpu.VMEM((GROUP, GROUP), F32),
            pltpu.VMEM((D, GROUP), BF),
        ],
        compiler_params=params(),
        cost_estimate=cost(38),
        name="attend",
    )(where, conv_in, tokens, mods, *projections)


def feed_kernel(
    tag_ref, second, gradient, mods, w_expand, w_shrink, kernel,
    shrunk, d_second, keep_expand, send_expand, keep_shrink, send_shrink, g_kernel,
    d_shrunk, d_shrunk_t, expand, shrink, field, slope, hidden, d_field, shrunk_sum, second_sum,
):
    step = pl.program_id(0)
    tag, core = tag_ref[0], tag_ref[1]

    @pl.when(step == 0)
    def _():
        gate = mods[5].reshape(1, 2, 1, 2, 8, D)
        value = gradient[...].astype(F32).reshape(4, 2, 8, 2, 8, D) * gate
        d_shrunk[...] = value.reshape(TOK, D).astype(BF)
        d_shrunk_t[...] = d_shrunk[...].T
        shrunk_sum[...] = jnp.zeros_like(shrunk_sum)
        second_sum[...] = jnp.zeros_like(second_sum)

    join_rows(w_expand, expand)
    for q in range(2):
        shrink[:, q * UC : (q + 1) * UC] = w_shrink[:, 0, q].reshape(D, UC)
    left, right = edge_columns(tag)
    keep = 1.0 - tag.astype(F32)
    field[...] = dot(second[...].reshape(TOK, D), expand[...], 1, 1).reshape(4, GROUP, CHUNK)
    slope[...] = dot(d_shrunk[...], shrink[...], 1, 0).reshape(4, GROUP, CHUNK)

    def lanes(i, _):
        cols = pl.ds(pl.multiple_of(i * 128, 128), 128)
        taps = [jnp.broadcast_to(kernel[t : t + 1, cols], (16, 128)) for t in range(9)]

        def load(g, p):
            return field[g, p * 16 : p * 16 + 16, cols]

        def load_slope(g, p):
            return slope[g, p * 16 : p * 16 + 16, cols]

        def emit(g, p, value):
            square = value * value
            half = 0.5 + 0.5 * jnp.tanh(value * (GELU_A + GELU_B * square))
            out = value * half
            hidden[g, p * 16 : p * 16 + 16, cols] = out.astype(BF)
            rate = half + (out - out * half) * (2.0 * GELU_A + 6.0 * GELU_B * square)
            slope[g, p * 16 : p * 16 + 16, cols] = load_slope(g, p) * rate

        conv_rows(load, taps, left, right, keep, emit)

        def emit_back(g, p, value):
            d_field[g, p * 16 : p * 16 + 16, cols] = value.astype(BF)

        sums = conv_back_rows(load_slope, load, taps, left, right, keep, emit_back)
        for t in range(9):
            g_kernel[t : t + 1, cols] = jnp.sum(sums[t], axis=0, keepdims=True)
        return 0

    lax.fori_loop(0, CHUNK // 128, lanes, 0)
    hid = hidden[...].reshape(TOK, CHUNK)
    d_fld = d_field[...].reshape(TOK, CHUNK)
    grad = dot(d_shrunk_t[...], hid, 1, 0).astype(BF)
    for q in range(2):
        part = grad[:, q * UC : (q + 1) * UC].reshape(NJ // 2, 2, UR, UC)
        keep_shrink[:, 0, q] = jnp.where(core == 0, part[:, 0], part[:, 1])
        send_shrink[:, 0, q] = jnp.where(core == 0, part[:, 1], part[:, 0])
    share_out(dot(d_fld, second[...].reshape(TOK, D), 0, 0), core, (0, 4), keep_expand, send_expand)
    shrunk_sum[...] += dot(hid, shrink[...], 1, 1).reshape(4, GROUP, D)
    second_sum[...] += dot(d_fld, expand[...], 1, 0).reshape(4, GROUP, D)

    @pl.when(step == pl.num_programs(0) - 1)
    def _():
        shrunk[...] = shrunk_sum[...].astype(BF)
        d_second[...] = second_sum[...].astype(BF)


def packed_half(units):
    return jax.ShapeDtypeStruct((NJ // 2, NK, units, UR, UC), BF)


def feed(tag, second, gradient, mods, packed, kernel):
    half = NJ // 2
    expand_spec = pl.BlockSpec((2, NK, 4, UR, UC), lambda c: (c, 0, 0, 0, 0))
    shrink_spec = pl.BlockSpec((half, 1, 2, UR, UC), lambda c: (0, c // 2, c % 2, 0, 0))
    return pl.pallas_call(
        feed_kernel,
        grid=(FF // CHUNK,),
        in_specs=[
            SMEM_SPEC,
            whole((4, GROUP, D)),
            whole((4, GROUP, D)),
            whole((6, 4, 8, D)),
            pl.BlockSpec((4, NK, 4, UR, UC), lambda c: (c, 0, 0, 0, 0)),
            pl.BlockSpec((NJ, 1, 2, UR, UC), lambda c: (0, c // 2, 2 + c % 2, 0, 0)),
            pl.BlockSpec((9, CHUNK), lambda c: (0, c)),
        ],
        out_specs=[
            whole((4, GROUP, D)),
            whole((4, GROUP, D)),
            expand_spec,
            expand_spec,
            shrink_spec,
            shrink_spec,
            pl.BlockSpec((9, CHUNK), lambda c: (0, c)),
        ],
        out_shape=[
            jax.ShapeDtypeStruct((4, GROUP, D), BF),
            jax.ShapeDtypeStruct((4, GROUP, D), BF),
            packed_half(4),
            packed_half(4),
            packed_half(4),
            packed_half(4),
            jax.ShapeDtypeStruct((9, FF), F32),
        ],
        scratch_shapes=[
            pltpu.VMEM((TOK, D), BF),
            pltpu.VMEM((D, TOK), BF),
            pltpu.VMEM((CHUNK, D), BF),
            pltpu.VMEM((D, CHUNK), BF),
            pltpu.VMEM((4, GROUP, CHUNK), F32),
            pltpu.VMEM((4, GROUP, CHUNK), F32),
            pltpu.VMEM((4, GROUP, CHUNK), BF),
            pltpu.VMEM((4, GROUP, CHUNK), BF),
            pltpu.VMEM((4, GROUP, D), F32),
            pltpu.VMEM((4, GROUP, D), F32),
        ],
        compiler_params=params(60),
        cost_estimate=cost(38),
        name="feed",
    )(tag, second, gradient, mods, packed, packed, kernel)


def attend_back_kernel(
    tag_ref, resid, shrunk, d_second, gradient, attn, mods, qkv, lse, proj_t,
    output, d_resid, d_qkv, d_attn_t, item_sums,
    bias, d_mixed, d_attn, sums,
):
    @pl.when(pl.program_id(0) == 0)
    def _():
        bias[...] = item_bias(tag_ref[0])
        sums[...] = jnp.zeros_like(sums)

    def rows_norm(i, _):
        rows = pl.ds(pl.multiple_of(i * 64, 64), 64)
        half = i // 2
        base = resid[0, rows, :]
        normal, factor = norm_stats(base)
        shrunk_rows = shrunk[0, rows, :].astype(F32)
        outward = gradient[0, rows, :].astype(F32)
        d_sec = d_second[0, rows, :].astype(F32)

        def by_item(value):
            return value.reshape(4, 2, 8, D)

        def add(index, value):
            sums[index, pl.ds(2 * half, 2)] += jnp.sum(by_item(value), axis=0)

        gated = (by_item(shrunk_rows) * quadrant_rows(mods, 5, half)).reshape(64, D)
        output[0, rows, :] = (base + gated).astype(BF)
        add(3, outward * shrunk_rows)
        add(1, d_sec)
        add(2, d_sec * normal)
        inner = (by_item(d_sec) * (1.0 + quadrant_rows(mods, 4, half))).reshape(64, D)
        mean = jnp.mean(inner, axis=-1, keepdims=True)
        along = jnp.mean(inner * normal, axis=-1, keepdims=True)
        back = outward + (inner - mean - normal * along) * factor
        d_resid[0, rows, :] = back.astype(BF)
        add(0, back * attn[0, rows, :].astype(F32))
        gated = (by_item(back) * quadrant_rows(mods, 2, half)).reshape(64, D)
        d_attn[rows, :] = gated.astype(BF)
        return 0

    lax.fori_loop(0, 4, rows_norm, 0)
    d_attn_t[...] = d_attn[...].T
    d_mixed[...] = dot(proj_t[...], d_attn[...], 1, 1).astype(BF)

    def head(h, _):
        rows = pl.ds(pl.multiple_of(h * HD, HD), HD)
        key_rows = pl.ds(pl.multiple_of(D + h * HD, HD), HD)
        value_rows = pl.ds(pl.multiple_of(2 * D + h * HD, HD), HD)
        queries = qkv[0, rows, :] * jnp.asarray(HD**-0.5, BF)
        keys = qkv[0, key_rows, :]
        values = qkv[0, value_rows, :]
        d_mix = d_mixed[rows, :]
        probs = jnp.exp(dot(keys, queries, 0, 0) + (bias[...] - lse[0, pl.ds(h, 1), :]))
        d_probs = dot(values, d_mix, 0, 0)
        d_qkv[value_rows, :] = dot(d_mix, probs.astype(BF), 1, 1).astype(BF)
        weighted = probs * d_probs
        inner = jnp.sum(weighted, axis=0, keepdims=True)
        d_scores = (weighted - probs * inner).astype(BF)
        d_qkv[rows, :] = (dot(keys, d_scores, 1, 0) * HD**-0.5).astype(BF)
        d_qkv[key_rows, :] = dot(queries, d_scores, 1, 1).astype(BF)
        return 0

    lax.fori_loop(0, H, head, 0, unroll=HEADS)

    @pl.when(pl.program_id(0) == pl.num_programs(0) - 1)
    def _():
        item_sums[...] = jnp.sum(sums[...], axis=2)


def attend_back(part, tag, resid, shrunk, d_second, gradient, attn, mods, qkv, lse, proj_t):
    first, count = PARTS[part]

    def pick_group(*shape):
        return pl.BlockSpec((1,) + shape, lambda g: (first + g,) + (0,) * len(shape))

    return pl.pallas_call(
        attend_back_kernel,
        grid=(count,),
        in_specs=[
            SMEM_SPEC,
            pick_group(GROUP, D),
            pick_group(GROUP, D),
            pick_group(GROUP, D),
            pick_group(GROUP, D),
            pick_group(GROUP, D),
            whole((6, 4, 8, D)),
            pick_group(3 * D, GROUP),
            pick_group(16, GROUP),
            whole((D, D)),
        ],
        out_specs=[
            group_spec(GROUP, D),
            group_spec(GROUP, D),
            pl.BlockSpec((3 * D, GROUP), lambda g: (0, g)),
            pl.BlockSpec((D, GROUP), lambda g: (0, g)),
            whole((4, 4, D)),
        ],
        out_shape=[
            jax.ShapeDtypeStruct((count, GROUP, D), BF),
            jax.ShapeDtypeStruct((count, GROUP, D), BF),
            jax.ShapeDtypeStruct((3 * D, count * GROUP), BF),
            jax.ShapeDtypeStruct((D, count * GROUP), BF),
            jax.ShapeDtypeStruct((4, 4, D), F32),
        ],
        scratch_shapes=[
            pltpu.VMEM((GROUP, GROUP), F32),
            pltpu.VMEM((D, GROUP), BF),
            pltpu.VMEM((GROUP, D), BF),
            pltpu.VMEM((4, 4, 8, D), F32),
        ],
        compiler_params=params(),
        cost_estimate=cost(9 * count),
        name=f"attend_back_{part}",
    )(tag, resid, shrunk, d_second, gradient, attn, mods, qkv, lse, proj_t)


PAIRS = 4
ROWS = 288 * PAIRS


def project_grads_kernel(
    tag_ref, d_qkv0, d_qkv1, d_attn0, d_attn1, conv_in, merged, keep_a, send_a, keep_b, send_b
):
    core = tag_ref[1]

    def against(low, high, field):
        return dot(low[...], field[0], 1, 0) + dot(
            high[...], field[1:4].reshape(3 * GROUP, D), 1, 0
        )

    grad = against(d_qkv0, d_qkv1, conv_in)
    share_out(grad, core, (0, 2), keep_a, send_a)
    share_out(grad, core, (2, 1), keep_b.at[:, :, 0:1], send_b.at[:, :, 0:1])
    grad = against(d_attn0, d_attn1, merged)
    share_out(grad, core, (0, 1), keep_b.at[:, :, 1:2], send_b.at[:, :, 1:2])


def column_specs(rows):
    return [pl.BlockSpec((rows, count * GROUP), lambda i: (i, 0)) for _, count in PARTS]


def project_grads(tag, d_qkv, d_attn, conv_in, merged):
    packed_spec = pl.BlockSpec((PAIRS, NK, 2, UR, UC), lambda i: (i, 0, 0, 0, 0))
    tall = column_specs(ROWS)
    short = column_specs(96 * PAIRS)
    return pl.pallas_call(
        project_grads_kernel,
        grid=(8 // PAIRS,),
        in_specs=[SMEM_SPEC, *tall, *short, whole((4, GROUP, D)), whole((4, GROUP, D))],
        out_specs=[packed_spec] * 4,
        out_shape=[packed_half(2)] * 4,
        compiler_params=params(),
        cost_estimate=cost(8),
        name="project_grads",
    )(tag, *d_qkv, *d_attn, conv_in, merged)


def conv_back_kernel(
    tag_ref, d_qkv0, d_qkv1, weight, norm, mods, kernel, later0, later1, g_ffn,
    d_first, pieces, d_conv, g_kernel, item_sums,
):
    step = pl.program_id(0)

    @pl.when(step == 0)
    def _():
        d_conv[...] = jnp.zeros_like(d_conv)

    d_conv[0] += dot(d_qkv0[...], weight[...], 0, 0)
    d_conv[1:4] += dot(d_qkv1[...], weight[...], 0, 0).reshape(3, GROUP, D)

    @pl.when(step == pl.num_programs(0) - 1)
    def _():
        tag = tag_ref[0]
        left, right = edge_columns(tag)
        keep = 1.0 - tag.astype(F32)

        def lanes(i, _):
            cols = pl.ds(pl.multiple_of(i * 128, 128), 128)
            taps = [jnp.broadcast_to(kernel[t : t + 1, cols], (16, 128)) for t in range(9)]
            sums = [[jnp.zeros((16, 128), F32) for _ in range(2)] for _ in range(2)]

            def load_grad(g, p):
                return d_conv[g, p * 16 : p * 16 + 16, cols]

            def load_field(g, p):
                q = 2 * (p // 8)
                shift = mods[0, q : q + 2, :, cols].reshape(16, 128)
                scale = mods[1, q : q + 2, :, cols].reshape(16, 128)
                return norm[g, p * 16 : p * 16 + 16, cols] * (1.0 + scale) + shift

            def emit(g, p, value):
                rows = slice(p * 16, p * 16 + 16)
                d_first[g, rows, cols] = value.astype(BF)
                sums[0][p // 8] += value
                sums[1][p // 8] += value * norm[g, rows, cols]

            grads = conv_back_rows(load_grad, load_field, taps, left, right, keep, emit)
            for t in range(9):
                g_kernel[t : t + 1, cols] = jnp.sum(grads[t], axis=0, keepdims=True)
            for kind in range(2):
                for item in range(4):
                    part = sums[kind][item // 2][8 * (item % 2) : 8 * (item % 2) + 8]
                    item_sums[kind, item : item + 1, cols] = jnp.sum(part, axis=0, keepdims=True)
            return 0

        lax.fori_loop(0, D // 128, lanes, 0)
        later = later0[...] + later1[...]
        rows = [item_sums[i] for i in range(2)] + [later[i] for i in range(4)]
        rows = jnp.concatenate(rows, axis=1)
        alone = jnp.concatenate([jnp.sum(rows, axis=0, keepdims=True), jnp.zeros((3, 6 * D), F32)])
        rows = jnp.where(tag == 1, rows, alone)
        slots, _, width = pieces.shape
        owners = 6 * D // width
        short, long = D // owners, FF // owners
        for j in range(owners):
            filters = jnp.concatenate(
                [
                    g_kernel[:, j * short : (j + 1) * short],
                    g_ffn[:, j * long : (j + 1) * long],
                    jnp.zeros((9, width - short - long), F32),
                ],
                axis=1,
            )
            part = [rows[:, j * width : (j + 1) * width], filters, jnp.zeros((3, width), F32)]
            part = jnp.concatenate(part, axis=0).astype(BF)
            for copy in range(slots // owners):
                pieces[j * (slots // owners) + copy] = part


def conv_back(slots, width, tag, d_qkv, weight, norm, mods, kernel, later, g_ffn):
    return pl.pallas_call(
        conv_back_kernel,
        grid=(8 // PAIRS,),
        in_specs=[
            SMEM_SPEC,
            *column_specs(ROWS),
            pl.BlockSpec((ROWS, D), lambda i: (i, 0)),
            whole((4, GROUP, D)),
            whole((2, 4, 8, D)),
            whole((9, D)),
            whole((4, 4, D)),
            whole((4, 4, D)),
            whole((9, FF)),
        ],
        out_specs=[whole((4, GROUP, D)), whole((slots, 16, width))],
        out_shape=[
            jax.ShapeDtypeStruct((4, GROUP, D), BF),
            jax.ShapeDtypeStruct((slots, 16, width), BF),
        ],
        scratch_shapes=[
            pltpu.VMEM((4, GROUP, D), F32),
            pltpu.VMEM((9, D), F32),
            pltpu.VMEM((2, 4, D), F32),
        ],
        compiler_params=params(),
        cost_estimate=cost(15),
        name="conv_back",
    )(tag, *d_qkv, weight, norm, mods, kernel, *later, g_ffn)


def finish_kernel(
    d_first, norm, factor, d_resid0, d_resid1, output0, output1, mods,
    block_output, input_grad, total,
):
    half = pl.program_id(0) // 2

    for g in range(4):
        base = (d_resid1[g - 1] if g else d_resid0[0]).astype(F32)
        value = d_first[g].astype(F32)
        normal = norm[g]
        inner = (value.reshape(4, 2, 8, D) * (1.0 + quadrant_rows(mods, 1, half))).reshape(64, D)
        mean = jnp.mean(inner, axis=-1, keepdims=True)
        along = jnp.mean(inner * normal, axis=-1, keepdims=True)
        total[g] = base + (inner - mean - normal * along) * factor[g]
    order = ungroup_matrix()
    grouped = total[...].reshape(256, D)
    high = grouped.astype(BF)
    rest = (grouped - high.astype(F32)).astype(BF)
    input_grad[...] = dot(order, high, 1, 0) + dot(order, rest, 1, 0)
    grouped = jnp.concatenate([output0[...], output1[...]], axis=0).reshape(256, D)
    block_output[...] = dot(order, grouped, 1, 0).astype(BF)


def finish(d_first, norm, factor, d_resid, output, mods):
    def split(groups, width):
        return pl.BlockSpec((groups, 64, width), lambda i: (0, i, 0))

    flat = pl.BlockSpec((256, D), lambda i: (i, 0))
    return pl.pallas_call(
        finish_kernel,
        grid=(4,),
        in_specs=[split(4, D), split(4, D), split(4, 1)]
        + [split(count, D) for _, count in PARTS] * 2
        + [whole((2, 4, 8, D))],
        out_specs=[flat, flat],
        out_shape=[
            jax.ShapeDtypeStruct((TOK, D), BF),
            jax.ShapeDtypeStruct((TOK, D), F32),
        ],
        scratch_shapes=[pltpu.VMEM((4, 64, D), F32)],
        compiler_params=params(),
        cost_estimate=cost(8),
        name="finish",
    )(d_first, norm, factor, *d_resid, *output, mods)


BOTH = ("dp", "fsdp")


def exchange(pieces):
    return lax.all_to_all(pieces, BOTH, 0, 0, tiled=True)


def units_of(weight):
    return weight.T.reshape(-1, UR, UC)


def low_units(shrink):
    return shrink.T.reshape(UR, 4, UC).transpose(1, 0, 2)


def gather_feed(nd, nf, expand, shrink):
    if (nd, nf) == (NJ, NK):
        rows = jnp.concatenate([units_of(expand), low_units(shrink)]).reshape(8 * UR, UC)
        return lax.all_gather(rows, BOTH).reshape(NJ, NK, 8, UR, UC)
    low = full_rows(shrink).reshape(NJ, UR, NK, 4, UC).transpose(0, 2, 3, 1, 4)
    return jnp.concatenate([all_units(full_rows(expand), 4), low], axis=2)


def full_rows(shard):
    rows = lax.all_gather(shard.T, "fsdp", axis=1, tiled=True)
    return lax.all_gather(rows, "dp", axis=0, tiled=True)


def all_units(weight, units):
    return weight.reshape(NJ, units, UR, NK, UC).transpose(0, 3, 1, 2, 4)


def project_turns(own):
    turns = [
        lax.ppermute(own, "dp", [(i, (i - 4 * step) % NJ) for i in range(NJ)])
        for step in range(1, 4)
    ]
    return turns


def widen(a, b, bit_a, bit_b):
    return jnp.stack([a, swap(a, bit_a)]), jnp.stack([b, swap(b, bit_b)])


def all_projections(qkv, proj):
    units = jnp.concatenate([all_units(full_rows(qkv), 3), all_units(full_rows(proj), 1)], axis=2)
    units = units.reshape((4, 2, 2) + units.shape[1:])
    first, rest = units[:, :, :, :, :2], units[:, :, :, :, 2:]
    a, b = first.transpose(2, 3, 1, 0, 4, 5, 6), rest.transpose(2, 1, 3, 0, 4, 5, 6)
    return a[0], b[0], a[1], b[1]


def pick(grads, index, axis):
    return lax.dynamic_index_in_dim(grads, index, axis, keepdims=False)


def swap(value, bit):
    if bit is None:
        return lax.ppermute(value, "fsdp", [(0, 1), (1, 0)])
    return lax.ppermute(value, "dp", [(i, i ^ bit) for i in range(NJ)])


def halve(keep, got, axis, bit):
    mine = lax.axis_index("fsdp") if bit is None else (lax.axis_index("dp") // bit) % 2
    kept = pick(keep, mine, axis) + pick(got, mine, axis)
    return kept, pick(keep, 1 - mine, axis) + pick(got, 1 - mine, axis)


def last_sends(total):
    place = lax.axis_index("dp") // 4
    return [pick(total, (place + step) % 4, 0) for step in range(1, 4)]


def last_swaps(sends):
    return [
        lax.ppermute(sent, "dp", [(i, (i + 4 * step) % NJ) for i in range(NJ)])
        for step, sent in enumerate(sends, 1)
    ]


def last_sum(total, got):
    own = pick(total, lax.axis_index("dp") // 4, 0).astype(F32)
    for value in got:
        own = own + value.astype(F32)
    return own


def after(value, *others):
    return lax.optimization_barrier((value,) + others)[0]


def own_shard(nd, nf, kind, units):
    if (nd, nf) == (NJ, NK):
        if kind == "shrink":
            return units.transpose(1, 0, 2).reshape(UR, 4 * UC).T
        return units.reshape(-1, UC).T
    if kind == "shrink":
        weight = units.transpose(0, 3, 1, 2, 4).reshape(NJ * UR, -1)
    else:
        weight = units.transpose(0, 2, 3, 1, 4).reshape(-1, NK * UC)
    columns = lax.psum_scatter(weight, "dp", scatter_dimension=0, tiled=True)
    piece = lax.psum_scatter(columns, "fsdp", scatter_dimension=1, tiled=True)
    return piece.astype(F32).T


def both_cores(keep, send):
    return jnp.stack([keep, send], axis=1).reshape((-1,) + keep.shape[1:])


def look_up(ids, step_table, class_table):
    first_row = lax.axis_index("fsdp") * step_table.shape[0]
    own = first_row + jnp.arange(step_table.shape[0], dtype=jnp.int32)
    step_hot = (ids[:, :4].reshape(-1, 1) == own[None, :]).astype(BF)
    class_hot = (ids[:, 4:].reshape(-1, 1) == own[None, :]).astype(BF)
    return step_hot, class_hot, dot(step_table, step_hot, 0, 1) + dot(class_table, class_hot, 0, 1)


def share_act(nd, cond, attn_kernel, ffn_kernel, beside):
    width, items = cond.shape
    act = jax.nn.silu(cond).astype(BF)
    filters = jnp.concatenate([attn_kernel, ffn_kernel], axis=1).reshape(-1)
    size = filters.shape[0]
    filters = jnp.pad(filters, (0, -size % items)).reshape(-1, items)
    sent = jnp.concatenate([act, filters], axis=0)[None]
    sent = lax.all_to_all(jnp.broadcast_to(sent, (nd,) + sent.shape[1:]), "dp", 0, 0, tiled=True)
    sent = after(sent, *beside)
    act_all = sent[:, :width].reshape(nd * width, items)
    filters = sent[:, width:].reshape(nd, -1)[:, :size]
    filters = filters.reshape(nd, 9, -1).astype(F32)
    attn_full = filters[:, :, : attn_kernel.shape[1]].transpose(1, 0, 2).reshape(9, -1)
    ffn_full = filters[:, :, attn_kernel.shape[1] :].transpose(1, 0, 2).reshape(9, -1)
    return act_all, attn_full, ffn_full


def exchange_columns(nd, nf, d_act):
    rows, items = d_act.shape
    half = lax.axis_index("fsdp")
    if (nd, nf) == (NJ, NK):
        spread = jnp.zeros((nd, 2 * rows // nd, items), BF)
        own = d_act.astype(BF).reshape(nd // 2, 2 * rows // nd, items)
        spread = lax.dynamic_update_slice_in_dim(spread, own, half * (nd // 2), axis=0)
        return lax.all_to_all(spread, "dp", 0, 0, tiled=True)
    spread = jnp.zeros((rows * nf, items), F32)
    spread = lax.dynamic_update_slice_in_dim(spread, d_act, half * rows, axis=0)
    spread = spread.reshape(nd, 1, -1, items)
    spread = jnp.broadcast_to(spread, (nd, nf) + spread.shape[2:])
    return exchange(spread.reshape((nd * nf,) + spread.shape[2:]))


def own_columns(nd, nf, terms):
    part = terms.astype(F32).sum(axis=0)
    if (nd, nf) != (NJ, NK):
        return part
    return part + swap(part, None)


def body(
    latents, size_tags, timesteps, classes, step_table, class_table, modulation_weight,
    attn_kernel, qkv_weight, proj_weight, expand_weight, ffn_kernel, shrink_weight, cotangent,
    *, nd, nf,
):
    slots = nd * nf
    tag = size_tags[0]
    square = (nd, nf) == (NJ, NK)
    if square:
        place = lax.axis_index("dp")
        where = [tag, place % 2, place // 4, (place // 2) % 2, lax.axis_index("fsdp")]
        where = jnp.stack(where).astype(jnp.int32)
    else:
        where = jnp.stack([tag] + [jnp.int32(0)] * 4)
    packed = gather_feed(nd, nf, expand_weight, shrink_weight)
    tokens, gradient, norm, factor = prepare(latents, cotangent)
    mine = jnp.concatenate([timesteps[0], classes[0]])[None]
    mine = jnp.broadcast_to(mine, (slots, 8))
    if square:
        own = jnp.concatenate([units_of(qkv_weight), units_of(proj_weight)])
        own = after(own, mine)
        turns = project_turns(own)
    ids = exchange(mine)
    if square:
        ids = after(ids, norm)
    step_hot, class_hot, part = look_up(ids, step_table, class_table)
    if square:
        cond = part + swap(part, None)
        own, *turns = (after(x, cond) for x in (own, *turns))
        a = jnp.stack([own[:2]] + [turn[:2] for turn in turns])
        b = jnp.stack([own[2:]] + [turn[2:] for turn in turns])
        next_a, next_b = swap(a, 2), swap(b, None)
        a, b = jnp.stack([a, next_a]), jnp.stack([b, next_b])
        beside = (a, b)
    else:
        beside = ()
        cond = lax.psum(part, "fsdp")
    act_all, attn_full, ffn_full = share_act(nd, cond, attn_kernel, ffn_kernel, beside)
    if square:
        next_a, next_b = swap(a, None), swap(b, 2)
        next_a, next_b = after(next_a, act_all), after(next_b, act_all)
    height, width = modulation_weight.shape
    act_rows = lax.dynamic_slice_in_dim(
        act_all, lax.axis_index("fsdp") * height, height, axis=0
    )
    terms = dot(act_rows, modulation_weight, 0, 0)
    terms = exchange(terms.reshape(slots, 1, 4 * width)).reshape(nd, nf, 4, width)
    if square:
        a, b = jnp.stack([a, next_a]), jnp.stack([b, next_b])
        projections = (a, b, swap(a, 1), swap(b, 1))
    else:
        projections = all_projections(qkv_weight, proj_weight)
    mod_rows = terms.sum(axis=1).transpose(1, 0, 2).reshape(4, nd * width)
    chosen = jnp.where(tag == 1, mod_rows, mod_rows[:1])
    mods = jnp.broadcast_to(chosen.reshape(4, 6, 1, D).transpose(1, 0, 2, 3), (6, 4, 8, D))

    conv_in = first_conv(size_tags, norm, mods, attn_full)
    qkv, merged, attn, resid, second, lse, proj_t, full_qkv = attend(
        where, conv_in, tokens, mods, projections
    )
    shrunk, d_second, keep_e, send_e, keep_s, send_s, g_ffn = feed(
        where, second, gradient, mods, packed, ffn_full
    )
    back = (gradient, attn, mods, qkv, lse)
    if square:
        got_e, got_s = swap(send_e, 1), swap(send_s, 1)
    output0, d_resid0, d_qkv0, d_attn0, later0 = attend_back(
        0, where, resid, shrunk, d_second, *back, proj_t
    )

    def grid(value):
        return value.reshape((4, 2) + value.shape[1:])

    if square:
        got_e, got_s = after(got_e, d_qkv0), after(got_s, d_qkv0)
        keep_e, out_e = halve(grid(keep_e), grid(got_e), 2, None)
        keep_s, out_s = halve(grid(keep_s), grid(got_s), 1, 2)
        d_second = after(d_second, out_e, out_s)
        got_e, got_s = swap(out_e, None), swap(out_s, 2)
    output1, d_resid1, d_qkv1, d_attn1, later1 = attend_back(
        1, where, resid, shrunk, d_second, *back, proj_t
    )
    if square:
        got_e, got_s = after(got_e, d_attn1), after(got_s, d_attn1)
        keep_e, out_e = halve(keep_e, got_e, 1, 2)
        keep_s, out_s = halve(keep_s, got_s, 1, None)
        d_attn0 = after(d_attn0, out_e, out_s)
        got_e, got_s = swap(out_e, 2), swap(out_s, None)
    d_qkv = (d_qkv0, d_qkv1)
    keep_a, send_a, keep_b, send_b = project_grads(
        where, d_qkv, (d_attn0, d_attn1), conv_in, merged
    )
    if square:
        got_e, got_s = after(got_e, keep_a), after(got_s, keep_a)
        got_a, got_b = swap(send_a, 1), swap(send_b, 1)
        e = halve(keep_e.reshape((2, 2) + keep_e.shape[1:]), got_e.reshape((2, 2) + got_e.shape[1:]), 1, 4)
        s = halve(keep_s.reshape((2, 2) + keep_s.shape[1:]), got_s.reshape((2, 2) + got_s.shape[1:]), 1, 4)
        feeding, out_f = (jnp.concatenate(pair, axis=1) for pair in zip(e, s))
        keep_a, out_a = halve(grid(keep_a), grid(got_a), 2, None)
        keep_b, out_b = halve(grid(keep_b), grid(got_b), 1, 2)
        full_qkv = after(full_qkv, out_a, out_b, out_f)
        got_a, got_b, got_f = swap(out_a, None), swap(out_b, 2), swap(out_f, 4)
    d_first, pieces = conv_back(
        slots, width, where, d_qkv, full_qkv, norm, mods, attn_full, (later0, later1), g_ffn
    )
    if square:
        got_a, got_b, got_f = (after(x, d_first) for x in (got_a, got_b, got_f))
        keep_a, out_a = halve(keep_a, got_a, 1, 2)
        keep_b, out_b = halve(keep_b, got_b, 1, None)
        feeding, out_f = halve(feeding, got_f, 0, 8)
    if square:
        d_first = after(d_first, out_a, out_b, out_f, pieces)
        got_a, got_b, got_f = swap(out_a, 2), swap(out_b, None), swap(out_f, 8)
    got = exchange(pieces)
    block_output, input_grad = finish(
        d_first, norm, factor, (d_resid0, d_resid1), (output0, output1), mods
    )
    if square:
        got = after(got, input_grad)
    d_mod_all = got[:, :4].reshape(slots * 4, width)
    d_act = dot(modulation_weight, d_mod_all, 1, 1)
    if square:
        got_a, got_b = after(got_a, d_act), after(got_b, d_act)
        total = jnp.concatenate([keep_a + got_a, keep_b + got_b], axis=1)
        sends = last_sends(total)
        last = last_swaps(sends)
    own_act = exchange_columns(nd, nf, d_act)
    if square:
        got_f = after(got_f, own_act)
        total = last_sum(total, last)
        feeding = feeding.astype(F32) + got_f.astype(F32)
        cuts = [total[:3], total[3:], feeding[:4], feeding[4:]]
    else:
        first, rest = both_cores(keep_a, send_a), both_cores(keep_b, send_b)
        cuts = [
            jnp.concatenate([first, rest[:, :, :1]], axis=2),
            rest[:, :, 1:],
            both_cores(keep_e, send_e),
            both_cores(keep_s, send_s),
        ]
    shards = [
        own_shard(nd, nf, kind, cut)
        for kind, cut in zip(("qkv", "proj", "expand", "shrink"), cuts)
    ]
    cut = attn_kernel.shape[1]
    filters = got[:, 4:13, : cut + ffn_kernel.shape[1]].astype(F32).sum(axis=0)
    modulation_grad = dot(act_rows, d_mod_all, 1, 0)
    gate = jax.nn.sigmoid(cond)
    d_cond = own_columns(nd, nf, own_act)
    d_cond = d_cond * (gate * (1.0 + cond * (1.0 - gate)))

    def table_grad(hot):
        return lax.dot_general(
            hot.astype(F32), d_cond, (((0,), (1,)), ((), ())), precision=lax.Precision.HIGHEST
        )

    return (
        block_output,
        input_grad,
        table_grad(step_hot),
        table_grad(class_hot),
        modulation_grad,
        filters[:, :cut],
        shards[0],
        shards[1],
        shards[2],
        filters[:, cut:],
        shards[3],
    )


def solution(mesh):
    matrix = P("fsdp", "dp")
    rows = P(BOTH, None)
    filters = P(None, "dp")
    in_specs = (
        rows, P(BOTH), rows, rows, matrix, matrix, matrix, filters, matrix, matrix, matrix,
        filters, matrix, rows,
    )
    out_specs = (
        rows, rows, matrix, matrix, matrix, filters, matrix, matrix, matrix, filters, matrix,
    )
    run = functools.partial(body, nd=mesh.shape["dp"], nf=mesh.shape["fsdp"])
    return jax.shard_map(run, mesh=mesh, in_specs=in_specs, out_specs=out_specs, check_vma=False)
```
